32 devices in a mesh: dp: 2 (over core), seq: 16 (over z, y, x).
Axes of the slice: x: 2, y: 2, z: 4, core: 2. Of those that a mesh axis runs over, the one named last changes fastest.
Arguments:
- block_input: bfloat16 [8192, 1024], P(('dp', 'seq')), may hold values from -6 to 6
- lengths: int32 [2, 2], P('dp'), may hold values from 1 to 1537, 2050 in all within a row
- attn_gain: float32 [1024], replicated, may hold values from 0.5 to 1.5
- w_query: bfloat16 [1024, 1024], replicated, may hold values from -0.1875 to 0.1875
- w_key: bfloat16 [1024, 2048], replicated, may hold values from -0.1875 to 0.1875
- w_value: bfloat16 [1024, 2048], replicated, may hold values from -0.1875 to 0.1875
- w_outgate: bfloat16 [1024, 1024], replicated, may hold values from -0.1875 to 0.1875
- w_beta: bfloat16 [1024, 16], replicated, may hold values from -0.1875 to 0.1875
- w_decay: bfloat16 [1024, 8], replicated, may hold values from -0.1875 to 0.1875
- beta_bias: float32 [16], replicated, may hold values from -3 to 1
- decay_rate: float32 [8], replicated, may hold values from 0.0002 to 0.05
- conv_query: float32 [4, 1024], replicated, may hold values from -3 to 3
- conv_key: float32 [4, 2048], replicated, may hold values from -3 to 3
- conv_value: float32 [4, 2048], replicated, may hold values from -3 to 3
- out_gain: float32 [128], replicated, may hold values from 0.5 to 1.5
- w_out: bfloat16 [1024, 1024], replicated, may hold values from -0.1875 to 0.1875
- mlp_gain: float32 [1024], replicated, may hold values from 0.5 to 1.5
- w_gate: bfloat16 [1024, 2816], replicated, may hold values from -0.1875 to 0.1875
- w_up: bfloat16 [1024, 2816], replicated, may hold values from -0.1875 to 0.1875
- w_down: bfloat16 [2816, 1024], replicated, may hold values from -0.109375 to 0.109375
- out_grad: bfloat16 [8192, 1024], P(('dp', 'seq')), may hold values from -6 to 6
Outputs:
- block_output: bfloat16 [8192, 1024], P(('dp', 'seq'))
- input_grad: bfloat16 [8192, 1024], P(('dp', 'seq'))
- grad_attn_gain: float32 [1024], P(('dp', 'seq'))
- grad_w_query: float32 [1024, 1024], P(('dp', 'seq'))
- grad_w_key: float32 [1024, 2048], P(('dp', 'seq'))
- grad_w_value: float32 [1024, 2048], P(('dp', 'seq'))
- grad_w_outgate: float32 [1024, 1024], P(('dp', 'seq'))
- grad_w_beta: float32 [1024, 16], P(('dp', 'seq'))
- grad_w_decay: float32 [1024, 8], P(('dp', 'seq'))
- grad_beta_bias: float32 [16], replicated
- grad_decay_rate: float32 [8], replicated
- grad_conv_query: float32 [4, 1024], replicated
- grad_conv_key: float32 [4, 2048], replicated
- grad_conv_value: float32 [4, 2048], replicated
- grad_out_gain: float32 [128], replicated
- grad_w_out: float32 [1024, 1024], P(None, ('dp', 'seq'))
- grad_mlp_gain: float32 [1024], P(('dp', 'seq'))
- grad_w_gate: float32 [1024, 2816], P(('dp', 'seq'))
- grad_w_up: float32 [1024, 2816], P(('dp', 'seq'))
- grad_w_down: float32 [2816, 1024], P(None, ('dp', 'seq'))
The draws below stay inside these ranges and needn't reach their ends.
Inputs may be any that keep to these rules, and one draw needn't show every extreme that they name: `lengths`: row r lists the 2 sequences of group r in packing order; the longest is at most 2560 tokens and every row sums to 2050.
All inputs are finite; a program needn't handle non-finite values.
Results may differ from the reference program's by a relative error of at most 0.022.
Values may be sent and summed in bfloat16 or wider, within the bound.
A program may use at most 512 MiB of HBM per device.

```python
import math
import jax
import jax.numpy as jnp
import numpy as np
from jax import lax

D = 1024
HEADS = 8
HEAD_DIM = 128
REFLECTS = 2
KW = 4
FF = 2816
BLOCK = 64
SHORTEST = 1024
GROUP = 4096
ALL_TOKENS = 8192
NSEQ = 2
LONGEST = 2560
N_DP = 2


def spiked(values, rng, source, target, blocks, factor):
    owner, partner = [(jnp.arange(values.shape[dim]) // (values.shape[dim] // blocks)).reshape([-1 if axis == dim else 1 for axis in range(values.ndim)]) for dim in (source, target)]
    chosen = jax.random.permutation(rng, blocks)[partner]
    strong = (owner == chosen) | (owner == (partner + blocks // 2) % blocks)
    return jnp.where(strong, factor * values, values)


def levels(stream_key, dims, split, low, largest):
    def one(axis_at, blocks):
        heights = jax.random.uniform(jax.random.fold_in(jax.random.fold_in(stream_key, 6), axis_at), (blocks,), jnp.float32, low / len(split), largest / len(split))
        return jnp.repeat(jnp.exp(heights), dims[axis_at] // blocks).reshape((-1,) + (1,) * (len(dims) - axis_at - 1))

    factor_of = one(*split[0])
    for cut in split[1:]:
        factor_of = factor_of * one(*cut)
    return factor_of


def split_up(count, total, bound, skew):
    portions = [(1 << 20) // math.isqrt(grade ** skew) + 1 for grade in range(2, count + 1)]
    surplus, given = total - bound - (count - 1), [1] * (count - 1)
    while surplus > 0:
        candidates = [i for i in range(count - 1) if given[i] < bound]
        pool, left = sum([portions[i] for i in candidates]), surplus
        for i in candidates:
            extra = min(bound - given[i], max(1, left * portions[i] // pool), surplus)
            given[i] = given[i] + extra
            surplus = surplus - extra
    return np.array([bound] + given)


def ragged(stream_key, count, total, reach, slope):
    if count == 2:
        one = jax.random.randint(stream_key, (), max(1, total - reach), min(reach, total - 1) + 1)
        return jnp.stack([one, total - one])
    sizes = jnp.asarray(split_up(count, total, reach, slope), jnp.int32)
    couples = (count - 1) // 2
    source_of, taker = sizes[1:1 + 2 * couples:2], sizes[2:2 + 2 * couples:2]
    margin = jnp.minimum(source_of - 1, reach - taker)
    shifted = jax.random.randint(jax.random.fold_in(stream_key, 1), (couples,), 0, 1 << 20) % (margin + 1)
    sizes = sizes.at[1:1 + 2 * couples:2].set(source_of - shifted).at[2:2 + 2 * couples:2].set(taker + shifted)
    return sizes[jax.random.permutation(jax.random.fold_in(stream_key, 2), count)]


def normal_values(own_key, extent, deviation, limit, pieces=(), kind=jnp.bfloat16):
    drawn = jax.random.normal(own_key, extent, jnp.float32) * deviation
    if len(pieces) > 0:
        drawn = levels(own_key, extent, pieces, -0.22, 0.18) * drawn
    return jnp.clip(drawn, min=-limit, max=limit).astype(kind)


def heavy_noise(own_key, extent, width, most, shards, heavy, kind=jnp.bfloat16):
    drawn = width * jax.random.normal(own_key, extent, jnp.float32)
    if shards:
        drawn = drawn * levels(own_key, extent, shards, -0.22, 0.18)
    return jnp.clip(spiked(drawn, jax.random.fold_in(own_key, 3), *heavy), -most, most).astype(kind)


def setup_inputs(seed: int = 0) -> dict:
    seeds = jax.random.split(jax.random.key(seed), 22)
    return {
        "block_input": heavy_noise(seeds[0], (ALL_TOKENS, D), 1.0, 6.0, ((0, 32),), (0, 1, 32, 2.75)),
        "lengths": jax.vmap(lambda own: ragged(own, NSEQ, GROUP - NSEQ * (SHORTEST - 1), LONGEST - SHORTEST + 1, 2))(jax.random.split(seeds[1], N_DP)).reshape((N_DP, NSEQ)).astype(jnp.int32),
        "attn_gain": jnp.clip(1.0 + 0.1 * jax.random.normal(seeds[2], (D,), jnp.float32), 0.5, 1.5),
        "w_query": normal_values(seeds[3], (D, HEADS * HEAD_DIM), D ** -0.5, 0.1875),
        "w_key": normal_values(seeds[4], (D, REFLECTS * HEADS * HEAD_DIM), D ** -0.5, 0.1875),
        "w_value": normal_values(seeds[5], (D, REFLECTS * HEADS * HEAD_DIM), D ** -0.5, 0.1875),
        "w_outgate": normal_values(seeds[6], (D, HEADS * HEAD_DIM), D ** -0.5, 0.1875),
        "w_beta": normal_values(seeds[7], (D, REFLECTS * HEADS), D ** -0.5, 0.1875),
        "w_decay": normal_values(seeds[8], (D, HEADS), D ** -0.5, 0.1875),
        "beta_bias": jnp.clip(jax.random.uniform(seeds[9], (REFLECTS * HEADS,), jnp.float32, -3.0, 1.0), -3.0, 1.0),
        "decay_rate": jnp.clip(jnp.exp(jax.random.uniform(seeds[10], (HEADS,), jnp.float32, math.log(0.0002), math.log(0.05))), 0.0002, 0.05),
        "conv_query": normal_values(seeds[11], (KW, HEADS * HEAD_DIM), KW ** -0.5, 3.0, (), jnp.float32),
        "conv_key": normal_values(seeds[12], (KW, REFLECTS * HEADS * HEAD_DIM), KW ** -0.5, 3.0, (), jnp.float32),
        "conv_value": normal_values(seeds[13], (KW, REFLECTS * HEADS * HEAD_DIM), KW ** -0.5, 3.0, (), jnp.float32),
        "out_gain": jnp.clip(1.0 + 0.1 * jax.random.normal(seeds[14], (HEAD_DIM,), jnp.float32), 0.5, 1.5),
        "w_out": normal_values(seeds[15], (HEADS * HEAD_DIM, D), (HEADS * HEAD_DIM) ** -0.5, 0.1875),
        "mlp_gain": jnp.clip(1.0 + 0.1 * jax.random.normal(seeds[16], (D,), jnp.float32), 0.5, 1.5),
        "w_gate": normal_values(seeds[17], (D, FF), D ** -0.5, 0.1875),
        "w_up": normal_values(seeds[18], (D, FF), D ** -0.5, 0.1875),
        "w_down": normal_values(seeds[19], (FF, D), FF ** -0.5, 0.109375),
        "out_grad": normal_values(seeds[20], (ALL_TOKENS, D), 1.0, 6.0, ((0, 32),)),
    }


@jax.custom_vjp
def low(v):
    return lax.optimization_barrier(v.astype(jnp.bfloat16)).astype(jnp.float32)

@jax.custom_vjp
def low_back(v):
    return v

def low_keep(v):
    return (low(v), None)

def low_pass(kept, grad):
    return (grad,)

def back_keep(v):
    return (v, None)

def back_low(kept, grad):
    return (low(grad),)
low.defvjp(low_keep, low_pass)
low_back.defvjp(back_keep, back_low)
EXACT_PRECISION = lax.Precision.HIGHEST
RESET_LOG = -80.0

def rms_scale(field, gain, epsilon):
    return field * lax.rsqrt(lax.optimization_barrier(jnp.mean(field * field, axis=-1, keepdims=True)) + epsilon) * gain

def seq_positions(extras, first, total_rows):
    sizes = (extras + (SHORTEST - 1)).astype(jnp.int32)
    ends = jnp.cumsum(sizes).astype(jnp.int32)
    starts = (ends - sizes).astype(jnp.int32)
    row_ids = (first + jnp.arange(total_rows, dtype=jnp.int32)).astype(jnp.int32)
    inside = (row_ids[:, None] >= starts[None, :]) & (row_ids[:, None] < ends[None, :])
    return (row_ids - lax.optimization_barrier(jnp.sum(jnp.where(inside, starts[None, :], 0), axis=1))).astype(jnp.int32)

def short_conv(padded, taps, places):
    total_rows = places.shape[0]
    result = jnp.zeros((total_rows, padded.shape[1]), jnp.float32)
    for offset in range(KW):
        back_steps = KW - 1 - offset
        live_rows = (places >= back_steps).astype(jnp.float32)[:, None]
        result = result + taps[offset] * padded[offset:offset + total_rows] * live_rows
    return result

def features(places, ext_query, ext_key, ext_value, conv_query, conv_key, conv_value, beta_in, decay_in, beta_bias, decay_rate):
    total_rows = places.shape[0]
    head_count = decay_in.shape[1]
    queries = jax.nn.silu(short_conv(ext_query, conv_query, places)).reshape(total_rows, head_count, -1)
    every_key_row = jax.nn.silu(short_conv(ext_key, conv_key, places)).reshape(total_rows, head_count, REFLECTS, -1)
    values_all = jax.nn.silu(short_conv(ext_value, conv_value, places)).reshape(total_rows, head_count, REFLECTS, -1)
    head_width = queries.shape[-1]
    queries = queries * lax.rsqrt(lax.optimization_barrier(jnp.sum(queries * queries, axis=-1, keepdims=True)) + 1e-06) * head_width ** (-0.5)
    every_key_row = every_key_row * lax.rsqrt(lax.optimization_barrier(jnp.sum(every_key_row * every_key_row, axis=-1, keepdims=True)) + 1e-06)
    betas = jax.nn.sigmoid(beta_in + beta_bias).reshape(total_rows, head_count, REFLECTS)
    log_rate = -decay_rate * jax.nn.softplus(decay_in)
    log_rate = jnp.where((places == 0)[:, None], RESET_LOG, log_rate)
    log_steps = jnp.concatenate([log_rate[:, :, None], jnp.zeros((total_rows, head_count, REFLECTS - 1), jnp.float32)], axis=-1)
    return (queries, every_key_row, values_all, betas, log_steps)

def step_layout(field, blocks):
    head_count = field.shape[1]
    moved = field.reshape((blocks, BLOCK) + field.shape[1:])
    moved = jnp.moveaxis(moved, 2, 1)
    return moved.reshape((blocks, head_count, BLOCK * REFLECTS) + field.shape[3:])

def block_step(state, parts):
    queries, every_key_row, values_all, betas, log_steps = parts
    steps = every_key_row.shape[1]
    cumul = jnp.cumsum(log_steps, axis=-1)
    index = jnp.arange(steps)
    lower_mask = index[:, None] >= index[None, :]
    strict_mask = index[:, None] > index[None, :]
    fading = jnp.exp(jnp.where(lower_mask, cumul[:, :, None] - cumul[:, None, :], -jnp.inf))
    key_inner_products = jnp.einsum('yqe,yfe->yqf', every_key_row, every_key_row, precision=EXACT_PRECISION)
    system = jnp.eye(steps, dtype=jnp.float32) + jnp.where(strict_mask, fading * key_inner_products, 0.0) * betas[:, :, None]
    growth = jnp.exp(cumul)
    known = jnp.einsum('hnd,hde->hne', every_key_row, state, precision=EXACT_PRECISION)
    rhs = betas[:, :, None] * (values_all - growth[:, :, None] * known)
    delta = jax.scipy.linalg.solve_triangular(system, rhs, lower=True, unit_diagonal=True)
    query_fade = fading[:, REFLECTS - 1::REFLECTS, :] * jnp.einsum('htd,hnd->htn', queries, every_key_row, precision=EXACT_PRECISION)
    result = growth[:, REFLECTS - 1::REFLECTS, None] * jnp.einsum('htd,hde->hte', queries, state, precision=EXACT_PRECISION)
    result = result + jnp.einsum('htn,hne->hte', query_fade, delta, precision=EXACT_PRECISION)
    tail_keys = jnp.exp(cumul[:, -1:] - cumul)[:, :, None] * every_key_row
    new_state = growth[:, -1][:, None, None] * state + jnp.einsum('hnd,hne->hde', tail_keys, delta, precision=EXACT_PRECISION)
    return (new_state, result)

def fdot(first_op, second_op):
    return jnp.dot(first_op.astype(jnp.float32), second_op.astype(jnp.float32), precision=EXACT_PRECISION, preferred_element_type=jnp.float32)

def layer(xf, places, attn_gain, w_query, w_key, w_value, w_outgate, w_beta, w_decay, beta_bias, decay_rate, conv_query, conv_key, conv_value, out_gain, w_out, mlp_gain, w_gate, w_up, w_down):
    total_rows = xf.shape[0]
    normed = low(rms_scale(xf, attn_gain, 1e-06))

    def project(matrix):
        return low_back(fdot(normed, matrix))

    def extend(field):
        return jnp.concatenate([jnp.zeros((KW - 1, field.shape[1]), jnp.float32), field], axis=0)
    ext_query = extend(low(project(w_query)))
    ext_key = extend(low(project(w_key)))
    ext_value = extend(low(project(w_value)))
    queries, every_key_row, values_all, betas, log_steps = features(places, ext_query, ext_key, ext_value, conv_query, conv_key, conv_value, project(w_beta), project(w_decay), beta_bias, decay_rate)
    queries = low(queries)
    every_key_row = low(every_key_row)
    values_all = low(values_all)
    head_count = queries.shape[1]
    head_width = queries.shape[2]
    blocks = total_rows // BLOCK
    q_blocks = queries.reshape(blocks, BLOCK, head_count, head_width).transpose(0, 2, 1, 3)
    start = jnp.zeros((head_count, head_width, head_width), jnp.float32)
    ended, outputs = lax.scan(jax.checkpoint(block_step), start, (q_blocks, step_layout(every_key_row, blocks), step_layout(values_all, blocks), step_layout(betas, blocks), step_layout(log_steps, blocks)))
    attended = outputs.transpose(0, 2, 1, 3).reshape(total_rows, head_count, head_width)
    gate_in = project(w_outgate).reshape(total_rows, head_count, head_width)
    gated = low(rms_scale(attended, out_gain, 1e-05) * jax.nn.silu(gate_in)).reshape(total_rows, head_count * head_width)
    resid = xf + low_back(fdot(gated, w_out))
    mlp_in = low(rms_scale(resid, mlp_gain, 1e-06))
    gate_act = low_back(fdot(mlp_in, w_gate))
    up_act = low_back(fdot(mlp_in, w_up))
    hidden = low(jax.nn.silu(gate_act) * up_act)
    return resid + fdot(hidden, w_down)

def reference(block_input, lengths, attn_gain, w_query, w_key, w_value, w_outgate, w_beta, w_decay, beta_bias, decay_rate, conv_query, conv_key, conv_value, out_gain, w_out, mlp_gain, w_gate, w_up, w_down, out_grad):
    params = (attn_gain, w_query, w_key, w_value, w_outgate, w_beta, w_decay, beta_bias, decay_rate, conv_query, conv_key, conv_value, out_gain, w_out, mlp_gain, w_gate, w_up, w_down)
    floats = tuple((item.astype(jnp.float32) for item in params))
    outputs = []
    input_grads = []
    totals = tuple((jnp.zeros(item.shape, jnp.float32) for item in params))
    for group in range(N_DP):
        first = group * GROUP
        places = seq_positions(lengths[group], 0, GROUP)

        def forward(inputs, *weights):
            return layer(inputs, places, *weights)
        result, pull = jax.vjp(forward, block_input[first:first + GROUP].astype(jnp.float32), *floats)
        grads = pull(out_grad[first:first + GROUP].astype(jnp.float32))
        outputs.append(result.astype(jnp.bfloat16))
        input_grads.append(grads[0].astype(jnp.bfloat16))
        totals = tuple((left + right for left, right in zip(totals, grads[1:])))
    out_all = jnp.concatenate(outputs, axis=0)
    grad_all = jnp.concatenate(input_grads, axis=0)
    return (out_all, grad_all, totals[0], totals[1], totals[2], totals[3], totals[4], totals[5], totals[6], totals[7], totals[8], totals[9], totals[10], totals[11], totals[12], totals[13], totals[14], totals[15], totals[16], totals[17])
```

```python
from functools import partial

import jax
import jax.numpy as jnp
from jax import lax
from jax.experimental import pallas as pl
from jax.experimental.pallas import tpu as pltpu
from jax.sharding import PartitionSpec as P

REFLECTS = 2
KW = 4
BLOCK = 64
SHORTEST = 1024
STEPS = BLOCK * REFLECTS
HALO = 8
RESET_LOG = -80.0
MESH = pl.DeviceIdType.MESH
F32 = jnp.float32
BF16 = jnp.bfloat16
NN = (((1,), (0,)), ((), ()))
NT = (((1,), (1,)), ((), ()))
TN = (((0,), (0,)), ((), ()))
VMEM_LIMIT = 56 * 1024 * 1024


def mm(a, b, dims=NN):
    return lax.dot_general(a.astype(BF16), b.astype(BF16), dims, preferred_element_type=F32)


def halves(a):
    high = a.astype(BF16)
    return high, (a - high.astype(F32)).astype(BF16)


def mm3(a, b):
    ah, al = halves(a)
    bh, bl = halves(b)
    return mm(ah, bh) + (mm(ah, bl) + mm(al, bh))


def mm2(a, b, dims=NN):
    ah, al = halves(a)
    return mm(ah, b, dims) + mm(al, b, dims)


def sigmoid(v):
    return 1.0 / (1.0 + jnp.exp(-v))


def step_ids(shape, axis):
    index = lax.broadcasted_iota(jnp.int32, shape, axis)
    return index % BLOCK, index // BLOCK


def step_masks():
    shape = (STEPS, STEPS)
    tm, jm = step_ids(shape, 0)
    tn, jn = step_ids(shape, 1)
    strict = (tm > tn) | ((tm == tn) & (jm > jn))
    size = 4
    first = tm // size == tn // size
    merges = []
    while size < BLOCK:
        merges.append((tm // (2 * size) == tn // (2 * size)) & (tm // size != tn // size))
        size = 2 * size
    eye = ((tm == tn) & (jm == jn)).astype(F32)
    return tm >= tn, strict, first, merges, eye


def unit_lower_inverse(systems, first, merges, eye):
    neg = [jnp.where(first, -a, 0.0) for a in systems]
    inv = [eye + n for n in neg]
    for _ in range(2):
        neg = [mm3(n, n) for n in neg]
        inv = [t + mm3(t, n) for t, n in zip(inv, neg)]
    for merge in merges:
        off = [mm3(jnp.where(merge, a, 0.0), t) for a, t in zip(systems, inv)]
        inv = [t - mm3(t, o) for t, o in zip(inv, off)]
    return inv


def conv_parts(ext_ref, taps, live, columns, rows):
    total = None
    for back in range(KW):
        part = ext_ref[pl.ds(HALO - back, rows), columns] * taps[KW - 1 - back : KW - back, :]
        if back > 0:
            part = part * live[:, back : back + 1]
        total = part if total is None else total + part
    return total


def head_features(ext_ref, tq, tk, tv, live, rows, width):
    conv = [
        conv_parts(ext_ref, tq[...], live, pl.ds(0, width), rows),
        conv_parts(ext_ref, tk[:, :width], live, pl.ds(width, width), rows),
        conv_parts(ext_ref, tk[:, width:], live, pl.ds(2 * width, width), rows),
        conv_parts(ext_ref, tv[:, :width], live, pl.ds(3 * width, width), rows),
        conv_parts(ext_ref, tv[:, width:], live, pl.ds(4 * width, width), rows),
    ]
    return conv


def unit_rows(act):
    return lax.rsqrt(jnp.sum(act * act, axis=-1, keepdims=True) + 1e-06)


def mixer_forward_kernel(
    xn_ref, wq_ref, wk_ref, wv_ref, wg_ref, tq_ref, tk_ref, tv_ref, live_ref, acol_ref, arow_ref,
    pre_ref, gate_ref, oloc_ref, oread_ref, inv_ref, delta_ref, state_ref, final_ref,
    ext_ref,
):
    rows, width = oloc_ref.shape
    blocks = rows // BLOCK
    xn = xn_ref[...]
    pre = jnp.concatenate(
        [mm(xn, wq_ref[...]), mm(xn, wk_ref[...]), mm(xn, wv_ref[...])], axis=1
    ).astype(BF16)
    pre_ref[0] = pre
    ext_ref[...] = pre.astype(F32)
    gate_ref[...] = mm(xn[HALO:], wg_ref[...])
    live = live_ref[...]
    conv = head_features(ext_ref, tq_ref, tk_ref, tv_ref, live, rows, width)
    act = [c * sigmoid(c) for c in conv]
    q = (act[0] * unit_rows(act[0]) * width ** (-0.5)).astype(BF16)
    k = [(a * unit_rows(a)).astype(BF16) for a in act[1:3]]
    v = [a.astype(BF16) for a in act[3:5]]
    reach, strict, first, merges, eye = step_masks()
    cut = [slice(b * BLOCK, (b + 1) * BLOCK) for b in range(blocks)]
    kb = [jnp.concatenate([k[0][s], k[1][s]], axis=0) for s in cut]
    vb = [jnp.concatenate([v[0][s], v[1][s]], axis=0) for s in cut]
    qb = [q[s] for s in cut]
    ccol = [acol_ref[0, b, :, 0:1] for b in range(blocks)]
    bcol = [acol_ref[0, b, :, 1:2] for b in range(blocks)]
    crow = [arow_ref[0, b, 0:1, :] for b in range(blocks)]
    brow = [arow_ref[0, b, 1:2, :] for b in range(blocks)]
    fade = [jnp.exp(jnp.where(reach, c - r, -1e30)) for c, r in zip(ccol, crow)]
    gram = [mm(x, x, NT) for x in kb]
    system = [jnp.where(strict, f * g, 0.0) * b for f, g, b in zip(fade, gram, bcol)]
    inv = unit_lower_inverse(system, first, merges, eye)
    for b in range(blocks):
        inv_ref[0, b] = inv[b]
    local = [mm2(t * b, x) for t, b, x in zip(inv, brow, vb)]
    reads = [mm2(t * (b * jnp.exp(c)), x) for t, b, c, x in zip(inv, brow, crow, kb)]
    score = [f[:BLOCK] * mm(x, y, NT) for f, x, y in zip(fade, qb, kb)]
    state = jnp.concatenate([jnp.zeros((width, width), F32), eye], axis=1)
    for b in range(blocks):
        state_ref[0, b] = state
        grow = jnp.exp(ccol[b])
        last = ccol[b][BLOCK - 1 : BLOCK]
        if b == 0:
            delta = jnp.concatenate([local[b], -reads[b]], axis=1)
        else:
            delta = jnp.concatenate([local[b], jnp.zeros((STEPS, width), F32)], axis=1) - mm(
                reads[b], state
            )
        delta_ref[0, b] = delta
        out = mm(score[b], delta) + grow[:BLOCK] * mm(qb[b], state)
        oloc_ref[cut[b], :] = out[:, :width]
        oread_ref[0, cut[b], :] = out[:, width:]
        tail = kb[b].astype(F32) * jnp.exp(last - ccol[b])
        state = jnp.exp(last) * state + mm(tail, delta, TN)
    final_ref[0] = state.astype(BF16)


def head_columns(rows, width):
    return pl.BlockSpec((rows, width), lambda h: (0, h))


def whole(shape):
    return pl.BlockSpec(shape, lambda h: (0,) * len(shape))


def per_head(shape):
    return pl.BlockSpec((1,) + shape, lambda h: (h,) + (0,) * len(shape))


def mixer_forward(xn, w_query, w_key, w_value, w_outgate, taps, live, acol, arow, heads, width):
    ext_rows, depth = xn.shape
    rows = ext_rows - HALO
    blocks = rows // BLOCK
    conv_query, conv_key, conv_value = taps
    out = jax.ShapeDtypeStruct
    return pl.pallas_call(
        mixer_forward_kernel,
        grid=(heads,),
        in_specs=[
            whole((ext_rows, depth)),
            head_columns(depth, width),
            head_columns(depth, 2 * width),
            head_columns(depth, 2 * width),
            head_columns(depth, width),
            head_columns(KW, width),
            head_columns(KW, 2 * width),
            head_columns(KW, 2 * width),
            whole(live.shape),
            per_head(acol.shape[1:]),
            per_head(arow.shape[1:]),
        ],
        out_specs=[
            per_head((ext_rows, 5 * width)),
            head_columns(rows, width),
            head_columns(rows, width),
            per_head((rows, width)),
            per_head((blocks, STEPS, STEPS)),
            per_head((blocks, STEPS, 2 * width)),
            per_head((blocks, width, 2 * width)),
            per_head((width, 2 * width)),
        ],
        out_shape=[
            out((heads, ext_rows, 5 * width), BF16),
            out((rows, heads * width), F32),
            out((rows, heads * width), F32),
            out((heads, rows, width), F32),
            out((heads, blocks, STEPS, STEPS), F32),
            out((heads, blocks, STEPS, 2 * width), F32),
            out((heads, blocks, width, 2 * width), F32),
            out((heads, width, 2 * width), BF16),
        ],
        scratch_shapes=[pltpu.VMEM((ext_rows, 5 * width), F32)],
        compiler_params=pltpu.CompilerParams(vmem_limit_bytes=VMEM_LIMIT),
        name="mixer_forward",
    )(xn, w_query, w_key, w_value, w_outgate, conv_query, conv_key, conv_value, live, acol, arow)


def conv_pull(ext_ref, pad_ref, d_conv, taps, live, columns, rows, dtap_ref):
    total = None
    for back in range(KW):
        part = d_conv if back == 0 else d_conv * live[:, back : back + 1]
        source = ext_ref[pl.ds(HALO - back, rows), columns]
        dtap_ref[KW - 1 - back : KW - back, :] = jnp.sum(part * source, axis=0, keepdims=True)
        pad_ref[pl.ds(HALO, rows), :] = part
        moved = pad_ref[pl.ds(back, rows + HALO), :] * taps[KW - 1 - back : KW - back, :]
        total = moved if total is None else total + moved
    return total


def silu_pull(c, grad):
    s = sigmoid(c)
    return grad * (s + c * s * (1.0 - s))


def unit_pull(act, grad, scale):
    r = unit_rows(act)
    return scale * r * (grad - act * (r * r * jnp.sum(act * grad, axis=-1, keepdims=True)))


def mixer_backward_kernel(
    pre_ref, tq_ref, tk_ref, tv_ref, live_ref, acol_ref, arow_ref,
    inv_ref, delta_ref, state_ref, start_ref, after_ref, dout_ref,
    dq_ref, dk_ref, dv_ref, rimq_ref, rimk_ref, rimv_ref, dtq_ref, dtk_ref, dtv_ref, aux_ref,
    ext_ref, pad_ref,
):
    rows, width = dout_ref.shape
    blocks = rows // BLOCK
    ext_ref[...] = pre_ref[0].astype(F32)
    live = live_ref[...]
    conv = head_features(ext_ref, tq_ref, tk_ref, tv_ref, live, rows, width)
    act = [c * sigmoid(c) for c in conv]
    q = (act[0] * unit_rows(act[0]) * width ** (-0.5)).astype(BF16)
    k = [(a * unit_rows(a)).astype(BF16) for a in act[1:3]]
    reach, strict, _, _, _ = step_masks()
    start = start_ref[0]
    after = after_ref[0].astype(F32)
    pieces = [None] * blocks
    for b in range(blocks - 1, -1, -1):
        s = slice(b * BLOCK, (b + 1) * BLOCK)
        kb = jnp.concatenate([k[0][s], k[1][s]], axis=0)
        kf = kb.astype(F32)
        qb = q[s]
        ccol = acol_ref[0, b, :, 0:1]
        bcol = acol_ref[0, b, :, 1:2]
        crow = arow_ref[0, b, 0:1, :]
        last = ccol[BLOCK - 1 : BLOCK]
        fade = jnp.exp(jnp.where(reach, ccol - crow, -1e30))
        grow = jnp.exp(ccol)
        weight = jnp.exp(last - ccol)
        dout = dout_ref[s, :]
        gdout = grow[:BLOCK] * dout
        delta = delta_ref[0, b, :, :width] + mm(delta_ref[0, b, :, width:], start)
        state = state_ref[0, b, :, :width] + mm(state_ref[0, b, :, width:], start)
        fade_q = fade[:BLOCK]
        score = fade_q * mm(qb, kb, NT)
        d_delta = mm(score, dout, TN) + weight * mm(kb, after)
        d_rhs = mm(inv_ref[0, b], d_delta, TN)
        d_score = fade_q * mm(dout, delta, NT)
        d_known = -(bcol * grow) * d_rhs
        d_tail = weight * mm(delta, after, NT)
        d_gram = jnp.where(strict, -bcol * fade * mm(d_rhs, delta, NT), 0.0)
        dq = mm(gdout, state, NT) + mm(d_score, kb)
        dk_row = mm(d_known, state, NT) + mm(d_gram, kb)
        dk_col = mm(d_gram, kb, TN) + mm(d_score, qb, TN) + d_tail
        d_beta = (1.0 - bcol) * jnp.sum(d_rhs * delta, axis=-1, keepdims=True)
        d_log = jnp.sum(kf * (dk_row - dk_col), axis=-1, keepdims=True)
        d_logq = jnp.sum(qb.astype(F32) * dq, axis=-1, keepdims=True)
        d_last = jnp.sum(kf * d_tail) + jnp.sum(jnp.exp(last) * after * state)
        tok = lax.broadcasted_iota(jnp.int32, (BLOCK, 1), 0)
        d_token = d_log[:BLOCK] + d_log[BLOCK:] + d_logq
        d_token = d_token + jnp.where(tok == BLOCK - 1, d_last, 0.0)
        aux_ref[0, b, :, 0:1] = d_beta
        aux_ref[0, b, 0:BLOCK, 1:2] = d_token
        dk = dk_row + dk_col
        pieces[b] = (dq, dk[:BLOCK], dk[BLOCK:], (bcol * d_rhs)[:BLOCK], (bcol * d_rhs)[BLOCK:])
        after = jnp.exp(last) * after + mm(qb, gdout, TN) + mm(kb, d_known, TN)
    d_act = [jnp.concatenate([pieces[b][i] for b in range(blocks)], axis=0) for i in range(5)]
    d_act[0] = unit_pull(act[0], d_act[0], width ** (-0.5))
    d_act[1] = unit_pull(act[1], d_act[1], 1.0)
    d_act[2] = unit_pull(act[2], d_act[2], 1.0)
    d_conv = [silu_pull(c, g) for c, g in zip(conv, d_act)]
    pad_ref[0:HALO, :] = jnp.zeros((HALO, width), F32)
    pad_ref[pl.ds(HALO + rows, HALO), :] = jnp.zeros((HALO, width), F32)
    sides = (
        (tq_ref, dq_ref, rimq_ref, dtq_ref, 0),
        (tk_ref, dk_ref, rimk_ref, dtk_ref, 0),
        (tk_ref, dk_ref, rimk_ref, dtk_ref, width),
        (tv_ref, dv_ref, rimv_ref, dtv_ref, 0),
        (tv_ref, dv_ref, rimv_ref, dtv_ref, width),
    )
    for i, (tap_ref, d_ref, rim_ref, dtap_ref, at) in enumerate(sides):
        lanes = pl.ds(at, width)
        grad = conv_pull(
            ext_ref, pad_ref, d_conv[i], tap_ref[:, lanes], live, pl.ds(i * width, width), rows,
            dtap_ref.at[:, lanes],
        )
        rim_ref[:, lanes] = grad[:HALO].astype(BF16)
        d_ref[:, lanes] = grad[HALO:].astype(BF16)


def mixer_backward(pre, taps, live, acol, arow, inv, delta, state, start, after, dout):
    heads, ext_rows, _ = pre.shape
    rows = ext_rows - HALO
    width = start.shape[-1]
    conv_query, conv_key, conv_value = taps
    out = jax.ShapeDtypeStruct
    columns = heads * width
    return pl.pallas_call(
        mixer_backward_kernel,
        grid=(heads,),
        in_specs=[
            per_head(pre.shape[1:]),
            head_columns(KW, width),
            head_columns(KW, 2 * width),
            head_columns(KW, 2 * width),
            whole(live.shape),
            per_head(acol.shape[1:]),
            per_head(arow.shape[1:]),
            per_head(inv.shape[1:]),
            per_head(delta.shape[1:]),
            per_head(state.shape[1:]),
            per_head((width, width)),
            per_head((width, width)),
            head_columns(rows, width),
        ],
        out_specs=[
            head_columns(rows, width),
            head_columns(rows, 2 * width),
            head_columns(rows, 2 * width),
            head_columns(HALO, width),
            head_columns(HALO, 2 * width),
            head_columns(HALO, 2 * width),
            head_columns(KW, width),
            head_columns(KW, 2 * width),
            head_columns(KW, 2 * width),
            per_head(acol.shape[1:]),
        ],
        out_shape=[
            out((rows, columns), BF16),
            out((rows, 2 * columns), BF16),
            out((rows, 2 * columns), BF16),
            out((HALO, columns), BF16),
            out((HALO, 2 * columns), BF16),
            out((HALO, 2 * columns), BF16),
            out((KW, columns), F32),
            out((KW, 2 * columns), F32),
            out((KW, 2 * columns), F32),
            out(acol.shape, F32),
        ],
        scratch_shapes=[
            pltpu.VMEM((ext_rows, 5 * width), F32),
            pltpu.VMEM((rows + 2 * HALO, width), F32),
        ],
        compiler_params=pltpu.CompilerParams(vmem_limit_bytes=VMEM_LIMIT),
        name="mixer_backward",
    )(pre, conv_query, conv_key, conv_value, live, acol, arow, inv, delta, state, start, after, dout)


def gated_forward_kernel(oloc_ref, oread_ref, start_ref, gate_ref, gain_ref, out_ref, gated_ref):
    out = oloc_ref[...] + mm(oread_ref[0], start_ref[0])
    out_ref[...] = out
    gate = gate_ref[...]
    r = lax.rsqrt(jnp.mean(out * out, axis=-1, keepdims=True) + 1e-05)
    gated_ref[...] = (out * r * gain_ref[...] * (gate * sigmoid(gate))).astype(BF16)


def gated_forward(oloc, oread, start, gate_pre, out_gain):
    heads, rows, width = oread.shape
    out = jax.ShapeDtypeStruct
    return pl.pallas_call(
        gated_forward_kernel,
        grid=(heads,),
        in_specs=[
            head_columns(rows, width),
            per_head((rows, width)),
            per_head((width, width)),
            head_columns(rows, width),
            whole((1, width)),
        ],
        out_specs=[head_columns(rows, width), head_columns(rows, width)],
        out_shape=[out(oloc.shape, F32), out(oloc.shape, BF16)],
        name="gated_forward",
    )(oloc, oread, start, gate_pre, out_gain[None, :])


def gated_backward_kernel(
    out_ref, gate_ref, gain_ref, dgated_ref, oread_ref, dout_ref, dgate_ref, part_ref, dgain_ref
):
    out = out_ref[...]
    gate = gate_ref[...]
    gain = gain_ref[...]
    grad = dgated_ref[...]
    r = lax.rsqrt(jnp.mean(out * out, axis=-1, keepdims=True) + 1e-05)
    s = sigmoid(gate)
    unit = out * r
    dgate_ref[...] = (grad * unit * gain * (s + gate * s * (1.0 - s))).astype(BF16)
    through = grad * (gate * s)
    dgain_ref[0] = jnp.sum(through * unit, axis=0, keepdims=True)
    through = through * gain
    dout = r * (through - unit * jnp.mean(unit * through, axis=-1, keepdims=True))
    dout_ref[...] = dout
    part_ref[0] = mm(oread_ref[0], dout, TN).astype(BF16)


def gated_backward(out_all, gate_pre, out_gain, d_gated, oread):
    heads, rows, width = oread.shape
    out = jax.ShapeDtypeStruct
    return pl.pallas_call(
        gated_backward_kernel,
        grid=(heads,),
        in_specs=[
            head_columns(rows, width),
            head_columns(rows, width),
            whole((1, width)),
            head_columns(rows, width),
            per_head((rows, width)),
        ],
        out_specs=[
            head_columns(rows, width),
            head_columns(rows, width),
            per_head((width, width)),
            per_head((1, width)),
        ],
        out_shape=[
            out(out_all.shape, F32),
            out(out_all.shape, BF16),
            out((heads, width, width), BF16),
            out((heads, 1, width), F32),
        ],
        name="gated_backward",
    )(out_all, gate_pre, out_gain[None, :], d_gated, oread)


def carry_kernel(count, heads, backward, *refs):
    if backward:
        part_ref, maps_ref, result_ref, inbox, outbox, landed, send_sem, recv_sem, back_sem, land_sem = refs
    else:
        part_ref, result_ref, maps_ref, inbox, outbox, landed, send_sem, recv_sem, back_sem, land_sem = refs
    place = lax.axis_index("seq")
    group = lax.axis_index("dp")
    width = result_ref.shape[-1]
    stride = count // 16

    def keeper(h):
        return (2 * h + group) * stride

    barrier = pltpu.get_barrier_semaphore()

    def greet(step, carry):
        peer = lax.rem(place + step, count)
        pl.semaphore_signal(barrier, inc=1, device_id=(group, peer), device_id_type=MESH)
        return carry

    lax.fori_loop(1, count, greet, 0)
    pl.semaphore_wait(barrier, count - 1)

    def outgoing(h):
        return pltpu.make_async_remote_copy(
            src_ref=part_ref.at[h],
            dst_ref=inbox.at[place],
            send_sem=send_sem.at[h],
            recv_sem=recv_sem.at[place],
            device_id=(group, keeper(h)),
            device_id_type=MESH,
        )

    for h in range(heads):

        @pl.when(place != keeper(h))
        def _(h=h):
            outgoing(h).start()

        @pl.when(place == keeper(h))
        def _(h=h):
            inbox[pl.ds(place, 1)] = part_ref[h : h + 1]

    def scan_head(h):
        def returning(where):
            return pltpu.make_async_remote_copy(
                src_ref=outbox.at[where],
                dst_ref=landed.at[h],
                send_sem=back_sem.at[where],
                recv_sem=land_sem.at[h],
                device_id=(group, where),
                device_id_type=MESH,
            )

        def lap(step, state):
            where = count - 1 - step if backward else step
            outbox[pl.ds(where, 1)] = state[None].astype(BF16)

            @pl.when(where != place)
            def _():
                returning(where).start()
                pltpu.make_async_remote_copy(
                    src_ref=part_ref.at[h],
                    dst_ref=inbox.at[where],
                    send_sem=send_sem.at[h],
                    recv_sem=recv_sem.at[where],
                    device_id=(group, where),
                    device_id_type=MESH,
                ).wait_recv()

            @pl.when(where == place)
            def _():
                landed[h : h + 1] = outbox[pl.ds(where, 1)]

            got = inbox[pl.ds(where, 1)][0]
            high, low = halves(state)
            if backward:
                step_map = maps_ref[pl.ds(where, 1)][0][:, width:]
                state = mm(step_map, high, TN) + mm(step_map, low, TN) + got.astype(F32)
            else:
                step_map = got[:, width:]
                state = mm(step_map, high) + mm(step_map, low) + got[:, :width].astype(F32)
            return state

        lax.fori_loop(0, count, lap, jnp.zeros((width, width), F32))

        def finish(where, carry):
            @pl.when(where != place)
            def _():
                returning(where).wait_send()

            return carry

        lax.fori_loop(0, count, finish, 0)

    for h in range(heads):

        @pl.when(place == keeper(h))
        def _(h=h):
            scan_head(h)

    for h in range(heads):

        @pl.when(place != keeper(h))
        def _(h=h):
            outgoing(h).wait_send()
            pltpu.make_async_remote_copy(
                src_ref=outbox.at[0],
                dst_ref=landed.at[h],
                send_sem=back_sem.at[0],
                recv_sem=land_sem.at[h],
                device_id=(group, keeper(h)),
                device_id_type=MESH,
            ).wait_recv()

    result_ref[...] = landed[...]
    if not backward:
        maps_ref[...] = inbox[...]


def carry_states(part, maps, count):
    heads, width, columns = part.shape
    backward = maps is not None
    out = jax.ShapeDtypeStruct
    vmem = pl.BlockSpec(memory_space=pltpu.VMEM)
    result = out((heads, width, width), BF16)
    return pl.pallas_call(
        partial(carry_kernel, count, heads, backward),
        in_specs=[vmem] * (2 if backward else 1),
        out_specs=vmem if backward else [vmem, vmem],
        out_shape=result if backward else [result, out((count, width, columns), BF16)],
        scratch_shapes=[
            pltpu.VMEM((count, width, columns), BF16),
            pltpu.VMEM((count, width, width), BF16),
            pltpu.VMEM((heads, width, width), BF16),
            pltpu.SemaphoreType.DMA((heads,)),
            pltpu.SemaphoreType.DMA((count,)),
            pltpu.SemaphoreType.DMA((count,)),
            pltpu.SemaphoreType.DMA((heads,)),
        ],
        compiler_params=pltpu.CompilerParams(
            collective_id=1 if backward else 0, has_side_effects=True, vmem_limit_bytes=VMEM_LIMIT
        ),
        name="carry_backward" if backward else "carry_forward",
    )(*((part, maps) if backward else (part,)))


def seq_positions(extras, first, total_rows):
    sizes = extras + (SHORTEST - 1)
    ends = jnp.cumsum(sizes)
    starts = ends - sizes
    row_ids = first + jnp.arange(total_rows, dtype=jnp.int32)
    inside = (row_ids[:, None] >= starts[None, :]) & (row_ids[:, None] < ends[None, :])
    return row_ids - jnp.sum(jnp.where(inside, starts[None, :], 0), axis=1)


def rms_scale(field, gain, epsilon):
    return field * lax.rsqrt(jnp.mean(field * field, axis=-1, keepdims=True) + epsilon) * gain


def rms_pull(field, gain, grad):
    scale = lax.rsqrt(jnp.mean(field * field, axis=-1, keepdims=True) + 1e-06)
    unit = field * scale
    through = grad * gain
    pulled = scale * (through - unit * jnp.mean(unit * through, axis=-1, keepdims=True))
    return pulled, jnp.sum(grad * unit, axis=0)


def dot32(a, b, dims=NN):
    return lax.dot_general(a, b, dims, preferred_element_type=F32)


def digits_of(count):
    radices = {16: (4, 2, 2), 128: (4, 4, 8)}.get(count)
    if radices is None:
        radices = ()
        left = count
        while left > 1:
            step = 4 if left % 4 == 0 else 2
            radices = radices + (step,)
            left = left // step
    return radices


def split_digits(index, radices):
    digits = []
    for radix in reversed(radices):
        digits.append(index % radix)
        index = index // radix
    return digits[::-1]


def join_digits(digits, radices):
    index = 0
    for digit, radix in zip(digits, radices):
        index = index * radix + digit
    return index


def relative_places(order, radices):
    here = split_digits(lax.axis_index("seq"), radices)
    count = 1
    for radix in radices:
        count *= radix
    place = jnp.arange(count, dtype=jnp.int32)
    moved = split_digits(place, [radices[axis] for axis in order])
    target = [None] * len(radices)
    for axis, move in zip(order, moved):
        target[axis] = (here[axis] + move) % radices[axis]
    return join_digits(target, radices)


def axis_shift(value, axis, move, radices):
    count = 1
    for radix in radices:
        count *= radix
    route = []
    for index in range(count):
        digits = split_digits(index, radices)
        digits[axis] = (digits[axis] + move) % radices[axis]
        route.append((index, join_digits(digits, radices)))
    return lax.ppermute(value, "seq", route)


def swap_core(value):
    count = lax.axis_size("dp")
    return lax.ppermute(value, "dp", [(i, (i + 1) % count) for i in range(count)])


def selector(depth, order, radices, group):
    places = relative_places(order, radices)
    count = places.shape[0]
    block = depth // (lax.axis_size("dp") * count)
    half = depth // lax.axis_size("dp")
    rows = (places[:, None] * block + jnp.arange(block, dtype=jnp.int32)).reshape(-1)
    source = group * half + rows
    return (jnp.arange(depth, dtype=jnp.int32)[:, None] == source[None, :]).astype(BF16)


def shard_sums(make, order, radices):
    count = 1
    for radix in radices:
        count *= radix
    first = count // radices[order[0]]
    arrived = [
        axis_shift(make(move * first, (move + 1) * first), order[0], move, radices)
        for move in range(1, radices[order[0]])
    ]
    total = make(0, first).astype(F32)
    for part in arrived:
        total = total + part.astype(F32)
    for axis in order[1:]:
        own = total.shape[0] // radices[axis]
        low = total.astype(BF16)
        arrived = [
            axis_shift(low[move * own : (move + 1) * own], axis, move, radices)
            for move in range(1, radices[axis])
        ]
        total = total[:own]
        for part in arrived:
            total = total + part.astype(F32)
    return total


def everywhere(value, radices):
    value = value + swap_core(value)
    for axis, radix in enumerate(radices):
        total = value
        if radix == 2:
            total = total + axis_shift(value, axis, 1, radices)
        else:
            step = 1
            while step < radix:
                total = total + exchange(total, axis, step, radices)
                step = 2 * step
        value = total
    return value


def exchange(value, axis, step, radices):
    count = 1
    for radix in radices:
        count *= radix
    route = []
    for index in range(count):
        digits = split_digits(index, radices)
        digits[axis] = digits[axis] ^ step
        route.append((index, join_digits(digits, radices)))
    return lax.ppermute(value, "seq", route)


def per_device(
    block_input, lengths, attn_gain, w_query, w_key, w_value, w_outgate, w_beta, w_decay, beta_bias,
    decay_rate, conv_query, conv_key, conv_value, out_gain, w_out, mlp_gain, w_gate, w_up, w_down,
    out_grad,
):
    rows, depth = block_input.shape
    heads = decay_rate.shape[0]
    width = out_gain.shape[0]
    blocks = rows // BLOCK
    count = lax.axis_size("seq")
    seq = lax.axis_index("seq")
    group = lax.axis_index("dp")
    radices = digits_of(count)
    axes = len(radices)
    order_a = tuple(range(axes - 1, -1, -1))
    order_b = (order_a[1], order_a[0]) + order_a[2:]
    places = seq_positions(lengths[0], seq * rows, rows)

    halo = lax.ppermute(block_input[rows - HALO :], "seq", [(i, i + 1) for i in range(count - 1)])
    xf = block_input.astype(F32)
    normed_b = rms_scale(xf, attn_gain, 1e-06).astype(BF16)
    ext_b = jnp.concatenate([rms_scale(halo.astype(F32), attn_gain, 1e-06).astype(BF16), normed_b], axis=0)
    rates = dot32(normed_b, jnp.concatenate([w_beta, w_decay], axis=1))
    beta_pre, decay_pre = rates[:, : heads * REFLECTS], rates[:, heads * REFLECTS :]
    betas = jax.nn.sigmoid(beta_pre + beta_bias)
    log_rate = jnp.where((places == 0)[:, None], RESET_LOG, -decay_rate * jax.nn.softplus(decay_pre))
    tri = jnp.tril(jnp.ones((BLOCK, BLOCK), F32))
    cumul = jnp.einsum(
        "ts,bsh->hbt", tri, log_rate.reshape(blocks, BLOCK, heads), precision=lax.Precision.HIGHEST
    )
    cumul = jnp.concatenate([cumul] * REFLECTS, axis=-1)
    beta_steps = betas.reshape(blocks, BLOCK, heads, REFLECTS).transpose(2, 0, 3, 1).reshape(heads, blocks, STEPS)
    arow = jnp.stack([cumul, beta_steps] + [jnp.zeros_like(cumul)] * 6, axis=2)
    acol = arow.transpose(0, 1, 3, 2)
    live = (places[:, None] >= jnp.arange(8, dtype=jnp.int32)[None, :]).astype(F32)
    taps = (conv_query, conv_key, conv_value)

    pre, gate_pre, oloc, oread, inv, delta, state, maps = mixer_forward(
        ext_b, w_query, w_key, w_value, w_outgate, taps, live, acol, arow, heads, width
    )
    start, all_maps = carry_states(maps, None, count)
    out_all, gated_b = gated_forward(oloc, oread, start, gate_pre, out_gain)

    resid = xf + dot32(gated_b, w_out)
    mlp_b = rms_scale(resid, mlp_gain, 1e-06).astype(BF16)
    gate_act = dot32(mlp_b, w_gate)
    up_act = dot32(mlp_b, w_up)
    gate_sig = jax.nn.sigmoid(gate_act)
    hidden_b = (gate_act * gate_sig * up_act).astype(BF16)
    block_output = (resid + dot32(hidden_b, w_down)).astype(BF16)
    d_hidden = dot32(out_grad, w_down, NT)
    d_gate_b = (d_hidden * up_act * (gate_sig + gate_act * gate_sig * (1.0 - gate_sig))).astype(BF16)
    d_up_b = (d_hidden * gate_act * gate_sig).astype(BF16)
    d_mlp = dot32(d_gate_b, w_gate, NT) + dot32(d_up_b, w_up, NT)
    d_resid_mlp, grad_mlp_gain = rms_pull(resid, mlp_gain, d_mlp)
    d_resid = out_grad.astype(F32) + d_resid_mlp
    d_branch_b = d_resid.astype(BF16)
    d_gated = dot32(d_branch_b, w_out, NT)
    d_out, d_outgate_b, part, grad_out_gain = gated_backward(out_all, gate_pre, out_gain, d_gated, oread)

    mine, other = selector(depth, order_a, radices, group), selector(depth, order_a, radices, 1 - group)

    def both(lhs, rhs):
        keep = dot32(lhs, mine).astype(BF16)
        gone = swap_core(dot32(lhs, other).astype(BF16))
        return jnp.concatenate([keep, gone], axis=0), jnp.concatenate([rhs, swap_core(rhs)], axis=0)

    first, second = radices[order_a[0]], radices[order_a[1]]

    def turned(lhs):
        tokens = lhs.shape[0]
        return lhs.reshape(tokens, first, second, -1).swapaxes(1, 2).reshape(tokens, -1)

    def maker(pairs):
        def make(begin, end):
            parts = []
            for lhs, rhs in pairs:
                block = lhs.shape[1] // count
                parts.append(dot32(lhs[:, begin * block : end * block], rhs, TN).astype(BF16))
            return parts[0] if len(parts) == 1 else jnp.concatenate(parts, axis=1)

        return make

    normed_l, outgate_r = both(normed_b, d_outgate_b)
    mlp_l, gate_r = both(mlp_b, d_gate_b)
    up_r = jnp.concatenate([d_up_b, swap_core(d_up_b)], axis=0)
    branch_l, gated_r = both(d_branch_b, gated_b)
    down_l, hidden_r = both(out_grad, hidden_b)
    early_a = shard_sums(maker([(mlp_l, gate_r), (branch_l, gated_r), (normed_l, outgate_r)]), order_a, radices)
    early_b = shard_sums(maker([(turned(mlp_l), up_r), (turned(down_l), hidden_r)]), order_b, radices)

    after = carry_states(part, all_maps, count)
    d_query, d_key, d_value, rim_q, rim_k, rim_v, tap_q, tap_k, tap_v, aux = mixer_backward(
        pre, taps, live, acol, arow, inv, delta, state, start, after, d_out
    )
    rim = lax.ppermute(
        jnp.concatenate([rim_q, rim_k, rim_v], axis=1), "seq", [(i, i - 1) for i in range(1, count)]
    )

    def settle(main, low):
        last = main[rows - HALO :].astype(F32) + low.astype(F32)
        return jnp.concatenate([main[: rows - HALO], last.astype(BF16)], axis=0)

    columns = heads * width
    d_query = settle(d_query, rim[:, :columns])
    d_key = settle(d_key, rim[:, columns : 3 * columns])
    d_value = settle(d_value, rim[:, 3 * columns :])
    d_beta = aux[:, :, :, 0].reshape(heads, blocks, REFLECTS, BLOCK).transpose(1, 3, 0, 2).reshape(rows, -1)
    d_log = jnp.einsum(
        "st,hbs->bth", tri, aux[:, :, :BLOCK, 1], precision=lax.Precision.HIGHEST
    ).reshape(rows, heads)
    d_log = jnp.where((places == 0)[:, None], 0.0, d_log)
    grad_decay_rate = jnp.sum(-jax.nn.softplus(decay_pre) * d_log, axis=0)
    d_decay = -decay_rate * jax.nn.sigmoid(decay_pre) * d_log
    grad_beta_bias = jnp.sum(d_beta, axis=0)
    d_rates_b = jnp.concatenate([d_beta, d_decay], axis=1).astype(BF16)

    rates_r = jnp.concatenate([d_rates_b, swap_core(d_rates_b)], axis=0)
    query_r = jnp.concatenate([d_query, swap_core(d_query)], axis=0)
    key_r = jnp.concatenate([d_key, swap_core(d_key)], axis=0)
    value_r = jnp.concatenate([d_value, swap_core(d_value)], axis=0)
    half = columns // 2
    late_a = shard_sums(
        maker([(normed_l, jnp.concatenate([key_r, query_r[:, :half]], axis=1))]), order_a, radices
    )
    late_b = shard_sums(
        maker([(turned(normed_l), jnp.concatenate([value_r, query_r[:, half:], rates_r], axis=1))]),
        order_b,
        radices,
    )

    d_normed = (
        dot32(d_query, w_query, NT)
        + dot32(d_key, w_key, NT)
        + dot32(d_value, w_value, NT)
        + dot32(d_outgate_b, w_outgate, NT)
        + dot32(d_rates_b, jnp.concatenate([w_beta, w_decay], axis=1), NT)
    )
    d_input_norm, grad_attn_gain = rms_pull(xf, attn_gain, d_normed)
    input_grad = (d_resid + d_input_norm).astype(BF16)

    small = [
        tap_q.reshape(-1),
        tap_k.reshape(-1),
        tap_v.reshape(-1),
        jnp.sum(grad_out_gain, axis=(0, 1)),
        grad_attn_gain,
        grad_mlp_gain,
        grad_beta_bias,
        grad_decay_rate,
    ]
    sizes = [piece.shape[0] for piece in small]
    flat = jnp.concatenate(small)
    lanes = 1024
    padded = jnp.pad(flat, (0, -flat.shape[0] % (8 * lanes))).reshape(-1, lanes)
    summed = everywhere(padded, radices).reshape(-1)
    pieces, begin = [], 0
    for size in sizes:
        pieces.append(summed[begin : begin + size])
        begin += size
    share = depth // (count * lax.axis_size("dp"))
    own = (group * count + seq) * share

    ff = w_gate.shape[1]
    return (
        block_output,
        input_grad,
        lax.dynamic_slice(pieces[4], (own,), (share,)),
        jnp.concatenate([late_a[:, 2 * columns :], late_b[:, 2 * columns : 2 * columns + half]], axis=1),
        late_a[:, : 2 * columns],
        late_b[:, : 2 * columns],
        early_a[:, ff + columns :],
        late_b[:, 2 * columns + half : 2 * columns + half + heads * REFLECTS],
        late_b[:, 2 * columns + half + heads * REFLECTS :],
        pieces[6],
        pieces[7],
        pieces[0].reshape(KW, -1),
        pieces[1].reshape(KW, -1),
        pieces[2].reshape(KW, -1),
        pieces[3],
        early_a[:, ff : ff + columns].T,
        lax.dynamic_slice(pieces[5], (own,), (share,)),
        early_a[:, :ff],
        early_b[:, :ff],
        early_b[:, ff:].T,
    )


def solution(mesh):
    tokens = P(("dp", "seq"), None)
    column = P(None, ("dp", "seq"))
    vector = P(("dp", "seq"))
    in_specs = (tokens, P("dp", None)) + (P(),) * 18 + (tokens,)
    out_specs = (
        (tokens, tokens, vector)
        + (tokens,) * 6
        + (P(),) * 6
        + (column, vector, tokens, tokens, column)
    )
    return jax.shard_map(
        per_device, mesh=mesh, in_specs=in_specs, out_specs=out_specs, check_vma=False
    )
```

```python
from functools import partial

import jax
import jax.numpy as jnp
from jax import lax
from jax.experimental import pallas as pl
from jax.experimental.pallas import tpu as pltpu
from jax.sharding import PartitionSpec as P

REFLECTS = 2
KW = 4
BLOCK = 64
SHORTEST = 1024
STEPS = BLOCK * REFLECTS
HALO = 8
RESET_LOG = -80.0
MESH = pl.DeviceIdType.MESH
F32 = jnp.float32
BF16 = jnp.bfloat16
NN = (((1,), (0,)), ((), ()))
NT = (((1,), (1,)), ((), ()))
TN = (((0,), (0,)), ((), ()))
VMEM_LIMIT = 56 * 1024 * 1024


def cost(microseconds):
    return pl.CostEstimate(
        flops=int(microseconds * 1e9), bytes_accessed=int(microseconds * 1e6), transcendentals=0
    )


def mm(a, b, dims=NN):
    return lax.dot_general(a.astype(BF16), b.astype(BF16), dims, preferred_element_type=F32)


def halves(a):
    high = a.astype(BF16)
    return high, (a - high.astype(F32)).astype(BF16)


def mm3(a, b):
    ah, al = halves(a)
    bh, bl = halves(b)
    return mm(ah, bh) + (mm(ah, bl) + mm(al, bh))


def mm2(a, b, dims=NN):
    ah, al = halves(a)
    return mm(ah, b, dims) + mm(al, b, dims)


def sigmoid(v):
    return 1.0 / (1.0 + jnp.exp(-v))


def step_ids(shape, axis):
    index = lax.broadcasted_iota(jnp.int32, shape, axis)
    return index % BLOCK, index // BLOCK


def step_masks():
    shape = (STEPS, STEPS)
    tm, jm = step_ids(shape, 0)
    tn, jn = step_ids(shape, 1)
    strict = (tm > tn) | ((tm == tn) & (jm > jn))
    size = 4
    first = tm // size == tn // size
    merges = []
    while size < BLOCK:
        merges.append((tm // (2 * size) == tn // (2 * size)) & (tm // size != tn // size))
        size = 2 * size
    eye = ((tm == tn) & (jm == jn)).astype(F32)
    return tm >= tn, strict, first, merges, eye


def unit_lower_inverse(systems, first, merges, eye):
    neg = [jnp.where(first, -a, 0.0) for a in systems]
    inv = [eye + n for n in neg]
    for _ in range(2):
        neg = [mm3(n, n) for n in neg]
        inv = [t + mm3(t, n) for t, n in zip(inv, neg)]
    for merge in merges:
        off = [mm3(jnp.where(merge, a, 0.0), t) for a, t in zip(systems, inv)]
        inv = [t - mm3(t, o) for t, o in zip(inv, off)]
    return inv


def conv_parts(ext_ref, taps, live, columns, rows):
    total = None
    for back in range(KW):
        part = ext_ref[pl.ds(HALO - back, rows), columns] * taps[KW - 1 - back : KW - back, :]
        if back > 0:
            part = part * live[:, back : back + 1]
        total = part if total is None else total + part
    return total


def head_features(ext_ref, tq, tk, tv, live, rows, width):
    conv = [
        conv_parts(ext_ref, tq[...], live, pl.ds(0, width), rows),
        conv_parts(ext_ref, tk[:, :width], live, pl.ds(width, width), rows),
        conv_parts(ext_ref, tk[:, width:], live, pl.ds(2 * width, width), rows),
        conv_parts(ext_ref, tv[:, :width], live, pl.ds(3 * width, width), rows),
        conv_parts(ext_ref, tv[:, width:], live, pl.ds(4 * width, width), rows),
    ]
    return conv


def unit_rows(act):
    return lax.rsqrt(jnp.sum(act * act, axis=-1, keepdims=True) + 1e-06)


def mixer_forward_kernel(
    xn_ref, wq_ref, wk_ref, wv_ref, wg_ref, tq_ref, tk_ref, tv_ref, live_ref, acol_ref, arow_ref,
    pre_ref, gate_ref, oloc_ref, oread_ref, inv_ref, delta_ref, state_ref, final_ref,
    ext_ref,
):
    rows, width = oloc_ref.shape
    blocks = rows // BLOCK
    xn = xn_ref[...]
    pre = jnp.concatenate(
        [mm(xn, wq_ref[...]), mm(xn, wk_ref[...]), mm(xn, wv_ref[...])], axis=1
    ).astype(BF16)
    pre_ref[0] = pre
    ext_ref[...] = pre.astype(F32)
    gate_ref[...] = mm(xn[HALO:], wg_ref[...])
    live = live_ref[...]
    conv = head_features(ext_ref, tq_ref, tk_ref, tv_ref, live, rows, width)
    act = [c * sigmoid(c) for c in conv]
    q = (act[0] * unit_rows(act[0]) * width ** (-0.5)).astype(BF16)
    k = [(a * unit_rows(a)).astype(BF16) for a in act[1:3]]
    v = [a.astype(BF16) for a in act[3:5]]
    reach, strict, first, merges, eye = step_masks()
    cut = [slice(b * BLOCK, (b + 1) * BLOCK) for b in range(blocks)]
    kb = [jnp.concatenate([k[0][s], k[1][s]], axis=0) for s in cut]
    vb = [jnp.concatenate([v[0][s], v[1][s]], axis=0) for s in cut]
    qb = [q[s] for s in cut]
    ccol = [acol_ref[0, b, :, 0:1] for b in range(blocks)]
    bcol = [acol_ref[0, b, :, 1:2] for b in range(blocks)]
    crow = [arow_ref[0, b, 0:1, :] for b in range(blocks)]
    brow = [arow_ref[0, b, 1:2, :] for b in range(blocks)]
    fade = [jnp.exp(jnp.where(reach, c - r, -1e30)) for c, r in zip(ccol, crow)]
    gram = [mm(x, x, NT) for x in kb]
    system = [jnp.where(strict, f * g, 0.0) * b for f, g, b in zip(fade, gram, bcol)]
    inv = unit_lower_inverse(system, first, merges, eye)
    for b in range(blocks):
        inv_ref[0, b] = inv[b]
    local = [mm2(t * b, x) for t, b, x in zip(inv, brow, vb)]
    reads = [mm2(t * (b * jnp.exp(c)), x) for t, b, c, x in zip(inv, brow, crow, kb)]
    score = [f[:BLOCK] * mm(x, y, NT) for f, x, y in zip(fade, qb, kb)]
    state = jnp.concatenate([jnp.zeros((width, width), F32), eye], axis=1)
    for b in range(blocks):
        state_ref[0, b] = state
        grow = jnp.exp(ccol[b])
        last = ccol[b][BLOCK - 1 : BLOCK]
        if b == 0:
            delta = jnp.concatenate([local[b], -reads[b]], axis=1)
        else:
            delta = jnp.concatenate([local[b], jnp.zeros((STEPS, width), F32)], axis=1) - mm(
                reads[b], state
            )
        delta_ref[0, b] = delta
        out = mm(score[b], delta) + grow[:BLOCK] * mm(qb[b], state)
        oloc_ref[cut[b], :] = out[:, :width]
        oread_ref[0, cut[b], :] = out[:, width:]
        tail = kb[b].astype(F32) * jnp.exp(last - ccol[b])
        state = jnp.exp(last) * state + mm(tail, delta, TN)
    final_ref[0] = state.astype(BF16)


def head_columns(rows, width):
    return pl.BlockSpec((rows, width), lambda h: (0, h))


def whole(shape):
    return pl.BlockSpec(shape, lambda h: (0,) * len(shape))


def per_head(shape):
    return pl.BlockSpec((1,) + shape, lambda h: (h,) + (0,) * len(shape))


def mixer_forward(xn, w_query, w_key, w_value, w_outgate, taps, live, acol, arow, heads, width):
    ext_rows, depth = xn.shape
    rows = ext_rows - HALO
    blocks = rows // BLOCK
    conv_query, conv_key, conv_value = taps
    out = jax.ShapeDtypeStruct
    return pl.pallas_call(
        mixer_forward_kernel,
        grid=(heads,),
        in_specs=[
            whole((ext_rows, depth)),
            head_columns(depth, width),
            head_columns(depth, 2 * width),
            head_columns(depth, 2 * width),
            head_columns(depth, width),
            head_columns(KW, width),
            head_columns(KW, 2 * width),
            head_columns(KW, 2 * width),
            whole(live.shape),
            per_head(acol.shape[1:]),
            per_head(arow.shape[1:]),
        ],
        out_specs=[
            per_head((ext_rows, 5 * width)),
            head_columns(rows, width),
            head_columns(rows, width),
            per_head((rows, width)),
            per_head((blocks, STEPS, STEPS)),
            per_head((blocks, STEPS, 2 * width)),
            per_head((blocks, width, 2 * width)),
            per_head((width, 2 * width)),
        ],
        out_shape=[
            out((heads, ext_rows, 5 * width), BF16),
            out((rows, heads * width), F32),
            out((rows, heads * width), F32),
            out((heads, rows, width), F32),
            out((heads, blocks, STEPS, STEPS), F32),
            out((heads, blocks, STEPS, 2 * width), F32),
            out((heads, blocks, width, 2 * width), F32),
            out((heads, width, 2 * width), BF16),
        ],
        scratch_shapes=[pltpu.VMEM((ext_rows, 5 * width), F32)],
        compiler_params=pltpu.CompilerParams(vmem_limit_bytes=VMEM_LIMIT),
        cost_estimate=cost(40),
        name="mixer_forward",
    )(xn, w_query, w_key, w_value, w_outgate, conv_query, conv_key, conv_value, live, acol, arow)


def conv_pull(ext_ref, pad_ref, d_conv, taps, live, columns, rows, dtap_ref):
    total = None
    for back in range(KW):
        part = d_conv if back == 0 else d_conv * live[:, back : back + 1]
        source = ext_ref[pl.ds(HALO - back, rows), columns]
        dtap_ref[KW - 1 - back : KW - back, :] = jnp.sum(part * source, axis=0, keepdims=True)
        pad_ref[pl.ds(HALO, rows), :] = part
        moved = pad_ref[pl.ds(back, rows + HALO), :] * taps[KW - 1 - back : KW - back, :]
        total = moved if total is None else total + moved
    return total


def silu_pull(c, grad):
    s = sigmoid(c)
    return grad * (s + c * s * (1.0 - s))


def unit_pull(act, grad, scale):
    r = unit_rows(act)
    return scale * r * (grad - act * (r * r * jnp.sum(act * grad, axis=-1, keepdims=True)))


def mixer_backward_kernel(
    pre_ref, tq_ref, tk_ref, tv_ref, live_ref, acol_ref, arow_ref,
    inv_ref, delta_ref, state_ref, start_ref, after_ref, dout_ref,
    d_ref, rim_ref, dtap_ref, aux_ref,
    ext_ref, pad_ref,
):
    rows, width = dout_ref.shape
    blocks = rows // BLOCK
    ext_ref[...] = pre_ref[0].astype(F32)
    live = live_ref[...]
    conv = head_features(ext_ref, tq_ref, tk_ref, tv_ref, live, rows, width)
    act = [c * sigmoid(c) for c in conv]
    q = (act[0] * unit_rows(act[0]) * width ** (-0.5)).astype(BF16)
    k = [(a * unit_rows(a)).astype(BF16) for a in act[1:3]]
    reach, strict, _, _, _ = step_masks()
    start = start_ref[0]
    after = after_ref[0].astype(F32)
    pieces = [None] * blocks
    for b in range(blocks - 1, -1, -1):
        s = slice(b * BLOCK, (b + 1) * BLOCK)
        kb = jnp.concatenate([k[0][s], k[1][s]], axis=0)
        kf = kb.astype(F32)
        qb = q[s]
        ccol = acol_ref[0, b, :, 0:1]
        bcol = acol_ref[0, b, :, 1:2]
        crow = arow_ref[0, b, 0:1, :]
        last = ccol[BLOCK - 1 : BLOCK]
        fade = jnp.exp(jnp.where(reach, ccol - crow, -1e30))
        grow = jnp.exp(ccol)
        weight = jnp.exp(last - ccol)
        dout = dout_ref[s, :]
        gdout = grow[:BLOCK] * dout
        delta = delta_ref[0, b, :, :width] + mm(delta_ref[0, b, :, width:], start)
        state = state_ref[0, b, :, :width] + mm(state_ref[0, b, :, width:], start)
        fade_q = fade[:BLOCK]
        score = fade_q * mm(qb, kb, NT)
        d_delta = mm(score, dout, TN) + weight * mm(kb, after)
        d_rhs = mm(inv_ref[0, b], d_delta, TN)
        d_score = fade_q * mm(dout, delta, NT)
        d_known = -(bcol * grow) * d_rhs
        d_tail = weight * mm(delta, after, NT)
        d_gram = jnp.where(strict, -bcol * fade * mm(d_rhs, delta, NT), 0.0)
        dq = mm(gdout, state, NT) + mm(d_score, kb)
        dk_row = mm(d_known, state, NT) + mm(d_gram, kb)
        dk_col = mm(d_gram, kb, TN) + mm(d_score, qb, TN) + d_tail
        d_beta = (1.0 - bcol) * jnp.sum(d_rhs * delta, axis=-1, keepdims=True)
        d_log = jnp.sum(kf * (dk_row - dk_col), axis=-1, keepdims=True)
        d_logq = jnp.sum(qb.astype(F32) * dq, axis=-1, keepdims=True)
        d_last = jnp.sum(kf * d_tail) + jnp.sum(jnp.exp(last) * after * state)
        tok = lax.broadcasted_iota(jnp.int32, (BLOCK, 1), 0)
        d_token = d_log[:BLOCK] + d_log[BLOCK:] + d_logq
        d_token = d_token + jnp.where(tok == BLOCK - 1, d_last, 0.0)
        aux_ref[0, b, :, 0:1] = d_beta
        aux_ref[0, b, 0:BLOCK, 1:2] = d_token
        dk = dk_row + dk_col
        pieces[b] = (dq, dk[:BLOCK], dk[BLOCK:], (bcol * d_rhs)[:BLOCK], (bcol * d_rhs)[BLOCK:])
        after = jnp.exp(last) * after + mm(qb, gdout, TN) + mm(kb, d_known, TN)
    d_act = [jnp.concatenate([pieces[b][i] for b in range(blocks)], axis=0) for i in range(5)]
    d_act[0] = unit_pull(act[0], d_act[0], width ** (-0.5))
    d_act[1] = unit_pull(act[1], d_act[1], 1.0)
    d_act[2] = unit_pull(act[2], d_act[2], 1.0)
    d_conv = [silu_pull(c, g) for c, g in zip(conv, d_act)]
    pad_ref[0:HALO, :] = jnp.zeros((HALO, width), F32)
    pad_ref[pl.ds(HALO + rows, HALO), :] = jnp.zeros((HALO, width), F32)
    sides = ((tq_ref, 0), (tk_ref, 0), (tk_ref, width), (tv_ref, 0), (tv_ref, width))
    for i, (tap_ref, at) in enumerate(sides):
        lanes = pl.ds(i * width, width)
        grad = conv_pull(
            ext_ref, pad_ref, d_conv[i], tap_ref[:, at : at + width], live, lanes, rows,
            dtap_ref.at[:, lanes],
        )
        rim_ref[:, lanes] = grad[:HALO].astype(BF16)
        d_ref[:, lanes] = grad[HALO:].astype(BF16)


def mixer_backward(pre, taps, live, acol, arow, inv, delta, state, start, after, dout):
    heads, ext_rows, _ = pre.shape
    rows = ext_rows - HALO
    width = start.shape[-1]
    conv_query, conv_key, conv_value = taps
    out = jax.ShapeDtypeStruct
    columns = heads * width
    return pl.pallas_call(
        mixer_backward_kernel,
        grid=(heads,),
        in_specs=[
            per_head(pre.shape[1:]),
            head_columns(KW, width),
            head_columns(KW, 2 * width),
            head_columns(KW, 2 * width),
            whole(live.shape),
            per_head(acol.shape[1:]),
            per_head(arow.shape[1:]),
            per_head(inv.shape[1:]),
            per_head(delta.shape[1:]),
            per_head(state.shape[1:]),
            per_head((width, width)),
            per_head((width, width)),
            head_columns(rows, width),
        ],
        out_specs=[
            head_columns(rows, 5 * width),
            head_columns(HALO, 5 * width),
            head_columns(KW, 5 * width),
            per_head(acol.shape[1:]),
        ],
        out_shape=[
            out((rows, 5 * columns), BF16),
            out((HALO, 5 * columns), BF16),
            out((KW, 5 * columns), F32),
            out(acol.shape, F32),
        ],
        scratch_shapes=[
            pltpu.VMEM((ext_rows, 5 * width), F32),
            pltpu.VMEM((rows + 2 * HALO, width), F32),
        ],
        compiler_params=pltpu.CompilerParams(vmem_limit_bytes=VMEM_LIMIT),
        cost_estimate=cost(35),
        name="mixer_backward",
    )(pre, conv_query, conv_key, conv_value, live, acol, arow, inv, delta, state, start, after, dout)


def gated_forward_kernel(oloc_ref, oread_ref, start_ref, gate_ref, gain_ref, out_ref, gated_ref):
    out = oloc_ref[...] + mm(oread_ref[0], start_ref[0])
    out_ref[...] = out
    gate = gate_ref[...]
    r = lax.rsqrt(jnp.mean(out * out, axis=-1, keepdims=True) + 1e-05)
    gated_ref[...] = (out * r * gain_ref[...] * (gate * sigmoid(gate))).astype(BF16)


def gated_forward(oloc, oread, start, gate_pre, out_gain):
    heads, rows, width = oread.shape
    out = jax.ShapeDtypeStruct
    return pl.pallas_call(
        gated_forward_kernel,
        grid=(heads,),
        in_specs=[
            head_columns(rows, width),
            per_head((rows, width)),
            per_head((width, width)),
            head_columns(rows, width),
            whole((1, width)),
        ],
        out_specs=[head_columns(rows, width), head_columns(rows, width)],
        out_shape=[out(oloc.shape, F32), out(oloc.shape, BF16)],
        cost_estimate=cost(6),
        name="gated_forward",
    )(oloc, oread, start, gate_pre, out_gain[None, :])


def gated_backward_kernel(
    out_ref, gate_ref, gain_ref, dgated_ref, oread_ref, dout_ref, dgate_ref, part_ref, dgain_ref
):
    out = out_ref[...]
    gate = gate_ref[...]
    gain = gain_ref[...]
    grad = dgated_ref[...]
    r = lax.rsqrt(jnp.mean(out * out, axis=-1, keepdims=True) + 1e-05)
    s = sigmoid(gate)
    unit = out * r
    dgate_ref[...] = (grad * unit * gain * (s + gate * s * (1.0 - s))).astype(BF16)
    through = grad * (gate * s)
    dgain_ref[0] = jnp.sum(through * unit, axis=0, keepdims=True)
    through = through * gain
    dout = r * (through - unit * jnp.mean(unit * through, axis=-1, keepdims=True))
    dout_ref[...] = dout
    part_ref[0] = mm(oread_ref[0], dout, TN).astype(BF16)


def gated_backward(out_all, gate_pre, out_gain, d_gated, oread):
    heads, rows, width = oread.shape
    out = jax.ShapeDtypeStruct
    return pl.pallas_call(
        gated_backward_kernel,
        grid=(heads,),
        in_specs=[
            head_columns(rows, width),
            head_columns(rows, width),
            whole((1, width)),
            head_columns(rows, width),
            per_head((rows, width)),
        ],
        out_specs=[
            head_columns(rows, width),
            head_columns(rows, width),
            per_head((width, width)),
            per_head((1, width)),
        ],
        out_shape=[
            out(out_all.shape, F32),
            out(out_all.shape, BF16),
            out((heads, width, width), BF16),
            out((heads, 1, width), F32),
        ],
        cost_estimate=cost(6),
        name="gated_backward",
    )(out_all, gate_pre, out_gain[None, :], d_gated, oread)


def carry_kernel(count, heads, backward, *refs):
    if backward:
        part_ref, maps_ref, result_ref, inbox, outbox, landed, send_sem, recv_sem, back_sem, land_sem = refs
    else:
        part_ref, result_ref, maps_ref, inbox, outbox, landed, send_sem, recv_sem, back_sem, land_sem = refs
    place = lax.axis_index("seq")
    group = lax.axis_index("dp")
    width = result_ref.shape[-1]
    stride = count // 16

    def keeper(h):
        return (2 * h + group) * stride

    barrier = pltpu.get_barrier_semaphore()

    def greet(step, carry):
        peer = lax.rem(place + step, count)
        pl.semaphore_signal(barrier, inc=1, device_id=(group, peer), device_id_type=MESH)
        return carry

    lax.fori_loop(1, count, greet, 0)
    pl.semaphore_wait(barrier, count - 1)

    def outgoing(h):
        return pltpu.make_async_remote_copy(
            src_ref=part_ref.at[h],
            dst_ref=inbox.at[place],
            send_sem=send_sem.at[h],
            recv_sem=recv_sem.at[place],
            device_id=(group, keeper(h)),
            device_id_type=MESH,
        )

    for h in range(heads):

        @pl.when(place != keeper(h))
        def _(h=h):
            outgoing(h).start()

        @pl.when(place == keeper(h))
        def _(h=h):
            inbox[pl.ds(place, 1)] = part_ref[h : h + 1]

    def scan_head(h):
        def returning(where):
            return pltpu.make_async_remote_copy(
                src_ref=outbox.at[where],
                dst_ref=landed.at[h],
                send_sem=back_sem.at[where],
                recv_sem=land_sem.at[h],
                device_id=(group, where),
                device_id_type=MESH,
            )

        def lap(step, state):
            where = count - 1 - step if backward else step
            outbox[pl.ds(where, 1)] = state[None].astype(BF16)

            @pl.when(where != place)
            def _():
                returning(where).start()
                pltpu.make_async_remote_copy(
                    src_ref=part_ref.at[h],
                    dst_ref=inbox.at[where],
                    send_sem=send_sem.at[h],
                    recv_sem=recv_sem.at[where],
                    device_id=(group, where),
                    device_id_type=MESH,
                ).wait_recv()

            @pl.when(where == place)
            def _():
                landed[h : h + 1] = outbox[pl.ds(where, 1)]

            got = inbox[pl.ds(where, 1)][0]
            high, low = halves(state)
            if backward:
                step_map = maps_ref[pl.ds(where, 1)][0][:, width:]
                state = mm(step_map, high, TN) + mm(step_map, low, TN) + got.astype(F32)
            else:
                step_map = got[:, width:]
                state = mm(step_map, high) + mm(step_map, low) + got[:, :width].astype(F32)
            return state

        lax.fori_loop(0, count, lap, jnp.zeros((width, width), F32))

        def finish(where, carry):
            @pl.when(where != place)
            def _():
                returning(where).wait_send()

            return carry

        lax.fori_loop(0, count, finish, 0)

    for h in range(heads):

        @pl.when(place == keeper(h))
        def _(h=h):
            scan_head(h)

    for h in range(heads):

        @pl.when(place != keeper(h))
        def _(h=h):
            outgoing(h).wait_send()
            pltpu.make_async_remote_copy(
                src_ref=outbox.at[0],
                dst_ref=landed.at[h],
                send_sem=back_sem.at[0],
                recv_sem=land_sem.at[h],
                device_id=(group, keeper(h)),
                device_id_type=MESH,
            ).wait_recv()

    result_ref[...] = landed[...]
    if not backward:
        maps_ref[...] = inbox[...]


def carry_states(part, maps, count):
    heads, width, columns = part.shape
    backward = maps is not None
    out = jax.ShapeDtypeStruct
    vmem = pl.BlockSpec(memory_space=pltpu.VMEM)
    result = out((heads, width, width), BF16)
    return pl.pallas_call(
        partial(carry_kernel, count, heads, backward),
        in_specs=[vmem] * (2 if backward else 1),
        out_specs=vmem if backward else [vmem, vmem],
        out_shape=result if backward else [result, out((count, width, columns), BF16)],
        scratch_shapes=[
            pltpu.VMEM((count, width, columns), BF16),
            pltpu.VMEM((count, width, width), BF16),
            pltpu.VMEM((heads, width, width), BF16),
            pltpu.SemaphoreType.DMA((heads,)),
            pltpu.SemaphoreType.DMA((count,)),
            pltpu.SemaphoreType.DMA((count,)),
            pltpu.SemaphoreType.DMA((heads,)),
        ],
        compiler_params=pltpu.CompilerParams(
            collective_id=1 if backward else 0, has_side_effects=True, vmem_limit_bytes=VMEM_LIMIT
        ),
        cost_estimate=cost(24),
        name="carry_backward" if backward else "carry_forward",
    )(*((part, maps) if backward else (part,)))


JOBS = 7
JOB = 768
LATE_JOBS = 10


def row_blocks(parity, sending):
    if sending:
        return (1, 3) if parity else (2, 3)
    return (0, 2) if parity else (0, 1)


def early_products_kernel(own_ref, got_ref, *refs):
    rhs_own, rhs_got, (send_a, send_b, keep_a, keep_b) = refs[:5], refs[5:10], refs[10:]
    tokens = rhs_own[0].shape[0]
    half = rhs_own[0].shape[1] // 2
    edge = got_ref.shape[0] // 4
    for parity, send_ref, keep_ref in ((0, send_a, keep_a), (1, send_b, keep_b)):
        segments = [(0, 0, parity * half, half), (0, 1, parity * half, half), (1, 2, parity * half, half)]
        segments.append((3, 4, 0, rhs_own[4].shape[1]) if parity else (2, 3, 0, rhs_own[3].shape[1]))
        for out_ref, sending in ((send_ref, True), (keep_ref, False)):
            at = 0
            for lhs, rhs, begin, size in segments:
                done = 0
                while done < size:
                    job, column = (at + done) // JOB, (at + done) % JOB
                    width = min(JOB - column, size - done)
                    lanes = slice(begin + done, begin + done + width)
                    for row, block in enumerate(row_blocks(parity, sending)):
                        rows = slice(block * edge, (block + 1) * edge)
                        cut = slice(lhs * tokens, (lhs + 1) * tokens)
                        total = mm(own_ref[rows, cut], rhs_own[rhs][:, lanes]) + mm(
                            got_ref[rows, cut], rhs_got[rhs][:, lanes]
                        )
                        out_ref[job, row * edge : (row + 1) * edge, column : column + width] = total.astype(BF16)
                    done += width
                at += size


def early_products(own, got, rhs_own, rhs_got):
    rows = got.shape[0] // 2
    shape = jax.ShapeDtypeStruct((JOBS, rows, JOB), BF16)
    vmem = pl.BlockSpec(memory_space=pltpu.VMEM)
    return pl.pallas_call(
        early_products_kernel,
        in_specs=[vmem] * 12,
        out_specs=[vmem] * 4,
        out_shape=[shape] * 4,
        compiler_params=pltpu.CompilerParams(vmem_limit_bytes=VMEM_LIMIT),
        cost_estimate=cost(10),
        name="early_products",
    )(own, got, *rhs_own, *rhs_got)


def input_pull_kernel(
    d_ref, rim_ref, dg_ref, rates_ref, wq_ref, wk_ref, wv_ref, wg_ref, wr_ref, x_ref, gain_ref, resid_ref,
    settled_ref, grad_ref, dgain_ref, total_ref,
):
    head = pl.program_id(0)
    rows = d_ref.shape[0]
    width = wq_ref.shape[1]
    last = d_ref[rows - HALO :, :].astype(F32) + rim_ref[...].astype(F32)
    settled = jnp.concatenate([d_ref[: rows - HALO, :], last.astype(BF16)], axis=0)
    settled_ref[...] = settled
    part = (
        mm(settled[:, :width], wq_ref[...], NT)
        + mm(settled[:, width : 3 * width], wk_ref[...], NT)
        + mm(settled[:, 3 * width :], wv_ref[...], NT)
        + mm(dg_ref[...], wg_ref[...], NT)
    )

    @pl.when(head == 0)
    def _():
        total_ref[...] = part + mm(rates_ref[...], wr_ref[...], NT)

    @pl.when(head > 0)
    def _():
        total_ref[...] += part

    @pl.when(head == pl.num_programs(0) - 1)
    def _():
        x = x_ref[...].astype(F32)
        grad = total_ref[...]
        r = lax.rsqrt(jnp.mean(x * x, axis=-1, keepdims=True) + 1e-06)
        unit = x * r
        through = grad * gain_ref[...]
        pulled = r * (through - unit * jnp.mean(unit * through, axis=-1, keepdims=True))
        grad_ref[...] = (resid_ref[...] + pulled).astype(BF16)
        dgain_ref[...] = jnp.sum(grad * unit, axis=0, keepdims=True)


def input_pull(d_all, rim, d_outgate, d_rates, weights, w_rates, x, gain, d_resid, heads):
    rows, depth = x.shape
    width = d_outgate.shape[1] // heads
    out = jax.ShapeDtypeStruct
    w_query, w_key, w_value, w_outgate = weights
    return pl.pallas_call(
        input_pull_kernel,
        grid=(heads,),
        in_specs=[
            head_columns(rows, 5 * width),
            head_columns(HALO, 5 * width),
            head_columns(rows, width),
            whole(d_rates.shape),
            head_columns(depth, width),
            head_columns(depth, 2 * width),
            head_columns(depth, 2 * width),
            head_columns(depth, width),
            whole(w_rates.shape),
            whole(x.shape),
            whole((1, depth)),
            whole(d_resid.shape),
        ],
        out_specs=[head_columns(rows, 5 * width), whole(x.shape), whole((1, depth))],
        out_shape=[out(d_all.shape, BF16), out(x.shape, BF16), out((1, depth), F32)],
        scratch_shapes=[pltpu.VMEM((rows, depth), F32)],
        compiler_params=pltpu.CompilerParams(vmem_limit_bytes=VMEM_LIMIT),
        cost_estimate=cost(10),
        name="input_pull",
    )(d_all, rim, d_outgate, d_rates, w_query, w_key, w_value, w_outgate, w_rates, x, gain[None, :], d_resid)


def reduce_kernel(
    arr_a, arr_b, keep_a, keep_b, own_ref, got_ref, rhs_ref, small_ref,
    early_ref, late_ref, total_ref,
    e_keep2, e_send2, e_got2, e_keep3, e_send3, e_got3,
    rhs_got, l_send1, l_got1, l_keep2, l_send2, l_got2, l_keep3, l_send3, l_got3, small_got,
    dp_sem, e_sem2, e_sem3, l_sem1, l_sem2, l_sem3, s_sem,
):
    seq = lax.axis_index("seq")
    group = lax.axis_index("dp")
    x, y, z = seq % 2, (seq // 2) % 2, seq // 4
    peers = (seq + 1 - 2 * x, seq + 2 - 4 * y)

    def above(move):
        return ((z + move) % 4) * 4 + seq % 4

    core = {"dp": 1 - group, "seq": seq}

    def at(place):
        return {"dp": group, "seq": place}

    def send(source, target, sems, index, device):
        return pltpu.make_async_remote_copy(
            src_ref=source,
            dst_ref=target,
            send_sem=sems.at[(0,) + index],
            recv_sem=sems.at[(1,) + index],
            device_id=device,
            device_id_type=MESH,
        )

    barrier = pltpu.get_barrier_semaphore()
    everyone = [core, at(peers[0]), at(peers[1])] + [at(above(move)) for move in (1, 2, 3)]
    for device in everyone:
        pl.semaphore_signal(barrier, inc=1, device_id=device, device_id_type=MESH)
    pl.semaphore_wait(barrier, len(everyone))

    swap = send(rhs_ref, rhs_got, dp_sem, (), core)
    swap.start()

    z1 = seq + 4 - 8 * (z % 2)
    z2 = (z + 2 - 4 * (z // 2)) * 4 + seq % 4
    hops = [core, at(peers[0]), at(peers[1]), at(z1), at(z2)]

    def hop(step):
        return send(total_ref.at[step], small_got.at[step], s_sem, (step,), hops[step])

    def next_hop(step):
        if step > 0:
            hop(step - 1).wait_recv()
            value = total_ref[step - 1] + small_got[step - 1]
        else:
            value = small_ref[...]
        total_ref[step] = value
        if step < len(hops):
            hop(step).start()

    next_hop(0)
    keeps, arrs = (keep_a, keep_b), (arr_a, arr_b)
    quarter = e_keep2.shape[2]
    share = e_keep3.shape[2]

    def copy2(p, i):
        return send(e_send2.at[p, i], e_got2.at[p, i], e_sem2, (p, i), at(peers[1 - p]))

    def copy3(p, i, move):
        return send(
            e_send3.at[p, i, pl.ds((move - 1) * share, share)],
            e_got3.at[p, i, move - 1],
            e_sem3,
            (p, i, move - 1),
            at(above(move)),
        )

    def early2(i, carry):
        for p in range(2):
            total = keeps[p][i].astype(F32) + arrs[p][i].astype(F32)
            e_keep2[p, i] = total[:quarter].astype(BF16)
            e_send2[p, i] = total[quarter:].astype(BF16)
            copy2(p, i).start()
        return carry

    lax.fori_loop(0, JOBS, early2, 0)
    next_hop(1)
    swap.wait_recv()
    job = l_got1.shape[-1]

    def product(lhs, lanes, p, sending):
        parts = []
        for block in row_blocks(p, sending):
            rows = pl.ds(block * quarter, quarter)
            parts.append(mm(own_ref[rows, :], rhs_ref[:, lanes]) + mm(got_ref[rows, :], rhs_got[:, lanes]))
        return parts

    def lanes_of(m):
        return pl.ds(pl.multiple_of(m * job, job), job)

    def late_copy1(p, i):
        return send(l_send1.at[p, i], l_got1.at[p, i], l_sem1, (p, i), at(peers[p]))

    def late_copy2(p, i):
        return send(l_send2.at[p, i], l_got2.at[p, i], l_sem2, (p, i), at(peers[1 - p]))

    def late_copy3(p, i, move):
        return send(
            l_send3.at[p, i, pl.ds((move - 1) * share, share)],
            l_got3.at[p, i, move - 1],
            l_sem3,
            (p, i, move - 1),
            at(above(move)),
        )

    def late1(i, carry):
        for p in range(2):
            low, high = product(None, lanes_of(2 * i + p), p, True)
            l_send1[p, i, 0:quarter] = low.astype(BF16)
            l_send1[p, i, quarter : 2 * quarter] = high.astype(BF16)
            late_copy1(p, i).start()
        return carry

    lax.fori_loop(0, LATE_JOBS // 2, late1, 0)
    next_hop(2)

    def early3(i, carry):
        for p in range(2):
            copy2(p, i).wait_recv()
            total = e_keep2[p, i].astype(F32) + e_got2[p, i].astype(F32)
            e_keep3[p, i] = total[:share].astype(BF16)
            e_send3[p, i] = total[share:].astype(BF16)
            for move in (1, 2, 3):
                copy3(p, i, move).start()
        return carry

    lax.fori_loop(0, JOBS, early3, 0)
    next_hop(3)

    def late2(i, carry):
        for p in range(2):
            low, high = product(None, lanes_of(2 * i + p), p, False)
            late_copy1(p, i).wait_recv()
            l_keep2[p, i] = (low + l_got1[p, i, 0:quarter].astype(F32)).astype(BF16)
            l_send2[p, i] = (high + l_got1[p, i, quarter : 2 * quarter].astype(F32)).astype(BF16)
            late_copy2(p, i).start()
        return carry

    lax.fori_loop(0, LATE_JOBS // 2, late2, 0)
    next_hop(4)

    def early_end(i, carry):
        for p in range(2):
            total = e_keep3[p, i].astype(F32)
            for move in (1, 2, 3):
                copy3(p, i, move).wait_recv()
                total = total + e_got3[p, i, move - 1].astype(F32)
            early_ref[p, i] = total
        return carry

    lax.fori_loop(0, JOBS, early_end, 0)
    next_hop(5)

    def late3(i, carry):
        for p in range(2):
            late_copy2(p, i).wait_recv()
            total = l_keep2[p, i].astype(F32) + l_got2[p, i].astype(F32)
            l_keep3[p, i] = total[:share].astype(BF16)
            l_send3[p, i] = total[share:].astype(BF16)
            for move in (1, 2, 3):
                late_copy3(p, i, move).start()
        return carry

    lax.fori_loop(0, LATE_JOBS // 2, late3, 0)

    def late_end(i, carry):
        for p in range(2):
            total = l_keep3[p, i].astype(F32)
            for move in (1, 2, 3):
                late_copy3(p, i, move).wait_recv()
                total = total + l_got3[p, i, move - 1].astype(F32)
            late_ref[p, i] = total
        return carry

    lax.fori_loop(0, LATE_JOBS // 2, late_end, 0)

    def early_sent(i, carry):
        for p in range(2):
            copy2(p, i).wait_send()
            for move in (1, 2, 3):
                copy3(p, i, move).wait_send()
        return carry

    def late_sent(i, carry):
        for p in range(2):
            late_copy1(p, i).wait_send()
            late_copy2(p, i).wait_send()
            for move in (1, 2, 3):
                late_copy3(p, i, move).wait_send()
        return carry

    lax.fori_loop(0, JOBS, early_sent, 0)
    lax.fori_loop(0, LATE_JOBS // 2, late_sent, 0)
    swap.wait_send()
    for step in range(len(hops)):
        hop(step).wait_send()


def reduce_all(arrived, kept, own, got, rhs, small):
    half = kept[0].shape[1]
    quarter, share = half // 2, half // 8
    count = LATE_JOBS // 2
    job = rhs.shape[1] // LATE_JOBS
    out = jax.ShapeDtypeStruct
    vmem = pl.BlockSpec(memory_space=pltpu.VMEM)
    buffers = []
    for jobs, width in ((JOBS, JOB), (count, job)):
        if width == job:
            buffers += [(rhs.shape, BF16), ((2, jobs, half, width), BF16), ((2, jobs, half, width), BF16)]
        buffers += [((2, jobs, quarter, width), BF16)] * 3
        buffers += [((2, jobs, share, width), BF16), ((2, jobs, 3 * share, width), BF16)]
        buffers += [((2, jobs, 3, share, width), BF16)]
    buffers += [((5,) + small.shape, F32)]
    dma = pltpu.SemaphoreType.DMA
    return pl.pallas_call(
        reduce_kernel,
        in_specs=[vmem] * 8,
        out_specs=[vmem] * 3,
        out_shape=[
            out((2, JOBS, share, JOB), F32),
            out((2, count, share, job), F32),
            out((6,) + small.shape, F32),
        ],
        scratch_shapes=[pltpu.VMEM(shape, kind) for shape, kind in buffers]
        + [
            dma((2,)),
            dma((2, 2, JOBS)),
            dma((2, 2, JOBS, 3)),
            dma((2, 2, count)),
            dma((2, 2, count)),
            dma((2, 2, count, 3)),
            dma((2, 5)),
        ],
        compiler_params=pltpu.CompilerParams(
            collective_id=2, has_side_effects=True, vmem_limit_bytes=VMEM_LIMIT
        ),
        cost_estimate=cost(90),
        name="reduce_all",
    )(*arrived, *kept, own, got, rhs, small)

def seq_positions(extras, first, total_rows):
    sizes = extras + (SHORTEST - 1)
    ends = jnp.cumsum(sizes)
    starts = ends - sizes
    row_ids = first + jnp.arange(total_rows, dtype=jnp.int32)
    inside = (row_ids[:, None] >= starts[None, :]) & (row_ids[:, None] < ends[None, :])
    return row_ids - jnp.sum(jnp.where(inside, starts[None, :], 0), axis=1)


def rms_scale(field, gain, epsilon):
    return field * lax.rsqrt(jnp.mean(field * field, axis=-1, keepdims=True) + epsilon) * gain


def rms_pull(field, gain, grad):
    scale = lax.rsqrt(jnp.mean(field * field, axis=-1, keepdims=True) + 1e-06)
    unit = field * scale
    through = grad * gain
    pulled = scale * (through - unit * jnp.mean(unit * through, axis=-1, keepdims=True))
    return pulled, jnp.sum(grad * unit, axis=0)


def dot32(a, b, dims=NN):
    return lax.dot_general(a, b, dims, preferred_element_type=F32)


def swap_core(value):
    count = lax.axis_size("dp")
    return lax.ppermute(value, "dp", [(i, (i + 1) % count) for i in range(count)])


def relative_selector(depth, group, seq):
    block = depth // 32
    index = jnp.arange(depth, dtype=jnp.int32)
    row, place, side = index % block, (index // block) % 16, index // (16 * block)
    x = (seq % 2) ^ (place // 8)
    y = ((seq // 2) % 2) ^ ((place // 4) % 2)
    z = (seq // 4 + place) % 4
    source = (((group + side) % 2) * 16 + z * 4 + y * 2 + x) * block + row
    return (index[:, None] == source[None, :]).astype(BF16)


def neighbour_route(bit):
    return [(i, i ^ bit) for i in range(16)]


def by_head(field, heads, begin, size):
    rows = field.shape[0]
    return field.reshape(rows, heads, -1)[:, :, begin : begin + size].reshape(rows, heads * size)


def per_device(
    block_input, lengths, attn_gain, w_query, w_key, w_value, w_outgate, w_beta, w_decay, beta_bias,
    decay_rate, conv_query, conv_key, conv_value, out_gain, w_out, mlp_gain, w_gate, w_up, w_down,
    out_grad,
):
    rows, depth = block_input.shape
    heads = decay_rate.shape[0]
    width = out_gain.shape[0]
    blocks = rows // BLOCK
    count = lax.axis_size("seq")
    seq = lax.axis_index("seq")
    group = lax.axis_index("dp")
    places = seq_positions(lengths[0], seq * rows, rows)

    halo = lax.ppermute(block_input[rows - HALO :], "seq", [(i, i + 1) for i in range(count - 1)])
    xf = block_input.astype(F32)
    normed_b = rms_scale(xf, attn_gain, 1e-06).astype(BF16)
    ext_b = jnp.concatenate([rms_scale(halo.astype(F32), attn_gain, 1e-06).astype(BF16), normed_b], axis=0)
    rates = dot32(normed_b, jnp.concatenate([w_beta, w_decay], axis=1))
    beta_pre, decay_pre = rates[:, : heads * REFLECTS], rates[:, heads * REFLECTS :]
    betas = jax.nn.sigmoid(beta_pre + beta_bias)
    log_rate = jnp.where((places == 0)[:, None], RESET_LOG, -decay_rate * jax.nn.softplus(decay_pre))
    tri = jnp.tril(jnp.ones((BLOCK, BLOCK), F32))
    cumul = jnp.einsum(
        "ts,bsh->hbt", tri, log_rate.reshape(blocks, BLOCK, heads), precision=lax.Precision.HIGHEST
    )
    cumul = jnp.concatenate([cumul] * REFLECTS, axis=-1)
    beta_steps = betas.reshape(blocks, BLOCK, heads, REFLECTS).transpose(2, 0, 3, 1).reshape(heads, blocks, STEPS)
    arow = jnp.stack([cumul, beta_steps] + [jnp.zeros_like(cumul)] * 6, axis=2)
    acol = arow.transpose(0, 1, 3, 2)
    live = (places[:, None] >= jnp.arange(8, dtype=jnp.int32)[None, :]).astype(F32)
    taps = (conv_query, conv_key, conv_value)

    pre, gate_pre, oloc, oread, inv, delta, state, maps = mixer_forward(
        ext_b, w_query, w_key, w_value, w_outgate, taps, live, acol, arow, heads, width
    )
    start, all_maps = carry_states(maps, None, count)
    out_all, gated_b = gated_forward(oloc, oread, start, gate_pre, out_gain)

    resid = xf + dot32(gated_b, w_out)
    mlp_b = rms_scale(resid, mlp_gain, 1e-06).astype(BF16)
    gate_act = dot32(mlp_b, w_gate)
    up_act = dot32(mlp_b, w_up)
    gate_sig = jax.nn.sigmoid(gate_act)
    hidden_b = (gate_act * gate_sig * up_act).astype(BF16)
    block_output = (resid + dot32(hidden_b, w_down)).astype(BF16)
    d_hidden = dot32(out_grad, w_down, NT)
    d_gate_b = (d_hidden * up_act * (gate_sig + gate_act * gate_sig * (1.0 - gate_sig))).astype(BF16)
    d_up_b = (d_hidden * gate_act * gate_sig).astype(BF16)
    d_mlp = dot32(d_gate_b, w_gate, NT) + dot32(d_up_b, w_up, NT)
    d_resid_mlp, grad_mlp_gain = rms_pull(resid, mlp_gain, d_mlp)
    d_resid = out_grad.astype(F32) + d_resid_mlp
    d_branch_b = d_resid.astype(BF16)
    d_gated = dot32(d_branch_b, w_out, NT)
    d_out, d_outgate_b, part, grad_out_gain = gated_backward(out_all, gate_pre, out_gain, d_gated, oread)

    w_rates = jnp.concatenate([w_beta, w_decay], axis=1)
    compact = count == 16
    rhs_own = (d_gate_b, d_up_b, hidden_b, gated_b, d_outgate_b)
    if compact:
        rhs_got = tuple(swap_core(rhs) for rhs in rhs_own)
        lhs = jnp.concatenate([mlp_b, out_grad, d_branch_b, normed_b], axis=0)
        own_l = lax.dot_general(
            relative_selector(depth, group, seq), lhs, (((0,), (1,)), ((), ())), preferred_element_type=F32
        ).astype(BF16)
        got_l = swap_core(own_l[depth // 2 :])
    after = carry_states(part, all_maps, count)
    if compact:
        rhs_own, rhs_got, own_l, got_l, after = lax.optimization_barrier((rhs_own, rhs_got, own_l, got_l, after))
        send_a, send_b, keep_a, keep_b = early_products(own_l, got_l, rhs_own, rhs_got)
        arr_a = lax.ppermute(send_a, "seq", neighbour_route(1))
        arr_b = lax.ppermute(send_b, "seq", neighbour_route(2))
        after = lax.optimization_barrier((after, keep_a))[0]
    d_all, rim, d_taps, aux = mixer_backward(
        pre, taps, live, acol, arow, inv, delta, state, start, after, d_out
    )
    rim = lax.ppermute(rim, "seq", [(i, i - 1) for i in range(1, count)])
    d_beta = aux[:, :, :, 0].reshape(heads, blocks, REFLECTS, BLOCK).transpose(1, 3, 0, 2).reshape(rows, -1)
    d_log = jnp.einsum(
        "st,hbs->bth", tri, aux[:, :, :BLOCK, 1], precision=lax.Precision.HIGHEST
    ).reshape(rows, heads)
    d_log = jnp.where((places == 0)[:, None], 0.0, d_log)
    grad_decay_rate = jnp.sum(-jax.nn.softplus(decay_pre) * d_log, axis=0)
    d_decay = -decay_rate * jax.nn.sigmoid(decay_pre) * d_log
    grad_beta_bias = jnp.sum(d_beta, axis=0)
    d_rates_b = jnp.concatenate([d_beta, d_decay], axis=1).astype(BF16)
    d_all, input_grad, grad_attn_gain = input_pull(
        d_all, rim, d_outgate_b, d_rates_b, (w_query, w_key, w_value, w_outgate), w_rates,
        block_input, attn_gain, d_resid, heads,
    )
    grad_rates = dot32(d_rates_b, normed_b, TN)
    misc = jnp.concatenate([jnp.sum(grad_out_gain, axis=(0, 1)), grad_beta_bias, grad_decay_rate])
    edge = misc.shape[0]
    small = jnp.concatenate(
        [
            d_taps.reshape(-1, depth),
            grad_attn_gain,
            grad_mlp_gain[None],
            jnp.pad(misc, (0, depth - edge))[None],
            jnp.zeros((1, depth), F32),
            grad_rates,
        ],
        axis=0,
    )
    devices = count * lax.axis_size("dp")
    share = depth // devices
    here = (group * count + seq) * share
    columns = heads * width
    ff = w_gate.shape[1]
    if compact:
        early, late, totals = reduce_all(
            (arr_a, arr_b), (keep_a, keep_b), own_l[: depth // 2, 3 * rows :], got_l[:, 3 * rows :], d_all, small
        )
        small = totals[-1]
        early = [early[p].transpose(1, 0, 2).reshape(share, -1) for p in range(2)]
        late = late.transpose(2, 1, 0, 3).reshape(share, -1)
        half = ff // 2
        sums = [
            jnp.concatenate([early[0][:, :half], early[1][:, :half]], axis=1),
            jnp.concatenate([early[0][:, half : 2 * half], early[1][:, half : 2 * half]], axis=1),
            jnp.concatenate([early[0][:, 2 * half : 3 * half], early[1][:, 2 * half : 3 * half]], axis=1),
            early[0][:, 3 * half : 3 * half + columns],
            early[1][:, 3 * half : 3 * half + columns],
        ]
    else:
        small = lax.psum(small, ("dp", "seq"))
        pairs = zip((mlp_b, mlp_b, out_grad, d_branch_b, normed_b, normed_b), rhs_own + (d_all,))
        sums = [
            lax.psum_scatter(dot32(lhs, rhs, TN), ("dp", "seq"), scatter_dimension=0, tiled=True)
            for lhs, rhs in pairs
        ]
        late = sums.pop()
    taps_sum = small[: KW * 5].reshape(KW, -1)
    own_small = lax.dynamic_slice(small[KW * 5 :], (0, here), (small.shape[0] - KW * 5, share))
    misc = small[KW * 5 + 2]
    marks = ((0, width), (width, 2 * width), (3 * width, 2 * width))
    taps_out = [by_head(taps_sum, heads, begin, size) for begin, size in marks]
    trunk = [by_head(late, heads, begin, size) for begin, size in marks]
    rates_sum = own_small[4:].T
    return (
        block_output,
        input_grad,
        own_small[0],
        trunk[0],
        trunk[1],
        trunk[2],
        sums[4],
        rates_sum[:, : heads * REFLECTS],
        rates_sum[:, heads * REFLECTS :],
        misc[width : width + heads * REFLECTS],
        misc[width + heads * REFLECTS : edge],
        taps_out[0],
        taps_out[1],
        taps_out[2],
        misc[:width],
        sums[3].T,
        own_small[1],
        sums[0],
        sums[1],
        sums[2].T,
    )


def solution(mesh):
    tokens = P(("dp", "seq"), None)
    column = P(None, ("dp", "seq"))
    vector = P(("dp", "seq"))
    in_specs = (tokens, P("dp", None)) + (P(),) * 18 + (tokens,)
    out_specs = (
        (tokens, tokens, vector)
        + (tokens,) * 6
        + (P(),) * 6
        + (column, vector, tokens, tokens, column)
    )
    return jax.shard_map(
        per_device, mesh=mesh, in_specs=in_specs, out_specs=out_specs, check_vma=False
    )
```

```python
from functools import partial

import jax
import jax.numpy as jnp
from jax import lax
from jax.experimental import pallas as pl
from jax.experimental.pallas import tpu as pltpu
from jax.sharding import PartitionSpec as P

REFLECTS = 2
KW = 4
BLOCK = 64
SHORTEST = 1024
STEPS = BLOCK * REFLECTS
HALO = 8
RESET_LOG = -80.0
MESH = pl.DeviceIdType.MESH
F32 = jnp.float32
BF16 = jnp.bfloat16
NN = (((1,), (0,)), ((), ()))
NT = (((1,), (1,)), ((), ()))
TN = (((0,), (0,)), ((), ()))
VMEM_LIMIT = 56 * 1024 * 1024
FORWARD_HEADS = 2
BACKWARD_HEADS = 2


def cost(microseconds):
    return pl.CostEstimate(
        flops=int(microseconds * 1e9), bytes_accessed=int(microseconds * 1e6), transcendentals=0
    )


def mm(a, b, dims=NN):
    return lax.dot_general(a.astype(BF16), b.astype(BF16), dims, preferred_element_type=F32)


def halves(a):
    high = a.astype(BF16)
    return high, (a - high.astype(F32)).astype(BF16)


def mm3(a, b):
    ah, al = halves(a)
    bh, bl = halves(b)
    return mm(jnp.concatenate([ah, al], axis=1), jnp.concatenate([bh, bh], axis=0)) + mm(ah, bl)


def mm2(a, b, dims=NN):
    ah, al = halves(a)
    return mm(ah, b, dims) + mm(al, b, dims)


def sigmoid(v):
    return 1.0 / (1.0 + jnp.exp(-v))


def step_ids(shape, axis):
    index = lax.broadcasted_iota(jnp.int32, shape, axis)
    return index % BLOCK, index // BLOCK


def step_masks():
    shape = (STEPS, STEPS)
    tm, jm = step_ids(shape, 0)
    tn, jn = step_ids(shape, 1)
    strict = (tm > tn) | ((tm == tn) & (jm > jn))
    size = 4
    first = tm // size == tn // size
    merges = []
    while size < BLOCK:
        merges.append((tm // (2 * size) == tn // (2 * size)) & (tm // size != tn // size))
        size = 2 * size
    eye = ((tm == tn) & (jm == jn)).astype(F32)
    return tm >= tn, strict, first, merges, eye


def unit_lower_inverse(systems, first, merges, eye):
    neg = [jnp.where(first, -a, 0.0) for a in systems]
    inv = [eye + n for n in neg]
    for _ in range(2):
        neg = [mm3(n, n) for n in neg]
        inv = [t + mm3(t, n) for t, n in zip(inv, neg)]
    for merge in merges:
        off = [mm3(jnp.where(merge, a, 0.0), t) for a, t in zip(systems, inv)]
        inv = [t - mm3(t, o) for t, o in zip(inv, off)]
    return inv


def conv_parts(ext_ref, taps, live, columns, rows):
    total = None
    for back in range(KW):
        part = ext_ref[pl.ds(HALO - back, rows), columns] * taps[KW - 1 - back : KW - back, :]
        if back > 0:
            part = part * live[:, back : back + 1]
        total = part if total is None else total + part
    return total


def head_features(ext_ref, tq, tk, tv, live, rows, width):
    conv = [
        conv_parts(ext_ref, tq, live, pl.ds(0, width), rows),
        conv_parts(ext_ref, tk[:, :width], live, pl.ds(width, width), rows),
        conv_parts(ext_ref, tk[:, width:], live, pl.ds(2 * width, width), rows),
        conv_parts(ext_ref, tv[:, :width], live, pl.ds(3 * width, width), rows),
        conv_parts(ext_ref, tv[:, width:], live, pl.ds(4 * width, width), rows),
    ]
    return conv


def unit_rows(act):
    return lax.rsqrt(jnp.sum(act * act, axis=-1, keepdims=True) + 1e-06)


def mixer_forward_kernel(
    xn_ref, wq_ref, wk_ref, wv_ref, wg_ref, tq_ref, tk_ref, tv_ref, live_ref, acol_ref, arow_ref,
    pre_ref, gate_ref, oloc_ref, oread_ref, inv_ref, delta_ref, state_ref, turn_ref, carry_ref, final_ref,
    ext_ref,
):
    heads, rows, width = oread_ref.shape
    blocks = rows // BLOCK
    xn = xn_ref[...]
    live = live_ref[...]
    gate_ref[...] = mm(xn[HALO:], wg_ref[...])
    query, key, value = mm(xn, wq_ref[...]), mm(xn, wk_ref[...]), mm(xn, wv_ref[...])
    reach, strict, first, merges, eye = step_masks()
    cut = [slice(b * BLOCK, (b + 1) * BLOCK) for b in range(blocks)]
    every = [(n, b) for n in range(heads) for b in range(blocks)]
    qb, kb, vb = {}, {}, {}
    for n in range(heads):
        one, two = slice(n * width, (n + 1) * width), slice(2 * n * width, 2 * (n + 1) * width)
        pre = jnp.concatenate([query[:, one], key[:, two], value[:, two]], axis=1).astype(BF16)
        pre_ref[n] = pre
        ext_ref[n] = pre.astype(F32)
        conv = head_features(ext_ref.at[n], tq_ref[:, one], tk_ref[:, two], tv_ref[:, two], live, rows, width)
        act = [c * sigmoid(c) for c in conv]
        q = (act[0] * unit_rows(act[0]) * width ** (-0.5)).astype(BF16)
        k = [(a * unit_rows(a)).astype(BF16) for a in act[1:3]]
        v = [a.astype(BF16) for a in act[3:5]]
        for b in range(blocks):
            qb[n, b] = q[cut[b]]
            kb[n, b] = jnp.concatenate([k[0][cut[b]], k[1][cut[b]]], axis=0)
            vb[n, b] = jnp.concatenate([v[0][cut[b]], v[1][cut[b]]], axis=0)
    ccol = {at: acol_ref[at[0], at[1], :, 0:1] for at in every}
    bcol = {at: acol_ref[at[0], at[1], :, 1:2] for at in every}
    crow = {at: arow_ref[at[0], at[1], 0:1, :] for at in every}
    brow = {at: arow_ref[at[0], at[1], 1:2, :] for at in every}
    fade = {at: jnp.exp(jnp.where(reach, ccol[at] - crow[at], -1e30)) for at in every}
    system = [jnp.where(strict, fade[at] * mm(kb[at], kb[at], NT), 0.0) * bcol[at] for at in every]
    inv = dict(zip(every, unit_lower_inverse(system, first, merges, eye)))
    for at in every:
        inv_ref[at[0], at[1]] = inv[at].astype(BF16)
    local = {at: mm2(inv[at] * brow[at], vb[at]) for at in every}
    reads = {at: mm2(inv[at] * (brow[at] * jnp.exp(crow[at])), kb[at]) for at in every}
    score = {at: fade[at][:BLOCK] * mm(qb[at], kb[at], NT) for at in every}
    grow = {at: jnp.exp(ccol[at]) for at in every}
    last = {at: ccol[at][BLOCK - 1 : BLOCK] for at in every}
    tail = {at: kb[at].astype(F32) * jnp.exp(last[at] - ccol[at]) for at in every}
    both = {at: jnp.concatenate([local[at], -reads[at]], axis=1).astype(BF16) for at in every}
    turn = {at: mm(tail[at], both[at], TN) for at in every}
    query_out = {at: mm(score[at], both[at]) for at in every}
    state = {}
    for n in range(heads):
        now = jnp.concatenate([jnp.zeros((width, width), F32), eye], axis=1)
        for b in range(blocks):
            at = (n, b)
            state[at] = now
            step = turn[at][:, width:].astype(BF16)
            turn_ref[n, b] = step
            fixed = jnp.concatenate([turn[at][:, :width], jnp.zeros((width, width), F32)], axis=1)
            now = jnp.exp(last[at]) * now + fixed + mm(step, now)
        final_ref[n] = now.astype(BF16)
    for at in every:
        n, b = at
        carried = query_out[at][:, width:] + grow[at][:BLOCK] * qb[at].astype(F32)
        low = state[at].astype(BF16)
        carry_ref[n, b] = carried.astype(BF16)
        state_ref[n, b] = low
        fixed = jnp.concatenate([local[at], jnp.zeros((STEPS, width), F32)], axis=1)
        delta_ref[n, b] = (fixed - mm(reads[at], low)).astype(BF16)
        out = mm(carried, low)
        oloc_ref[cut[b], n * width : (n + 1) * width] = out[:, :width] + query_out[at][:, :width]
        oread_ref[n, cut[b], :] = out[:, width:].astype(BF16)


def head_columns(rows, width):
    return pl.BlockSpec((rows, width), lambda h: (0, h))


def whole(shape):
    return pl.BlockSpec(shape, lambda h: (0,) * len(shape))


def per_head(shape, group=1):
    return pl.BlockSpec((group,) + shape, lambda h: (h,) + (0,) * len(shape))


def mixer_forward(xn, w_query, w_key, w_value, w_outgate, taps, live, acol, arow, heads, width):
    ext_rows, depth = xn.shape
    rows = ext_rows - HALO
    blocks = rows // BLOCK
    conv_query, conv_key, conv_value = taps
    out = jax.ShapeDtypeStruct
    return pl.pallas_call(
        mixer_forward_kernel,
        grid=(heads // FORWARD_HEADS,),
        in_specs=[
            whole((ext_rows, depth)),
            head_columns(depth, FORWARD_HEADS * width),
            head_columns(depth, 2 * FORWARD_HEADS * width),
            head_columns(depth, 2 * FORWARD_HEADS * width),
            head_columns(depth, FORWARD_HEADS * width),
            head_columns(KW, FORWARD_HEADS * width),
            head_columns(KW, 2 * FORWARD_HEADS * width),
            head_columns(KW, 2 * FORWARD_HEADS * width),
            whole(live.shape),
            per_head(acol.shape[1:], FORWARD_HEADS),
            per_head(arow.shape[1:], FORWARD_HEADS),
        ],
        out_specs=[
            per_head((ext_rows, 5 * width), FORWARD_HEADS),
            head_columns(rows, FORWARD_HEADS * width),
            head_columns(rows, FORWARD_HEADS * width),
            per_head((rows, width), FORWARD_HEADS),
            per_head((blocks, STEPS, STEPS), FORWARD_HEADS),
            per_head((blocks, STEPS, 2 * width), FORWARD_HEADS),
            per_head((blocks, width, 2 * width), FORWARD_HEADS),
            per_head((blocks, width, width), FORWARD_HEADS),
            per_head((blocks, BLOCK, width), FORWARD_HEADS),
            per_head((width, 2 * width), FORWARD_HEADS),
        ],
        out_shape=[
            out((heads, ext_rows, 5 * width), BF16),
            out((rows, heads * width), F32),
            out((rows, heads * width), F32),
            out((heads, rows, width), BF16),
            out((heads, blocks, STEPS, STEPS), BF16),
            out((heads, blocks, STEPS, 2 * width), BF16),
            out((heads, blocks, width, 2 * width), BF16),
            out((heads, blocks, width, width), BF16),
            out((heads, blocks, BLOCK, width), BF16),
            out((heads, width, 2 * width), BF16),
        ],
        scratch_shapes=[pltpu.VMEM((FORWARD_HEADS, ext_rows, 5 * width), F32)],
        compiler_params=pltpu.CompilerParams(vmem_limit_bytes=VMEM_LIMIT),
        cost_estimate=cost(40),
        name="mixer_forward",
    )(xn, w_query, w_key, w_value, w_outgate, conv_query, conv_key, conv_value, live, acol, arow)


def conv_pull(ext_ref, pad_ref, d_conv, taps, live, columns, rows, dtap_ref):
    total = None
    for back in range(KW):
        part = d_conv if back == 0 else d_conv * live[:, back : back + 1]
        source = ext_ref[pl.ds(HALO - back, rows), columns]
        dtap_ref[KW - 1 - back : KW - back, :] = jnp.sum(part * source, axis=0, keepdims=True)
        pad_ref[pl.ds(HALO, rows), :] = part
        moved = pad_ref[pl.ds(back, rows + HALO), :] * taps[KW - 1 - back : KW - back, :]
        total = moved if total is None else total + moved
    return total


def silu_pull(c, grad):
    s = sigmoid(c)
    return grad * (s + c * s * (1.0 - s))


def unit_pull(act, grad, scale):
    r = unit_rows(act)
    return scale * r * (grad - act * (r * r * jnp.sum(act * grad, axis=-1, keepdims=True)))


def mixer_backward_kernel(
    pre_ref, tq_ref, tk_ref, tv_ref, live_ref, acol_ref, arow_ref,
    inv_ref, delta_ref, state_ref, turn_ref, carry_ref, start_ref, after_ref, dout_ref,
    d_ref, dtq_ref, dtk_ref, dtv_ref, aux_ref,
    ext_ref, pad_ref,
):
    heads = pre_ref.shape[0]
    rows = dout_ref.shape[0]
    width = start_ref.shape[-1]
    blocks = rows // BLOCK
    live = live_ref[...]
    every = [(n, b) for n in range(heads) for b in range(blocks)]
    cut = [slice(b * BLOCK, (b + 1) * BLOCK) for b in range(blocks)]
    conv, act, qb, kb, dout = {}, {}, {}, {}, {}
    for n in range(heads):
        one, two = slice(n * width, (n + 1) * width), slice(2 * n * width, 2 * (n + 1) * width)
        ext_ref[n] = pre_ref[n].astype(F32)
        conv[n] = head_features(ext_ref.at[n], tq_ref[:, one], tk_ref[:, two], tv_ref[:, two], live, rows, width)
        act[n] = [c * sigmoid(c) for c in conv[n][:3]]
        q = (act[n][0] * unit_rows(act[n][0]) * width ** (-0.5)).astype(BF16)
        k = [(a * unit_rows(a)).astype(BF16) for a in act[n][1:]]
        for b in range(blocks):
            qb[n, b] = q[cut[b]]
            kb[n, b] = jnp.concatenate([k[0][cut[b]], k[1][cut[b]]], axis=0)
            dout[n, b] = dout_ref[cut[b], one]
    reach, strict, _, _, _ = step_masks()
    ccol = {at: acol_ref[at[0], at[1], :, 0:1] for at in every}
    bcol = {at: acol_ref[at[0], at[1], :, 1:2] for at in every}
    crow = {at: arow_ref[at[0], at[1], 0:1, :] for at in every}
    last = {at: ccol[at][BLOCK - 1 : BLOCK] for at in every}
    grow = {at: jnp.exp(ccol[at]) for at in every}
    weight = {at: jnp.exp(last[at] - ccol[at]) for at in every}
    ahead = {at: mm(carry_ref[at[0], at[1]], dout[at], TN) for at in every}
    after = {}
    for n in range(heads):
        now = after_ref[n].astype(F32)
        for b in range(blocks - 1, -1, -1):
            after[n, b] = now
            now = jnp.exp(last[n, b]) * now + ahead[n, b] + mm(turn_ref[n, b], now, TN)
    fade = {at: jnp.exp(jnp.where(reach, ccol[at] - crow[at], -1e30)) for at in every}
    delta = {
        at: delta_ref[at[0], at[1], :, :width].astype(F32) + mm(delta_ref[at[0], at[1], :, width:], start_ref[at[0]])
        for at in every
    }
    state = {
        at: state_ref[at[0], at[1], :, :width].astype(F32) + mm(state_ref[at[0], at[1], :, width:], start_ref[at[0]])
        for at in every
    }
    score = {at: fade[at][:BLOCK] * mm(qb[at], kb[at], NT) for at in every}
    d_delta = {at: mm(score[at], dout[at], TN) + weight[at] * mm(kb[at], after[at]) for at in every}
    d_rhs = {at: mm(inv_ref[at[0], at[1]], d_delta[at], TN) for at in every}
    d_score = {at: (fade[at][:BLOCK] * mm(dout[at], delta[at], NT)).astype(BF16) for at in every}
    d_tail = {at: weight[at] * mm(delta[at], after[at], NT) for at in every}
    d_gram = {
        at: jnp.where(strict, -bcol[at] * fade[at] * mm(d_rhs[at], delta[at], NT), 0.0).astype(BF16) for at in every
    }
    dq = {at: mm(grow[at][:BLOCK] * dout[at], state[at], NT) + mm(d_score[at], kb[at]) for at in every}
    dk_row = {
        at: mm(-(bcol[at] * grow[at]) * d_rhs[at], state[at], NT) + mm(d_gram[at], kb[at]) for at in every
    }
    dk_col = {at: mm(d_gram[at], kb[at], TN) + mm(d_score[at], qb[at], TN) + d_tail[at] for at in every}
    tok = lax.broadcasted_iota(jnp.int32, (BLOCK, 1), 0)
    for at in every:
        kf = kb[at].astype(F32)
        d_beta = (1.0 - bcol[at]) * jnp.sum(d_rhs[at] * delta[at], axis=-1, keepdims=True)
        d_log = jnp.sum(kf * (dk_row[at] - dk_col[at]), axis=-1, keepdims=True)
        d_logq = jnp.sum(qb[at].astype(F32) * dq[at], axis=-1, keepdims=True)
        d_last = jnp.sum(kf * d_tail[at]) + jnp.sum(jnp.exp(last[at]) * after[at] * state[at])
        d_token = d_log[:BLOCK] + d_log[BLOCK:] + d_logq + jnp.where(tok == BLOCK - 1, d_last, 0.0)
        aux_ref[at[0], at[1], :, 0:1] = d_beta
        aux_ref[at[0], at[1], 0:BLOCK, 1:2] = d_token
    pad_ref[0:HALO, :] = jnp.zeros((HALO, width), F32)
    pad_ref[pl.ds(HALO + rows, HALO), :] = jnp.zeros((HALO, width), F32)
    for n in range(heads):
        keys = {b: dk_row[n, b] + dk_col[n, b] for b in range(blocks)}
        values = {b: bcol[n, b] * d_rhs[n, b] for b in range(blocks)}
        d_act = [
            jnp.concatenate([dq[n, b] for b in range(blocks)], axis=0),
            jnp.concatenate([keys[b][:BLOCK] for b in range(blocks)], axis=0),
            jnp.concatenate([keys[b][BLOCK:] for b in range(blocks)], axis=0),
            jnp.concatenate([values[b][:BLOCK] for b in range(blocks)], axis=0),
            jnp.concatenate([values[b][BLOCK:] for b in range(blocks)], axis=0),
        ]
        for i, scale in enumerate((width ** (-0.5), 1.0, 1.0)):
            d_act[i] = unit_pull(act[n][i], d_act[i], scale)
        sides = (
            (tq_ref, dtq_ref, n),
            (tk_ref, dtk_ref, 2 * n),
            (tk_ref, dtk_ref, 2 * n + 1),
            (tv_ref, dtv_ref, 2 * n),
            (tv_ref, dtv_ref, 2 * n + 1),
        )
        for i, (tap_ref, dtap_ref, at) in enumerate(sides):
            lanes = pl.ds(at * width, width)
            grad = conv_pull(
                ext_ref.at[n], pad_ref, silu_pull(conv[n][i], d_act[i]), tap_ref[:, lanes], live,
                pl.ds(i * width, width), rows, dtap_ref.at[:, lanes],
            )
            target = pl.ds((5 * n + i) * width, width)
            d_ref[0:rows, target] = grad[HALO:].astype(BF16)
            d_ref[rows : rows + HALO, target] = grad[:HALO].astype(BF16)


def mixer_backward(pre, taps, live, acol, arow, saved, start, after, dout):
    heads, ext_rows, _ = pre.shape
    rows = ext_rows - HALO
    width = start.shape[-1]
    conv_query, conv_key, conv_value = taps
    out = jax.ShapeDtypeStruct
    columns = heads * width
    group = BACKWARD_HEADS
    tap_specs = [head_columns(KW, times * group * width) for times in (1, 2, 2)]
    return pl.pallas_call(
        mixer_backward_kernel,
        grid=(heads // group,),
        in_specs=[per_head(pre.shape[1:], group)]
        + tap_specs
        + [whole(live.shape)]
        + [per_head(value.shape[1:], group) for value in (acol, arow, *saved, start, after)]
        + [head_columns(rows, group * width)],
        out_specs=[head_columns(ext_rows, 5 * group * width)] + tap_specs + [per_head(acol.shape[1:], group)],
        out_shape=[
            out((ext_rows, 5 * columns), BF16),
            out((KW, columns), F32),
            out((KW, 2 * columns), F32),
            out((KW, 2 * columns), F32),
            out(acol.shape, F32),
        ],
        scratch_shapes=[
            pltpu.VMEM((group, ext_rows, 5 * width), F32),
            pltpu.VMEM((rows + 2 * HALO, width), F32),
        ],
        compiler_params=pltpu.CompilerParams(vmem_limit_bytes=VMEM_LIMIT),
        cost_estimate=cost(35),
        name="mixer_backward",
    )(pre, conv_query, conv_key, conv_value, live, acol, arow, *saved, start, after, dout)


def carry_kernel(count, heads, backward, *refs):
    if backward:
        part_ref, maps_ref, result_ref, inbox, outbox, landed, send_sem, recv_sem, back_sem, land_sem = refs
    else:
        part_ref, result_ref, maps_ref, inbox, outbox, landed, send_sem, recv_sem, back_sem, land_sem = refs
    place = lax.axis_index("seq")
    group = lax.axis_index("dp")
    width = result_ref.shape[-1]
    stride = count // 16

    def keeper(h):
        return (2 * h + group) * stride

    barrier = pltpu.get_barrier_semaphore()

    def greet(step, carry):
        peer = lax.rem(place + step, count)
        pl.semaphore_signal(barrier, inc=1, device_id=(group, peer), device_id_type=MESH)
        return carry

    lax.fori_loop(1, count, greet, 0)
    pl.semaphore_wait(barrier, count - 1)

    def outgoing(h):
        return pltpu.make_async_remote_copy(
            src_ref=part_ref.at[h],
            dst_ref=inbox.at[place],
            send_sem=send_sem.at[h],
            recv_sem=recv_sem.at[place],
            device_id=(group, keeper(h)),
            device_id_type=MESH,
        )

    for h in range(heads):

        @pl.when(place != keeper(h))
        def _(h=h):
            outgoing(h).start()

        @pl.when(place == keeper(h))
        def _(h=h):
            inbox[pl.ds(place, 1)] = part_ref[h : h + 1]

    def scan_head(h):
        def returning(where):
            return pltpu.make_async_remote_copy(
                src_ref=outbox.at[where],
                dst_ref=landed.at[h],
                send_sem=back_sem.at[where],
                recv_sem=land_sem.at[h],
                device_id=(group, where),
                device_id_type=MESH,
            )

        def lap(step, state):
            where = count - 1 - step if backward else step
            outbox[pl.ds(where, 1)] = state[None].astype(BF16)

            @pl.when(where != place)
            def _():
                returning(where).start()
                pltpu.make_async_remote_copy(
                    src_ref=part_ref.at[h],
                    dst_ref=inbox.at[where],
                    send_sem=send_sem.at[h],
                    recv_sem=recv_sem.at[where],
                    device_id=(group, where),
                    device_id_type=MESH,
                ).wait_recv()

            @pl.when(where == place)
            def _():
                landed[h : h + 1] = outbox[pl.ds(where, 1)]

            got = inbox[pl.ds(where, 1)][0]
            high, low = halves(state)
            if backward:
                step_map = maps_ref[pl.ds(where, 1)][0][:, width:]
                state = mm(step_map, high, TN) + mm(step_map, low, TN) + got.astype(F32)
            else:
                step_map = got[:, width:]
                state = mm(step_map, high) + mm(step_map, low) + got[:, :width].astype(F32)
            return state

        lax.fori_loop(0, count, lap, jnp.zeros((width, width), F32))

        def finish(where, carry):
            @pl.when(where != place)
            def _():
                returning(where).wait_send()

            return carry

        lax.fori_loop(0, count, finish, 0)

    for h in range(heads):

        @pl.when(place == keeper(h))
        def _(h=h):
            scan_head(h)

    for h in range(heads):

        @pl.when(place != keeper(h))
        def _(h=h):
            outgoing(h).wait_send()
            pltpu.make_async_remote_copy(
                src_ref=outbox.at[0],
                dst_ref=landed.at[h],
                send_sem=back_sem.at[0],
                recv_sem=land_sem.at[h],
                device_id=(group, keeper(h)),
                device_id_type=MESH,
            ).wait_recv()

    result_ref[...] = landed[...]
    if not backward:
        maps_ref[...] = inbox[...]


def carry_states(part, maps, count):
    heads, width, columns = part.shape
    backward = maps is not None
    out = jax.ShapeDtypeStruct
    vmem = pl.BlockSpec(memory_space=pltpu.VMEM)
    result = out((heads, width, width), BF16)
    return pl.pallas_call(
        partial(carry_kernel, count, heads, backward),
        in_specs=[vmem] * (2 if backward else 1),
        out_specs=vmem if backward else [vmem, vmem],
        out_shape=result if backward else [result, out((count, width, columns), BF16)],
        scratch_shapes=[
            pltpu.VMEM((count, width, columns), BF16),
            pltpu.VMEM((count, width, width), BF16),
            pltpu.VMEM((heads, width, width), BF16),
            pltpu.SemaphoreType.DMA((heads,)),
            pltpu.SemaphoreType.DMA((count,)),
            pltpu.SemaphoreType.DMA((count,)),
            pltpu.SemaphoreType.DMA((heads,)),
        ],
        compiler_params=pltpu.CompilerParams(
            collective_id=1 if backward else 0, has_side_effects=True, vmem_limit_bytes=VMEM_LIMIT
        ),
        cost_estimate=cost(24),
        name="carry_backward" if backward else "carry_forward",
    )(*((part, maps) if backward else (part,)))


JOBS = 7
JOB = 768
LATE_JOBS = 10


def row_blocks(parity, sending):
    if sending:
        return (1, 3) if parity else (2, 3)
    return (0, 2) if parity else (0, 1)


def early_products_kernel(own_ref, got_ref, *refs):
    rhs_own, rhs_got, (send_a, send_b, keep_a, keep_b) = refs[:5], refs[5:10], refs[10:]
    tokens = rhs_own[0].shape[0]
    half = rhs_own[0].shape[1] // 2
    edge = got_ref.shape[0] // 4
    for parity, send_ref, keep_ref in ((0, send_a, keep_a), (1, send_b, keep_b)):
        segments = [(0, 0, parity * half, half), (0, 1, parity * half, half), (1, 2, parity * half, half)]
        segments.append((3, 4, 0, rhs_own[4].shape[1]) if parity else (2, 3, 0, rhs_own[3].shape[1]))
        for out_ref, sending in ((send_ref, True), (keep_ref, False)):
            at = 0
            for lhs, rhs, begin, size in segments:
                done = 0
                while done < size:
                    job, column = (at + done) // JOB, (at + done) % JOB
                    width = min(JOB - column, size - done)
                    lanes = slice(begin + done, begin + done + width)
                    for row, block in enumerate(row_blocks(parity, sending)):
                        rows = slice(block * edge, (block + 1) * edge)
                        cut = slice(lhs * tokens, (lhs + 1) * tokens)
                        total = mm(own_ref[rows, cut], rhs_own[rhs][:, lanes]) + mm(
                            got_ref[rows, cut], rhs_got[rhs][:, lanes]
                        )
                        out_ref[job, row * edge : (row + 1) * edge, column : column + width] = total.astype(BF16)
                    done += width
                at += size


def early_products(own, got, rhs_own, rhs_got):
    rows = got.shape[0] // 2
    shape = jax.ShapeDtypeStruct((JOBS, rows, JOB), BF16)
    vmem = pl.BlockSpec(memory_space=pltpu.VMEM)
    return pl.pallas_call(
        early_products_kernel,
        in_specs=[vmem] * 12,
        out_specs=[vmem] * 4,
        out_shape=[shape] * 4,
        compiler_params=pltpu.CompilerParams(vmem_limit_bytes=VMEM_LIMIT),
        cost_estimate=cost(10),
        name="early_products",
    )(own, got, *rhs_own, *rhs_got)


def input_pull_kernel(
    d_ref, dg_ref, wq_ref, wk_ref, wv_ref, wg_ref, aux_ref, raw_ref, live_ref, rate_ref, wr_ref, ext_ref,
    x_ref, halo_ref, gain_ref, resid_ref,
    grad_ref, edge_ref, rim_ref, dgain_ref, drates_ref, misc_ref, total_ref, rates_ref,
):
    head = pl.program_id(0)
    rows = dg_ref.shape[0]
    width = dg_ref.shape[1] // PULL_HEADS
    group = PULL_HEADS
    part = None
    for n in range(group):
        d = d_ref[:, n * 5 * width : (n + 1) * 5 * width]
        two = slice(2 * n * width, 2 * (n + 1) * width)
        term = (
            mm(d[:, :width], wq_ref[:, n * width : (n + 1) * width], NT)
            + mm(d[:, width : 3 * width], wk_ref[:, two], NT)
            + mm(d[:, 3 * width :], wv_ref[:, two], NT)
        )
        part = term if part is None else part + term
    more = mm(dg_ref[...], wg_ref[...], NT)

    @pl.when(head == 0)
    def _():
        heads, blocks = aux_ref.shape[:2]
        wide = heads * REFLECTS
        rates_ref[...] = jnp.zeros_like(rates_ref)
        for h in range(heads):
            for b in range(blocks):
                tokens = slice(b * BLOCK, (b + 1) * BLOCK)
                for j in range(REFLECTS):
                    at = h * REFLECTS + j
                    rates_ref[tokens, at : at + 1] = aux_ref[h, b, j * BLOCK : (j + 1) * BLOCK, 0:1]
                rates_ref[tokens, wide + h : wide + h + 1] = aux_ref[h, b, 0:BLOCK, 1:2]
        value, raw = rates_ref[...], raw_ref[...]
        d_log = exact_sum(block_sums(rows, True), value) * live_ref[:, 1:2]
        lane = lax.broadcasted_iota(jnp.int32, raw.shape, 1)
        d_raw = jnp.where(lane < wide, value, -rate_ref[...] * sigmoid(raw) * d_log)
        summed = jnp.where(lane < wide, value, -softplus(raw) * d_log)
        misc_ref[...] = jnp.sum(summed, axis=0, keepdims=True)
        d_raw = d_raw.astype(BF16)
        drates_ref[...] = mm(d_raw, ext_ref[pl.ds(HALO, rows), :], TN)[: drates_ref.shape[0]]
        total_ref[...] = part
        total_ref[0:rows, :] += more + mm(d_raw, wr_ref[...], NT)

    @pl.when(head > 0)
    def _():
        total_ref[...] += part
        total_ref[0:rows, :] += more

    @pl.when(head == pl.num_programs(0) - 1)
    def _():
        grad = total_ref[...]
        unit, pulled = norm_pull(x_ref[...].astype(F32), gain_ref[...], grad[:rows])
        grad_ref[...] = (resid_ref[...] + pulled).astype(BF16)
        halo_unit, _ = norm_pull(halo_ref[...].astype(F32), gain_ref[...], grad[rows:])
        dgain_ref[...] = jnp.sum(grad[:rows] * unit, axis=0, keepdims=True) + jnp.sum(
            grad[rows:] * halo_unit, axis=0, keepdims=True
        )
        edge_ref[...] = grad[rows - HALO : rows]
        rim_ref[...] = grad[rows:]


def norm_pull(x, gain, grad):
    r = lax.rsqrt(jnp.mean(x * x, axis=-1, keepdims=True) + 1e-06)
    unit = x * r
    through = grad * gain
    return unit, r * (through - unit * jnp.mean(unit * through, axis=-1, keepdims=True))


PULL_HEADS = 2


def input_pull(d_all, d_outgate, weights, aux, raw, live, rate, w_rates, ext_b, x, halo, gain, d_resid, heads):
    rows, depth = x.shape
    ext_rows = rows + HALO
    width = d_outgate.shape[1] // heads * PULL_HEADS
    out = jax.ShapeDtypeStruct
    w_query, w_key, w_value, w_outgate = weights
    rates = heads * (REFLECTS + 1)
    return pl.pallas_call(
        input_pull_kernel,
        grid=(heads // PULL_HEADS,),
        in_specs=[
            head_columns(ext_rows, 5 * width),
            head_columns(rows, width),
            head_columns(depth, width),
            head_columns(depth, 2 * width),
            head_columns(depth, 2 * width),
            head_columns(depth, width),
            whole(aux.shape),
            whole(raw.shape),
            whole(live.shape),
            whole(rate.shape),
            whole(w_rates.shape),
            whole(ext_b.shape),
            whole(x.shape),
            whole(halo.shape),
            whole((1, depth)),
            whole(d_resid.shape),
        ],
        out_specs=[
            whole((rows, depth)), whole((HALO, depth)), whole((HALO, depth)), whole((1, depth)),
            whole((rates, depth)), whole((1, raw.shape[1])),
        ],
        out_shape=[
            out((rows, depth), BF16),
            out((HALO, depth), F32),
            out((HALO, depth), F32),
            out((1, depth), F32),
            out((rates, depth), F32),
            out((1, raw.shape[1]), F32),
        ],
        scratch_shapes=[pltpu.VMEM((ext_rows, depth), F32), pltpu.VMEM(raw.shape, F32)],
        compiler_params=pltpu.CompilerParams(vmem_limit_bytes=VMEM_LIMIT),
        cost_estimate=cost(12),
        name="input_pull",
    )(
        d_all, d_outgate, w_query, w_key, w_value, w_outgate, aux, raw, live, rate, w_rates, ext_b,
        x, halo, gain[None, :], d_resid,
    )


def exact_sum(ones, value):
    total = None
    for _ in range(3):
        part = value.astype(BF16)
        value = value - part.astype(F32)
        term = mm(ones, part)
        total = term if total is None else total + term
    return total


def block_sums(rows, reverse):
    shape = (rows, rows)
    one, two = lax.broadcasted_iota(jnp.int32, shape, 0), lax.broadcasted_iota(jnp.int32, shape, 1)
    order = (one <= two) if reverse else (one >= two)
    return ((one // BLOCK == two // BLOCK) & order).astype(BF16)


def softplus(v):
    return jnp.maximum(v, 0.0) + jnp.log1p(jnp.exp(-jnp.abs(v)))


def rates_kernel(
    heads, lengths_ref, x_ref, halo_ref, gain_ref, weight_ref, bias_ref, rate_ref,
    ext_ref, raw_ref, live_ref, acol_ref, arow_ref,
):
    rows = x_ref.shape[0]
    blocks = rows // BLOCK
    wide = heads * REFLECTS

    def normed(field):
        field = field.astype(F32)
        return (
            field * lax.rsqrt(jnp.mean(field * field, axis=-1, keepdims=True) + 1e-06) * gain_ref[...]
        ).astype(BF16)

    xn = normed(x_ref[...])
    ext_ref[0:HALO, :] = normed(halo_ref[...])
    ext_ref[pl.ds(HALO, rows), :] = xn
    raw = mm(xn, weight_ref[...])
    raw_ref[...] = raw
    row = lax.axis_index("seq") * rows + lax.broadcasted_iota(jnp.int32, (rows, 1), 0)
    place, end = row, 0
    for i in range(lengths_ref.shape[1]):
        begin, end = end, end + lengths_ref[0, i] + (SHORTEST - 1)
        place = jnp.where((row >= begin) & (row < end), row - begin, place)
    live_ref[...] = (place >= lax.broadcasted_iota(jnp.int32, (rows, 8), 1)).astype(F32)
    beta = sigmoid(raw + bias_ref[...])
    log_rate = jnp.where(place == 0, RESET_LOG, -rate_ref[...] * softplus(raw))
    lane = lax.broadcasted_iota(jnp.int32, raw.shape, 1)
    both = jnp.where(lane < wide, beta, exact_sum(block_sums(rows, False), log_rate))
    turned = both.T
    arow_ref[...] = jnp.zeros_like(arow_ref)
    acol_ref[...] = jnp.zeros_like(acol_ref)
    for h in range(heads):
        for b in range(blocks):
            tokens = slice(b * BLOCK, (b + 1) * BLOCK)
            for j in range(REFLECTS):
                steps = slice(j * BLOCK, (j + 1) * BLOCK)
                at = h * REFLECTS + j
                acol_ref[h, b, steps, 0:1] = both[tokens, wide + h : wide + h + 1]
                acol_ref[h, b, steps, 1:2] = both[tokens, at : at + 1]
                arow_ref[h, b, 0:1, steps] = turned[wide + h : wide + h + 1, tokens]
                arow_ref[h, b, 1:2, steps] = turned[at : at + 1, tokens]


def rates_forward(lengths, x, halo, gain, w_rates, bias, rate, heads):
    rows, depth = x.shape
    blocks = rows // BLOCK
    out = jax.ShapeDtypeStruct
    vmem = pl.BlockSpec(memory_space=pltpu.VMEM)
    return pl.pallas_call(
        partial(rates_kernel, heads),
        in_specs=[pl.BlockSpec(memory_space=pltpu.SMEM)] + [vmem] * 6,
        out_specs=[vmem] * 5,
        out_shape=[
            out((rows + HALO, depth), BF16),
            out((rows, w_rates.shape[1]), F32),
            out((rows, 8), F32),
            out((heads, blocks, STEPS, 8), F32),
            out((heads, blocks, 8, STEPS), F32),
        ],
        compiler_params=pltpu.CompilerParams(vmem_limit_bytes=VMEM_LIMIT),
        cost_estimate=cost(4),
        name="rates_forward",
    )(lengths, x, halo, gain[None, :], w_rates, bias, rate)


CHUNK = 256


def middle_kernel(
    oloc_ref, oread_ref, start_ref, gate_ref, ogain_ref, x_ref, ext_ref, mgain_ref, ograd_ref, source_ref,
    wout_hbm, wgate_hbm, wup_hbm, wdown_hbm,
    block_ref, dout_ref, part_ref, gated_ref, hidden_ref, dgate_ref, dup_ref, doutgate_ref, dresid_ref,
    own_ref, other_ref, mlp_ref, branch_ref, dmgain_ref, dogain_ref,
    wout, wgate, wup, wdown, out_ref, resid_ref, down_ref, dmlp_ref, sem_out, sems,
):
    heads, rows, width = oread_ref.shape
    depth = x_ref.shape[1]
    chunks = wdown.shape[0]
    fetch_out = pltpu.make_async_copy(wout_hbm, wout, sem_out)
    fetch_out.start()

    def fetches(c):
        lanes = pl.ds(pl.multiple_of(c * CHUNK, CHUNK), CHUNK)
        return (
            pltpu.make_async_copy(wgate_hbm.at[:, lanes], wgate.at[c], sems.at[c, 0]),
            pltpu.make_async_copy(wup_hbm.at[:, lanes], wup.at[c], sems.at[c, 1]),
            pltpu.make_async_copy(wdown_hbm.at[lanes, :], wdown.at[c], sems.at[c, 2]),
        )

    def begin(c, carry):
        for copy in fetches(c):
            copy.start()
        return carry

    lax.fori_loop(0, chunks, begin, 0)
    ogain = ogain_ref[...]
    for h in range(heads):
        lanes = slice(h * width, (h + 1) * width)
        out = oloc_ref[:, lanes] + mm(oread_ref[h], start_ref[h])
        out_ref[:, lanes] = out
        gate = gate_ref[:, lanes]
        r = lax.rsqrt(jnp.mean(out * out, axis=-1, keepdims=True) + 1e-05)
        gated_ref[:, lanes] = (out * r * ogain * (gate * sigmoid(gate))).astype(BF16)
    fetch_out.wait()
    resid = x_ref[...].astype(F32) + mm(gated_ref[...], wout[...])
    resid_ref[...] = resid
    r = lax.rsqrt(jnp.mean(resid * resid, axis=-1, keepdims=True) + 1e-06)
    mlp_ref[...] = (resid * r * mgain_ref[...]).astype(BF16)
    down_ref[...] = jnp.zeros_like(down_ref)
    dmlp_ref[...] = jnp.zeros_like(dmlp_ref)

    def one(c, carry):
        for copy in fetches(c):
            copy.wait()
        mlp, ograd = mlp_ref[...], ograd_ref[...]
        lanes = pl.ds(pl.multiple_of(c * CHUNK, CHUNK), CHUNK)
        gate, up = mm(mlp, wgate[c]), mm(mlp, wup[c])
        d_hidden = mm(ograd, wdown[c], NT)
        s = sigmoid(gate)
        act = gate * s
        hidden = (act * up).astype(BF16)
        d_gate = (d_hidden * up * (s + act * (1.0 - s))).astype(BF16)
        d_up = (d_hidden * act).astype(BF16)
        hidden_ref[:, lanes] = hidden
        dgate_ref[:, lanes] = d_gate
        dup_ref[:, lanes] = d_up
        down_ref[...] += mm(hidden, wdown[c])
        dmlp_ref[...] += mm(d_gate, wgate[c], NT) + mm(d_up, wup[c], NT)
        return carry

    lax.fori_loop(0, chunks, one, 0)
    block_ref[...] = (resid_ref[...] + down_ref[...]).astype(BF16)
    grad = dmlp_ref[...]
    unit, pulled = norm_pull(resid_ref[...], mgain_ref[...], grad)
    dmgain_ref[...] = jnp.sum(grad * unit, axis=0, keepdims=True)
    d_resid = ograd_ref[...].astype(F32) + pulled
    dresid_ref[...] = d_resid
    branch_ref[...] = d_resid.astype(BF16)
    dogain = jnp.zeros((1, width), F32)
    for h in range(heads):
        lanes = slice(h * width, (h + 1) * width)
        grad = mm(branch_ref[...], wout[lanes, :], NT)
        out = out_ref[:, lanes]
        gate = gate_ref[:, lanes]
        r = lax.rsqrt(jnp.mean(out * out, axis=-1, keepdims=True) + 1e-05)
        s = sigmoid(gate)
        unit = out * r
        doutgate_ref[:, lanes] = (grad * unit * ogain * (s + gate * s * (1.0 - s))).astype(BF16)
        through = grad * (gate * s)
        dogain += jnp.sum(through * unit, axis=0, keepdims=True)
        through = through * ogain
        dout = r * (through - unit * jnp.mean(unit * through, axis=-1, keepdims=True))
        dout_ref[:, lanes] = dout
        part_ref[h] = mm(oread_ref[h], dout, TN).astype(BF16)
    dogain_ref[...] = dogain
    lane = lax.broadcasted_iota(jnp.int32, (depth, depth), 1)
    chosen = (lane == source_ref[...]).astype(BF16)
    half = depth // 2
    lhs = (mlp_ref[...], ograd_ref[...], branch_ref[...], ext_ref[pl.ds(HALO, rows), :], ext_ref[0:HALO, :])
    at = 0
    for value in lhs:
        turned = mm(chosen, value, NT).astype(BF16)
        own_ref[:, at : at + value.shape[0]] = turned[:half]
        other_ref[:, at : at + value.shape[0]] = turned[half:]
        at += value.shape[0]


def middle(oloc, oread, start, gate_pre, out_gain, x, ext_b, mlp_gain, out_grad, source, w_out, w_gate, w_up, w_down):
    heads, rows, width = oread.shape
    depth = x.shape[1]
    ff = w_gate.shape[1]
    out = jax.ShapeDtypeStruct
    vmem, hbm = pl.BlockSpec(memory_space=pltpu.VMEM), pl.BlockSpec(memory_space=pl.ANY)
    tokens = 4 * rows + HALO
    columns = heads * width
    chunks = ff // CHUNK
    shapes = [
        ((rows, depth), BF16), ((rows, columns), F32), ((heads, width, width), BF16), ((rows, columns), BF16),
        ((rows, ff), BF16), ((rows, ff), BF16), ((rows, ff), BF16), ((rows, columns), BF16), ((rows, depth), F32),
        ((depth // 2, tokens), BF16), ((depth // 2, tokens), BF16), ((rows, depth), BF16), ((rows, depth), BF16),
        ((1, depth), F32), ((1, width), F32),
    ]
    return pl.pallas_call(
        middle_kernel,
        in_specs=[vmem] * 10 + [hbm] * 4,
        out_specs=[vmem] * len(shapes),
        out_shape=[out(*shape) for shape in shapes],
        scratch_shapes=[
            pltpu.VMEM(w_out.shape, BF16),
            pltpu.VMEM((chunks, depth, CHUNK), BF16),
            pltpu.VMEM((chunks, depth, CHUNK), BF16),
            pltpu.VMEM((chunks, CHUNK, depth), BF16),
            pltpu.VMEM((rows, columns), F32),
            pltpu.VMEM((rows, depth), F32),
            pltpu.VMEM((rows, depth), F32),
            pltpu.VMEM((rows, depth), F32),
            pltpu.SemaphoreType.DMA,
            pltpu.SemaphoreType.DMA((chunks, 3)),
        ],
        compiler_params=pltpu.CompilerParams(vmem_limit_bytes=VMEM_LIMIT),
        cost_estimate=cost(20),
        name="middle",
    )(
        oloc, oread, start, gate_pre, out_gain[None, :], x, ext_b, mlp_gain[None, :], out_grad, source,
        w_out, w_gate, w_up, w_down,
    )


def column_pieces(parity, job, ff, columns):
    half = ff // 2
    at, pieces = 0, []
    for output, begin, size in (
        (0, parity * half, half),
        (1, parity * half, half),
        (2, parity * half, half),
        (4 if parity else 3, 0, columns),
    ):
        low, high = max(at, job * JOB), min(at + size, (job + 1) * JOB)
        if low < high:
            pieces.append((output, begin + low - at, low - job * JOB, high - low))
        at += size
    return pieces


def reduce_kernel(
    heads, arr_a, arr_b, keep_a, keep_b, own_ref, got_ref, rhs_ref, tq_ref, tk_ref, tv_ref, gain_ref, rates_ref,
    edge_ref, rim_ref, x_ref, again_ref, resid_ref,
    gate_out, up_out, down_out, out_out, outgate_out, q_out, k_out, v_out, tq_out, tk_out, tv_out, rest_out,
    edge_out,
    e_keep, e_send, e_got2, e_got3, e_got4,
    rhs_got, l_first, l_send, l_keep, l_got1, l_got2, l_got3, l_got4, small_sum, small_got, rim_got,
    dp_sem, e_sem, l_sem, s_sem,
):
    seq = lax.axis_index("seq")
    group = lax.axis_index("dp")
    count = lax.axis_size("seq")
    x, y, z = seq % 2, (seq // 2) % 2, seq // 4
    near = (seq + 1 - 2 * x, seq + 2 - 4 * y)
    low_z = seq + 4 - 8 * (z % 2)
    high_z = seq + 8 - 16 * (z // 2)

    def at(place):
        return {"dp": group, "seq": place}

    core = {"dp": 1 - group, "seq": seq}
    before, behind = lax.rem(seq + count - 1, count), lax.rem(seq + 1, count)

    def send(source, target, sems, index, device):
        return pltpu.make_async_remote_copy(
            src_ref=source,
            dst_ref=target,
            send_sem=sems.at[(0,) + index],
            recv_sem=sems.at[(1,) + index],
            device_id=device,
            device_id_type=MESH,
        )

    barrier = pltpu.get_barrier_semaphore()
    everyone = [core] + [at(place) for place in (near[0], near[1], low_z, high_z, before, behind)]
    for device in everyone:
        pl.semaphore_signal(barrier, inc=1, device_id=device, device_id_type=MESH)
    pl.semaphore_wait(barrier, len(everyone))

    rim = send(rim_ref, rim_got, dp_sem, (1,), at(before))
    rim.start()
    hops = [core, at(near[0]), at(near[1]), at(low_z), at(high_z)]

    def hop(step):
        return send(small_sum.at[step], small_got.at[step], s_sem, (step,), hops[step])

    def next_hop(step):
        hop(step - 1).wait_recv()
        small_sum[step] = small_sum[step - 1] + small_got[step - 1]
        if step < len(hops):
            hop(step).start()

    depth = tq_ref.shape[1]
    small_sum[0, 0:KW] = tq_ref[...]
    for half in range(2):
        lanes = pl.ds(half * depth, depth)
        small_sum[0, KW * (1 + half) : KW * (2 + half)] = tk_ref[:, lanes]
        small_sum[0, KW * (3 + half) : KW * (4 + half)] = tv_ref[:, lanes]
    small_sum[0, 5 * KW : 6 * KW] = gain_ref[...]
    small_sum[0, 6 * KW :] = rates_ref[...]
    hop(0).start()
    swap = send(rhs_ref, rhs_got, dp_sem, (0,), core)
    swap.start()

    keeps, arrs = (keep_a, keep_b), (arr_a, arr_b)
    quarter = e_got2.shape[2]
    eighth, share = quarter // 2, quarter // 4

    def exchange(p, i, stage, sent, got, sems):
        begin = (0, 0, quarter, quarter + eighth)[stage]
        target = (near[p], near[1 - p], low_z, high_z)[stage]
        return send(sent.at[p, i, pl.ds(begin, got.shape[2])], got.at[p, i], sems, (p, i, stage), at(target))

    def early(p, i, stage):
        return exchange(p, i, stage, e_send, (None, e_got2, e_got3, e_got4)[stage], e_sem)

    def late(p, i, stage):
        sent = l_first if stage == 0 else l_send
        return exchange(p, i, stage, sent, (l_got1, l_got2, l_got3, l_got4)[stage], l_sem)

    def early2(i, carry):
        for p in range(2):
            total = keeps[p][i].astype(F32) + arrs[p][i].astype(F32)
            e_keep[p, i] = total[:quarter].astype(BF16)
            e_send[p, i, 0:quarter] = total[quarter:].astype(BF16)
            early(p, i, 1).start()
        return carry

    def onward(p, i, copy_of, keep, sent, got, stage, begin):
        copy_of(p, i, stage).wait_recv()
        rows = got.shape[2]
        half = rows // 2
        total = keep[p, i, 0:rows].astype(F32) + got[p, i].astype(F32)
        keep[p, i, 0:half] = total[:half].astype(BF16)
        sent[p, i, begin : begin + half] = total[half:].astype(BF16)
        copy_of(p, i, stage + 1).start()

    def later(i, carry, copy_of, keep, sent, got, stage, begin):
        for p in range(2):
            onward(p, i, copy_of, keep, sent, got, stage, begin)
        return carry

    lax.fori_loop(0, JOBS, early2, 0)
    next_hop(1)
    swap.wait_recv()
    job = l_got1.shape[-1]
    late_jobs = LATE_JOBS // 2
    tokens = rhs_ref.shape[0]
    lhs_lanes = pl.ds(own_ref.shape[1] - tokens, tokens)

    def product(m, p, sending):
        lanes = pl.ds(pl.multiple_of(m * job, job), job)
        parts = []
        for block in row_blocks(p, sending):
            rows = pl.ds(block * quarter, quarter)
            parts.append(
                mm(own_ref[rows, lhs_lanes], rhs_ref[:, lanes]) + mm(got_ref[rows, lhs_lanes], rhs_got[:, lanes])
            )
        return parts

    def late1(i, carry):
        for p in range(2):
            low, high = product(2 * i + p, p, True)
            l_first[p, i, 0:quarter] = low.astype(BF16)
            l_first[p, i, quarter : 2 * quarter] = high.astype(BF16)
            late(p, i, 0).start()
        return carry

    def late2(i, carry):
        for p in range(2):
            low, high = product(2 * i + p, p, False)
            late(p, i, 0).wait_recv()
            l_keep[p, i] = (low + l_got1[p, i, 0:quarter].astype(F32)).astype(BF16)
            l_send[p, i, 0:quarter] = (high + l_got1[p, i, quarter : 2 * quarter].astype(F32)).astype(BF16)
            late(p, i, 1).start()
        return carry

    lag = JOBS - late_jobs

    def low_turn(i, carry):
        later(i, carry, early, e_keep, e_send, e_got2, 1, quarter)

        @pl.when(i >= lag)
        def _():
            late1(i - lag, carry)

        return carry

    def high_turn(i, carry):
        later(i, carry, early, e_keep, e_send, e_got3, 2, quarter + eighth)

        @pl.when(i >= lag)
        def _():
            late2(i - lag, carry)

        return carry

    lax.fori_loop(0, JOBS, low_turn, 0)
    next_hop(2)
    lax.fori_loop(0, JOBS, high_turn, 0)
    next_hop(3)
    rim.wait_recv()
    inside = (seq < count - 1).astype(F32)
    _, pulled = norm_pull(x_ref[...].astype(F32), again_ref[...], edge_ref[...] + inside * rim_got[...])
    edge_out[...] = (resid_ref[...] + pulled).astype(BF16)
    late_low = partial(later, copy_of=late, keep=l_keep, sent=l_send, got=l_got2, stage=1, begin=quarter)
    lax.fori_loop(0, late_jobs, late_low, 0)
    next_hop(4)
    late_high = partial(later, copy_of=late, keep=l_keep, sent=l_send, got=l_got3, stage=2, begin=quarter + eighth)
    lax.fori_loop(0, late_jobs, late_high, 0)
    early_outs = (gate_out, up_out, down_out, out_out, outgate_out)
    for i in range(JOBS):
        for p in range(2):
            early(p, i, 3).wait_recv()
            total = e_keep[p, i, 0:share].astype(F32) + e_got4[p, i].astype(F32)
            for output, to, begin, width in column_pieces(p, i, gate_out.shape[1], out_out.shape[1]):
                early_outs[output][:, to : to + width] = total[:, begin : begin + width]
    next_hop(5)
    tq_out[...] = small_sum[5, 0:KW]
    for half in range(2):
        lanes = pl.ds(half * depth, depth)
        tk_out[:, lanes] = small_sum[5, KW * (1 + half) : KW * (2 + half)]
        tv_out[:, lanes] = small_sum[5, KW * (3 + half) : KW * (4 + half)]
    rest_out[...] = small_sum[5, 5 * KW :]
    width = q_out.shape[1] // heads
    for i in range(late_jobs):
        for p in range(2):
            late(p, i, 3).wait_recv()
            total = l_keep[p, i, 0:share].astype(F32) + l_got4[p, i].astype(F32)
            for begin in range(0, job, width):
                head, part = divmod(((2 * i + p) * job + begin) // width, 5)
                if part == 0:
                    target, to = q_out, head * width
                else:
                    target, to = (k_out, v_out)[(part - 1) // 2], (2 * head + (part - 1) % 2) * width
                target[:, to : to + width] = total[:, begin : begin + width]

    def early_sent(i, carry):
        for p in range(2):
            for stage in (1, 2, 3):
                early(p, i, stage).wait_send()
        return carry

    def late_sent(i, carry):
        for p in range(2):
            for stage in (0, 1, 2, 3):
                late(p, i, stage).wait_send()
        return carry

    lax.fori_loop(0, JOBS, early_sent, 0)
    lax.fori_loop(0, late_jobs, late_sent, 0)
    swap.wait_send()
    rim.wait_send()
    for step in range(len(hops)):
        hop(step).wait_send()


def reduce_all(arrived, kept, own, got, rhs, taps, gains, rates, edge, rim, x_edge, gain, resid_edge, ff, heads):
    half = kept[0].shape[1]
    quarter, eighth, share = half // 2, half // 4, half // 8
    count = LATE_JOBS // 2
    columns = rhs.shape[1] // 5
    job = rhs.shape[1] // LATE_JOBS
    depth = gains.shape[1]
    small_rows = 5 * KW + gains.shape[0] + rates.shape[0]
    out = jax.ShapeDtypeStruct
    vmem = pl.BlockSpec(memory_space=pltpu.VMEM)

    def stages(jobs, width):
        return [((2, jobs, rows, width), BF16) for rows in (quarter, eighth, share)]

    buffers = [((2, JOBS, quarter, JOB), BF16), ((2, JOBS, half, JOB), BF16)] + stages(JOBS, JOB)
    buffers += [(rhs.shape, BF16)] + [((2, count, half, job), BF16)] * 2 + [((2, count, quarter, job), BF16)]
    buffers += [((2, count, half, job), BF16)] + stages(count, job)
    buffers += [((6, small_rows, depth), F32), ((5, small_rows, depth), F32), (rim.shape, F32)]
    dma = pltpu.SemaphoreType.DMA
    shapes = [(share, ff)] * 3 + [(share, columns)] * 3 + [(share, 2 * columns)] * 2
    shapes += [tap.shape for tap in taps] + [(small_rows - 5 * KW, depth)]
    return pl.pallas_call(
        partial(reduce_kernel, heads),
        in_specs=[vmem] * 17,
        out_specs=[vmem] * 13,
        out_shape=[out(shape, F32) for shape in shapes] + [out(edge.shape, BF16)],
        scratch_shapes=[pltpu.VMEM(shape, kind) for shape, kind in buffers]
        + [dma((2, 2)), dma((2, 2, JOBS, 4)), dma((2, 2, count, 4)), dma((2, 5))],
        compiler_params=pltpu.CompilerParams(
            collective_id=2, has_side_effects=True, vmem_limit_bytes=VMEM_LIMIT
        ),
        cost_estimate=cost(90),
        name="reduce_all",
    )(*arrived, *kept, own, got, rhs, *taps, gains, rates, edge, rim, x_edge, gain, resid_edge)


def finish_kernel(marks, grad_ref, edge_ref, mine_ref, rest_ref, *refs):
    count = (len(refs) - 8) // 2
    sources, (grad_out, *outs) = refs[:count], refs[count:]
    rows = grad_ref.shape[0]
    grad_out[0 : rows - HALO, :] = grad_ref[0 : rows - HALO, :]
    grad_out[rows - HALO :, :] = edge_ref[...]
    for source, target in zip(sources, outs):
        value = source[...]
        target[...] = value if source.shape == target.shape else value.T
    again, mlp, rates_b, rates_d, gain, bias, decay = outs[count:]
    again[...] = mine_ref[0:1, :]
    mlp[...] = mine_ref[1:2, :]
    rates = mine_ref[4:, :].T
    rates_b[...] = rates[:, : rates_b.shape[1]]
    rates_d[...] = rates[:, rates_b.shape[1] :]
    for target, begin in zip((gain, bias, decay), marks):
        target[...] = rest_ref[2:3, begin : begin + target.shape[1]]


def finish(input_grad, edge_grad, mine, rest, straight, turned, width, heads):
    share = mine.shape[1]
    wide, narrow = heads * REFLECTS, heads
    shapes = [value.shape for value in straight] + [value.shape[::-1] for value in turned]
    shapes += [(1, share)] * 2 + [(share, wide), (share, narrow), (1, width), (1, wide), (1, narrow)]
    out = jax.ShapeDtypeStruct
    vmem = pl.BlockSpec(memory_space=pltpu.VMEM)
    return pl.pallas_call(
        partial(finish_kernel, (0, width, width + wide)),
        in_specs=[vmem] * (4 + len(straight) + len(turned)),
        out_specs=[vmem] * (1 + len(shapes)),
        out_shape=[out(input_grad.shape, BF16)] + [out(shape, F32) for shape in shapes],
        compiler_params=pltpu.CompilerParams(vmem_limit_bytes=VMEM_LIMIT),
        cost_estimate=cost(3),
        name="finish",
    )(input_grad, edge_grad, mine, rest, *straight, *turned)


def dot32(a, b, dims=NN):
    return lax.dot_general(a, b, dims, preferred_element_type=F32)


def swap_core(value):
    count = lax.axis_size("dp")
    return lax.ppermute(value, "dp", [(i, (i + 1) % count) for i in range(count)])


def relative_source(depth, group, seq):
    block = depth // 32
    index = jnp.arange(depth, dtype=jnp.int32)
    row, place, side = index % block, (index // block) % 16, index // (16 * block)
    x = (seq % 2) ^ (place // 8)
    y = ((seq // 2) % 2) ^ ((place // 4) % 2)
    z = (seq // 4) ^ ((place // 2) % 2 + 2 * (place % 2))
    return ((((group + side) % 2) * 16 + z * 4 + y * 2 + x) * block + row)[:, None]


def neighbour_route(bit):
    return [(i, i ^ bit) for i in range(16)]


def by_head(field, heads, begin, size):
    rows = field.shape[0]
    return field.reshape(rows, heads, -1)[:, :, begin : begin + size].reshape(rows, heads * size)


def per_device(
    block_input, lengths, attn_gain, w_query, w_key, w_value, w_outgate, w_beta, w_decay, beta_bias,
    decay_rate, conv_query, conv_key, conv_value, out_gain, w_out, mlp_gain, w_gate, w_up, w_down,
    out_grad,
):
    rows, depth = block_input.shape
    heads = decay_rate.shape[0]
    width = out_gain.shape[0]
    count = lax.axis_size("seq")
    seq = lax.axis_index("seq")
    group = lax.axis_index("dp")
    compact = count == 16
    wide = heads * REFLECTS
    spare = 128 - wide - heads

    halo = lax.ppermute(block_input[rows - HALO :], "seq", [(i, i + 1) for i in range(count - 1)])
    w_rates = jnp.pad(jnp.concatenate([w_beta, w_decay], axis=1), ((0, 0), (0, spare)))
    bias = jnp.pad(beta_bias, (0, heads + spare))[None]
    rate = jnp.pad(decay_rate, (wide, spare))[None]
    ext_b, raw, live, acol, arow = rates_forward(
        lengths, block_input, halo, attn_gain, w_rates, bias, rate, heads
    )
    taps = (conv_query, conv_key, conv_value)
    pre, gate_pre, oloc, oread, *saved, maps = mixer_forward(
        ext_b, w_query, w_key, w_value, w_outgate, taps, live, acol, arow, heads, width
    )
    start, all_maps = carry_states(maps, None, count)
    (
        block_output, d_out, part, gated_b, hidden_b, d_gate_b, d_up_b, d_outgate_b, d_resid,
        own_l, other_l, mlp_b, d_branch_b, grad_mlp_gain, grad_out_gain,
    ) = middle(
        oloc, oread, start, gate_pre, out_gain, block_input, ext_b, mlp_gain, out_grad,
        relative_source(depth, group, seq), w_out, w_gate, w_up, w_down,
    )
    rhs_own = (d_gate_b, d_up_b, hidden_b, gated_b, d_outgate_b)
    if compact:
        rhs_got = tuple(swap_core(rhs) for rhs in rhs_own)
        got_l = swap_core(other_l)
    after = carry_states(part, all_maps, count)
    if compact:
        rhs_own, rhs_got, own_l, got_l, after = lax.optimization_barrier((rhs_own, rhs_got, own_l, got_l, after))
        send_a, send_b, keep_a, keep_b = early_products(own_l, got_l, rhs_own, rhs_got)
        arr_a = lax.ppermute(send_a, "seq", neighbour_route(1))
        arr_b = lax.ppermute(send_b, "seq", neighbour_route(2))
        after = lax.optimization_barrier((after, keep_a))[0]
    d_all, d_tap_q, d_tap_k, d_tap_v, aux = mixer_backward(
        pre, taps, live, acol, arow, saved, start, after, d_out
    )
    input_grad, edge, rim, grad_attn_gain, grad_rates, misc = input_pull(
        d_all, d_outgate_b, (w_query, w_key, w_value, w_outgate), aux, raw, live, rate, w_rates, ext_b,
        block_input, halo, attn_gain, d_resid, heads,
    )
    misc = jnp.concatenate([grad_out_gain, misc, jnp.zeros((1, depth - width - 128), F32)], axis=1)
    last = width + wide + heads
    gains = jnp.concatenate([grad_attn_gain, grad_mlp_gain, misc, jnp.zeros((1, depth), F32)], axis=0)
    d_taps = (d_tap_q, d_tap_k, d_tap_v)
    devices = count * lax.axis_size("dp")
    share = depth // devices
    here = (group * count + seq) * share
    if compact:
        sums = reduce_all(
            (arr_a, arr_b), (keep_a, keep_b), own_l, got_l, d_all, d_taps, gains, grad_rates,
            edge, rim, block_input[rows - HALO :], attn_gain[None, :], d_resid[rows - HALO :],
            w_gate.shape[1], heads,
        )
        trunk, taps_out, rest, edge_grad = sums[5:8], sums[8:11], sums[11], sums[12]
    else:
        normed_e = jnp.concatenate([ext_b[HALO:], ext_b[:HALO]], axis=0)
        normed_b = ext_b[HALO:]
        xf = block_input.astype(F32)
        tail = edge + lax.ppermute(rim, "seq", [(i, i - 1) for i in range(1, count)])
        _, pulled = norm_pull(xf[rows - HALO :], attn_gain[None, :], tail)
        edge_grad = (d_resid[rows - HALO :] + pulled).astype(BF16)
        small = lax.psum(d_taps + (gains, grad_rates), ("dp", "seq"))
        taps_out, rest = small[:3], jnp.concatenate(small[3:], axis=0)
        trunk = [by_head(d_all, heads, begin * width, size * width) for begin, size in ((0, 1), (1, 2), (3, 2))]
        pairs = zip(
            (mlp_b, mlp_b, out_grad, d_branch_b, normed_b) + (normed_e,) * 3, rhs_own + tuple(trunk)
        )
        sums = [
            lax.psum_scatter(dot32(lhs, rhs, TN), ("dp", "seq"), scatter_dimension=0, tiled=True)
            for lhs, rhs in pairs
        ]
        trunk = sums[5:]
    mine = lax.dynamic_slice(rest, (0, here), (rest.shape[0], share))
    straight = (*trunk, sums[4], *taps_out, sums[0], sums[1])
    done = finish(input_grad, edge_grad, mine, rest, straight, (sums[3], sums[2]), width, heads)
    (
        input_grad, g_query, g_key, g_value, g_outgate, g_conv_q, g_conv_k, g_conv_v, g_gate, g_up, g_out, g_down,
        g_attn, g_mlp, g_beta, g_decay, g_gain, g_bias, g_rate,
    ) = done
    return (
        block_output,
        input_grad,
        g_attn[0],
        g_query,
        g_key,
        g_value,
        g_outgate,
        g_beta,
        g_decay,
        g_bias[0],
        g_rate[0],
        g_conv_q,
        g_conv_k,
        g_conv_v,
        g_gain[0],
        g_out,
        g_mlp[0],
        g_gate,
        g_up,
        g_down,
    )


def solution(mesh):
    tokens = P(("dp", "seq"), None)
    column = P(None, ("dp", "seq"))
    vector = P(("dp", "seq"))
    in_specs = (tokens, P("dp", None)) + (P(),) * 18 + (tokens,)
    out_specs = (
        (tokens, tokens, vector)
        + (tokens,) * 6
        + (P(),) * 6
        + (column, vector, tokens, tokens, column)
    )
    return jax.shard_map(
        per_device, mesh=mesh, in_specs=in_specs, out_specs=out_specs, check_vma=False
    )
```

```python
from functools import partial

import jax
import jax.numpy as jnp
from jax import lax
from jax.experimental import pallas as pl
from jax.experimental.pallas import tpu as pltpu
from jax.sharding import PartitionSpec as P

REFLECTS = 2
KW = 4
BLOCK = 64
SHORTEST = 1024
STEPS = BLOCK * REFLECTS
HALO = 8
RESET_LOG = -80.0
MESH = pl.DeviceIdType.MESH
F32 = jnp.float32
BF16 = jnp.bfloat16
NN = (((1,), (0,)), ((), ()))
NT = (((1,), (1,)), ((), ()))
TN = (((0,), (0,)), ((), ()))
VMEM_LIMIT = 56 * 1024 * 1024
FORWARD_HEADS = 2
BACKWARD_HEADS = 2


def cost(microseconds):
    return pl.CostEstimate(
        flops=int(microseconds * 1e9), bytes_accessed=int(microseconds * 1e6), transcendentals=0
    )


def mm(a, b, dims=NN):
    return lax.dot_general(a.astype(BF16), b.astype(BF16), dims, preferred_element_type=F32)


def halves(a):
    high = a.astype(BF16)
    return high, (a - high.astype(F32)).astype(BF16)


def mm3(a, b):
    ah, al = halves(a)
    bh, bl = halves(b)
    return mm(jnp.concatenate([ah, al], axis=1), jnp.concatenate([bh, bh], axis=0)) + mm(ah, bl)


def mm2(a, b, dims=NN):
    ah, al = halves(a)
    return mm(ah, b, dims) + mm(al, b, dims)


def sigmoid(v):
    return 1.0 / (1.0 + jnp.exp(-v))


def step_ids(shape, axis):
    index = lax.broadcasted_iota(jnp.int32, shape, axis)
    return index % BLOCK, index // BLOCK


def step_masks():
    shape = (STEPS, STEPS)
    tm, jm = step_ids(shape, 0)
    tn, jn = step_ids(shape, 1)
    strict = (tm > tn) | ((tm == tn) & (jm > jn))
    size = 4
    first = tm // size == tn // size
    merges = []
    while size < BLOCK:
        merges.append((tm // (2 * size) == tn // (2 * size)) & (tm // size != tn // size))
        size = 2 * size
    eye = ((tm == tn) & (jm == jn)).astype(F32)
    return tm >= tn, strict, first, merges, eye


def unit_lower_inverse(systems, first, merges, eye):
    neg = [jnp.where(first, -a, 0.0) for a in systems]
    inv = [eye + n for n in neg]
    for _ in range(2):
        neg = [mm3(n, n) for n in neg]
        inv = [t + mm3(t, n) for t, n in zip(inv, neg)]
    for merge in merges:
        off = [mm3(jnp.where(merge, a, 0.0), t) for a, t in zip(systems, inv)]
        inv = [t - mm3(t, o) for t, o in zip(inv, off)]
    return inv


def conv_parts(ext_ref, taps, live, columns, rows):
    total = None
    for back in range(KW):
        part = ext_ref[pl.ds(HALO - back, rows), columns] * taps[KW - 1 - back : KW - back, :]
        if back > 0:
            part = part * live[:, back : back + 1]
        total = part if total is None else total + part
    return total


def head_features(ext_ref, tq, tk, tv, live, rows, width):
    conv = [
        conv_parts(ext_ref, tq, live, pl.ds(0, width), rows),
        conv_parts(ext_ref, tk[:, :width], live, pl.ds(width, width), rows),
        conv_parts(ext_ref, tk[:, width:], live, pl.ds(2 * width, width), rows),
        conv_parts(ext_ref, tv[:, :width], live, pl.ds(3 * width, width), rows),
        conv_parts(ext_ref, tv[:, width:], live, pl.ds(4 * width, width), rows),
    ]
    return conv


def unit_rows(act):
    return lax.rsqrt(jnp.sum(act * act, axis=-1, keepdims=True) + 1e-06)


def mixer_forward_kernel(
    xn_ref, wq_ref, wk_ref, wv_ref, wg_ref, tq_ref, tk_ref, tv_ref, live_ref, acol_ref, arow_ref,
    pre_ref, gate_ref, oloc_ref, oread_ref, inv_ref, delta_ref, state_ref, turn_ref, carry_ref, final_ref,
    ext_ref,
):
    heads, rows, width = oread_ref.shape
    blocks = rows // BLOCK
    xn = xn_ref[...]
    live = live_ref[...]
    gate_ref[...] = mm(xn[HALO:], wg_ref[...])
    query, key, value = mm(xn, wq_ref[...]), mm(xn, wk_ref[...]), mm(xn, wv_ref[...])
    reach, strict, first, merges, eye = step_masks()
    cut = [slice(b * BLOCK, (b + 1) * BLOCK) for b in range(blocks)]
    every = [(n, b) for n in range(heads) for b in range(blocks)]
    qb, kb, vb = {}, {}, {}
    for n in range(heads):
        one, two = slice(n * width, (n + 1) * width), slice(2 * n * width, 2 * (n + 1) * width)
        pre = jnp.concatenate([query[:, one], key[:, two], value[:, two]], axis=1).astype(BF16)
        pre_ref[n] = pre
        ext_ref[n] = pre.astype(F32)
        conv = head_features(ext_ref.at[n], tq_ref[:, one], tk_ref[:, two], tv_ref[:, two], live, rows, width)
        act = [c * sigmoid(c) for c in conv]
        q = (act[0] * unit_rows(act[0]) * width ** (-0.5)).astype(BF16)
        k = [(a * unit_rows(a)).astype(BF16) for a in act[1:3]]
        v = [a.astype(BF16) for a in act[3:5]]
        for b in range(blocks):
            qb[n, b] = q[cut[b]]
            kb[n, b] = jnp.concatenate([k[0][cut[b]], k[1][cut[b]]], axis=0)
            vb[n, b] = jnp.concatenate([v[0][cut[b]], v[1][cut[b]]], axis=0)
    ccol = {at: acol_ref[at[0], at[1], :, 0:1] for at in every}
    bcol = {at: acol_ref[at[0], at[1], :, 1:2] for at in every}
    crow = {at: arow_ref[at[0], at[1], 0:1, :] for at in every}
    brow = {at: arow_ref[at[0], at[1], 1:2, :] for at in every}
    fade = {at: jnp.exp(jnp.where(reach, ccol[at] - crow[at], -1e30)) for at in every}
    system = [jnp.where(strict, fade[at] * mm(kb[at], kb[at], NT), 0.0) * bcol[at] for at in every]
    inv = dict(zip(every, unit_lower_inverse(system, first, merges, eye)))
    for at in every:
        inv_ref[at[0], at[1]] = inv[at].astype(BF16)
    local = {at: mm2(inv[at] * brow[at], vb[at]) for at in every}
    reads = {at: mm2(inv[at] * (brow[at] * jnp.exp(crow[at])), kb[at]) for at in every}
    score = {at: fade[at][:BLOCK] * mm(qb[at], kb[at], NT) for at in every}
    grow = {at: jnp.exp(ccol[at]) for at in every}
    last = {at: ccol[at][BLOCK - 1 : BLOCK] for at in every}
    tail = {at: kb[at].astype(F32) * jnp.exp(last[at] - ccol[at]) for at in every}
    both = {at: jnp.concatenate([local[at], -reads[at]], axis=1).astype(BF16) for at in every}
    turn = {at: mm(tail[at], both[at], TN) for at in every}
    query_out = {at: mm(score[at], both[at]) for at in every}
    state = {}
    for n in range(heads):
        now = jnp.concatenate([jnp.zeros((width, width), F32), eye], axis=1)
        for b in range(blocks):
            at = (n, b)
            state[at] = now
            step = turn[at][:, width:].astype(BF16)
            turn_ref[n, b] = step
            fixed = jnp.concatenate([turn[at][:, :width], jnp.zeros((width, width), F32)], axis=1)
            now = jnp.exp(last[at]) * now + fixed + mm(step, now)
        final_ref[n] = now.astype(BF16)
    for at in every:
        n, b = at
        carried = query_out[at][:, width:] + grow[at][:BLOCK] * qb[at].astype(F32)
        low = state[at].astype(BF16)
        carry_ref[n, b] = carried.astype(BF16)
        state_ref[n, b] = low
        fixed = jnp.concatenate([local[at], jnp.zeros((STEPS, width), F32)], axis=1)
        delta_ref[n, b] = (fixed - mm(reads[at], low)).astype(BF16)
        out = mm(carried, low)
        oloc_ref[cut[b], n * width : (n + 1) * width] = out[:, :width] + query_out[at][:, :width]
        oread_ref[n, cut[b], :] = out[:, width:].astype(BF16)


def head_columns(rows, width):
    return pl.BlockSpec((rows, width), lambda h: (0, h))


def whole(shape):
    return pl.BlockSpec(shape, lambda h: (0,) * len(shape))


def per_head(shape, group=1):
    return pl.BlockSpec((group,) + shape, lambda h: (h,) + (0,) * len(shape))


def mixer_forward(xn, w_query, w_key, w_value, w_outgate, taps, live, acol, arow, heads, width):
    ext_rows, depth = xn.shape
    rows = ext_rows - HALO
    blocks = rows // BLOCK
    conv_query, conv_key, conv_value = taps
    out = jax.ShapeDtypeStruct
    return pl.pallas_call(
        mixer_forward_kernel,
        grid=(heads // FORWARD_HEADS,),
        in_specs=[
            whole((ext_rows, depth)),
            head_columns(depth, FORWARD_HEADS * width),
            head_columns(depth, 2 * FORWARD_HEADS * width),
            head_columns(depth, 2 * FORWARD_HEADS * width),
            head_columns(depth, FORWARD_HEADS * width),
            head_columns(KW, FORWARD_HEADS * width),
            head_columns(KW, 2 * FORWARD_HEADS * width),
            head_columns(KW, 2 * FORWARD_HEADS * width),
            whole(live.shape),
            per_head(acol.shape[1:], FORWARD_HEADS),
            per_head(arow.shape[1:], FORWARD_HEADS),
        ],
        out_specs=[
            per_head((ext_rows, 5 * width), FORWARD_HEADS),
            head_columns(rows, FORWARD_HEADS * width),
            head_columns(rows, FORWARD_HEADS * width),
            per_head((rows, width), FORWARD_HEADS),
            per_head((blocks, STEPS, STEPS), FORWARD_HEADS),
            per_head((blocks, STEPS, 2 * width), FORWARD_HEADS),
            per_head((blocks, width, 2 * width), FORWARD_HEADS),
            per_head((blocks, width, width), FORWARD_HEADS),
            per_head((blocks, BLOCK, width), FORWARD_HEADS),
            per_head((width, 2 * width), FORWARD_HEADS),
        ],
        out_shape=[
            out((heads, ext_rows, 5 * width), BF16),
            out((rows, heads * width), F32),
            out((rows, heads * width), F32),
            out((heads, rows, width), BF16),
            out((heads, blocks, STEPS, STEPS), BF16),
            out((heads, blocks, STEPS, 2 * width), BF16),
            out((heads, blocks, width, 2 * width), BF16),
            out((heads, blocks, width, width), BF16),
            out((heads, blocks, BLOCK, width), BF16),
            out((heads, width, 2 * width), BF16),
        ],
        scratch_shapes=[pltpu.VMEM((FORWARD_HEADS, ext_rows, 5 * width), F32)],
        compiler_params=pltpu.CompilerParams(vmem_limit_bytes=VMEM_LIMIT),
        cost_estimate=cost(40),
        name="mixer_forward",
    )(xn, w_query, w_key, w_value, w_outgate, conv_query, conv_key, conv_value, live, acol, arow)


def conv_pull(ext_ref, pad_ref, d_conv, taps, live, columns, rows, dtap_ref):
    total = None
    for back in range(KW):
        part = d_conv if back == 0 else d_conv * live[:, back : back + 1]
        source = ext_ref[pl.ds(HALO - back, rows), columns]
        dtap_ref[KW - 1 - back : KW - back, :] = jnp.sum(part * source, axis=0, keepdims=True)
        pad_ref[pl.ds(HALO, rows), :] = part
        moved = pad_ref[pl.ds(back, rows + HALO), :] * taps[KW - 1 - back : KW - back, :]
        total = moved if total is None else total + moved
    return total


def silu_pull(c, grad):
    s = sigmoid(c)
    return grad * (s + c * s * (1.0 - s))


def unit_pull(act, grad, scale):
    r = unit_rows(act)
    return scale * r * (grad - act * (r * r * jnp.sum(act * grad, axis=-1, keepdims=True)))


def mixer_backward_kernel(
    pre_ref, tq_ref, tk_ref, tv_ref, live_ref, acol_ref, arow_ref,
    inv_ref, delta_ref, state_ref, turn_ref, carry_ref, start_ref, after_ref, dout_ref,
    d_ref, dtq_ref, dtk_ref, dtv_ref, aux_ref,
    ext_ref, pad_ref,
):
    heads = pre_ref.shape[0]
    rows = dout_ref.shape[0]
    width = start_ref.shape[-1]
    blocks = rows // BLOCK
    live = live_ref[...]
    every = [(n, b) for n in range(heads) for b in range(blocks)]
    cut = [slice(b * BLOCK, (b + 1) * BLOCK) for b in range(blocks)]
    conv, act, qb, kb, dout = {}, {}, {}, {}, {}
    for n in range(heads):
        one, two = slice(n * width, (n + 1) * width), slice(2 * n * width, 2 * (n + 1) * width)
        ext_ref[n] = pre_ref[n].astype(F32)
        conv[n] = head_features(ext_ref.at[n], tq_ref[:, one], tk_ref[:, two], tv_ref[:, two], live, rows, width)
        act[n] = [c * sigmoid(c) for c in conv[n][:3]]
        q = (act[n][0] * unit_rows(act[n][0]) * width ** (-0.5)).astype(BF16)
        k = [(a * unit_rows(a)).astype(BF16) for a in act[n][1:]]
        for b in range(blocks):
            qb[n, b] = q[cut[b]]
            kb[n, b] = jnp.concatenate([k[0][cut[b]], k[1][cut[b]]], axis=0)
            dout[n, b] = dout_ref[cut[b], one]
    reach, strict, _, _, _ = step_masks()
    ccol = {at: acol_ref[at[0], at[1], :, 0:1] for at in every}
    bcol = {at: acol_ref[at[0], at[1], :, 1:2] for at in every}
    crow = {at: arow_ref[at[0], at[1], 0:1, :] for at in every}
    last = {at: ccol[at][BLOCK - 1 : BLOCK] for at in every}
    grow = {at: jnp.exp(ccol[at]) for at in every}
    weight = {at: jnp.exp(last[at] - ccol[at]) for at in every}
    ahead = {at: mm(carry_ref[at[0], at[1]], dout[at], TN) for at in every}
    after = {}
    for n in range(heads):
        now = after_ref[n].astype(F32)
        for b in range(blocks - 1, -1, -1):
            after[n, b] = now
            now = jnp.exp(last[n, b]) * now + ahead[n, b] + mm(turn_ref[n, b], now, TN)
    fade = {at: jnp.exp(jnp.where(reach, ccol[at] - crow[at], -1e30)) for at in every}
    delta = {
        at: delta_ref[at[0], at[1], :, :width].astype(F32) + mm(delta_ref[at[0], at[1], :, width:], start_ref[at[0]])
        for at in every
    }
    state = {
        at: state_ref[at[0], at[1], :, :width].astype(F32) + mm(state_ref[at[0], at[1], :, width:], start_ref[at[0]])
        for at in every
    }
    score = {at: fade[at][:BLOCK] * mm(qb[at], kb[at], NT) for at in every}
    d_delta = {at: mm(score[at], dout[at], TN) + weight[at] * mm(kb[at], after[at]) for at in every}
    d_rhs = {at: mm(inv_ref[at[0], at[1]], d_delta[at], TN) for at in every}
    d_score = {at: (fade[at][:BLOCK] * mm(dout[at], delta[at], NT)).astype(BF16) for at in every}
    d_tail = {at: weight[at] * mm(delta[at], after[at], NT) for at in every}
    d_gram = {
        at: jnp.where(strict, -bcol[at] * fade[at] * mm(d_rhs[at], delta[at], NT), 0.0).astype(BF16) for at in every
    }
    dq = {at: mm(grow[at][:BLOCK] * dout[at], state[at], NT) + mm(d_score[at], kb[at]) for at in every}
    dk_row = {
        at: mm(-(bcol[at] * grow[at]) * d_rhs[at], state[at], NT) + mm(d_gram[at], kb[at]) for at in every
    }
    dk_col = {at: mm(d_gram[at], kb[at], TN) + mm(d_score[at], qb[at], TN) + d_tail[at] for at in every}
    tok = lax.broadcasted_iota(jnp.int32, (BLOCK, 1), 0)
    for at in every:
        kf = kb[at].astype(F32)
        d_beta = (1.0 - bcol[at]) * jnp.sum(d_rhs[at] * delta[at], axis=-1, keepdims=True)
        d_log = jnp.sum(kf * (dk_row[at] - dk_col[at]), axis=-1, keepdims=True)
        d_logq = jnp.sum(qb[at].astype(F32) * dq[at], axis=-1, keepdims=True)
        d_last = jnp.sum(kf * d_tail[at]) + jnp.sum(jnp.exp(last[at]) * after[at] * state[at])
        d_token = d_log[:BLOCK] + d_log[BLOCK:] + d_logq + jnp.where(tok == BLOCK - 1, d_last, 0.0)
        aux_ref[at[0], at[1], :, 0:1] = d_beta
        aux_ref[at[0], at[1], 0:BLOCK, 1:2] = d_token
    pad_ref[0:HALO, :] = jnp.zeros((HALO, width), F32)
    pad_ref[pl.ds(HALO + rows, HALO), :] = jnp.zeros((HALO, width), F32)
    for n in range(heads):
        keys = {b: dk_row[n, b] + dk_col[n, b] for b in range(blocks)}
        values = {b: bcol[n, b] * d_rhs[n, b] for b in range(blocks)}
        d_act = [
            jnp.concatenate([dq[n, b] for b in range(blocks)], axis=0),
            jnp.concatenate([keys[b][:BLOCK] for b in range(blocks)], axis=0),
            jnp.concatenate([keys[b][BLOCK:] for b in range(blocks)], axis=0),
            jnp.concatenate([values[b][:BLOCK] for b in range(blocks)], axis=0),
            jnp.concatenate([values[b][BLOCK:] for b in range(blocks)], axis=0),
        ]
        for i, scale in enumerate((width ** (-0.5), 1.0, 1.0)):
            d_act[i] = unit_pull(act[n][i], d_act[i], scale)
        sides = (
            (tq_ref, dtq_ref, n),
            (tk_ref, dtk_ref, 2 * n),
            (tk_ref, dtk_ref, 2 * n + 1),
            (tv_ref, dtv_ref, 2 * n),
            (tv_ref, dtv_ref, 2 * n + 1),
        )
        for i, (tap_ref, dtap_ref, at) in enumerate(sides):
            lanes = pl.ds(at * width, width)
            grad = conv_pull(
                ext_ref.at[n], pad_ref, silu_pull(conv[n][i], d_act[i]), tap_ref[:, lanes], live,
                pl.ds(i * width, width), rows, dtap_ref.at[:, lanes],
            )
            target = pl.ds((5 * n + i) * width, width)
            d_ref[0:rows, target] = grad[HALO:].astype(BF16)
            d_ref[rows : rows + HALO, target] = grad[:HALO].astype(BF16)


def mixer_backward(pre, taps, live, acol, arow, saved, start, after, dout):
    heads, ext_rows, _ = pre.shape
    rows = ext_rows - HALO
    width = start.shape[-1]
    conv_query, conv_key, conv_value = taps
    out = jax.ShapeDtypeStruct
    columns = heads * width
    group = BACKWARD_HEADS
    tap_specs = [head_columns(KW, times * group * width) for times in (1, 2, 2)]
    return pl.pallas_call(
        mixer_backward_kernel,
        grid=(heads // group,),
        in_specs=[per_head(pre.shape[1:], group)]
        + tap_specs
        + [whole(live.shape)]
        + [per_head(value.shape[1:], group) for value in (acol, arow, *saved, start, after)]
        + [head_columns(rows, group * width)],
        out_specs=[head_columns(ext_rows, 5 * group * width)] + tap_specs + [per_head(acol.shape[1:], group)],
        out_shape=[
            out((ext_rows, 5 * columns), BF16),
            out((KW, columns), F32),
            out((KW, 2 * columns), F32),
            out((KW, 2 * columns), F32),
            out(acol.shape, F32),
        ],
        scratch_shapes=[
            pltpu.VMEM((group, ext_rows, 5 * width), F32),
            pltpu.VMEM((rows + 2 * HALO, width), F32),
        ],
        compiler_params=pltpu.CompilerParams(vmem_limit_bytes=VMEM_LIMIT),
        cost_estimate=cost(35),
        name="mixer_backward",
    )(pre, conv_query, conv_key, conv_value, live, acol, arow, *saved, start, after, dout)


def greet_group(count):
    place, group = lax.axis_index("seq"), lax.axis_index("dp")
    barrier = pltpu.get_barrier_semaphore()

    def greet(step, carry):
        peer = lax.rem(place + step, count)
        pl.semaphore_signal(barrier, inc=1, device_id=(group, peer), device_id_type=MESH)
        return carry

    lax.fori_loop(1, count, greet, 0)
    return barrier


def carry_steps(count, heads, backward, part_ref, maps_ref, inbox, outbox, landed, sems):
    send_sem, recv_sem, back_sem, land_sem = sems
    place, group = lax.axis_index("seq"), lax.axis_index("dp")
    width = landed.shape[-1]
    stride = count // 16

    def keeper(h):
        return (2 * h + group) * stride

    def outgoing(h):
        return pltpu.make_async_remote_copy(
            src_ref=part_ref.at[h],
            dst_ref=inbox.at[place],
            send_sem=send_sem.at[h],
            recv_sem=recv_sem.at[place],
            device_id=(group, keeper(h)),
            device_id_type=MESH,
        )

    def send(h):
        @pl.when(place != keeper(h))
        def _():
            outgoing(h).start()

        @pl.when(place == keeper(h))
        def _():
            inbox[pl.ds(place, 1)] = part_ref[h : h + 1]

    def scan_head(h):
        def returning(where):
            return pltpu.make_async_remote_copy(
                src_ref=outbox.at[where],
                dst_ref=landed.at[h],
                send_sem=back_sem.at[where],
                recv_sem=land_sem.at[h],
                device_id=(group, where),
                device_id_type=MESH,
            )

        def lap(step, state):
            where = count - 1 - step if backward else step
            outbox[pl.ds(where, 1)] = state[None].astype(BF16)

            @pl.when(where != place)
            def _():
                returning(where).start()
                pltpu.make_async_remote_copy(
                    src_ref=part_ref.at[h],
                    dst_ref=inbox.at[where],
                    send_sem=send_sem.at[h],
                    recv_sem=recv_sem.at[where],
                    device_id=(group, where),
                    device_id_type=MESH,
                ).wait_recv()

            @pl.when(where == place)
            def _():
                landed[h : h + 1] = outbox[pl.ds(where, 1)]

            got = inbox[pl.ds(where, 1)][0]
            high, low = halves(state)
            both = jnp.concatenate([high, low], axis=1)
            if backward:
                moved = mm(maps_ref[pl.ds(where, 1)][0][:, width:], both, TN)
            else:
                moved = mm(got[:, width:], both)
            return moved[:, :width] + moved[:, width:] + got[:, :width].astype(F32)

        lax.fori_loop(0, count, lap, jnp.zeros((width, width), F32))

        def finish(where, carry):
            @pl.when(where != place)
            def _():
                returning(where).wait_send()

            return carry

        return lambda: lax.fori_loop(0, count, finish, 0)

    def scan():
        for h in range(heads):

            @pl.when(place == keeper(h))
            def _(h=h):
                scan_head(h)()

    def take():
        for h in range(heads):

            @pl.when(place != keeper(h))
            def _(h=h):
                outgoing(h).wait_send()
                pltpu.make_async_remote_copy(
                    src_ref=outbox.at[0],
                    dst_ref=landed.at[h],
                    send_sem=back_sem.at[0],
                    recv_sem=land_sem.at[h],
                    device_id=(group, keeper(h)),
                    device_id_type=MESH,
                ).wait_recv()

    return send, scan, take


def carry_scratch(count, heads, width, columns):
    dma = pltpu.SemaphoreType.DMA
    return [
        pltpu.VMEM((count, width, columns), BF16),
        pltpu.VMEM((count, width, width), BF16),
        pltpu.VMEM((heads, width, width), BF16),
        dma((heads,)),
        dma((count,)),
        dma((count,)),
        dma((heads,)),
    ]


def carry_kernel(count, heads, backward, *refs):
    part_ref, other, third, inbox, outbox, landed, *sems = refs
    maps_ref, result_ref = (other, third) if backward else (third, other)
    barrier = greet_group(count)
    pl.semaphore_wait(barrier, count - 1)
    send, scan, take = carry_steps(count, heads, backward, part_ref, maps_ref, inbox, outbox, landed, sems)
    for h in range(heads):
        send(h)
    scan()
    take()
    result_ref[...] = landed[...]
    if not backward:
        maps_ref[...] = inbox[...]


def carry_states(part, maps, count):
    heads, width, columns = part.shape
    backward = maps is not None
    out = jax.ShapeDtypeStruct
    vmem = pl.BlockSpec(memory_space=pltpu.VMEM)
    result = out((heads, width, width), BF16)
    return pl.pallas_call(
        partial(carry_kernel, count, heads, backward),
        in_specs=[vmem] * (2 if backward else 1),
        out_specs=vmem if backward else [vmem, vmem],
        out_shape=result if backward else [result, out((count, width, columns), BF16)],
        scratch_shapes=carry_scratch(count, heads, width, columns),
        compiler_params=pltpu.CompilerParams(
            collective_id=1 if backward else 0, has_side_effects=True, vmem_limit_bytes=VMEM_LIMIT
        ),
        cost_estimate=cost(24),
        name="carry_backward" if backward else "carry_forward",
    )(*((part, maps) if backward else (part,)))


JOBS = 7
JOB = 512
GROUPS = 3
LATE_JOBS = 10
EARLY_LINKS = ((0, 1, 2, 3), (1, 2, 0, 3), (2, 0, 1, 3))
LATE_LINKS = ((0, 1, 2, 3), (1, 0, 2, 3))


def half_rows(lhs, links, sending, lanes=slice(None)):
    edge = lhs.shape[0] // 8
    parts = []
    for second in range(2):
        for third in range(2):
            move = {links[0]: int(sending), links[1]: second, links[2]: third}
            block = 4 * move[0] + 2 * move[1] + move[2]
            parts.append(lhs[block * edge : (block + 1) * edge, lanes])
    return jnp.concatenate(parts, axis=0)


def column_pieces(sizes, begin, end):
    at, pieces = 0, []
    for index, size in enumerate(sizes):
        low, high = max(at, begin), min(at + size, end)
        if low < high:
            pieces.append((index, low - at, low - begin, high - low))
        at += size
    return pieces


def input_pull_kernel(
    d_ref, dg_ref, wq_ref, wk_ref, wv_ref, wg_ref, aux_ref, raw_ref, live_ref, rate_ref, wr_ref, ext_ref,
    x_ref, halo_ref, gain_ref, resid_ref,
    grad_ref, edge_ref, rim_ref, dgain_ref, drates_ref, misc_ref, total_ref, rates_ref,
):
    head = pl.program_id(0)
    rows = dg_ref.shape[0]
    width = dg_ref.shape[1] // PULL_HEADS
    group = PULL_HEADS
    part = None
    for n in range(group):
        d = d_ref[:, n * 5 * width : (n + 1) * 5 * width]
        two = slice(2 * n * width, 2 * (n + 1) * width)
        term = (
            mm(d[:, :width], wq_ref[:, n * width : (n + 1) * width], NT)
            + mm(d[:, width : 3 * width], wk_ref[:, two], NT)
            + mm(d[:, 3 * width :], wv_ref[:, two], NT)
        )
        part = term if part is None else part + term
    more = mm(dg_ref[...], wg_ref[...], NT)

    @pl.when(head == 0)
    def _():
        heads, blocks = aux_ref.shape[:2]
        wide = heads * REFLECTS
        rates_ref[...] = jnp.zeros_like(rates_ref)
        for h in range(heads):
            for b in range(blocks):
                tokens = slice(b * BLOCK, (b + 1) * BLOCK)
                for j in range(REFLECTS):
                    at = h * REFLECTS + j
                    rates_ref[tokens, at : at + 1] = aux_ref[h, b, j * BLOCK : (j + 1) * BLOCK, 0:1]
                rates_ref[tokens, wide + h : wide + h + 1] = aux_ref[h, b, 0:BLOCK, 1:2]
        value, raw = rates_ref[...], raw_ref[...]
        d_log = exact_sum(block_sums(rows, True), value) * live_ref[:, 1:2]
        lane = lax.broadcasted_iota(jnp.int32, raw.shape, 1)
        d_raw = jnp.where(lane < wide, value, -rate_ref[...] * sigmoid(raw) * d_log)
        summed = jnp.where(lane < wide, value, -softplus(raw) * d_log)
        misc_ref[...] = jnp.sum(summed, axis=0, keepdims=True)
        d_raw = d_raw.astype(BF16)
        drates_ref[...] = mm(d_raw, ext_ref[pl.ds(HALO, rows), :], TN)[: drates_ref.shape[0]]
        total_ref[...] = part
        total_ref[0:rows, :] += more + mm(d_raw, wr_ref[...])

    @pl.when(head > 0)
    def _():
        total_ref[...] += part
        total_ref[0:rows, :] += more

    @pl.when(head == pl.num_programs(0) - 1)
    def _():
        grad = total_ref[...]
        unit, pulled = norm_pull(x_ref[...].astype(F32), gain_ref[...], grad[:rows])
        grad_ref[...] = (resid_ref[...] + pulled).astype(BF16)
        halo_unit, _ = norm_pull(halo_ref[...].astype(F32), gain_ref[...], grad[rows:])
        dgain_ref[...] = jnp.sum(grad[:rows] * unit, axis=0, keepdims=True) + jnp.sum(
            grad[rows:] * halo_unit, axis=0, keepdims=True
        )
        edge_ref[0] = grad[rows - HALO : rows]
        edge_ref[1] = x_ref[rows - HALO :, :].astype(F32)
        edge_ref[2] = resid_ref[rows - HALO :, :]
        rim_ref[...] = grad[rows:]


def norm_pull(x, gain, grad):
    r = lax.rsqrt(jnp.mean(x * x, axis=-1, keepdims=True) + 1e-06)
    unit = x * r
    through = grad * gain
    return unit, r * (through - unit * jnp.mean(unit * through, axis=-1, keepdims=True))


PULL_HEADS = 2


def input_pull(d_all, d_outgate, weights, aux, raw, live, rate, w_rates, ext_b, x, halo, gain, d_resid, heads):
    rows, depth = x.shape
    ext_rows = rows + HALO
    width = d_outgate.shape[1] // heads * PULL_HEADS
    out = jax.ShapeDtypeStruct
    w_query, w_key, w_value, w_outgate = weights
    rates = heads * (REFLECTS + 1)
    return pl.pallas_call(
        input_pull_kernel,
        grid=(heads // PULL_HEADS,),
        in_specs=[
            head_columns(ext_rows, 5 * width),
            head_columns(rows, width),
            head_columns(depth, width),
            head_columns(depth, 2 * width),
            head_columns(depth, 2 * width),
            head_columns(depth, width),
            whole(aux.shape),
            whole(raw.shape),
            whole(live.shape),
            whole(rate.shape),
            whole(w_rates.shape),
            whole(ext_b.shape),
            whole(x.shape),
            whole(halo.shape),
            whole((1, depth)),
            whole(d_resid.shape),
        ],
        out_specs=[
            whole((rows, depth)), whole((3, HALO, depth)), whole((HALO, depth)), whole((1, depth)),
            whole((rates, depth)), whole((1, raw.shape[1])),
        ],
        out_shape=[
            out((rows, depth), BF16),
            out((3, HALO, depth), F32),
            out((HALO, depth), F32),
            out((1, depth), F32),
            out((rates, depth), F32),
            out((1, raw.shape[1]), F32),
        ],
        scratch_shapes=[pltpu.VMEM((ext_rows, depth), F32), pltpu.VMEM(raw.shape, F32)],
        compiler_params=pltpu.CompilerParams(vmem_limit_bytes=VMEM_LIMIT),
        cost_estimate=cost(12),
        name="input_pull",
    )(
        d_all, d_outgate, w_query, w_key, w_value, w_outgate, aux, raw, live, rate, w_rates, ext_b,
        x, halo, gain[None, :], d_resid,
    )


def exact_sum(ones, value):
    total = None
    for _ in range(3):
        part = value.astype(BF16)
        value = value - part.astype(F32)
        term = mm(ones, part)
        total = term if total is None else total + term
    return total


def block_sums(rows, reverse):
    shape = (rows, rows)
    one, two = lax.broadcasted_iota(jnp.int32, shape, 0), lax.broadcasted_iota(jnp.int32, shape, 1)
    order = (one <= two) if reverse else (one >= two)
    return ((one // BLOCK == two // BLOCK) & order).astype(BF16)


def softplus(v):
    return jnp.maximum(v, 0.0) + jnp.log1p(jnp.exp(-jnp.abs(v)))


def rates_kernel(
    heads, lengths_ref, x_ref, gain_ref, wbeta_ref, wdecay_ref, bias_in_ref, rate_in_ref,
    ext_ref, raw_ref, live_ref, acol_ref, arow_ref, halo_ref, weight_ref, rate_ref,
    edge_ref, got_ref, sems,
):
    rows = x_ref.shape[0]
    blocks = rows // BLOCK
    wide = heads * REFLECTS
    seq, count = lax.axis_index("seq"), lax.axis_size("seq")
    behind, before = lax.rem(seq + 1, count), lax.rem(seq + count - 1, count)
    barrier = pltpu.get_barrier_semaphore()
    for place in (behind, before):
        pl.semaphore_signal(barrier, inc=1, device_id={"seq": place}, device_id_type=MESH)
    edge_ref[...] = x_ref[rows - HALO :, :]
    copy = pltpu.make_async_remote_copy(
        src_ref=edge_ref,
        dst_ref=got_ref,
        send_sem=sems.at[0],
        recv_sem=sems.at[1],
        device_id={"seq": behind},
        device_id_type=MESH,
    )

    def normed(field):
        field = field.astype(F32)
        return (
            field * lax.rsqrt(jnp.mean(field * field, axis=-1, keepdims=True) + 1e-06) * gain_ref[...]
        ).astype(BF16)

    pl.semaphore_wait(barrier, 2)
    copy.start()
    xn = normed(x_ref[...])
    ext_ref[pl.ds(HALO, rows), :] = xn
    blank = jnp.zeros((128 - wide - heads, wbeta_ref.shape[1]), F32)
    weight = jnp.concatenate([wbeta_ref[...].astype(F32), wdecay_ref[...].astype(F32), blank], axis=0).astype(BF16)
    weight_ref[...] = weight
    empty = jnp.zeros((1, 128 - wide - heads), F32)
    bias = jnp.concatenate([bias_in_ref[...], jnp.zeros((1, heads), F32), empty], axis=1)
    rate = jnp.concatenate([jnp.zeros((1, wide), F32), rate_in_ref[...], empty], axis=1)
    rate_ref[...] = rate
    raw = mm(xn, weight, NT)
    raw_ref[...] = raw
    row = lax.axis_index("seq") * rows + lax.broadcasted_iota(jnp.int32, (rows, 1), 0)
    place, end = row, 0
    for i in range(lengths_ref.shape[1]):
        begin, end = end, end + lengths_ref[0, i] + (SHORTEST - 1)
        place = jnp.where((row >= begin) & (row < end), row - begin, place)
    live_ref[...] = (place >= lax.broadcasted_iota(jnp.int32, (rows, 8), 1)).astype(F32)
    beta = sigmoid(raw + bias)
    log_rate = jnp.where(place == 0, RESET_LOG, -rate * softplus(raw))
    lane = lax.broadcasted_iota(jnp.int32, raw.shape, 1)
    both = jnp.where(lane < wide, beta, exact_sum(block_sums(rows, False), log_rate))
    turned = both.T
    arow_ref[...] = jnp.zeros_like(arow_ref)
    acol_ref[...] = jnp.zeros_like(acol_ref)
    for h in range(heads):
        for b in range(blocks):
            tokens = slice(b * BLOCK, (b + 1) * BLOCK)
            for j in range(REFLECTS):
                steps = slice(j * BLOCK, (j + 1) * BLOCK)
                at = h * REFLECTS + j
                acol_ref[h, b, steps, 0:1] = both[tokens, wide + h : wide + h + 1]
                acol_ref[h, b, steps, 1:2] = both[tokens, at : at + 1]
                arow_ref[h, b, 0:1, steps] = turned[wide + h : wide + h + 1, tokens]
                arow_ref[h, b, 1:2, steps] = turned[at : at + 1, tokens]
    copy.wait()
    halo = jnp.where(seq > 0, got_ref[...].astype(F32), 0.0)
    halo_ref[...] = halo.astype(BF16)
    ext_ref[0:HALO, :] = normed(halo)


def rates_forward(lengths, x, gain, w_beta, w_decay, bias, rate, heads):
    rows, depth = x.shape
    blocks = rows // BLOCK
    out = jax.ShapeDtypeStruct
    vmem = pl.BlockSpec(memory_space=pltpu.VMEM)
    return pl.pallas_call(
        partial(rates_kernel, heads),
        in_specs=[pl.BlockSpec(memory_space=pltpu.SMEM)] + [vmem] * 6,
        out_specs=[vmem] * 8,
        out_shape=[
            out((rows + HALO, depth), BF16),
            out((rows, 128), F32),
            out((rows, 8), F32),
            out((heads, blocks, STEPS, 8), F32),
            out((heads, blocks, 8, STEPS), F32),
            out((HALO, depth), BF16),
            out((128, depth), BF16),
            out((1, 128), F32),
        ],
        scratch_shapes=[
            pltpu.VMEM((HALO, depth), BF16), pltpu.VMEM((HALO, depth), BF16), pltpu.SemaphoreType.DMA((2,)),
        ],
        compiler_params=pltpu.CompilerParams(
            collective_id=4, has_side_effects=True, vmem_limit_bytes=VMEM_LIMIT
        ),
        cost_estimate=cost(6),
        name="rates_forward",
    )(lengths, x, gain[None, :], w_beta.T, w_decay.T, bias[None, :], rate[None, :])


CHUNK = 256
RING = 4


def flip(bit, other):
    return bit + other - 2 * bit * other


def relative_source(depth):
    block = depth // 32
    seq, group = lax.axis_index("seq"), lax.axis_index("dp")
    index = lax.broadcasted_iota(jnp.int32, (depth, 1), 0)
    row, place, side = index % block, (index // block) % 16, index // (16 * block)
    x = flip(seq % 2, place // 8)
    y = flip((seq // 2) % 2, (place // 4) % 2)
    z = flip((seq // 4) % 2, (place // 2) % 2) + 2 * flip(seq // 8, place % 2)
    return ((((group + side) % 2) * 16 + z * 4 + y * 2 + x) * block + row)


def middle_kernel(
    compact, count, oloc_ref, oread_ref, start_ref, gate_ref, ogain_ref, x_ref, ext_ref, mgain_ref, ograd_ref,
    maps_ref, wout_hbm, wgate_hbm, wup_hbm, wdown_hbm,
    block_ref, dout_ref, part_ref, dresid_ref, dmgain_ref, dogain_ref,
    *refs,
):
    if compact:
        products, (own_out, got_out, after_ref) = refs[: 2 * GROUPS], refs[2 * GROUPS : 2 * GROUPS + 3]
        refs = refs[2 * GROUPS + 3 :]
        gated_ref, hidden_ref, dgate_ref, dup_ref, doutgate_ref, mlp_ref, branch_ref = refs[:7]
        gated_got, hidden_got, dgate_got, dup_got, doutgate_got, own_ref, other_ref, got_ref = refs[7:15]
        other_edge, got_edge, core_sem, chunk_sem, inbox, outbox, landed = refs[15:22]
        carry_sems, staged, stage_sem, refs = refs[22:26], refs[26 : 26 + 2 * GROUPS], refs[26 + 2 * GROUPS], refs[27 + 2 * GROUPS :]
    else:
        gated_ref, hidden_ref, dgate_ref, dup_ref, doutgate_ref, mlp_ref, branch_ref = refs[:7]
        refs = refs[7:]
    wout, wgate, wup, wdown, down_ref, dmlp_ref, sem_out, sems = refs
    heads, rows, width = oread_ref.shape
    depth = x_ref.shape[1]
    chunks = hidden_ref.shape[1] // CHUNK
    fetch_out = pltpu.make_async_copy(wout_hbm, wout, sem_out)
    fetch_out.start()

    def lanes_of(c):
        return pl.ds(pl.multiple_of(c * CHUNK, CHUNK), CHUNK)

    def fetches(c):
        slot = c % RING
        return (
            pltpu.make_async_copy(wgate_hbm.at[:, lanes_of(c)], wgate.at[slot], sems.at[slot, 0]),
            pltpu.make_async_copy(wup_hbm.at[:, lanes_of(c)], wup.at[slot], sems.at[slot, 1]),
            pltpu.make_async_copy(wdown_hbm.at[lanes_of(c), :], wdown.at[slot], sems.at[slot, 2]),
        )

    for c in range(RING):
        for copy in fetches(c):
            copy.start()
    core = {"dp": 1 - lax.axis_index("dp")}

    def to_core(source, target, sems, index):
        return pltpu.make_async_remote_copy(
            src_ref=source,
            dst_ref=target,
            send_sem=sems.at[(0,) + index],
            recv_sem=sems.at[(1,) + index],
            device_id=core,
            device_id_type=MESH,
        )

    if compact:
        barrier = greet_group(count)
        pl.semaphore_signal(barrier, inc=1, device_id=core, device_id_type=MESH)
        give, scan, take = carry_steps(
            count, heads, True, part_ref, maps_ref, inbox, outbox, landed, carry_sems
        )
        half = depth // 2
        lane = lax.broadcasted_iota(jnp.int32, (depth, depth), 1)
        chosen = (lane == relative_source(depth)).astype(BF16)
        swaps = []

        def turn(at, value, index):
            turned = mm(chosen, value, NT).astype(BF16)
            cut = slice(at, at + value.shape[0])
            own_ref[:, cut] = turned[:half]
            other_ref[:, cut] = turned[half:]
            swap(other_ref.at[:, cut], got_ref.at[:, cut], index)

        def turn_tokens():
            value = jnp.concatenate([ext_ref[pl.ds(HALO, rows), :], ext_ref[0:HALO, :]], axis=0)
            turned = mm(chosen, value, NT).astype(BF16)
            own_out[...] = turned[:half]
            other_edge[...] = turned[half:]
            swap(other_edge, got_edge, 3)

        def swap(source, target, index):
            swaps.append(to_core(source, target, core_sem, (index,)))
            swaps[-1].start()

    ogain = ogain_ref[...]
    for h in range(heads):
        lanes = slice(h * width, (h + 1) * width)
        out = oloc_ref[:, lanes] + mm(oread_ref[h], start_ref[h])
        dout_ref[:, lanes] = out
        gate = gate_ref[:, lanes]
        r = lax.rsqrt(jnp.mean(out * out, axis=-1, keepdims=True) + 1e-05)
        gated_ref[:, lanes] = (out * r * ogain * (gate * sigmoid(gate))).astype(BF16)
    fetch_out.wait()
    resid = x_ref[...].astype(F32) + mm(gated_ref[...], wout[...])
    dresid_ref[...] = resid
    r = lax.rsqrt(jnp.mean(resid * resid, axis=-1, keepdims=True) + 1e-06)
    mlp_ref[...] = (resid * r * mgain_ref[...]).astype(BF16)
    if compact:
        pl.semaphore_wait(barrier, count)
        swap(gated_ref, gated_got, 4)
        turn(rows, ograd_ref[...], 1)
        turn_tokens()
        turn(0, mlp_ref[...], 0)
    down_ref[...] = jnp.zeros_like(down_ref)
    dmlp_ref[...] = jnp.zeros_like(dmlp_ref)

    def chunk_swaps(c):
        pairs = ((hidden_ref, hidden_got), (dgate_ref, dgate_got), (dup_ref, dup_got))
        return [
            to_core(own.at[:, lanes_of(c)], got.at[:, lanes_of(c)], chunk_sem, (c, i))
            for i, (own, got) in enumerate(pairs)
        ]

    def one(c, carry):
        slot = c % RING
        for copy in fetches(c):
            copy.wait()
        mlp, ograd = mlp_ref[...], ograd_ref[...]
        lanes = lanes_of(c)
        gate, up = mm(mlp, wgate[slot]), mm(mlp, wup[slot])
        d_hidden = mm(ograd, wdown[slot], NT)
        s = sigmoid(gate)
        act = gate * s
        hidden = (act * up).astype(BF16)
        d_gate = (d_hidden * up * (s + act * (1.0 - s))).astype(BF16)
        d_up = (d_hidden * act).astype(BF16)
        hidden_ref[:, lanes] = hidden
        dgate_ref[:, lanes] = d_gate
        dup_ref[:, lanes] = d_up
        if compact:
            for copy in chunk_swaps(c):
                copy.start()
        down_ref[...] += mm(hidden, wdown[slot])
        dmlp_ref[...] += mm(d_gate, wgate[slot], NT) + mm(d_up, wup[slot], NT)

        @pl.when(c + RING < chunks)
        def _():
            for copy in fetches(c + RING):
                copy.start()

        return carry

    lax.fori_loop(0, chunks, one, 0)
    resid = dresid_ref[...]
    block_ref[...] = (resid + down_ref[...]).astype(BF16)
    grad = dmlp_ref[...]
    unit, pulled = norm_pull(resid, mgain_ref[...], grad)
    dmgain_ref[...] = jnp.sum(grad * unit, axis=0, keepdims=True)
    d_resid = ograd_ref[...].astype(F32) + pulled
    dresid_ref[...] = d_resid
    branch_ref[...] = d_resid.astype(BF16)
    if compact:
        turn(2 * rows, branch_ref[...], 2)
    dogain = jnp.zeros((1, width), F32)
    for h in range(heads):
        lanes = slice(h * width, (h + 1) * width)
        grad = mm(branch_ref[...], wout[lanes, :], NT)
        out = dout_ref[:, lanes]
        gate = gate_ref[:, lanes]
        r = lax.rsqrt(jnp.mean(out * out, axis=-1, keepdims=True) + 1e-05)
        s = sigmoid(gate)
        unit = out * r
        doutgate_ref[:, lanes] = (grad * unit * ogain * (s + gate * s * (1.0 - s))).astype(BF16)
        through = grad * (gate * s)
        dogain += jnp.sum(through * unit, axis=0, keepdims=True)
        through = through * ogain
        dout = r * (through - unit * jnp.mean(unit * through, axis=-1, keepdims=True))
        dout_ref[:, lanes] = dout
        part_ref[h] = mm(oread_ref[h], dout, TN).astype(BF16)
        if compact:
            give(h)
    dogain_ref[...] = dogain
    if compact:
        swap(doutgate_ref, doutgate_got, 5)

        def arrived(c, carry):
            for copy in chunk_swaps(c):
                copy.wait()
            return carry

        lax.fori_loop(0, chunks, arrived, 0)
        rhs_own = (dgate_ref, dup_ref, hidden_ref, gated_ref, doutgate_ref)
        rhs_got = (dgate_got, dup_got, hidden_got, gated_got, doutgate_got)
        for copy in swaps[:4]:
            copy.wait()
        lhs_own, lhs_got = (own_ref, own_out), (got_ref, got_edge)
        targets = [staged[2 * group : 2 * group + 2] for group in range(GROUPS)]
        early_products(lhs_own, lhs_got, rhs_own, rhs_got, targets, (0, 1, 2))
        outgoing = [
            pltpu.make_async_copy(source, target, stage_sem.at[i])
            for i, (source, target) in enumerate(zip(staged, products))
        ]
        for copy in outgoing[: 2 * GROUPS - 2]:
            copy.start()
        scan()
        for copy in swaps[4:]:
            copy.wait()
        early_products(lhs_own, lhs_got, rhs_own, rhs_got, targets, (3, 4))
        for copy in outgoing[2 * GROUPS - 2 :]:
            copy.start()
        got_out[...] = got_edge[...]
        for copy in outgoing:
            copy.wait()
        take()
        after_ref[...] = landed[...]


def early_products(lhs_own, lhs_got, rhs_own, rhs_got, targets, which):
    tokens = rhs_own[0].shape[0]
    sizes = [rhs.shape[1] for rhs in rhs_own]
    sides = (0, 0, 1, 2, 3)
    for group in range(GROUPS):
        for sending in (True, False):
            turned = {}
            for job in range(JOBS):
                begin = (group * JOBS + job) * JOB
                for index, column, offset, width in column_pieces(sizes, begin, begin + JOB):
                    if index not in which:
                        continue
                    side = sides[index]
                    if side not in turned:
                        cut = slice(side % 3 * tokens, (side % 3 + 1) * tokens)
                        turned[side] = [
                            half_rows(lhs[side // 3], EARLY_LINKS[group], sending, cut) for lhs in (lhs_own, lhs_got)
                        ]
                    lanes = slice(column, column + width)
                    total = mm(turned[side][0], rhs_own[index][:, lanes]) + mm(
                        turned[side][1], rhs_got[index][:, lanes]
                    )
                    targets[group][0 if sending else 1][job, :, offset : offset + width] = total.astype(BF16)


def middle(
    compact, count, oloc, oread, start, gate_pre, out_gain, x, ext_b, mlp_gain, out_grad, maps,
    w_out, w_gate, w_up, w_down,
):
    heads, rows, width = oread.shape
    depth = x.shape[1]
    ff = w_gate.shape[1]
    out = jax.ShapeDtypeStruct
    vmem, hbm = pl.BlockSpec(memory_space=pltpu.VMEM), pl.BlockSpec(memory_space=pl.ANY)
    columns = heads * width
    chunks = ff // CHUNK
    half = depth // 2
    outs = [
        ((rows, depth), BF16), ((rows, columns), F32), ((heads, width, width), BF16), ((rows, depth), F32),
        ((1, depth), F32), ((1, width), F32),
    ]
    rhs = [((rows, columns), BF16)] + [((rows, ff), BF16)] * 3 + [((rows, columns), BF16)]
    kept = rhs + [((rows, depth), BF16)] * 2
    scratch = []
    dma = pltpu.SemaphoreType.DMA
    if compact:
        product = ((JOBS, half // 2, JOB), BF16)
        outs += [product] * (2 * GROUPS) + [((half, rows + HALO), BF16)] * 2
        outs += [((heads, width, width), BF16), ((rows, columns), BF16)]
        buffers = kept[:4] + kept[5:] + rhs + [((half, 3 * rows), BF16)] * 3 + [((half, rows + HALO), BF16)] * 2
        scratch += [pltpu.VMEM(*buffer) for buffer in buffers] + [dma((2, 6)), dma((2, chunks, 3))]
        scratch += carry_scratch(count, heads, width, width)
        scratch += [pltpu.VMEM(*product)] * (2 * GROUPS) + [dma((2 * GROUPS,))]
    else:
        outs += kept
    scratch += [
        pltpu.VMEM(w_out.shape, BF16),
        pltpu.VMEM((RING, depth, CHUNK), BF16),
        pltpu.VMEM((RING, depth, CHUNK), BF16),
        pltpu.VMEM((RING, CHUNK, depth), BF16),
        pltpu.VMEM((rows, depth), F32),
        pltpu.VMEM((rows, depth), F32),
        dma,
        dma((RING, 3)),
    ]

    def kernel(*refs):
        if not compact:
            middle_kernel(compact, count, *refs)
            return
        late = 20 + 2 * GROUPS + 3
        rest = refs[late + 1 :]
        middle_kernel(compact, count, *refs[:late], *rest[:4], refs[late], *rest[4:])

    params = {"collective_id": 3, "has_side_effects": True} if compact else {}
    return pl.pallas_call(
        kernel,
        in_specs=[vmem] * 10 + [hbm] * 4,
        out_specs=[hbm if compact and shape == product else vmem for shape in outs],
        out_shape=[out(*shape) for shape in outs],
        scratch_shapes=scratch,
        compiler_params=pltpu.CompilerParams(vmem_limit_bytes=VMEM_LIMIT, **params),
        cost_estimate=cost(30),
        name="middle",
    )(
        oloc, oread, start, gate_pre, out_gain[None, :], x, ext_b, mlp_gain[None, :], out_grad, maps,
        w_out, w_gate, w_up, w_down,
    )


def reduce_kernel(
    heads, arr_a, arr_b, arr_c, keep_a, keep_b, keep_c, own_ref, got_ref, rhs_ref, tq_ref, tk_ref, tv_ref, attn_ref, mlp_ref, ogain_ref,
    misc_ref, rates_ref, edge_ref, rim_ref, again_ref,
    gate_out, up_out, down_out, out_out, outgate_out, q_out, k_out, v_out, tq_out, tk_out, tv_out, rest_out,
    edge_out,
    fetched, e_keep, e_send, e_got2, e_got3, e_got4,
    rhs_got, lhs_ref, l_first, l_send, l_keep, l_got1, l_got2, l_got3, l_got4, small_sum, small_got, rim_got,
    dp_sem, e_sem, l_sem, s_sem, f_sem,
):
    seq = lax.axis_index("seq")
    group = lax.axis_index("dp")
    count = lax.axis_size("seq")
    x, y, z = seq % 2, (seq // 2) % 2, seq // 4
    near = (seq + 1 - 2 * x, seq + 2 - 4 * y)
    low_z = seq + 4 - 8 * (z % 2)
    high_z = seq + 8 - 16 * (z // 2)

    def at(place):
        return {"dp": group, "seq": place}

    core = {"dp": 1 - group, "seq": seq}
    before, behind = lax.rem(seq + count - 1, count), lax.rem(seq + 1, count)

    def send(source, target, sems, index, device):
        return pltpu.make_async_remote_copy(
            src_ref=source,
            dst_ref=target,
            send_sem=sems.at[(0,) + index],
            recv_sem=sems.at[(1,) + index],
            device_id=device,
            device_id_type=MESH,
        )

    def fetches(i):
        return [
            pltpu.make_async_copy(source.at[i], fetched.at[j, i], f_sem.at[j, i])
            for j, source in enumerate((arr_a, arr_b, arr_c, keep_a, keep_b, keep_c))
        ]

    def fetch(i, carry):
        for copy in fetches(i):
            copy.start()
        return carry

    lax.fori_loop(0, JOBS, fetch, 0)
    barrier = pltpu.get_barrier_semaphore()
    everyone = [core] + [at(place) for place in (near[0], near[1], low_z, high_z, before, behind)]
    for device in everyone:
        pl.semaphore_signal(barrier, inc=1, device_id=device, device_id_type=MESH)
    pl.semaphore_wait(barrier, len(everyone))

    rim = send(rim_ref, rim_got, dp_sem, (1,), at(before))
    rim.start()
    hops = [core, at(high_z), at(low_z), at(near[0]), at(near[1])]

    def hop(step):
        return send(small_sum.at[step], small_got.at[step], s_sem, (step,), hops[step])

    def next_hop(step):
        hop(step - 1).wait_recv()
        small_sum[step] = small_sum[step - 1] + small_got[step - 1]
        if step < len(hops):
            hop(step).start()

    depth = tq_ref.shape[1]
    small_sum[0, 0:KW] = tq_ref[...]
    for half in range(2):
        lanes = pl.ds(half * depth, depth)
        small_sum[0, KW * (1 + half) : KW * (2 + half)] = tk_ref[:, lanes]
        small_sum[0, KW * (3 + half) : KW * (4 + half)] = tv_ref[:, lanes]
    small_sum[0, 5 * KW : 6 * KW] = jnp.zeros((KW, depth), F32)
    small_sum[0, 5 * KW : 5 * KW + 1] = attn_ref[...]
    small_sum[0, 5 * KW + 1 : 5 * KW + 2] = mlp_ref[...]
    gains = ogain_ref.shape[1]
    small_sum[0, 5 * KW + 2 : 5 * KW + 3, 0:gains] = ogain_ref[...]
    small_sum[0, 5 * KW + 2 : 5 * KW + 3, gains : gains + misc_ref.shape[1]] = misc_ref[...]
    small_sum[0, 6 * KW :] = rates_ref[...]
    hop(0).start()
    swap = send(rhs_ref, rhs_got, dp_sem, (0,), core)
    swap.start()

    places = (near[0], near[1], low_z, high_z)
    quarter = e_got2.shape[2]
    eighth, share = quarter // 2, quarter // 4

    def exchange(p, i, stage, sent, got, sems, links):
        begin = (0, 0, quarter, quarter + eighth)[stage]
        target = places[links[p][stage]]
        return send(sent.at[p, i, pl.ds(begin, got.shape[2])], got.at[p, i], sems, (p, i, stage), at(target))

    def early(p, i, stage):
        return exchange(p, i, stage, e_send, (None, e_got2, e_got3, e_got4)[stage], e_sem, EARLY_LINKS)

    def late(p, i, stage):
        sent = l_first if stage == 0 else l_send
        return exchange(p, i, stage, sent, (l_got1, l_got2, l_got3, l_got4)[stage], l_sem, LATE_LINKS)

    def early2(i, carry):
        for copy in fetches(i):
            copy.wait()
        for p in range(GROUPS):
            total = fetched[p, i].astype(F32) + fetched[GROUPS + p, i].astype(F32)
            e_keep[p, i] = total[:quarter].astype(BF16)
            e_send[p, i, 0:quarter] = total[quarter:].astype(BF16)
            early(p, i, 1).start()
        return carry

    def onward(p, i, copy_of, keep, sent, got, stage, begin):
        copy_of(p, i, stage).wait_recv()
        rows = got.shape[2]
        half = rows // 2
        total = keep[p, i, 0:rows].astype(F32) + got[p, i].astype(F32)
        keep[p, i, 0:half] = total[:half].astype(BF16)
        sent[p, i, begin : begin + half] = total[half:].astype(BF16)
        copy_of(p, i, stage + 1).start()

    def later(i, carry, copy_of, keep, sent, got, stage, begin):
        for p in range(keep.shape[0]):
            onward(p, i, copy_of, keep, sent, got, stage, begin)
        return carry

    for p in range(2):
        for side, lhs in enumerate((own_ref, got_ref)):
            for sending in range(2):
                lhs_ref[p, side, sending] = half_rows(lhs[...], LATE_LINKS[p], sending)
    next_hop(1)
    lax.fori_loop(0, JOBS, early2, 0)
    next_hop(2)
    swap.wait_recv()
    job = l_got1.shape[-1]
    late_jobs = LATE_JOBS // 2
    tokens = rhs_ref.shape[0]

    def product(m, p, sending):
        lanes = pl.ds(pl.multiple_of(m * job, job), job)
        total = mm(lhs_ref[p, 0, int(sending)], rhs_ref[:, lanes]) + mm(
            lhs_ref[p, 1, int(sending)], rhs_got[:, lanes]
        )
        return total[:quarter], total[quarter:]

    def late1(i, carry):
        for p in range(2):
            low, high = product(2 * i + p, p, True)
            l_first[p, i, 0:quarter] = low.astype(BF16)
            l_first[p, i, quarter : 2 * quarter] = high.astype(BF16)
            late(p, i, 0).start()
        return carry

    def late2(i, carry):
        for p in range(2):
            low, high = product(2 * i + p, p, False)
            late(p, i, 0).wait_recv()
            l_keep[p, i] = (low + l_got1[p, i, 0:quarter].astype(F32)).astype(BF16)
            l_send[p, i, 0:quarter] = (high + l_got1[p, i, quarter : 2 * quarter].astype(F32)).astype(BF16)
            late(p, i, 1).start()
        return carry

    lag = JOBS - late_jobs

    def low_turn(i, carry):
        later(i, carry, early, e_keep, e_send, e_got2, 1, quarter)

        @pl.when(i >= lag)
        def _():
            late1(i - lag, carry)

        return carry

    def high_turn(i, carry):
        later(i, carry, early, e_keep, e_send, e_got3, 2, quarter + eighth)

        @pl.when(i >= lag)
        def _():
            late2(i - lag, carry)

        return carry

    lax.fori_loop(0, JOBS, low_turn, 0)
    next_hop(3)
    lax.fori_loop(0, JOBS, high_turn, 0)
    next_hop(4)
    rim.wait_recv()
    inside = (seq < count - 1).astype(F32)
    _, pulled = norm_pull(edge_ref[1], again_ref[...], edge_ref[0] + inside * rim_got[...])
    edge_out[...] = (edge_ref[2] + pulled).astype(BF16)
    late_low = partial(later, copy_of=late, keep=l_keep, sent=l_send, got=l_got2, stage=1, begin=quarter)
    lax.fori_loop(0, late_jobs, late_low, 0)
    next_hop(5)
    late_high = partial(later, copy_of=late, keep=l_keep, sent=l_send, got=l_got3, stage=2, begin=quarter + eighth)
    lax.fori_loop(0, late_jobs, late_high, 0)
    early_outs = (gate_out, up_out, down_out, out_out, outgate_out)
    for i in range(JOBS):
        for p in range(GROUPS):
            early(p, i, 3).wait_recv()
            total = e_keep[p, i, 0:share].astype(F32) + e_got4[p, i].astype(F32)
            first = (p * JOBS + i) * JOB
            for output, to, begin, width in column_pieces([o.shape[1] for o in early_outs], first, first + JOB):
                early_outs[output][:, to : to + width] = total[:, begin : begin + width]
    tq_out[...] = small_sum[5, 0:KW]
    for half in range(2):
        lanes = pl.ds(half * depth, depth)
        tk_out[:, lanes] = small_sum[5, KW * (1 + half) : KW * (2 + half)]
        tv_out[:, lanes] = small_sum[5, KW * (3 + half) : KW * (4 + half)]
    rest_out[...] = small_sum[5, 5 * KW :]
    width = q_out.shape[1] // heads
    for i in range(late_jobs):
        for p in range(2):
            late(p, i, 3).wait_recv()
            total = l_keep[p, i, 0:share].astype(F32) + l_got4[p, i].astype(F32)
            for begin in range(0, job, width):
                head, part = divmod(((2 * i + p) * job + begin) // width, 5)
                if part == 0:
                    target, to = q_out, head * width
                else:
                    target, to = (k_out, v_out)[(part - 1) // 2], (2 * head + (part - 1) % 2) * width
                target[:, to : to + width] = total[:, begin : begin + width]

    def early_sent(i, carry):
        for p in range(GROUPS):
            for stage in (1, 2, 3):
                early(p, i, stage).wait_send()
        return carry

    def late_sent(i, carry):
        for p in range(2):
            for stage in (0, 1, 2, 3):
                late(p, i, stage).wait_send()
        return carry

    lax.fori_loop(0, JOBS, early_sent, 0)
    lax.fori_loop(0, late_jobs, late_sent, 0)
    swap.wait_send()
    rim.wait_send()
    for step in range(len(hops)):
        hop(step).wait_send()


def reduce_all(arrived, kept, own, got, rhs, taps, gains, rates, edge, rim, gain, ff, heads):
    half = own.shape[0] // 2
    quarter, eighth, share = half // 2, half // 4, half // 8
    count = LATE_JOBS // 2
    columns = rhs.shape[1] // 5
    job = rhs.shape[1] // LATE_JOBS
    depth = rates.shape[1]
    small_rows = 6 * KW + rates.shape[0]
    out = jax.ShapeDtypeStruct
    vmem = pl.BlockSpec(memory_space=pltpu.VMEM)

    def stages(groups, jobs, width):
        return [((groups, jobs, rows, width), BF16) for rows in (quarter, eighth, share)]

    buffers = [((2 * GROUPS, JOBS, half, JOB), BF16)]
    buffers += [((GROUPS, JOBS, quarter, JOB), BF16), ((GROUPS, JOBS, half, JOB), BF16)]
    buffers += stages(GROUPS, JOBS, JOB)
    buffers += [(rhs.shape, BF16), ((2, 2, 2, half, own.shape[1]), BF16)] + [((2, count, half, job), BF16)] * 2 + [((2, count, quarter, job), BF16)]
    buffers += [((2, count, half, job), BF16)] + stages(2, count, job)
    buffers += [((6, small_rows, depth), F32), ((5, small_rows, depth), F32), (rim.shape, F32)]
    dma = pltpu.SemaphoreType.DMA
    shapes = [(share, ff)] * 3 + [(share, columns)] * 3 + [(share, 2 * columns)] * 2
    shapes += [tap.shape for tap in taps] + [(small_rows - 5 * KW, depth)]
    return pl.pallas_call(
        partial(reduce_kernel, heads),
        in_specs=[pl.BlockSpec(memory_space=pl.ANY)] * (2 * GROUPS) + [vmem] * 14,
        out_specs=[vmem] * 13,
        out_shape=[out(shape, F32) for shape in shapes] + [out(rim.shape, BF16)],
        scratch_shapes=[pltpu.VMEM(shape, kind) for shape, kind in buffers]
        + [dma((2, 2)), dma((2, GROUPS, JOBS, 4)), dma((2, 2, count, 4)), dma((2, 5)), dma((2 * GROUPS, JOBS))],
        compiler_params=pltpu.CompilerParams(
            collective_id=2, has_side_effects=True, vmem_limit_bytes=VMEM_LIMIT
        ),
        cost_estimate=cost(90),
        name="reduce_all",
    )(*arrived, *kept, own, got, rhs, *taps, *gains, rates, edge, rim, gain)


def finish_kernel(marks, grad_ref, edge_ref, rest_ref, *refs):
    count = (len(refs) - 8) // 2
    sources, (grad_out, *outs) = refs[:count], refs[count:]
    rows = grad_ref.shape[0]
    grad_out[0 : rows - HALO, :] = grad_ref[0 : rows - HALO, :]
    grad_out[rows - HALO :, :] = edge_ref[...]
    for source, target in zip(sources, outs):
        target[...] = source[...]
    again, mlp, beta, rate, gain, bias, decay = outs[count:]
    rest = rest_ref[...]
    share, depth = again.shape[1], rest.shape[1]
    place = lax.axis_index("dp") * lax.axis_size("seq") + lax.axis_index("seq")
    own = pltpu.roll(rest, lax.rem(depth - place * share, depth), 1)[:, :share]
    again[...] = own[0:1]
    mlp[...] = own[1:2]
    beta[...] = own[4 : 4 + beta.shape[0]]
    rate[...] = own[4 + beta.shape[0] :]
    for target, begin in zip((gain, bias, decay), marks):
        target[...] = rest_ref[2:3, begin : begin + target.shape[1]]


def finish(input_grad, edge_grad, rest, values, share, width, heads):
    wide, narrow = heads * REFLECTS, heads
    shapes = [value.shape for value in values]
    shapes += [(1, share)] * 2 + [(wide, share), (narrow, share), (1, width), (1, wide), (1, narrow)]
    out = jax.ShapeDtypeStruct
    vmem = pl.BlockSpec(memory_space=pltpu.VMEM)
    return pl.pallas_call(
        partial(finish_kernel, (0, width, width + wide)),
        in_specs=[vmem] * (3 + len(values)),
        out_specs=[vmem] * (1 + len(shapes)),
        out_shape=[out(input_grad.shape, BF16)] + [out(shape, F32) for shape in shapes],
        compiler_params=pltpu.CompilerParams(vmem_limit_bytes=VMEM_LIMIT),
        cost_estimate=cost(3),
        name="finish",
    )(input_grad, edge_grad, rest, *values)


def dot32(a, b, dims=NN):
    return lax.dot_general(a, b, dims, preferred_element_type=F32)


def swap_core(value):
    count = lax.axis_size("dp")
    return lax.ppermute(value, "dp", [(i, (i + 1) % count) for i in range(count)])


def neighbour_route(bit):
    return [(i, i ^ bit) for i in range(16)]


def by_head(field, heads, begin, size):
    rows = field.shape[0]
    return field.reshape(rows, heads, -1)[:, :, begin : begin + size].reshape(rows, heads * size)


def per_device(
    block_input, lengths, attn_gain, w_query, w_key, w_value, w_outgate, w_beta, w_decay, beta_bias,
    decay_rate, conv_query, conv_key, conv_value, out_gain, w_out, mlp_gain, w_gate, w_up, w_down,
    out_grad,
):
    rows, depth = block_input.shape
    heads = decay_rate.shape[0]
    width = out_gain.shape[0]
    count = lax.axis_size("seq")
    seq = lax.axis_index("seq")
    group = lax.axis_index("dp")
    compact = count == 16
    wide = heads * REFLECTS
    ext_b, raw, live, acol, arow, halo, w_rates, rate = rates_forward(
        lengths, block_input, attn_gain, w_beta, w_decay, beta_bias, decay_rate, heads
    )
    taps = (conv_query, conv_key, conv_value)
    pre, gate_pre, oloc, oread, *saved, maps = mixer_forward(
        ext_b, w_query, w_key, w_value, w_outgate, taps, live, acol, arow, heads, width
    )
    start, all_maps = carry_states(maps, None, count)
    block_output, d_out, part, d_resid, grad_mlp_gain, grad_out_gain, *rest = middle(
        compact, count, oloc, oread, start, gate_pre, out_gain, block_input, ext_b, mlp_gain, out_grad,
        all_maps, w_out, w_gate, w_up, w_down,
    )
    if compact:
        products, (own_l, got_l, after, d_outgate_b) = rest[: 2 * GROUPS], rest[2 * GROUPS :]
        arrived = [
            lax.ppermute(sent, "seq", neighbour_route(1 << links[0])) for sent, links in zip(products[::2], EARLY_LINKS)
        ]
    else:
        gated_b, hidden_b, d_gate_b, d_up_b, d_outgate_b, mlp_b, d_branch_b = rest
        after = carry_states(part, all_maps, count)
    d_all, d_tap_q, d_tap_k, d_tap_v, aux = mixer_backward(
        pre, taps, live, acol, arow, saved, start, after, d_out
    )
    input_grad, edge, rim, grad_attn_gain, grad_rates, misc = input_pull(
        d_all, d_outgate_b, (w_query, w_key, w_value, w_outgate), aux, raw, live, rate, w_rates, ext_b,
        block_input, halo, attn_gain, d_resid, heads,
    )
    last = width + wide + heads
    gains = (grad_attn_gain, grad_mlp_gain, grad_out_gain, misc)
    d_taps = (d_tap_q, d_tap_k, d_tap_v)
    devices = count * lax.axis_size("dp")
    share = depth // devices
    if compact:
        sums = reduce_all(
            arrived, products[1::2], own_l, got_l, d_all, d_taps, gains, grad_rates,
            edge, rim, attn_gain[None, :], w_gate.shape[1], heads,
        )
        trunk, taps_out, rest, edge_grad = sums[5:8], sums[8:11], sums[11], sums[12]
    else:
        normed_e = jnp.concatenate([ext_b[HALO:], ext_b[:HALO]], axis=0)
        normed_b = ext_b[HALO:]
        xf = block_input.astype(F32)
        tail = edge[0] + lax.ppermute(rim, "seq", [(i, i - 1) for i in range(1, count)])
        _, pulled = norm_pull(edge[1], attn_gain[None, :], tail)
        edge_grad = (edge[2] + pulled).astype(BF16)
        line = jnp.pad(jnp.concatenate(gains[2:], axis=1), ((0, 0), (0, depth - width - 128)))
        line = jnp.concatenate([*gains[:2], line, jnp.zeros((1, depth), F32)], axis=0)
        small = lax.psum(d_taps + (line, grad_rates), ("dp", "seq"))
        taps_out, rest = small[:3], jnp.concatenate(small[3:], axis=0)
        trunk = [by_head(d_all, heads, begin * width, size * width) for begin, size in ((0, 1), (1, 2), (3, 2))]
        pairs = zip(
            (mlp_b, mlp_b, out_grad, d_branch_b, normed_b) + (normed_e,) * 3, (d_gate_b, d_up_b, hidden_b, gated_b, d_outgate_b) + tuple(trunk)
        )
        sums = [
            lax.psum_scatter(dot32(lhs, rhs, TN), ("dp", "seq"), scatter_dimension=0, tiled=True)
            for lhs, rhs in pairs
        ]
        trunk = sums[5:]
    values = (*trunk, sums[4], *taps_out, sums[0], sums[1], sums[3], sums[2])
    done = finish(input_grad, edge_grad, rest, values, share, width, heads)
    (
        input_grad, g_query, g_key, g_value, g_outgate, g_conv_q, g_conv_k, g_conv_v, g_gate, g_up, g_out, g_down,
        g_attn, g_mlp, g_beta, g_decay, g_gain, g_bias, g_rate,
    ) = done
    return (
        block_output,
        input_grad,
        g_attn[0],
        g_query,
        g_key,
        g_value,
        g_outgate,
        g_beta.T,
        g_decay.T,
        g_bias[0],
        g_rate[0],
        g_conv_q,
        g_conv_k,
        g_conv_v,
        g_gain[0],
        g_out.T,
        g_mlp[0],
        g_gate,
        g_up,
        g_down.T,
    )


def solution(mesh):
    tokens = P(("dp", "seq"), None)
    column = P(None, ("dp", "seq"))
    vector = P(("dp", "seq"))
    in_specs = (tokens, P("dp", None)) + (P(),) * 18 + (tokens,)
    out_specs = (
        (tokens, tokens, vector)
        + (tokens,) * 6
        + (P(),) * 6
        + (column, vector, tokens, tokens, column)
    )
    return jax.shard_map(
        per_device, mesh=mesh, in_specs=in_specs, out_specs=out_specs, check_vma=False
    )
```

```python
from functools import partial

import jax
import jax.numpy as jnp
from jax import lax
from jax.experimental import pallas as pl
from jax.experimental.pallas import tpu as pltpu
from jax.sharding import PartitionSpec as P

REFLECTS = 2
KW = 4
BLOCK = 64
SHORTEST = 1024
STEPS = BLOCK * REFLECTS
HALO = 8
RESET_LOG = -80.0
MESH = pl.DeviceIdType.MESH
F32 = jnp.float32
BF16 = jnp.bfloat16
NN = (((1,), (0,)), ((), ()))
NT = (((1,), (1,)), ((), ()))
TN = (((0,), (0,)), ((), ()))
VMEM_LIMIT = 56 * 1024 * 1024
FORWARD_HEADS = 2
BACKWARD_HEADS = 2


def cost(microseconds):
    return pl.CostEstimate(
        flops=int(microseconds * 1e9), bytes_accessed=int(microseconds * 1e6), transcendentals=0
    )


def mm(a, b, dims=NN):
    return lax.dot_general(a.astype(BF16), b.astype(BF16), dims, preferred_element_type=F32)


def halves(a):
    high = a.astype(BF16)
    return high, (a - high.astype(F32)).astype(BF16)


def mm3(a, b):
    ah, al = halves(a)
    bh, bl = halves(b)
    return mm(jnp.concatenate([ah, al], axis=1), jnp.concatenate([bh, bh], axis=0)) + mm(ah, bl)


def mm2(a, b, dims=NN):
    ah, al = halves(a)
    return mm(ah, b, dims) + mm(al, b, dims)


def mm2t(a, b, dims=NN):
    bh, bl = halves(b)
    return mm(a, bh, dims) + mm(a, bl, dims)


def sigmoid(v):
    return 1.0 / (1.0 + jnp.exp(-v))


def step_ids(shape, axis):
    index = lax.broadcasted_iota(jnp.int32, shape, axis)
    return index % BLOCK, index // BLOCK


def step_masks():
    shape = (STEPS, STEPS)
    tm, jm = step_ids(shape, 0)
    tn, jn = step_ids(shape, 1)
    strict = (tm > tn) | ((tm == tn) & (jm > jn))
    size = 4
    first = tm // size == tn // size
    merges = []
    while size < BLOCK:
        merges.append((tm // (2 * size) == tn // (2 * size)) & (tm // size != tn // size))
        size = 2 * size
    eye = ((tm == tn) & (jm == jn)).astype(F32)
    return tm >= tn, strict, first, merges, eye


def unit_lower_inverse(systems, first, merges, eye):
    neg = [jnp.where(first, -a, 0.0) for a in systems]
    inv = [eye + n for n in neg]
    for _ in range(2):
        neg = [mm3(n, n) for n in neg]
        inv = [t + mm3(t, n) for t, n in zip(inv, neg)]
    for merge in merges:
        off = [mm3(jnp.where(merge, a, 0.0), t) for a, t in zip(systems, inv)]
        inv = [t - mm3(t, o) for t, o in zip(inv, off)]
    return inv


def conv_parts(ext_ref, taps, live, columns, rows):
    total = None
    for back in range(KW):
        part = ext_ref[pl.ds(HALO - back, rows), columns] * taps[KW - 1 - back : KW - back, :]
        if back > 0:
            part = part * live[:, back : back + 1]
        total = part if total is None else total + part
    return total


def head_features(ext_ref, tq, tk, tv, live, rows, width):
    conv = [
        conv_parts(ext_ref, tq, live, pl.ds(0, width), rows),
        conv_parts(ext_ref, tk[:, :width], live, pl.ds(width, width), rows),
        conv_parts(ext_ref, tk[:, width:], live, pl.ds(2 * width, width), rows),
        conv_parts(ext_ref, tv[:, :width], live, pl.ds(3 * width, width), rows),
        conv_parts(ext_ref, tv[:, width:], live, pl.ds(4 * width, width), rows),
    ]
    return conv


def unit_rows(act):
    return lax.rsqrt(jnp.sum(act * act, axis=-1, keepdims=True) + 1e-06)


def greet_group(count):
    place, group = lax.axis_index("seq"), lax.axis_index("dp")
    barrier = pltpu.get_barrier_semaphore()

    def greet(step, carry):
        peer = lax.rem(place + step, count)
        pl.semaphore_signal(barrier, inc=1, device_id=(group, peer), device_id_type=MESH)
        return carry

    lax.fori_loop(1, count, greet, 0)
    return barrier


def carry_steps(count, heads, backward, part_ref, maps_ref, inbox, outbox, landed, sems):
    send_sem, recv_sem, back_sem, land_sem = sems
    place, group = lax.axis_index("seq"), lax.axis_index("dp")
    width = landed.shape[-1]
    stride = count // 16

    def keeper(h):
        return (2 * h + group) * stride

    def outgoing(h):
        return pltpu.make_async_remote_copy(
            src_ref=part_ref.at[h],
            dst_ref=inbox.at[place],
            send_sem=send_sem.at[h],
            recv_sem=recv_sem.at[place],
            device_id=(group, keeper(h)),
            device_id_type=MESH,
        )

    def send(h):
        @pl.when(place != keeper(h))
        def _():
            outgoing(h).start()

        @pl.when(place == keeper(h))
        def _():
            inbox[pl.ds(place, 1)] = part_ref[pl.ds(h, 1)]

    def scan_head(h):
        def returning(where):
            return pltpu.make_async_remote_copy(
                src_ref=outbox.at[where],
                dst_ref=landed.at[h],
                send_sem=back_sem.at[where],
                recv_sem=land_sem.at[h],
                device_id=(group, where),
                device_id_type=MESH,
            )

        def lap(step, state):
            where = count - 1 - step if backward else step
            outbox[pl.ds(where, 1)] = state[None].astype(BF16)

            @pl.when(where != place)
            def _():
                returning(where).start()
                pltpu.make_async_remote_copy(
                    src_ref=part_ref.at[h],
                    dst_ref=inbox.at[where],
                    send_sem=send_sem.at[h],
                    recv_sem=recv_sem.at[where],
                    device_id=(group, where),
                    device_id_type=MESH,
                ).wait_recv()

            @pl.when(where == place)
            def _():
                landed[h : h + 1] = outbox[pl.ds(where, 1)]

            got = inbox[pl.ds(where, 1)][0]
            high, low = halves(state)
            both = jnp.concatenate([high, low], axis=1)
            if backward:
                moved = mm(maps_ref[pl.ds(where, 1)][0][:, width:], both, TN)
            else:
                moved = mm(got[:, width:], both)
            return moved[:, :width] + moved[:, width:] + got[:, :width].astype(F32)

        lax.fori_loop(0, count, lap, jnp.zeros((width, width), F32))

        def finish(where, carry):
            @pl.when(where != place)
            def _():
                returning(where).wait_send()

            return carry

        return lambda: lax.fori_loop(0, count, finish, 0)

    def scan():
        for h in range(heads):

            @pl.when(place == keeper(h))
            def _(h=h):
                scan_head(h)()

    def take():
        for h in range(heads):

            @pl.when(place != keeper(h))
            def _(h=h):
                outgoing(h).wait_send()
                pltpu.make_async_remote_copy(
                    src_ref=outbox.at[0],
                    dst_ref=landed.at[h],
                    send_sem=back_sem.at[0],
                    recv_sem=land_sem.at[h],
                    device_id=(group, keeper(h)),
                    device_id_type=MESH,
                ).wait_recv()

    return send, scan, take


def carry_scratch(count, heads, width, columns):
    dma = pltpu.SemaphoreType.DMA
    return [
        pltpu.VMEM((count, width, columns), BF16),
        pltpu.VMEM((count, width, width), BF16),
        pltpu.VMEM((heads, width, width), BF16),
        dma((heads,)),
        dma((count,)),
        dma((count,)),
        dma((heads,)),
    ]


def mixer_forward_kernel(
    count, every_head, xn_ref, wq_ref, wk_ref, wv_ref, wg_ref, tq_ref, tk_ref, tv_ref, live_ref, acol_ref, arow_ref,
    pre_ref, gate_ref, oloc_ref, oread_ref, inv_ref, delta_ref, state_ref, turn_ref, carry_ref, start_ref, maps_ref,
    ext_ref, part_ref, inbox, outbox, landed, *sems,
):
    heads, rows, width = oread_ref.shape
    turn_at = pl.program_id(0)
    barrier = pltpu.get_barrier_semaphore()

    @pl.when(turn_at == 0)
    def _():
        greet_group(count)

    give, scan, take = carry_steps(count, every_head, False, part_ref, None, inbox, outbox, landed, sems)
    blocks = rows // BLOCK
    xn = xn_ref[...]
    live = live_ref[...]
    gate_ref[...] = mm(xn[HALO:], wg_ref[...])
    query, key, value = mm(xn, wq_ref[...]), mm(xn, wk_ref[...]), mm(xn, wv_ref[...])
    reach, strict, first, merges, eye = step_masks()
    cut = [slice(b * BLOCK, (b + 1) * BLOCK) for b in range(blocks)]
    every = [(n, b) for n in range(heads) for b in range(blocks)]
    qb, kb, vb = {}, {}, {}
    for n in range(heads):
        one, two = slice(n * width, (n + 1) * width), slice(2 * n * width, 2 * (n + 1) * width)
        pre = jnp.concatenate([query[:, one], key[:, two], value[:, two]], axis=1).astype(BF16)
        pre_ref[n] = pre
        ext_ref[n] = pre.astype(F32)
        conv = head_features(ext_ref.at[n], tq_ref[:, one], tk_ref[:, two], tv_ref[:, two], live, rows, width)
        act = [c * sigmoid(c) for c in conv]
        q = (act[0] * unit_rows(act[0]) * width ** (-0.5)).astype(BF16)
        k = [(a * unit_rows(a)).astype(BF16) for a in act[1:3]]
        v = [a.astype(BF16) for a in act[3:5]]
        for b in range(blocks):
            qb[n, b] = q[cut[b]]
            kb[n, b] = jnp.concatenate([k[0][cut[b]], k[1][cut[b]]], axis=0)
            vb[n, b] = jnp.concatenate([v[0][cut[b]], v[1][cut[b]]], axis=0)
    ccol = {at: acol_ref[at[0], at[1], :, 0:1] for at in every}
    bcol = {at: acol_ref[at[0], at[1], :, 1:2] for at in every}
    crow = {at: arow_ref[at[0], at[1], 0:1, :] for at in every}
    brow = {at: arow_ref[at[0], at[1], 1:2, :] for at in every}
    fade = {at: jnp.exp(jnp.where(reach, ccol[at] - crow[at], -1e30)) for at in every}
    system = [jnp.where(strict, fade[at] * mm(kb[at], kb[at], NT), 0.0) * bcol[at] for at in every]
    inv = dict(zip(every, unit_lower_inverse(system, first, merges, eye)))
    for at in every:
        inv_ref[at[0], at[1]] = inv[at].astype(BF16)
    local = {at: mm2(inv[at] * brow[at], vb[at]) for at in every}
    reads = {at: mm2(inv[at] * (brow[at] * jnp.exp(crow[at])), kb[at]) for at in every}
    score = {at: fade[at][:BLOCK] * mm(qb[at], kb[at], NT) for at in every}
    grow = {at: jnp.exp(ccol[at]) for at in every}
    last = {at: ccol[at][BLOCK - 1 : BLOCK] for at in every}
    tail = {at: kb[at].astype(F32) * jnp.exp(last[at] - ccol[at]) for at in every}
    both = {at: jnp.concatenate([local[at], -reads[at]], axis=1).astype(BF16) for at in every}
    turn = {at: mm(tail[at], both[at], TN) for at in every}
    query_out = {at: mm(score[at], both[at]) for at in every}
    state = {}
    for n in range(heads):
        now = jnp.concatenate([jnp.zeros((width, width), F32), eye], axis=1)
        for b in range(blocks):
            at = (n, b)
            state[at] = now
            step = turn[at][:, width:].astype(BF16)
            turn_ref[n, b] = step
            fixed = jnp.concatenate([turn[at][:, :width], jnp.zeros((width, width), F32)], axis=1)
            now = jnp.exp(last[at]) * now + fixed + mm(step, now)
        part_ref[pl.ds(turn_at * heads + n, 1)] = now.astype(BF16)[None]
    for at in every:
        n, b = at
        carried = query_out[at][:, width:] + grow[at][:BLOCK] * qb[at].astype(F32)
        low = state[at].astype(BF16)
        carry_ref[n, b] = carried.astype(BF16)
        state_ref[n, b] = low
        fixed = jnp.concatenate([local[at], jnp.zeros((STEPS, width), F32)], axis=1)
        delta_ref[n, b] = (fixed - mm(reads[at], low)).astype(BF16)
        out = mm(carried, low)
        oloc_ref[cut[b], n * width : (n + 1) * width] = out[:, :width] + query_out[at][:, :width]
        oread_ref[n, cut[b], :] = out[:, width:].astype(BF16)

    @pl.when(turn_at == 0)
    def _():
        pl.semaphore_wait(barrier, count - 1)

    for n in range(heads):
        give(turn_at * heads + n)

    @pl.when(turn_at == pl.num_programs(0) - 1)
    def _():
        scan()
        take()
        start_ref[...] = landed[...]
        maps_ref[...] = inbox[...]


def head_columns(rows, width):
    return pl.BlockSpec((rows, width), lambda h: (0, h))


def whole(shape):
    return pl.BlockSpec(shape, lambda h: (0,) * len(shape))


def per_head(shape, group=1):
    return pl.BlockSpec((group,) + shape, lambda h: (h,) + (0,) * len(shape))


def mixer_forward(xn, w_query, w_key, w_value, w_outgate, taps, live, acol, arow, heads, width, count):
    ext_rows, depth = xn.shape
    rows = ext_rows - HALO
    blocks = rows // BLOCK
    conv_query, conv_key, conv_value = taps
    out = jax.ShapeDtypeStruct
    return pl.pallas_call(
        partial(mixer_forward_kernel, count, heads),
        grid=(heads // FORWARD_HEADS,),
        in_specs=[
            whole((ext_rows, depth)),
            head_columns(depth, FORWARD_HEADS * width),
            head_columns(depth, 2 * FORWARD_HEADS * width),
            head_columns(depth, 2 * FORWARD_HEADS * width),
            head_columns(depth, FORWARD_HEADS * width),
            head_columns(KW, FORWARD_HEADS * width),
            head_columns(KW, 2 * FORWARD_HEADS * width),
            head_columns(KW, 2 * FORWARD_HEADS * width),
            whole(live.shape),
            per_head(acol.shape[1:], FORWARD_HEADS),
            per_head(arow.shape[1:], FORWARD_HEADS),
        ],
        out_specs=[
            per_head((ext_rows, 5 * width), FORWARD_HEADS),
            head_columns(rows, FORWARD_HEADS * width),
            head_columns(rows, FORWARD_HEADS * width),
            per_head((rows, width), FORWARD_HEADS),
            per_head((blocks, STEPS, STEPS), FORWARD_HEADS),
            per_head((blocks, STEPS, 2 * width), FORWARD_HEADS),
            per_head((blocks, width, 2 * width), FORWARD_HEADS),
            per_head((blocks, width, width), FORWARD_HEADS),
            per_head((blocks, BLOCK, width), FORWARD_HEADS),
            whole((heads, width, width)),
            whole((count, width, 2 * width)),
        ],
        out_shape=[
            out((heads, ext_rows, 5 * width), BF16),
            out((rows, heads * width), F32),
            out((rows, heads * width), F32),
            out((heads, rows, width), BF16),
            out((heads, blocks, STEPS, STEPS), BF16),
            out((heads, blocks, STEPS, 2 * width), BF16),
            out((heads, blocks, width, 2 * width), BF16),
            out((heads, blocks, width, width), BF16),
            out((heads, blocks, BLOCK, width), BF16),
            out((heads, width, width), BF16),
            out((count, width, 2 * width), BF16),
        ],
        scratch_shapes=[
            pltpu.VMEM((FORWARD_HEADS, ext_rows, 5 * width), F32),
            pltpu.VMEM((heads, width, 2 * width), BF16),
        ]
        + carry_scratch(count, heads, width, 2 * width),
        compiler_params=pltpu.CompilerParams(
            collective_id=0, has_side_effects=True, vmem_limit_bytes=VMEM_LIMIT
        ),
        cost_estimate=cost(40),
        name="mixer_forward",
    )(xn, w_query, w_key, w_value, w_outgate, conv_query, conv_key, conv_value, live, acol, arow)


def conv_pull(ext_ref, pad_ref, d_conv, taps, live, columns, rows, dtap_ref):
    total = None
    for back in range(KW):
        part = d_conv if back == 0 else d_conv * live[:, back : back + 1]
        source = ext_ref[pl.ds(HALO - back, rows), columns]
        dtap_ref[KW - 1 - back : KW - back, :] = jnp.sum(part * source, axis=0, keepdims=True)
        pad_ref[pl.ds(HALO, rows), :] = part
        moved = pad_ref[pl.ds(back, rows + HALO), :] * taps[KW - 1 - back : KW - back, :]
        total = moved if total is None else total + moved
    return total


def silu_pull(c, grad):
    s = sigmoid(c)
    return grad * (s + c * s * (1.0 - s))


def unit_pull(act, grad, scale):
    r = unit_rows(act)
    return scale * r * (grad - act * (r * r * jnp.sum(act * grad, axis=-1, keepdims=True)))


def mixer_backward_kernel(
    pre_ref, tq_ref, tk_ref, tv_ref, live_ref, acol_ref, arow_ref,
    inv_ref, delta_ref, state_ref, turn_ref, carry_ref, start_ref, after_ref, dout_ref,
    d_ref, dtq_ref, dtk_ref, dtv_ref, aux_ref,
    ext_ref, pad_ref,
):
    heads = pre_ref.shape[0]
    rows = dout_ref.shape[0]
    width = start_ref.shape[-1]
    blocks = rows // BLOCK
    live = live_ref[...]
    every = [(n, b) for n in range(heads) for b in range(blocks)]
    cut = [slice(b * BLOCK, (b + 1) * BLOCK) for b in range(blocks)]
    conv, act, qb, kb, dout = {}, {}, {}, {}, {}
    for n in range(heads):
        one, two = slice(n * width, (n + 1) * width), slice(2 * n * width, 2 * (n + 1) * width)
        ext_ref[n] = pre_ref[n].astype(F32)
        conv[n] = head_features(ext_ref.at[n], tq_ref[:, one], tk_ref[:, two], tv_ref[:, two], live, rows, width)
        act[n] = [c * sigmoid(c) for c in conv[n][:3]]
        q = (act[n][0] * unit_rows(act[n][0]) * width ** (-0.5)).astype(BF16)
        k = [(a * unit_rows(a)).astype(BF16) for a in act[n][1:]]
        for b in range(blocks):
            qb[n, b] = q[cut[b]]
            kb[n, b] = jnp.concatenate([k[0][cut[b]], k[1][cut[b]]], axis=0)
            dout[n, b] = dout_ref[cut[b], one]
    reach, strict, _, _, _ = step_masks()
    ccol = {at: acol_ref[at[0], at[1], :, 0:1] for at in every}
    bcol = {at: acol_ref[at[0], at[1], :, 1:2] for at in every}
    crow = {at: arow_ref[at[0], at[1], 0:1, :] for at in every}
    last = {at: ccol[at][BLOCK - 1 : BLOCK] for at in every}
    grow = {at: jnp.exp(ccol[at]) for at in every}
    weight = {at: jnp.exp(last[at] - ccol[at]) for at in every}
    ahead = {at: mm(carry_ref[at[0], at[1]], dout[at], TN) for at in every}
    after = {}
    for n in range(heads):
        now = after_ref[n].astype(F32)
        for b in range(blocks - 1, -1, -1):
            after[n, b] = now
            now = jnp.exp(last[n, b]) * now + ahead[n, b] + mm(turn_ref[n, b], now, TN)
    fade = {at: jnp.exp(jnp.where(reach, ccol[at] - crow[at], -1e30)) for at in every}
    delta = {
        at: delta_ref[at[0], at[1], :, :width].astype(F32) + mm(delta_ref[at[0], at[1], :, width:], start_ref[at[0]])
        for at in every
    }
    state = {
        at: state_ref[at[0], at[1], :, :width].astype(F32) + mm(state_ref[at[0], at[1], :, width:], start_ref[at[0]])
        for at in every
    }
    score = {at: fade[at][:BLOCK] * mm(qb[at], kb[at], NT) for at in every}
    d_delta = {at: mm(score[at], dout[at], TN) + weight[at] * mm2t(kb[at], after[at]) for at in every}
    d_rhs = {at: mm2t(inv_ref[at[0], at[1]], d_delta[at], TN) for at in every}
    d_score = {at: (fade[at][:BLOCK] * mm(dout[at], delta[at], NT)).astype(BF16) for at in every}
    d_tail = {at: weight[at] * mm(delta[at], after[at], NT) for at in every}
    d_gram = {
        at: jnp.where(strict, -bcol[at] * fade[at] * mm(d_rhs[at], delta[at], NT), 0.0).astype(BF16) for at in every
    }
    dq = {at: mm(grow[at][:BLOCK] * dout[at], state[at], NT) + mm(d_score[at], kb[at]) for at in every}
    dk_row = {
        at: mm(-(bcol[at] * grow[at]) * d_rhs[at], state[at], NT) + mm(d_gram[at], kb[at]) for at in every
    }
    dk_col = {at: mm(d_gram[at], kb[at], TN) + mm(d_score[at], qb[at], TN) + d_tail[at] for at in every}
    tok = lax.broadcasted_iota(jnp.int32, (BLOCK, 1), 0)
    for at in every:
        kf = kb[at].astype(F32)
        d_beta = (1.0 - bcol[at]) * jnp.sum(d_rhs[at] * delta[at], axis=-1, keepdims=True)
        d_log = jnp.sum(kf * (dk_row[at] - dk_col[at]), axis=-1, keepdims=True)
        d_logq = jnp.sum(qb[at].astype(F32) * dq[at], axis=-1, keepdims=True)
        d_last = jnp.sum(kf * d_tail[at]) + jnp.sum(jnp.exp(last[at]) * after[at] * state[at])
        d_token = d_log[:BLOCK] + d_log[BLOCK:] + d_logq + jnp.where(tok == BLOCK - 1, d_last, 0.0)
        aux_ref[at[0], at[1], :, 0:1] = d_beta
        aux_ref[at[0], at[1], 0:BLOCK, 1:2] = d_token
    pad_ref[0:HALO, :] = jnp.zeros((HALO, width), F32)
    pad_ref[pl.ds(HALO + rows, HALO), :] = jnp.zeros((HALO, width), F32)
    for n in range(heads):
        keys = {b: dk_row[n, b] + dk_col[n, b] for b in range(blocks)}
        values = {b: bcol[n, b] * d_rhs[n, b] for b in range(blocks)}
        d_act = [
            jnp.concatenate([dq[n, b] for b in range(blocks)], axis=0),
            jnp.concatenate([keys[b][:BLOCK] for b in range(blocks)], axis=0),
            jnp.concatenate([keys[b][BLOCK:] for b in range(blocks)], axis=0),
            jnp.concatenate([values[b][:BLOCK] for b in range(blocks)], axis=0),
            jnp.concatenate([values[b][BLOCK:] for b in range(blocks)], axis=0),
        ]
        for i, scale in enumerate((width ** (-0.5), 1.0, 1.0)):
            d_act[i] = unit_pull(act[n][i], d_act[i], scale)
        sides = (
            (tq_ref, dtq_ref, n),
            (tk_ref, dtk_ref, 2 * n),
            (tk_ref, dtk_ref, 2 * n + 1),
            (tv_ref, dtv_ref, 2 * n),
            (tv_ref, dtv_ref, 2 * n + 1),
        )
        for i, (tap_ref, dtap_ref, at) in enumerate(sides):
            lanes = pl.ds(at * width, width)
            grad = conv_pull(
                ext_ref.at[n], pad_ref, silu_pull(conv[n][i], d_act[i]), tap_ref[:, lanes], live,
                pl.ds(i * width, width), rows, dtap_ref.at[:, lanes],
            )
            target = pl.ds((5 * n + i) * width, width)
            d_ref[0:rows, target] = grad[HALO:].astype(BF16)
            d_ref[rows : rows + HALO, target] = grad[:HALO].astype(BF16)


def mixer_backward(pre, taps, live, acol, arow, saved, start, after, dout):
    heads, ext_rows, _ = pre.shape
    rows = ext_rows - HALO
    width = start.shape[-1]
    conv_query, conv_key, conv_value = taps
    out = jax.ShapeDtypeStruct
    columns = heads * width
    group = BACKWARD_HEADS
    tap_specs = [head_columns(KW, times * group * width) for times in (1, 2, 2)]
    return pl.pallas_call(
        mixer_backward_kernel,
        grid=(heads // group,),
        in_specs=[per_head(pre.shape[1:], group)]
        + tap_specs
        + [whole(live.shape)]
        + [per_head(value.shape[1:], group) for value in (acol, arow, *saved, start, after)]
        + [head_columns(rows, group * width)],
        out_specs=[head_columns(ext_rows, 5 * group * width)] + tap_specs + [per_head(acol.shape[1:], group)],
        out_shape=[
            out((ext_rows, 5 * columns), BF16),
            out((KW, columns), F32),
            out((KW, 2 * columns), F32),
            out((KW, 2 * columns), F32),
            out(acol.shape, F32),
        ],
        scratch_shapes=[
            pltpu.VMEM((group, ext_rows, 5 * width), F32),
            pltpu.VMEM((rows + 2 * HALO, width), F32),
        ],
        compiler_params=pltpu.CompilerParams(vmem_limit_bytes=VMEM_LIMIT),
        cost_estimate=cost(35),
        name="mixer_backward",
    )(pre, conv_query, conv_key, conv_value, live, acol, arow, *saved, start, after, dout)


def carry_kernel(count, heads, part_ref, maps_ref, result_ref, inbox, outbox, landed, *sems):
    barrier = greet_group(count)
    pl.semaphore_wait(barrier, count - 1)
    send, scan, take = carry_steps(count, heads, True, part_ref, maps_ref, inbox, outbox, landed, sems)
    for h in range(heads):
        send(h)
    scan()
    take()
    result_ref[...] = landed[...]


def carry_back(part, maps, count):
    heads, width, _ = part.shape
    vmem = pl.BlockSpec(memory_space=pltpu.VMEM)
    return pl.pallas_call(
        partial(carry_kernel, count, heads),
        in_specs=[vmem] * 2,
        out_specs=vmem,
        out_shape=jax.ShapeDtypeStruct((heads, width, width), BF16),
        scratch_shapes=carry_scratch(count, heads, width, width),
        compiler_params=pltpu.CompilerParams(
            collective_id=1, has_side_effects=True, vmem_limit_bytes=VMEM_LIMIT
        ),
        cost_estimate=cost(24),
        name="carry_back",
    )(part, maps)


JOBS = 7
JOB = 512
GROUPS = 3
LATE_JOBS = 10
EARLY_LINKS = ((0, 1, 2, 3), (1, 2, 0, 3), (2, 0, 1, 3))
LATE_LINKS = ((0, 1, 2, 3), (1, 0, 2, 3))


def half_rows(lhs, links, sending, lanes=slice(None)):
    edge = lhs.shape[0] // 8
    parts = []
    for second in range(2):
        for third in range(2):
            move = {links[0]: int(sending), links[1]: second, links[2]: third}
            block = 4 * move[0] + 2 * move[1] + move[2]
            parts.append(lhs[block * edge : (block + 1) * edge, lanes])
    return jnp.concatenate(parts, axis=0)


def column_pieces(sizes, begin, end):
    at, pieces = 0, []
    for index, size in enumerate(sizes):
        low, high = max(at, begin), min(at + size, end)
        if low < high:
            pieces.append((index, low - at, low - begin, high - low))
        at += size
    return pieces


def input_pull_kernel(
    d_ref, dg_ref, wq_ref, wk_ref, wv_ref, wg_ref, aux_ref, raw_ref, live_ref, rate_ref, wr_ref, ext_ref,
    x_ref, halo_ref, gain_ref, resid_ref,
    grad_ref, edge_ref, rim_ref, dgain_ref, drates_ref, misc_ref, total_ref, rates_ref,
):
    head = pl.program_id(0)
    rows = dg_ref.shape[0]
    width = dg_ref.shape[1] // PULL_HEADS
    group = PULL_HEADS
    part = None
    for n in range(group):
        d = d_ref[:, n * 5 * width : (n + 1) * 5 * width]
        two = slice(2 * n * width, 2 * (n + 1) * width)
        term = (
            mm(d[:, :width], wq_ref[:, n * width : (n + 1) * width], NT)
            + mm(d[:, width : 3 * width], wk_ref[:, two], NT)
            + mm(d[:, 3 * width :], wv_ref[:, two], NT)
        )
        part = term if part is None else part + term
    more = mm(dg_ref[...], wg_ref[...], NT)

    @pl.when(head == 0)
    def _():
        heads, blocks = aux_ref.shape[:2]
        wide = heads * REFLECTS
        rates_ref[...] = jnp.zeros_like(rates_ref)
        for h in range(heads):
            for b in range(blocks):
                tokens = slice(b * BLOCK, (b + 1) * BLOCK)
                for j in range(REFLECTS):
                    at = h * REFLECTS + j
                    rates_ref[tokens, at : at + 1] = aux_ref[h, b, j * BLOCK : (j + 1) * BLOCK, 0:1]
                rates_ref[tokens, wide + h : wide + h + 1] = aux_ref[h, b, 0:BLOCK, 1:2]
        value, raw = rates_ref[...], raw_ref[...]
        d_log = exact_sum(block_sums(rows, True), value) * live_ref[:, 1:2]
        lane = lax.broadcasted_iota(jnp.int32, raw.shape, 1)
        d_raw = jnp.where(lane < wide, value, -rate_ref[...] * sigmoid(raw) * d_log)
        summed = jnp.where(lane < wide, value, -softplus(raw) * d_log)
        misc_ref[...] = jnp.sum(summed, axis=0, keepdims=True)
        d_raw = d_raw.astype(BF16)
        drates_ref[...] = mm(d_raw, ext_ref[pl.ds(HALO, rows), :], TN)[: drates_ref.shape[0]]
        total_ref[...] = part
        total_ref[0:rows, :] += more + mm(d_raw, wr_ref[...])

    @pl.when(head > 0)
    def _():
        total_ref[...] += part
        total_ref[0:rows, :] += more

    @pl.when(head == pl.num_programs(0) - 1)
    def _():
        grad = total_ref[...]
        unit, pulled = norm_pull(x_ref[...].astype(F32), gain_ref[...], grad[:rows])
        grad_ref[...] = (resid_ref[...] + pulled).astype(BF16)
        halo_unit, _ = norm_pull(halo_ref[...].astype(F32), gain_ref[...], grad[rows:])
        dgain_ref[...] = jnp.sum(grad[:rows] * unit, axis=0, keepdims=True) + jnp.sum(
            grad[rows:] * halo_unit, axis=0, keepdims=True
        )
        edge_ref[0] = grad[rows - HALO : rows]
        edge_ref[1] = x_ref[rows - HALO :, :].astype(F32)
        edge_ref[2] = resid_ref[rows - HALO :, :]
        rim_ref[...] = grad[rows:]


def norm_pull(x, gain, grad):
    r = lax.rsqrt(jnp.mean(x * x, axis=-1, keepdims=True) + 1e-06)
    unit = x * r
    through = grad * gain
    return unit, r * (through - unit * jnp.mean(unit * through, axis=-1, keepdims=True))


PULL_HEADS = 2


def input_pull(d_all, d_outgate, weights, aux, raw, live, rate, w_rates, ext_b, x, halo, gain, d_resid, heads):
    rows, depth = x.shape
    ext_rows = rows + HALO
    width = d_outgate.shape[1] // heads * PULL_HEADS
    out = jax.ShapeDtypeStruct
    w_query, w_key, w_value, w_outgate = weights
    rates = heads * (REFLECTS + 1)
    return pl.pallas_call(
        input_pull_kernel,
        grid=(heads // PULL_HEADS,),
        in_specs=[
            head_columns(ext_rows, 5 * width),
            head_columns(rows, width),
            head_columns(depth, width),
            head_columns(depth, 2 * width),
            head_columns(depth, 2 * width),
            head_columns(depth, width),
            whole(aux.shape),
            whole(raw.shape),
            whole(live.shape),
            whole(rate.shape),
            whole(w_rates.shape),
            whole(ext_b.shape),
            whole(x.shape),
            whole(halo.shape),
            whole((1, depth)),
            whole(d_resid.shape),
        ],
        out_specs=[
            whole((rows, depth)), whole((3, HALO, depth)), whole((HALO, depth)), whole((1, depth)),
            whole((rates, depth)), whole((1, raw.shape[1])),
        ],
        out_shape=[
            out((rows, depth), BF16),
            out((3, HALO, depth), F32),
            out((HALO, depth), F32),
            out((1, depth), F32),
            out((rates, depth), F32),
            out((1, raw.shape[1]), F32),
        ],
        scratch_shapes=[pltpu.VMEM((ext_rows, depth), F32), pltpu.VMEM(raw.shape, F32)],
        compiler_params=pltpu.CompilerParams(vmem_limit_bytes=VMEM_LIMIT),
        cost_estimate=cost(12),
        name="input_pull",
    )(
        d_all, d_outgate, w_query, w_key, w_value, w_outgate, aux, raw, live, rate, w_rates, ext_b,
        x, halo, gain[None, :], d_resid,
    )


def exact_sum(ones, value):
    total = None
    for _ in range(3):
        part = value.astype(BF16)
        value = value - part.astype(F32)
        term = mm(ones, part)
        total = term if total is None else total + term
    return total


def block_sums(rows, reverse):
    shape = (rows, rows)
    one, two = lax.broadcasted_iota(jnp.int32, shape, 0), lax.broadcasted_iota(jnp.int32, shape, 1)
    order = (one <= two) if reverse else (one >= two)
    return ((one // BLOCK == two // BLOCK) & order).astype(BF16)


def softplus(v):
    return jnp.maximum(v, 0.0) + jnp.log1p(jnp.exp(-jnp.abs(v)))


def rates_kernel(
    heads, lengths_ref, x_ref, gain_ref, wbeta_ref, wdecay_ref, bias_in_ref, rate_in_ref,
    ext_ref, raw_ref, live_ref, acol_ref, arow_ref, halo_ref, weight_ref, rate_ref,
    edge_ref, got_ref, sems,
):
    rows = x_ref.shape[0]
    blocks = rows // BLOCK
    wide = heads * REFLECTS
    seq, count = lax.axis_index("seq"), lax.axis_size("seq")
    behind, before = lax.rem(seq + 1, count), lax.rem(seq + count - 1, count)
    barrier = pltpu.get_barrier_semaphore()
    for place in (behind, before):
        pl.semaphore_signal(barrier, inc=1, device_id={"seq": place}, device_id_type=MESH)
    edge_ref[...] = x_ref[rows - HALO :, :]
    copy = pltpu.make_async_remote_copy(
        src_ref=edge_ref,
        dst_ref=got_ref,
        send_sem=sems.at[0],
        recv_sem=sems.at[1],
        device_id={"seq": behind},
        device_id_type=MESH,
    )

    def normed(field):
        field = field.astype(F32)
        return (
            field * lax.rsqrt(jnp.mean(field * field, axis=-1, keepdims=True) + 1e-06) * gain_ref[...]
        ).astype(BF16)

    pl.semaphore_wait(barrier, 2)
    copy.start()
    xn = normed(x_ref[...])
    ext_ref[pl.ds(HALO, rows), :] = xn
    blank = jnp.zeros((128 - wide - heads, wbeta_ref.shape[1]), F32)
    weight = jnp.concatenate([wbeta_ref[...].astype(F32), wdecay_ref[...].astype(F32), blank], axis=0).astype(BF16)
    weight_ref[...] = weight
    empty = jnp.zeros((1, 128 - wide - heads), F32)
    bias = jnp.concatenate([bias_in_ref[...], jnp.zeros((1, heads), F32), empty], axis=1)
    rate = jnp.concatenate([jnp.zeros((1, wide), F32), rate_in_ref[...], empty], axis=1)
    rate_ref[...] = rate
    raw = mm(xn, weight, NT)
    raw_ref[...] = raw
    row = lax.axis_index("seq") * rows + lax.broadcasted_iota(jnp.int32, (rows, 1), 0)
    place, end = row, 0
    for i in range(lengths_ref.shape[1]):
        begin, end = end, end + lengths_ref[0, i] + (SHORTEST - 1)
        place = jnp.where((row >= begin) & (row < end), row - begin, place)
    live_ref[...] = (place >= lax.broadcasted_iota(jnp.int32, (rows, 8), 1)).astype(F32)
    beta = sigmoid(raw + bias)
    log_rate = jnp.where(place == 0, RESET_LOG, -rate * softplus(raw))
    lane = lax.broadcasted_iota(jnp.int32, raw.shape, 1)
    both = jnp.where(lane < wide, beta, exact_sum(block_sums(rows, False), log_rate))
    turned = both.T
    arow_ref[...] = jnp.zeros_like(arow_ref)
    acol_ref[...] = jnp.zeros_like(acol_ref)
    for h in range(heads):
        for b in range(blocks):
            tokens = slice(b * BLOCK, (b + 1) * BLOCK)
            for j in range(REFLECTS):
                steps = slice(j * BLOCK, (j + 1) * BLOCK)
                at = h * REFLECTS + j
                acol_ref[h, b, steps, 0:1] = both[tokens, wide + h : wide + h + 1]
                acol_ref[h, b, steps, 1:2] = both[tokens, at : at + 1]
                arow_ref[h, b, 0:1, steps] = turned[wide + h : wide + h + 1, tokens]
                arow_ref[h, b, 1:2, steps] = turned[at : at + 1, tokens]
    copy.wait()
    halo = jnp.where(seq > 0, got_ref[...].astype(F32), 0.0)
    halo_ref[...] = halo.astype(BF16)
    ext_ref[0:HALO, :] = normed(halo)


def rates_forward(lengths, x, gain, w_beta, w_decay, bias, rate, heads):
    rows, depth = x.shape
    blocks = rows // BLOCK
    out = jax.ShapeDtypeStruct
    vmem = pl.BlockSpec(memory_space=pltpu.VMEM)
    return pl.pallas_call(
        partial(rates_kernel, heads),
        in_specs=[pl.BlockSpec(memory_space=pltpu.SMEM)] + [vmem] * 6,
        out_specs=[vmem] * 8,
        out_shape=[
            out((rows + HALO, depth), BF16),
            out((rows, 128), F32),
            out((rows, 8), F32),
            out((heads, blocks, STEPS, 8), F32),
            out((heads, blocks, 8, STEPS), F32),
            out((HALO, depth), BF16),
            out((128, depth), BF16),
            out((1, 128), F32),
        ],
        scratch_shapes=[
            pltpu.VMEM((HALO, depth), BF16), pltpu.VMEM((HALO, depth), BF16), pltpu.SemaphoreType.DMA((2,)),
        ],
        compiler_params=pltpu.CompilerParams(
            collective_id=4, has_side_effects=True, vmem_limit_bytes=VMEM_LIMIT
        ),
        cost_estimate=cost(6),
        name="rates_forward",
    )(lengths, x, gain[None, :], w_beta.T, w_decay.T, bias[None, :], rate[None, :])


CHUNK = 256
RING = 6


def flip(bit, other):
    return bit + other - 2 * bit * other


def relative_source(depth):
    block = depth // 32
    seq, group = lax.axis_index("seq"), lax.axis_index("dp")
    index = lax.broadcasted_iota(jnp.int32, (depth, 1), 0)
    row, place, side = index % block, (index // block) % 16, index // (16 * block)
    x = flip(seq % 2, place // 8)
    y = flip((seq // 2) % 2, (place // 4) % 2)
    z = flip((seq // 4) % 2, (place // 2) % 2) + 2 * flip(seq // 8, place % 2)
    return ((((group + side) % 2) * 16 + z * 4 + y * 2 + x) * block + row)


def middle_kernel(
    compact, count, oloc_ref, oread_ref, start_ref, gate_ref, ogain_ref, x_ref, ext_ref, mgain_ref, ograd_ref,
    maps_ref, wout_hbm, wgate_hbm, wup_hbm, wdown_hbm,
    block_ref, dout_ref, part_ref, dresid_ref, dmgain_ref, dogain_ref,
    *refs,
):
    if compact:
        products, (own_out, got_out, after_ref) = refs[: 2 * GROUPS], refs[2 * GROUPS : 2 * GROUPS + 3]
        refs = refs[2 * GROUPS + 3 :]
        gated_ref, hidden_ref, dgate_ref, dup_ref, doutgate_ref, mlp_ref, branch_ref = refs[:7]
        gated_got, hidden_got, dgate_got, dup_got, doutgate_got, own_ref, other_ref, got_ref = refs[7:15]
        other_edge, got_edge, core_sem, chunk_sem, inbox, outbox, landed = refs[15:22]
        carry_sems, staged, stage_sem, refs = refs[22:26], refs[26 : 26 + 2 * GROUPS], refs[26 + 2 * GROUPS], refs[27 + 2 * GROUPS :]
    else:
        gated_ref, hidden_ref, dgate_ref, dup_ref, doutgate_ref, mlp_ref, branch_ref = refs[:7]
        refs = refs[7:]
    wout, wgate, wup, wdown, down_ref, dmlp_ref, sem_out, sems = refs
    heads, rows, width = oread_ref.shape
    depth = x_ref.shape[1]
    chunks = hidden_ref.shape[1] // CHUNK
    fetch_out = pltpu.make_async_copy(wout_hbm, wout, sem_out)
    fetch_out.start()

    def lanes_of(c):
        return pl.ds(pl.multiple_of(c * CHUNK, CHUNK), CHUNK)

    def fetches(c):
        slot = c % RING
        return (
            pltpu.make_async_copy(wgate_hbm.at[:, lanes_of(c)], wgate.at[slot], sems.at[slot, 0]),
            pltpu.make_async_copy(wup_hbm.at[:, lanes_of(c)], wup.at[slot], sems.at[slot, 1]),
            pltpu.make_async_copy(wdown_hbm.at[lanes_of(c), :], wdown.at[slot], sems.at[slot, 2]),
        )

    for c in range(RING):
        for copy in fetches(c):
            copy.start()
    core = {"dp": 1 - lax.axis_index("dp")}

    def to_core(source, target, sems, index):
        return pltpu.make_async_remote_copy(
            src_ref=source,
            dst_ref=target,
            send_sem=sems.at[(0,) + index],
            recv_sem=sems.at[(1,) + index],
            device_id=core,
            device_id_type=MESH,
        )

    if compact:
        barrier = greet_group(count)
        pl.semaphore_signal(barrier, inc=1, device_id=core, device_id_type=MESH)
        give, scan, take = carry_steps(
            count, heads, True, part_ref, maps_ref, inbox, outbox, landed, carry_sems
        )
        half = depth // 2
        lane = lax.broadcasted_iota(jnp.int32, (depth, depth), 1)
        chosen = (lane == relative_source(depth)).astype(BF16)
        swaps = []

        def turn(at, value, index):
            turned = mm(chosen, value, NT).astype(BF16)
            cut = slice(at, at + value.shape[0])
            own_ref[:, cut] = turned[:half]
            other_ref[:, cut] = turned[half:]
            swap(other_ref.at[:, cut], got_ref.at[:, cut], index)

        def turn_tokens():
            value = jnp.concatenate([ext_ref[pl.ds(HALO, rows), :], ext_ref[0:HALO, :]], axis=0)
            turned = mm(chosen, value, NT).astype(BF16)
            own_out[...] = turned[:half]
            other_edge[...] = turned[half:]
            swap(other_edge, got_edge, 3)

        def swap(source, target, index):
            swaps.append(to_core(source, target, core_sem, (index,)))
            swaps[-1].start()

    ogain = ogain_ref[...]
    for h in range(heads):
        lanes = slice(h * width, (h + 1) * width)
        out = oloc_ref[:, lanes] + mm(oread_ref[h], start_ref[h])
        dout_ref[:, lanes] = out
        gate = gate_ref[:, lanes]
        r = lax.rsqrt(jnp.mean(out * out, axis=-1, keepdims=True) + 1e-05)
        gated_ref[:, lanes] = (out * r * ogain * (gate * sigmoid(gate))).astype(BF16)
    fetch_out.wait()
    resid = x_ref[...].astype(F32) + mm(gated_ref[...], wout[...])
    dresid_ref[...] = resid
    r = lax.rsqrt(jnp.mean(resid * resid, axis=-1, keepdims=True) + 1e-06)
    mlp_ref[...] = (resid * r * mgain_ref[...]).astype(BF16)
    if compact:
        pl.semaphore_wait(barrier, count)
        swap(gated_ref, gated_got, 4)
        turn(rows, ograd_ref[...], 1)
        turn_tokens()
        turn(0, mlp_ref[...], 0)
    down_ref[...] = jnp.zeros_like(down_ref)
    dmlp_ref[...] = jnp.zeros_like(dmlp_ref)

    def chunk_swaps(c):
        pairs = ((hidden_ref, hidden_got), (dgate_ref, dgate_got), (dup_ref, dup_got))
        return [
            to_core(own.at[:, lanes_of(c)], got.at[:, lanes_of(c)], chunk_sem, (c, i))
            for i, (own, got) in enumerate(pairs)
        ]

    def one(c, carry):
        slot = c % RING
        for copy in fetches(c):
            copy.wait()
        mlp, ograd = mlp_ref[...], ograd_ref[...]
        lanes = lanes_of(c)
        gate, up = mm(mlp, wgate[slot]), mm(mlp, wup[slot])
        d_hidden = mm(ograd, wdown[slot], NT)
        s = sigmoid(gate)
        act = gate * s
        hidden = (act * up).astype(BF16)
        d_gate = (d_hidden * up * (s + act * (1.0 - s))).astype(BF16)
        d_up = (d_hidden * act).astype(BF16)
        hidden_ref[:, lanes] = hidden
        dgate_ref[:, lanes] = d_gate
        dup_ref[:, lanes] = d_up
        if compact:
            for copy in chunk_swaps(c):
                copy.start()
        down_ref[...] += mm(hidden, wdown[slot])
        dmlp_ref[...] += mm(d_gate, wgate[slot], NT) + mm(d_up, wup[slot], NT)

        @pl.when(c + RING < chunks)
        def _():
            for copy in fetches(c + RING):
                copy.start()

        return carry

    lax.fori_loop(0, chunks, one, 0)
    resid = dresid_ref[...]
    block_ref[...] = (resid + down_ref[...]).astype(BF16)
    grad = dmlp_ref[...]
    unit, pulled = norm_pull(resid, mgain_ref[...], grad)
    dmgain_ref[...] = jnp.sum(grad * unit, axis=0, keepdims=True)
    d_resid = ograd_ref[...].astype(F32) + pulled
    dresid_ref[...] = d_resid
    branch_ref[...] = d_resid.astype(BF16)
    if compact:
        turn(2 * rows, branch_ref[...], 2)
    dogain = jnp.zeros((1, width), F32)
    for h in range(heads):
        lanes = slice(h * width, (h + 1) * width)
        grad = mm(branch_ref[...], wout[lanes, :], NT)
        out = dout_ref[:, lanes]
        gate = gate_ref[:, lanes]
        r = lax.rsqrt(jnp.mean(out * out, axis=-1, keepdims=True) + 1e-05)
        s = sigmoid(gate)
        unit = out * r
        doutgate_ref[:, lanes] = (grad * unit * ogain * (s + gate * s * (1.0 - s))).astype(BF16)
        through = grad * (gate * s)
        dogain += jnp.sum(through * unit, axis=0, keepdims=True)
        through = through * ogain
        dout = r * (through - unit * jnp.mean(unit * through, axis=-1, keepdims=True))
        dout_ref[:, lanes] = dout
        part_ref[h] = mm(oread_ref[h], dout, TN).astype(BF16)
        if compact:
            give(h)
    dogain_ref[...] = dogain
    if compact:
        swap(doutgate_ref, doutgate_got, 5)

        def arrived(c, carry):
            for copy in chunk_swaps(c):
                copy.wait()
            return carry

        lax.fori_loop(0, chunks, arrived, 0)
        rhs_own = (dgate_ref, dup_ref, hidden_ref, gated_ref, doutgate_ref)
        rhs_got = (dgate_got, dup_got, hidden_got, gated_got, doutgate_got)
        for copy in swaps[:4]:
            copy.wait()
        lhs_own, lhs_got = (own_ref, own_out), (got_ref, got_edge)
        targets = [staged[2 * group : 2 * group + 2] for group in range(GROUPS)]
        early_products(lhs_own, lhs_got, rhs_own, rhs_got, targets, (0, 1, 2))
        outgoing = [
            pltpu.make_async_copy(source, target, stage_sem.at[i])
            for i, (source, target) in enumerate(zip(staged, products))
        ]
        for copy in outgoing[: 2 * GROUPS - 2]:
            copy.start()
        scan()
        for copy in swaps[4:]:
            copy.wait()
        early_products(lhs_own, lhs_got, rhs_own, rhs_got, targets, (3, 4))
        for copy in outgoing[2 * GROUPS - 2 :]:
            copy.start()
        got_out[...] = got_edge[...]
        for copy in outgoing:
            copy.wait()
        take()
        after_ref[...] = landed[...]


def early_products(lhs_own, lhs_got, rhs_own, rhs_got, targets, which):
    tokens = rhs_own[0].shape[0]
    sizes = [rhs.shape[1] for rhs in rhs_own]
    sides = (0, 0, 1, 2, 3)
    for group in range(GROUPS):
        for sending in (True, False):
            turned = {}
            for job in range(JOBS):
                begin = (group * JOBS + job) * JOB
                for index, column, offset, width in column_pieces(sizes, begin, begin + JOB):
                    if index not in which:
                        continue
                    side = sides[index]
                    if side not in turned:
                        cut = slice(side % 3 * tokens, (side % 3 + 1) * tokens)
                        turned[side] = [
                            half_rows(lhs[side // 3], EARLY_LINKS[group], sending, cut) for lhs in (lhs_own, lhs_got)
                        ]
                    lanes = slice(column, column + width)
                    total = mm(turned[side][0], rhs_own[index][:, lanes]) + mm(
                        turned[side][1], rhs_got[index][:, lanes]
                    )
                    targets[group][0 if sending else 1][job, :, offset : offset + width] = total.astype(BF16)


def middle(
    compact, count, oloc, oread, start, gate_pre, out_gain, x, ext_b, mlp_gain, out_grad, maps,
    w_out, w_gate, w_up, w_down,
):
    heads, rows, width = oread.shape
    depth = x.shape[1]
    ff = w_gate.shape[1]
    out = jax.ShapeDtypeStruct
    vmem, hbm = pl.BlockSpec(memory_space=pltpu.VMEM), pl.BlockSpec(memory_space=pl.ANY)
    columns = heads * width
    chunks = ff // CHUNK
    half = depth // 2
    outs = [
        ((rows, depth), BF16), ((rows, columns), F32), ((heads, width, width), BF16), ((rows, depth), F32),
        ((1, depth), F32), ((1, width), F32),
    ]
    rhs = [((rows, columns), BF16)] + [((rows, ff), BF16)] * 3 + [((rows, columns), BF16)]
    kept = rhs + [((rows, depth), BF16)] * 2
    scratch = []
    dma = pltpu.SemaphoreType.DMA
    if compact:
        product = ((JOBS, half // 2, JOB), BF16)
        outs += [product] * (2 * GROUPS) + [((half, rows + HALO), BF16)] * 2
        outs += [((heads, width, width), BF16), ((rows, columns), BF16)]
        buffers = kept[:4] + kept[5:] + rhs + [((half, 3 * rows), BF16)] * 3 + [((half, rows + HALO), BF16)] * 2
        scratch += [pltpu.VMEM(*buffer) for buffer in buffers] + [dma((2, 6)), dma((2, chunks, 3))]
        scratch += carry_scratch(count, heads, width, width)
        scratch += [pltpu.VMEM(*product)] * (2 * GROUPS) + [dma((2 * GROUPS,))]
    else:
        outs += kept
    scratch += [
        pltpu.VMEM(w_out.shape, BF16),
        pltpu.VMEM((RING, depth, CHUNK), BF16),
        pltpu.VMEM((RING, depth, CHUNK), BF16),
        pltpu.VMEM((RING, CHUNK, depth), BF16),
        pltpu.VMEM((rows, depth), F32),
        pltpu.VMEM((rows, depth), F32),
        dma,
        dma((RING, 3)),
    ]

    def kernel(*refs):
        if not compact:
            middle_kernel(compact, count, *refs)
            return
        late = 20 + 2 * GROUPS + 3
        rest = refs[late + 1 :]
        middle_kernel(compact, count, *refs[:late], *rest[:4], refs[late], *rest[4:])

    params = {"collective_id": 3, "has_side_effects": True} if compact else {}
    return pl.pallas_call(
        kernel,
        in_specs=[vmem] * 10 + [hbm] * 4,
        out_specs=[hbm if compact and shape == product else vmem for shape in outs],
        out_shape=[out(*shape) for shape in outs],
        scratch_shapes=scratch,
        compiler_params=pltpu.CompilerParams(vmem_limit_bytes=VMEM_LIMIT, **params),
        cost_estimate=cost(30),
        name="middle",
    )(
        oloc, oread, start, gate_pre, out_gain[None, :], x, ext_b, mlp_gain[None, :], out_grad, maps,
        w_out, w_gate, w_up, w_down,
    )


def reduce_kernel(
    heads, arr_a, arr_b, arr_c, keep_a, keep_b, keep_c, own_ref, got_ref, rhs_ref, tq_ref, tk_ref, tv_ref, attn_ref, mlp_ref, ogain_ref,
    misc_ref, rates_ref, edge_ref, rim_ref, again_ref,
    gate_out, up_out, down_out, out_out, outgate_out, q_out, k_out, v_out, tq_out, tk_out, tv_out, rest_out,
    edge_out,
    fetched, e_keep, e_send, e_got2, e_got3, e_got4,
    rhs_got, lhs_ref, l_first, l_send, l_keep, l_got1, l_got2, l_got3, l_got4, small_sum, small_got, rim_got,
    dp_sem, e_sem, l_sem, s_sem, f_sem,
):
    seq = lax.axis_index("seq")
    group = lax.axis_index("dp")
    count = lax.axis_size("seq")
    x, y, z = seq % 2, (seq // 2) % 2, seq // 4
    near = (seq + 1 - 2 * x, seq + 2 - 4 * y)
    low_z = seq + 4 - 8 * (z % 2)
    high_z = seq + 8 - 16 * (z // 2)

    def at(place):
        return {"dp": group, "seq": place}

    core = {"dp": 1 - group, "seq": seq}
    before, behind = lax.rem(seq + count - 1, count), lax.rem(seq + 1, count)

    def send(source, target, sems, index, device):
        return pltpu.make_async_remote_copy(
            src_ref=source,
            dst_ref=target,
            send_sem=sems.at[(0,) + index],
            recv_sem=sems.at[(1,) + index],
            device_id=device,
            device_id_type=MESH,
        )

    def fetches(i):
        return [
            pltpu.make_async_copy(source.at[i], fetched.at[j, i], f_sem.at[j, i])
            for j, source in enumerate((arr_a, arr_b, arr_c, keep_a, keep_b, keep_c))
        ]

    def fetch(i, carry):
        for copy in fetches(i):
            copy.start()
        return carry

    lax.fori_loop(0, JOBS, fetch, 0)
    barrier = pltpu.get_barrier_semaphore()
    everyone = [core] + [at(place) for place in (near[0], near[1], low_z, high_z, before, behind)]
    for device in everyone:
        pl.semaphore_signal(barrier, inc=1, device_id=device, device_id_type=MESH)
    pl.semaphore_wait(barrier, len(everyone))

    rim = send(rim_ref, rim_got, dp_sem, (1,), at(before))
    rim.start()
    hops = [core, at(high_z), at(low_z), at(near[0]), at(near[1])]

    def hop(step):
        return send(small_sum.at[step], small_got.at[step], s_sem, (step,), hops[step])

    def next_hop(step):
        hop(step - 1).wait_recv()
        small_sum[step] = small_sum[step - 1] + small_got[step - 1]
        if step < len(hops):
            hop(step).start()

    depth = tq_ref.shape[1]
    small_sum[0, 0:KW] = tq_ref[...]
    for half in range(2):
        lanes = pl.ds(half * depth, depth)
        small_sum[0, KW * (1 + half) : KW * (2 + half)] = tk_ref[:, lanes]
        small_sum[0, KW * (3 + half) : KW * (4 + half)] = tv_ref[:, lanes]
    small_sum[0, 5 * KW : 6 * KW] = jnp.zeros((KW, depth), F32)
    small_sum[0, 5 * KW : 5 * KW + 1] = attn_ref[...]
    small_sum[0, 5 * KW + 1 : 5 * KW + 2] = mlp_ref[...]
    gains = ogain_ref.shape[1]
    small_sum[0, 5 * KW + 2 : 5 * KW + 3, 0:gains] = ogain_ref[...]
    small_sum[0, 5 * KW + 2 : 5 * KW + 3, gains : gains + misc_ref.shape[1]] = misc_ref[...]
    small_sum[0, 6 * KW :] = rates_ref[...]
    hop(0).start()
    swap = send(rhs_ref, rhs_got, dp_sem, (0,), core)
    swap.start()

    places = (near[0], near[1], low_z, high_z)
    quarter = e_got2.shape[2]
    eighth, share = quarter // 2, quarter // 4

    def exchange(p, i, stage, sent, got, sems, links):
        begin = (0, 0, quarter, quarter + eighth)[stage]
        target = places[links[p][stage]]
        return send(sent.at[p, i, pl.ds(begin, got.shape[2])], got.at[p, i], sems, (p, i, stage), at(target))

    def early(p, i, stage):
        return exchange(p, i, stage, e_send, (None, e_got2, e_got3, e_got4)[stage], e_sem, EARLY_LINKS)

    def late(p, i, stage):
        sent = l_first if stage == 0 else l_send
        return exchange(p, i, stage, sent, (l_got1, l_got2, l_got3, l_got4)[stage], l_sem, LATE_LINKS)

    def early2(i, carry):
        for copy in fetches(i):
            copy.wait()
        for p in range(GROUPS):
            total = fetched[p, i].astype(F32) + fetched[GROUPS + p, i].astype(F32)
            e_keep[p, i] = total[:quarter].astype(BF16)
            e_send[p, i, 0:quarter] = total[quarter:].astype(BF16)
            early(p, i, 1).start()
        return carry

    def onward(p, i, copy_of, keep, sent, got, stage, begin):
        copy_of(p, i, stage).wait_recv()
        rows = got.shape[2]
        half = rows // 2
        total = keep[p, i, 0:rows].astype(F32) + got[p, i].astype(F32)
        keep[p, i, 0:half] = total[:half].astype(BF16)
        sent[p, i, begin : begin + half] = total[half:].astype(BF16)
        copy_of(p, i, stage + 1).start()

    def later(i, carry, copy_of, keep, sent, got, stage, begin):
        for p in range(keep.shape[0]):
            onward(p, i, copy_of, keep, sent, got, stage, begin)
        return carry

    for p in range(2):
        for side, lhs in enumerate((own_ref, got_ref)):
            for sending in range(2):
                lhs_ref[p, side, sending] = half_rows(lhs[...], LATE_LINKS[p], sending)
    next_hop(1)
    lax.fori_loop(0, JOBS, early2, 0)
    next_hop(2)
    swap.wait_recv()
    job = l_got1.shape[-1]
    late_jobs = LATE_JOBS // 2
    tokens = rhs_ref.shape[0]

    def product(m, p, sending):
        lanes = pl.ds(pl.multiple_of(m * job, job), job)
        total = mm(lhs_ref[p, 0, int(sending)], rhs_ref[:, lanes]) + mm(
            lhs_ref[p, 1, int(sending)], rhs_got[:, lanes]
        )
        return total[:quarter], total[quarter:]

    def late1(i, carry):
        for p in range(2):
            low, high = product(2 * i + p, p, True)
            l_first[p, i, 0:quarter] = low.astype(BF16)
            l_first[p, i, quarter : 2 * quarter] = high.astype(BF16)
            late(p, i, 0).start()
        return carry

    def late2(i, carry):
        for p in range(2):
            low, high = product(2 * i + p, p, False)
            late(p, i, 0).wait_recv()
            l_keep[p, i] = (low + l_got1[p, i, 0:quarter].astype(F32)).astype(BF16)
            l_send[p, i, 0:quarter] = (high + l_got1[p, i, quarter : 2 * quarter].astype(F32)).astype(BF16)
            late(p, i, 1).start()
        return carry

    lag = JOBS - late_jobs

    def low_turn(i, carry):
        later(i, carry, early, e_keep, e_send, e_got2, 1, quarter)

        @pl.when(i >= lag)
        def _():
            late1(i - lag, carry)

        return carry

    def high_turn(i, carry):
        later(i, carry, early, e_keep, e_send, e_got3, 2, quarter + eighth)

        @pl.when(i >= lag)
        def _():
            late2(i - lag, carry)

        return carry

    lax.fori_loop(0, JOBS, low_turn, 0)
    next_hop(3)
    lax.fori_loop(0, JOBS, high_turn, 0)
    next_hop(4)
    rim.wait_recv()
    inside = (seq < count - 1).astype(F32)
    _, pulled = norm_pull(edge_ref[1], again_ref[...], edge_ref[0] + inside * rim_got[...])
    edge_out[...] = (edge_ref[2] + pulled).astype(BF16)
    late_low = partial(later, copy_of=late, keep=l_keep, sent=l_send, got=l_got2, stage=1, begin=quarter)
    lax.fori_loop(0, late_jobs, late_low, 0)
    next_hop(5)
    late_high = partial(later, copy_of=late, keep=l_keep, sent=l_send, got=l_got3, stage=2, begin=quarter + eighth)
    lax.fori_loop(0, late_jobs, late_high, 0)
    early_outs = (gate_out, up_out, down_out, out_out, outgate_out)
    for i in range(JOBS):
        for p in range(GROUPS):
            early(p, i, 3).wait_recv()
            total = e_keep[p, i, 0:share].astype(F32) + e_got4[p, i].astype(F32)
            first = (p * JOBS + i) * JOB
            for output, to, begin, width in column_pieces([o.shape[1] for o in early_outs], first, first + JOB):
                early_outs[output][:, to : to + width] = total[:, begin : begin + width]
    tq_out[...] = small_sum[5, 0:KW]
    for half in range(2):
        lanes = pl.ds(half * depth, depth)
        tk_out[:, lanes] = small_sum[5, KW * (1 + half) : KW * (2 + half)]
        tv_out[:, lanes] = small_sum[5, KW * (3 + half) : KW * (4 + half)]
    rest_out[...] = small_sum[5, 5 * KW :]
    width = q_out.shape[1] // heads
    for i in range(late_jobs):
        for p in range(2):
            late(p, i, 3).wait_recv()
            total = l_keep[p, i, 0:share].astype(F32) + l_got4[p, i].astype(F32)
            for begin in range(0, job, width):
                head, part = divmod(((2 * i + p) * job + begin) // width, 5)
                if part == 0:
                    target, to = q_out, head * width
                else:
                    target, to = (k_out, v_out)[(part - 1) // 2], (2 * head + (part - 1) % 2) * width
                target[:, to : to + width] = total[:, begin : begin + width]

    def early_sent(i, carry):
        for p in range(GROUPS):
            for stage in (1, 2, 3):
                early(p, i, stage).wait_send()
        return carry

    def late_sent(i, carry):
        for p in range(2):
            for stage in (0, 1, 2, 3):
                late(p, i, stage).wait_send()
        return carry

    lax.fori_loop(0, JOBS, early_sent, 0)
    lax.fori_loop(0, late_jobs, late_sent, 0)
    swap.wait_send()
    rim.wait_send()
    for step in range(len(hops)):
        hop(step).wait_send()


def reduce_all(arrived, kept, own, got, rhs, taps, gains, rates, edge, rim, gain, ff, heads):
    half = own.shape[0] // 2
    quarter, eighth, share = half // 2, half // 4, half // 8
    count = LATE_JOBS // 2
    columns = rhs.shape[1] // 5
    job = rhs.shape[1] // LATE_JOBS
    depth = rates.shape[1]
    small_rows = 6 * KW + rates.shape[0]
    out = jax.ShapeDtypeStruct
    vmem = pl.BlockSpec(memory_space=pltpu.VMEM)

    def stages(groups, jobs, width):
        return [((groups, jobs, rows, width), BF16) for rows in (quarter, eighth, share)]

    buffers = [((2 * GROUPS, JOBS, half, JOB), BF16)]
    buffers += [((GROUPS, JOBS, quarter, JOB), BF16), ((GROUPS, JOBS, half, JOB), BF16)]
    buffers += stages(GROUPS, JOBS, JOB)
    buffers += [(rhs.shape, BF16), ((2, 2, 2, half, own.shape[1]), BF16)] + [((2, count, half, job), BF16)] * 2 + [((2, count, quarter, job), BF16)]
    buffers += [((2, count, half, job), BF16)] + stages(2, count, job)
    buffers += [((6, small_rows, depth), F32), ((5, small_rows, depth), F32), (rim.shape, F32)]
    dma = pltpu.SemaphoreType.DMA
    shapes = [(share, ff)] * 3 + [(share, columns)] * 3 + [(share, 2 * columns)] * 2
    shapes += [tap.shape for tap in taps] + [(small_rows - 5 * KW, depth)]
    return pl.pallas_call(
        partial(reduce_kernel, heads),
        in_specs=[pl.BlockSpec(memory_space=pl.ANY)] * (2 * GROUPS) + [vmem] * 14,
        out_specs=[vmem] * 13,
        out_shape=[out(shape, F32) for shape in shapes] + [out(rim.shape, BF16)],
        scratch_shapes=[pltpu.VMEM(shape, kind) for shape, kind in buffers]
        + [dma((2, 2)), dma((2, GROUPS, JOBS, 4)), dma((2, 2, count, 4)), dma((2, 5)), dma((2 * GROUPS, JOBS))],
        compiler_params=pltpu.CompilerParams(
            collective_id=2, has_side_effects=True, vmem_limit_bytes=VMEM_LIMIT
        ),
        cost_estimate=cost(90),
        name="reduce_all",
    )(*arrived, *kept, own, got, rhs, *taps, *gains, rates, edge, rim, gain)


def finish_kernel(marks, grad_ref, edge_ref, rest_ref, *refs):
    count = (len(refs) - 8) // 2
    sources, (grad_out, *outs) = refs[:count], refs[count:]
    rows = grad_ref.shape[0]
    grad_out[0 : rows - HALO, :] = grad_ref[0 : rows - HALO, :]
    grad_out[rows - HALO :, :] = edge_ref[...]
    for source, target in zip(sources, outs):
        target[...] = source[...]
    again, mlp, beta, rate, gain, bias, decay = outs[count:]
    rest = rest_ref[...]
    share, depth = again.shape[1], rest.shape[1]
    place = lax.axis_index("dp") * lax.axis_size("seq") + lax.axis_index("seq")
    own = pltpu.roll(rest, lax.rem(depth - place * share, depth), 1)[:, :share]
    again[...] = own[0:1]
    mlp[...] = own[1:2]
    beta[...] = own[4 : 4 + beta.shape[0]]
    rate[...] = own[4 + beta.shape[0] :]
    for target, begin in zip((gain, bias, decay), marks):
        target[...] = rest_ref[2:3, begin : begin + target.shape[1]]


def finish(input_grad, edge_grad, rest, values, share, width, heads):
    wide, narrow = heads * REFLECTS, heads
    shapes = [value.shape for value in values]
    shapes += [(1, share)] * 2 + [(wide, share), (narrow, share), (1, width), (1, wide), (1, narrow)]
    out = jax.ShapeDtypeStruct
    vmem = pl.BlockSpec(memory_space=pltpu.VMEM)
    return pl.pallas_call(
        partial(finish_kernel, (0, width, width + wide)),
        in_specs=[vmem] * (3 + len(values)),
        out_specs=[vmem] * (1 + len(shapes)),
        out_shape=[out(input_grad.shape, BF16)] + [out(shape, F32) for shape in shapes],
        compiler_params=pltpu.CompilerParams(vmem_limit_bytes=VMEM_LIMIT),
        cost_estimate=cost(3),
        name="finish",
    )(input_grad, edge_grad, rest, *values)


def dot32(a, b, dims=NN):
    return lax.dot_general(a, b, dims, preferred_element_type=F32)


def swap_core(value):
    count = lax.axis_size("dp")
    return lax.ppermute(value, "dp", [(i, (i + 1) % count) for i in range(count)])


def neighbour_route(bit):
    return [(i, i ^ bit) for i in range(16)]


def by_head(field, heads, begin, size):
    rows = field.shape[0]
    return field.reshape(rows, heads, -1)[:, :, begin : begin + size].reshape(rows, heads * size)


def per_device(
    block_input, lengths, attn_gain, w_query, w_key, w_value, w_outgate, w_beta, w_decay, beta_bias,
    decay_rate, conv_query, conv_key, conv_value, out_gain, w_out, mlp_gain, w_gate, w_up, w_down,
    out_grad,
):
    rows, depth = block_input.shape
    heads = decay_rate.shape[0]
    width = out_gain.shape[0]
    count = lax.axis_size("seq")
    seq = lax.axis_index("seq")
    group = lax.axis_index("dp")
    compact = count == 16
    wide = heads * REFLECTS
    ext_b, raw, live, acol, arow, halo, w_rates, rate = rates_forward(
        lengths, block_input, attn_gain, w_beta, w_decay, beta_bias, decay_rate, heads
    )
    taps = (conv_query, conv_key, conv_value)
    pre, gate_pre, oloc, oread, *saved, start, all_maps = mixer_forward(
        ext_b, w_query, w_key, w_value, w_outgate, taps, live, acol, arow, heads, width, count
    )
    block_output, d_out, part, d_resid, grad_mlp_gain, grad_out_gain, *rest = middle(
        compact, count, oloc, oread, start, gate_pre, out_gain, block_input, ext_b, mlp_gain, out_grad,
        all_maps, w_out, w_gate, w_up, w_down,
    )
    if compact:
        products, (own_l, got_l, after, d_outgate_b) = rest[: 2 * GROUPS], rest[2 * GROUPS :]
        arrived = [
            lax.ppermute(sent, "seq", neighbour_route(1 << links[0])) for sent, links in zip(products[::2], EARLY_LINKS)
        ]
    else:
        gated_b, hidden_b, d_gate_b, d_up_b, d_outgate_b, mlp_b, d_branch_b = rest
        after = carry_back(part, all_maps, count)
    d_all, d_tap_q, d_tap_k, d_tap_v, aux = mixer_backward(
        pre, taps, live, acol, arow, saved, start, after, d_out
    )
    input_grad, edge, rim, grad_attn_gain, grad_rates, misc = input_pull(
        d_all, d_outgate_b, (w_query, w_key, w_value, w_outgate), aux, raw, live, rate, w_rates, ext_b,
        block_input, halo, attn_gain, d_resid, heads,
    )
    last = width + wide + heads
    gains = (grad_attn_gain, grad_mlp_gain, grad_out_gain, misc)
    d_taps = (d_tap_q, d_tap_k, d_tap_v)
    devices = count * lax.axis_size("dp")
    share = depth // devices
    if compact:
        sums = reduce_all(
            arrived, products[1::2], own_l, got_l, d_all, d_taps, gains, grad_rates,
            edge, rim, attn_gain[None, :], w_gate.shape[1], heads,
        )
        trunk, taps_out, rest, edge_grad = sums[5:8], sums[8:11], sums[11], sums[12]
    else:
        normed_e = jnp.concatenate([ext_b[HALO:], ext_b[:HALO]], axis=0)
        normed_b = ext_b[HALO:]
        xf = block_input.astype(F32)
        tail = edge[0] + lax.ppermute(rim, "seq", [(i, i - 1) for i in range(1, count)])
        _, pulled = norm_pull(edge[1], attn_gain[None, :], tail)
        edge_grad = (edge[2] + pulled).astype(BF16)
        line = jnp.pad(jnp.concatenate(gains[2:], axis=1), ((0, 0), (0, depth - width - 128)))
        line = jnp.concatenate([*gains[:2], line, jnp.zeros((1, depth), F32)], axis=0)
        small = lax.psum(d_taps + (line, grad_rates), ("dp", "seq"))
        taps_out, rest = small[:3], jnp.concatenate(small[3:], axis=0)
        trunk = [by_head(d_all, heads, begin * width, size * width) for begin, size in ((0, 1), (1, 2), (3, 2))]
        pairs = zip(
            (mlp_b, mlp_b, out_grad, d_branch_b, normed_b) + (normed_e,) * 3, (d_gate_b, d_up_b, hidden_b, gated_b, d_outgate_b) + tuple(trunk)
        )
        sums = [
            lax.psum_scatter(dot32(lhs, rhs, TN), ("dp", "seq"), scatter_dimension=0, tiled=True)
            for lhs, rhs in pairs
        ]
        trunk = sums[5:]
    values = (*trunk, sums[4], *taps_out, sums[0], sums[1], sums[3], sums[2])
    done = finish(input_grad, edge_grad, rest, values, share, width, heads)
    (
        input_grad, g_query, g_key, g_value, g_outgate, g_conv_q, g_conv_k, g_conv_v, g_gate, g_up, g_out, g_down,
        g_attn, g_mlp, g_beta, g_decay, g_gain, g_bias, g_rate,
    ) = done
    return (
        block_output,
        input_grad,
        g_attn[0],
        g_query,
        g_key,
        g_value,
        g_outgate,
        g_beta.T,
        g_decay.T,
        g_bias[0],
        g_rate[0],
        g_conv_q,
        g_conv_k,
        g_conv_v,
        g_gain[0],
        g_out.T,
        g_mlp[0],
        g_gate,
        g_up,
        g_down.T,
    )


def solution(mesh):
    tokens = P(("dp", "seq"), None)
    column = P(None, ("dp", "seq"))
    vector = P(("dp", "seq"))
    in_specs = (tokens, P("dp", None)) + (P(),) * 18 + (tokens,)
    out_specs = (
        (tokens, tokens, vector)
        + (tokens,) * 6
        + (P(),) * 6
        + (column, vector, tokens, tokens, column)
    )
    return jax.shard_map(
        per_device, mesh=mesh, in_specs=in_specs, out_specs=out_specs, check_vma=False
    )
```

```python
from functools import partial

import jax
import jax.numpy as jnp
from jax import lax
from jax.experimental import pallas as pl
from jax.experimental.pallas import tpu as pltpu
from jax.sharding import PartitionSpec as P

REFLECTS = 2
KW = 4
BLOCK = 64
SHORTEST = 1024
STEPS = BLOCK * REFLECTS
HALO = 8
RESET_LOG = -80.0
MESH = pl.DeviceIdType.MESH
F32 = jnp.float32
BF16 = jnp.bfloat16
NN = (((1,), (0,)), ((), ()))
NT = (((1,), (1,)), ((), ()))
TN = (((0,), (0,)), ((), ()))
VMEM_LIMIT = 56 * 1024 * 1024
FORWARD_HEADS = 2
BACKWARD_HEADS = 1


def cost(microseconds):
    return pl.CostEstimate(
        flops=int(microseconds * 1e9), bytes_accessed=int(microseconds * 1e6), transcendentals=0
    )


def mm(a, b, dims=NN):
    return lax.dot_general(a.astype(BF16), b.astype(BF16), dims, preferred_element_type=F32)


def halves(a):
    high = a.astype(BF16)
    return high, (a - high.astype(F32)).astype(BF16)


def mm3(a, b):
    ah, al = halves(a)
    bh, bl = halves(b)
    return mm(jnp.concatenate([ah, al], axis=1), jnp.concatenate([bh, bh], axis=0)) + mm(ah, bl)


def mm2(a, b, dims=NN):
    ah, al = halves(a)
    return mm(ah, b, dims) + mm(al, b, dims)


def mm2t(a, b, dims=NN):
    bh, bl = halves(b)
    return mm(a, bh, dims) + mm(a, bl, dims)


def sigmoid(v):
    return 1.0 / (1.0 + jnp.exp(-v))


def step_ids(shape, axis):
    index = lax.broadcasted_iota(jnp.int32, shape, axis)
    return index % BLOCK, index // BLOCK


def step_masks():
    shape = (STEPS, STEPS)
    tm, jm = step_ids(shape, 0)
    tn, jn = step_ids(shape, 1)
    strict = (tm > tn) | ((tm == tn) & (jm > jn))
    size = 4
    first = tm // size == tn // size
    merges = []
    while size < BLOCK:
        merges.append((tm // (2 * size) == tn // (2 * size)) & (tm // size != tn // size))
        size = 2 * size
    eye = ((tm == tn) & (jm == jn)).astype(F32)
    return tm >= tn, strict, first, merges, eye


def unit_lower_inverse(systems, first, merges, eye):
    neg = [jnp.where(first, -a, 0.0) for a in systems]
    inv = [eye + n for n in neg]
    for _ in range(2):
        neg = [mm3(n, n) for n in neg]
        inv = [t + mm3(t, n) for t, n in zip(inv, neg)]
    for merge in merges:
        off = [mm3(jnp.where(merge, a, 0.0), t) for a, t in zip(systems, inv)]
        inv = [t - mm3(t, o) for t, o in zip(inv, off)]
    return inv


def conv_parts(ext_ref, taps, live, columns, rows):
    total = None
    for back in range(KW):
        part = ext_ref[pl.ds(HALO - back, rows), columns] * taps[KW - 1 - back : KW - back, :]
        if back > 0:
            part = part * live[:, back : back + 1]
        total = part if total is None else total + part
    return total


def head_features(ext_ref, tq, tk, tv, live, rows, width):
    conv = [
        conv_parts(ext_ref, tq, live, pl.ds(0, width), rows),
        conv_parts(ext_ref, tk[:, :width], live, pl.ds(width, width), rows),
        conv_parts(ext_ref, tk[:, width:], live, pl.ds(2 * width, width), rows),
        conv_parts(ext_ref, tv[:, :width], live, pl.ds(3 * width, width), rows),
        conv_parts(ext_ref, tv[:, width:], live, pl.ds(4 * width, width), rows),
    ]
    return conv


def unit_rows(act):
    return lax.rsqrt(jnp.sum(act * act, axis=-1, keepdims=True) + 1e-06)


def greet_group(count):
    place, group = lax.axis_index("seq"), lax.axis_index("dp")
    barrier = pltpu.get_barrier_semaphore()

    def greet(step, carry):
        peer = lax.rem(place + step, count)
        pl.semaphore_signal(barrier, inc=1, device_id=(group, peer), device_id_type=MESH)
        return carry

    lax.fori_loop(1, count, greet, 0)
    return barrier


def carry_steps(count, heads, backward, part_ref, maps_ref, inbox, outbox, landed, sems):
    send_sem, recv_sem, back_sem, land_sem = sems
    place, group = lax.axis_index("seq"), lax.axis_index("dp")
    width = landed.shape[-1]
    stride = count // 16

    def keeper(h):
        return (2 * h + group) * stride

    def outgoing(h):
        return pltpu.make_async_remote_copy(
            src_ref=part_ref.at[h],
            dst_ref=inbox.at[place],
            send_sem=send_sem.at[h],
            recv_sem=recv_sem.at[place],
            device_id=(group, keeper(h)),
            device_id_type=MESH,
        )

    def send(h):
        @pl.when(place != keeper(h))
        def _():
            outgoing(h).start()

        @pl.when(place == keeper(h))
        def _():
            inbox[pl.ds(place, 1)] = part_ref[pl.ds(h, 1)]

    def scan_head(h):
        def returning(where):
            return pltpu.make_async_remote_copy(
                src_ref=outbox.at[where],
                dst_ref=landed.at[h],
                send_sem=back_sem.at[where],
                recv_sem=land_sem.at[h],
                device_id=(group, where),
                device_id_type=MESH,
            )

        def lap(step, state):
            where = count - 1 - step if backward else step
            outbox[pl.ds(where, 1)] = state[None].astype(BF16)

            @pl.when(where != place)
            def _():
                returning(where).start()
                pltpu.make_async_remote_copy(
                    src_ref=part_ref.at[h],
                    dst_ref=inbox.at[where],
                    send_sem=send_sem.at[h],
                    recv_sem=recv_sem.at[where],
                    device_id=(group, where),
                    device_id_type=MESH,
                ).wait_recv()

            @pl.when(where == place)
            def _():
                landed[h : h + 1] = outbox[pl.ds(where, 1)]

            got = inbox[pl.ds(where, 1)][0]
            high, low = halves(state)
            both = jnp.concatenate([high, low], axis=1)
            if backward:
                moved = mm(maps_ref[pl.ds(where, 1)][0][:, width:], both, TN)
            else:
                moved = mm(got[:, width:], both)
            return moved[:, :width] + moved[:, width:] + got[:, :width].astype(F32)

        lax.fori_loop(0, count, lap, jnp.zeros((width, width), F32))

        def finish(where, carry):
            @pl.when(where != place)
            def _():
                returning(where).wait_send()

            return carry

        return lambda: lax.fori_loop(0, count, finish, 0)

    def scan():
        for h in range(heads):

            @pl.when(place == keeper(h))
            def _(h=h):
                scan_head(h)()

    def take():
        for h in range(heads):

            @pl.when(place != keeper(h))
            def _(h=h):
                outgoing(h).wait_send()
                pltpu.make_async_remote_copy(
                    src_ref=outbox.at[0],
                    dst_ref=landed.at[h],
                    send_sem=back_sem.at[0],
                    recv_sem=land_sem.at[h],
                    device_id=(group, keeper(h)),
                    device_id_type=MESH,
                ).wait_recv()

    return send, scan, take


def carry_scratch(count, heads, width, columns):
    dma = pltpu.SemaphoreType.DMA
    return [
        pltpu.VMEM((count, width, columns), BF16),
        pltpu.VMEM((count, width, width), BF16),
        pltpu.VMEM((heads, width, width), BF16),
        dma((heads,)),
        dma((count,)),
        dma((count,)),
        dma((heads,)),
    ]


def mixer_forward_kernel(
    count, every_head, xn_ref, wq_ref, wk_ref, wv_ref, wg_ref, tq_ref, tk_ref, tv_ref, live_ref, acol_ref, arow_ref,
    pre_ref, gate_ref, oloc_ref, oread_ref, inv_ref, delta_ref, state_ref, turn_ref, carry_ref, start_ref, maps_ref,
    ext_ref, part_ref, inbox, outbox, landed, *sems,
):
    heads, rows, width = oread_ref.shape
    turn_at = pl.program_id(0)
    barrier = pltpu.get_barrier_semaphore()

    @pl.when(turn_at == 0)
    def _():
        greet_group(count)

    give, scan, take = carry_steps(count, every_head, False, part_ref, None, inbox, outbox, landed, sems)
    blocks = rows // BLOCK
    xn = xn_ref[...]
    live = live_ref[...]
    gate_ref[...] = mm(xn[HALO:], wg_ref[...])
    query, key, value = mm(xn, wq_ref[...]), mm(xn, wk_ref[...]), mm(xn, wv_ref[...])
    reach, strict, first, merges, eye = step_masks()
    cut = [slice(b * BLOCK, (b + 1) * BLOCK) for b in range(blocks)]
    every = [(n, b) for n in range(heads) for b in range(blocks)]
    qb, kb, vb = {}, {}, {}
    for n in range(heads):
        one, two = slice(n * width, (n + 1) * width), slice(2 * n * width, 2 * (n + 1) * width)
        pre = jnp.concatenate([query[:, one], key[:, two], value[:, two]], axis=1).astype(BF16)
        pre_ref[n] = pre
        ext_ref[n] = pre.astype(F32)
        conv = head_features(ext_ref.at[n], tq_ref[:, one], tk_ref[:, two], tv_ref[:, two], live, rows, width)
        act = [c * sigmoid(c) for c in conv]
        q = (act[0] * unit_rows(act[0]) * width ** (-0.5)).astype(BF16)
        k = [(a * unit_rows(a)).astype(BF16) for a in act[1:3]]
        v = [a.astype(BF16) for a in act[3:5]]
        for b in range(blocks):
            qb[n, b] = q[cut[b]]
            kb[n, b] = jnp.concatenate([k[0][cut[b]], k[1][cut[b]]], axis=0)
            vb[n, b] = jnp.concatenate([v[0][cut[b]], v[1][cut[b]]], axis=0)
    ccol = {at: acol_ref[at[0], at[1], :, 0:1] for at in every}
    bcol = {at: acol_ref[at[0], at[1], :, 1:2] for at in every}
    crow = {at: arow_ref[at[0], at[1], 0:1, :] for at in every}
    brow = {at: arow_ref[at[0], at[1], 1:2, :] for at in every}
    fade = {at: jnp.exp(jnp.where(reach, ccol[at] - crow[at], -1e30)) for at in every}
    system = [jnp.where(strict, fade[at] * mm(kb[at], kb[at], NT), 0.0) * bcol[at] for at in every]
    inv = dict(zip(every, unit_lower_inverse(system, first, merges, eye)))
    for at in every:
        inv_ref[at[0], at[1]] = inv[at].astype(BF16)
    local = {at: mm2(inv[at] * brow[at], vb[at]) for at in every}
    reads = {at: mm2(inv[at] * (brow[at] * jnp.exp(crow[at])), kb[at]) for at in every}
    score = {at: fade[at][:BLOCK] * mm(qb[at], kb[at], NT) for at in every}
    grow = {at: jnp.exp(ccol[at]) for at in every}
    last = {at: ccol[at][BLOCK - 1 : BLOCK] for at in every}
    tail = {at: kb[at].astype(F32) * jnp.exp(last[at] - ccol[at]) for at in every}
    both = {at: jnp.concatenate([local[at], -reads[at]], axis=1).astype(BF16) for at in every}
    turn = {at: mm(tail[at], both[at], TN) for at in every}
    query_out = {at: mm(score[at], both[at]) for at in every}
    state = {}
    for n in range(heads):
        now = jnp.concatenate([jnp.zeros((width, width), F32), eye], axis=1)
        for b in range(blocks):
            at = (n, b)
            state[at] = now
            step = turn[at][:, width:].astype(BF16)
            turn_ref[n, b] = step
            fixed = jnp.concatenate([turn[at][:, :width], jnp.zeros((width, width), F32)], axis=1)
            now = jnp.exp(last[at]) * now + fixed + mm(step, now)
        part_ref[pl.ds(turn_at * heads + n, 1)] = now.astype(BF16)[None]

    @pl.when(turn_at == 0)
    def _():
        pl.semaphore_wait(barrier, count - 1)

    for n in range(heads):
        give(turn_at * heads + n)
    for at in every:
        n, b = at
        carried = query_out[at][:, width:] + grow[at][:BLOCK] * qb[at].astype(F32)
        low = state[at].astype(BF16)
        carry_ref[n, b] = carried.astype(BF16)
        state_ref[n, b] = low
        fixed = jnp.concatenate([local[at], jnp.zeros((STEPS, width), F32)], axis=1)
        delta_ref[n, b] = (fixed - mm(reads[at], low)).astype(BF16)
        out = mm(carried, low)
        oloc_ref[cut[b], n * width : (n + 1) * width] = out[:, :width] + query_out[at][:, :width]
        oread_ref[n, cut[b], :] = out[:, width:].astype(BF16)

    @pl.when(turn_at == pl.num_programs(0) - 1)
    def _():
        scan()
        take()
        start_ref[...] = landed[...]
        maps_ref[...] = inbox[...]


def head_columns(rows, width):
    return pl.BlockSpec((rows, width), lambda h: (0, h))


def whole(shape):
    return pl.BlockSpec(shape, lambda h: (0,) * len(shape))


def per_head(shape, group=1):
    return pl.BlockSpec((group,) + shape, lambda h: (h,) + (0,) * len(shape))


def mixer_forward(xn, w_query, w_key, w_value, w_outgate, taps, live, acol, arow, heads, width, count):
    ext_rows, depth = xn.shape
    rows = ext_rows - HALO
    blocks = rows // BLOCK
    conv_query, conv_key, conv_value = taps
    out = jax.ShapeDtypeStruct
    return pl.pallas_call(
        partial(mixer_forward_kernel, count, heads),
        grid=(heads // FORWARD_HEADS,),
        in_specs=[
            whole((ext_rows, depth)),
            head_columns(depth, FORWARD_HEADS * width),
            head_columns(depth, 2 * FORWARD_HEADS * width),
            head_columns(depth, 2 * FORWARD_HEADS * width),
            head_columns(depth, FORWARD_HEADS * width),
            head_columns(KW, FORWARD_HEADS * width),
            head_columns(KW, 2 * FORWARD_HEADS * width),
            head_columns(KW, 2 * FORWARD_HEADS * width),
            whole(live.shape),
            per_head(acol.shape[1:], FORWARD_HEADS),
            per_head(arow.shape[1:], FORWARD_HEADS),
        ],
        out_specs=[
            per_head((ext_rows, 5 * width), FORWARD_HEADS),
            head_columns(rows, FORWARD_HEADS * width),
            head_columns(rows, FORWARD_HEADS * width),
            per_head((rows, width), FORWARD_HEADS),
            per_head((blocks, STEPS, STEPS), FORWARD_HEADS),
            per_head((blocks, STEPS, 2 * width), FORWARD_HEADS),
            per_head((blocks, width, 2 * width), FORWARD_HEADS),
            per_head((blocks, width, width), FORWARD_HEADS),
            per_head((blocks, BLOCK, width), FORWARD_HEADS),
            whole((heads, width, width)),
            whole((count, width, 2 * width)),
        ],
        out_shape=[
            out((heads, ext_rows, 5 * width), BF16),
            out((rows, heads * width), F32),
            out((rows, heads * width), F32),
            out((heads, rows, width), BF16),
            out((heads, blocks, STEPS, STEPS), BF16),
            out((heads, blocks, STEPS, 2 * width), BF16),
            out((heads, blocks, width, 2 * width), BF16),
            out((heads, blocks, width, width), BF16),
            out((heads, blocks, BLOCK, width), BF16),
            out((heads, width, width), BF16),
            out((count, width, 2 * width), BF16),
        ],
        scratch_shapes=[
            pltpu.VMEM((FORWARD_HEADS, ext_rows, 5 * width), F32),
            pltpu.VMEM((heads, width, 2 * width), BF16),
        ]
        + carry_scratch(count, heads, width, 2 * width),
        compiler_params=pltpu.CompilerParams(
            collective_id=0, has_side_effects=True, vmem_limit_bytes=VMEM_LIMIT
        ),
        cost_estimate=cost(40),
        name="mixer_forward",
    )(xn, w_query, w_key, w_value, w_outgate, conv_query, conv_key, conv_value, live, acol, arow)


def conv_pull(ext_ref, pad_ref, d_conv, taps, live, columns, rows, dtap_ref):
    total = None
    for back in range(KW):
        part = d_conv if back == 0 else d_conv * live[:, back : back + 1]
        source = ext_ref[pl.ds(HALO - back, rows), columns]
        dtap_ref[KW - 1 - back : KW - back, :] = jnp.sum(part * source, axis=0, keepdims=True)
        pad_ref[pl.ds(HALO, rows), :] = part
        moved = pad_ref[pl.ds(back, rows + HALO), :] * taps[KW - 1 - back : KW - back, :]
        total = moved if total is None else total + moved
    return total


def silu_pull(c, grad):
    s = sigmoid(c)
    return grad * (s + c * s * (1.0 - s))


def unit_pull(act, grad, scale):
    r = unit_rows(act)
    return scale * r * (grad - act * (r * r * jnp.sum(act * grad, axis=-1, keepdims=True)))


def mixer_backward_kernel(
    pre_ref, tq_ref, tk_ref, tv_ref, live_ref, acol_ref, arow_ref,
    inv_ref, delta_ref, state_ref, turn_ref, carry_ref, start_ref, after_ref, dout_ref,
    d_ref, dtq_ref, dtk_ref, dtv_ref, aux_ref,
    ext_ref, pad_ref,
):
    heads = pre_ref.shape[0]
    rows = dout_ref.shape[0]
    width = start_ref.shape[-1]
    blocks = rows // BLOCK
    live = live_ref[...]
    every = [(n, b) for n in range(heads) for b in range(blocks)]
    cut = [slice(b * BLOCK, (b + 1) * BLOCK) for b in range(blocks)]
    conv, act, qb, kb, dout = {}, {}, {}, {}, {}
    for n in range(heads):
        one, two = slice(n * width, (n + 1) * width), slice(2 * n * width, 2 * (n + 1) * width)
        ext_ref[n] = pre_ref[n].astype(F32)
        conv[n] = head_features(ext_ref.at[n], tq_ref[:, one], tk_ref[:, two], tv_ref[:, two], live, rows, width)
        act[n] = [c * sigmoid(c) for c in conv[n][:3]]
        q = (act[n][0] * unit_rows(act[n][0]) * width ** (-0.5)).astype(BF16)
        k = [(a * unit_rows(a)).astype(BF16) for a in act[n][1:]]
        for b in range(blocks):
            qb[n, b] = q[cut[b]]
            kb[n, b] = jnp.concatenate([k[0][cut[b]], k[1][cut[b]]], axis=0)
            dout[n, b] = dout_ref[cut[b], one]
    reach, strict, _, _, _ = step_masks()
    ccol = {at: acol_ref[at[0], at[1], :, 0:1] for at in every}
    bcol = {at: acol_ref[at[0], at[1], :, 1:2] for at in every}
    crow = {at: arow_ref[at[0], at[1], 0:1, :] for at in every}
    last = {at: ccol[at][BLOCK - 1 : BLOCK] for at in every}
    grow = {at: jnp.exp(ccol[at]) for at in every}
    weight = {at: jnp.exp(last[at] - ccol[at]) for at in every}
    ahead = {at: mm(carry_ref[at[0], at[1]], dout[at], TN) for at in every}
    after = {}
    for n in range(heads):
        now = after_ref[n].astype(F32)
        for b in range(blocks - 1, -1, -1):
            after[n, b] = now
            now = jnp.exp(last[n, b]) * now + ahead[n, b] + mm(turn_ref[n, b], now, TN)
    fade = {at: jnp.exp(jnp.where(reach, ccol[at] - crow[at], -1e30)) for at in every}
    delta = {
        at: delta_ref[at[0], at[1], :, :width].astype(F32) + mm(delta_ref[at[0], at[1], :, width:], start_ref[at[0]])
        for at in every
    }
    state = {
        at: state_ref[at[0], at[1], :, :width].astype(F32) + mm(state_ref[at[0], at[1], :, width:], start_ref[at[0]])
        for at in every
    }
    score = {at: fade[at][:BLOCK] * mm(qb[at], kb[at], NT) for at in every}
    d_delta = {at: mm(score[at], dout[at], TN) + weight[at] * mm2t(kb[at], after[at]) for at in every}
    d_rhs = {at: mm2t(inv_ref[at[0], at[1]], d_delta[at], TN) for at in every}
    d_score = {at: (fade[at][:BLOCK] * mm(dout[at], delta[at], NT)).astype(BF16) for at in every}
    d_tail = {at: weight[at] * mm(delta[at], after[at], NT) for at in every}
    d_gram = {
        at: jnp.where(strict, -bcol[at] * fade[at] * mm(d_rhs[at], delta[at], NT), 0.0).astype(BF16) for at in every
    }
    dq = {at: mm(grow[at][:BLOCK] * dout[at], state[at], NT) + mm(d_score[at], kb[at]) for at in every}
    dk_row = {
        at: mm(-(bcol[at] * grow[at]) * d_rhs[at], state[at], NT) + mm(d_gram[at], kb[at]) for at in every
    }
    dk_col = {at: mm(d_gram[at], kb[at], TN) + mm(d_score[at], qb[at], TN) + d_tail[at] for at in every}
    tok = lax.broadcasted_iota(jnp.int32, (BLOCK, 1), 0)
    for at in every:
        kf = kb[at].astype(F32)
        d_beta = (1.0 - bcol[at]) * jnp.sum(d_rhs[at] * delta[at], axis=-1, keepdims=True)
        d_log = jnp.sum(kf * (dk_row[at] - dk_col[at]), axis=-1, keepdims=True)
        d_logq = jnp.sum(qb[at].astype(F32) * dq[at], axis=-1, keepdims=True)
        d_last = jnp.sum(kf * d_tail[at]) + jnp.sum(jnp.exp(last[at]) * after[at] * state[at])
        d_token = d_log[:BLOCK] + d_log[BLOCK:] + d_logq + jnp.where(tok == BLOCK - 1, d_last, 0.0)
        aux_ref[at[0], at[1], :, 0:1] = d_beta
        aux_ref[at[0], at[1], 0:BLOCK, 1:2] = d_token
    pad_ref[0:HALO, :] = jnp.zeros((HALO, width), F32)
    pad_ref[pl.ds(HALO + rows, HALO), :] = jnp.zeros((HALO, width), F32)
    for n in range(heads):
        keys = {b: dk_row[n, b] + dk_col[n, b] for b in range(blocks)}
        values = {b: bcol[n, b] * d_rhs[n, b] for b in range(blocks)}
        d_act = [
            jnp.concatenate([dq[n, b] for b in range(blocks)], axis=0),
            jnp.concatenate([keys[b][:BLOCK] for b in range(blocks)], axis=0),
            jnp.concatenate([keys[b][BLOCK:] for b in range(blocks)], axis=0),
            jnp.concatenate([values[b][:BLOCK] for b in range(blocks)], axis=0),
            jnp.concatenate([values[b][BLOCK:] for b in range(blocks)], axis=0),
        ]
        for i, scale in enumerate((width ** (-0.5), 1.0, 1.0)):
            d_act[i] = unit_pull(act[n][i], d_act[i], scale)
        sides = (
            (tq_ref, dtq_ref, n),
            (tk_ref, dtk_ref, 2 * n),
            (tk_ref, dtk_ref, 2 * n + 1),
            (tv_ref, dtv_ref, 2 * n),
            (tv_ref, dtv_ref, 2 * n + 1),
        )
        for i, (tap_ref, dtap_ref, at) in enumerate(sides):
            lanes = pl.ds(at * width, width)
            grad = conv_pull(
                ext_ref.at[n], pad_ref, silu_pull(conv[n][i], d_act[i]), tap_ref[:, lanes], live,
                pl.ds(i * width, width), rows, dtap_ref.at[:, lanes],
            )
            target = pl.ds((5 * n + i) * width, width)
            d_ref[0:rows, target] = grad[HALO:].astype(BF16)
            d_ref[rows : rows + HALO, target] = grad[:HALO].astype(BF16)


def mixer_backward(pre, taps, live, acol, arow, saved, start, after, dout):
    heads, ext_rows, _ = pre.shape
    rows = ext_rows - HALO
    width = start.shape[-1]
    conv_query, conv_key, conv_value = taps
    out = jax.ShapeDtypeStruct
    columns = heads * width
    group = BACKWARD_HEADS
    tap_specs = [head_columns(KW, times * group * width) for times in (1, 2, 2)]
    return pl.pallas_call(
        mixer_backward_kernel,
        grid=(heads // group,),
        in_specs=[per_head(pre.shape[1:], group)]
        + tap_specs
        + [whole(live.shape)]
        + [per_head(value.shape[1:], group) for value in (acol, arow, *saved, start, after)]
        + [head_columns(rows, group * width)],
        out_specs=[head_columns(ext_rows, 5 * group * width)] + tap_specs + [per_head(acol.shape[1:], group)],
        out_shape=[
            out((ext_rows, 5 * columns), BF16),
            out((KW, columns), F32),
            out((KW, 2 * columns), F32),
            out((KW, 2 * columns), F32),
            out(acol.shape, F32),
        ],
        scratch_shapes=[
            pltpu.VMEM((group, ext_rows, 5 * width), F32),
            pltpu.VMEM((rows + 2 * HALO, width), F32),
        ],
        compiler_params=pltpu.CompilerParams(vmem_limit_bytes=VMEM_LIMIT),
        cost_estimate=cost(35),
        name="mixer_backward",
    )(pre, conv_query, conv_key, conv_value, live, acol, arow, *saved, start, after, dout)


def carry_kernel(count, heads, part_ref, maps_ref, result_ref, inbox, outbox, landed, *sems):
    barrier = greet_group(count)
    pl.semaphore_wait(barrier, count - 1)
    send, scan, take = carry_steps(count, heads, True, part_ref, maps_ref, inbox, outbox, landed, sems)
    for h in range(heads):
        send(h)
    scan()
    take()
    result_ref[...] = landed[...]


def carry_back(part, maps, count):
    heads, width, _ = part.shape
    vmem = pl.BlockSpec(memory_space=pltpu.VMEM)
    return pl.pallas_call(
        partial(carry_kernel, count, heads),
        in_specs=[vmem] * 2,
        out_specs=vmem,
        out_shape=jax.ShapeDtypeStruct((heads, width, width), BF16),
        scratch_shapes=carry_scratch(count, heads, width, width),
        compiler_params=pltpu.CompilerParams(
            collective_id=1, has_side_effects=True, vmem_limit_bytes=VMEM_LIMIT
        ),
        cost_estimate=cost(24),
        name="carry_back",
    )(part, maps)


JOBS = 7
JOB = 512
GROUPS = 3
LATE_JOBS = 10
EARLY_LINKS = ((0, 1, 2, 3), (1, 2, 0, 3), (2, 0, 1, 3))
LATE_LINKS = ((0, 1, 2, 3), (1, 0, 2, 3))


def half_rows(lhs, links, sending, lanes=slice(None)):
    edge = lhs.shape[0] // 8
    parts = []
    for second in range(2):
        for third in range(2):
            move = {links[0]: int(sending), links[1]: second, links[2]: third}
            block = 4 * move[0] + 2 * move[1] + move[2]
            parts.append(lhs[block * edge : (block + 1) * edge, lanes])
    return jnp.concatenate(parts, axis=0)


def column_pieces(sizes, begin, end):
    at, pieces = 0, []
    for index, size in enumerate(sizes):
        low, high = max(at, begin), min(at + size, end)
        if low < high:
            pieces.append((index, low - at, low - begin, high - low))
        at += size
    return pieces


def input_pull_kernel(
    d_ref, dg_ref, wq_ref, wk_ref, wv_ref, wg_ref, aux_ref, raw_ref, live_ref, rate_ref, wr_ref, ext_ref,
    x_ref, halo_ref, gain_ref, resid_ref,
    grad_ref, edge_ref, rim_ref, dgain_ref, drates_ref, misc_ref, total_ref, rates_ref,
):
    head = pl.program_id(0)
    rows = dg_ref.shape[0]
    width = dg_ref.shape[1] // PULL_HEADS
    group = PULL_HEADS
    part = None
    for n in range(group):
        d = d_ref[:, n * 5 * width : (n + 1) * 5 * width]
        two = slice(2 * n * width, 2 * (n + 1) * width)
        term = (
            mm(d[:, :width], wq_ref[:, n * width : (n + 1) * width], NT)
            + mm(d[:, width : 3 * width], wk_ref[:, two], NT)
            + mm(d[:, 3 * width :], wv_ref[:, two], NT)
        )
        part = term if part is None else part + term
    more = mm(dg_ref[...], wg_ref[...], NT)

    @pl.when(head == 0)
    def _():
        heads, blocks = aux_ref.shape[:2]
        wide = heads * REFLECTS
        rates_ref[...] = jnp.zeros_like(rates_ref)
        for h in range(heads):
            for b in range(blocks):
                tokens = slice(b * BLOCK, (b + 1) * BLOCK)
                for j in range(REFLECTS):
                    at = h * REFLECTS + j
                    rates_ref[tokens, at : at + 1] = aux_ref[h, b, j * BLOCK : (j + 1) * BLOCK, 0:1]
                rates_ref[tokens, wide + h : wide + h + 1] = aux_ref[h, b, 0:BLOCK, 1:2]
        value, raw = rates_ref[...], raw_ref[...]
        d_log = exact_sum(block_sums(rows, True), value) * live_ref[:, 1:2]
        lane = lax.broadcasted_iota(jnp.int32, raw.shape, 1)
        d_raw = jnp.where(lane < wide, value, -rate_ref[...] * sigmoid(raw) * d_log)
        summed = jnp.where(lane < wide, value, -softplus(raw) * d_log)
        misc_ref[...] = jnp.sum(summed, axis=0, keepdims=True)
        d_raw = d_raw.astype(BF16)
        drates_ref[...] = mm(d_raw, ext_ref[pl.ds(HALO, rows), :], TN)[: drates_ref.shape[0]]
        total_ref[...] = part
        total_ref[0:rows, :] += more + mm(d_raw, wr_ref[...])

    @pl.when(head > 0)
    def _():
        total_ref[...] += part
        total_ref[0:rows, :] += more

    @pl.when(head == pl.num_programs(0) - 1)
    def _():
        grad = total_ref[...]
        unit, pulled = norm_pull(x_ref[...].astype(F32), gain_ref[...], grad[:rows])
        grad_ref[...] = (resid_ref[...] + pulled).astype(BF16)
        halo_unit, _ = norm_pull(halo_ref[...].astype(F32), gain_ref[...], grad[rows:])
        dgain_ref[...] = jnp.sum(grad[:rows] * unit, axis=0, keepdims=True) + jnp.sum(
            grad[rows:] * halo_unit, axis=0, keepdims=True
        )
        edge_ref[0] = grad[rows - HALO : rows]
        edge_ref[1] = x_ref[rows - HALO :, :].astype(F32)
        edge_ref[2] = resid_ref[rows - HALO :, :]
        rim_ref[...] = grad[rows:]


def norm_pull(x, gain, grad):
    r = lax.rsqrt(jnp.mean(x * x, axis=-1, keepdims=True) + 1e-06)
    unit = x * r
    through = grad * gain
    return unit, r * (through - unit * jnp.mean(unit * through, axis=-1, keepdims=True))


PULL_HEADS = 2


def input_pull(d_all, d_outgate, weights, aux, raw, live, rate, w_rates, ext_b, x, halo, gain, d_resid, heads):
    rows, depth = x.shape
    ext_rows = rows + HALO
    width = d_outgate.shape[1] // heads * PULL_HEADS
    out = jax.ShapeDtypeStruct
    w_query, w_key, w_value, w_outgate = weights
    rates = heads * (REFLECTS + 1)
    return pl.pallas_call(
        input_pull_kernel,
        grid=(heads // PULL_HEADS,),
        in_specs=[
            head_columns(ext_rows, 5 * width),
            head_columns(rows, width),
            head_columns(depth, width),
            head_columns(depth, 2 * width),
            head_columns(depth, 2 * width),
            head_columns(depth, width),
            whole(aux.shape),
            whole(raw.shape),
            whole(live.shape),
            whole(rate.shape),
            whole(w_rates.shape),
            whole(ext_b.shape),
            whole(x.shape),
            whole(halo.shape),
            whole((1, depth)),
            whole(d_resid.shape),
        ],
        out_specs=[
            whole((rows, depth)), whole((3, HALO, depth)), whole((HALO, depth)), whole((1, depth)),
            whole((rates, depth)), whole((1, raw.shape[1])),
        ],
        out_shape=[
            out((rows, depth), BF16),
            out((3, HALO, depth), F32),
            out((HALO, depth), F32),
            out((1, depth), F32),
            out((rates, depth), F32),
            out((1, raw.shape[1]), F32),
        ],
        scratch_shapes=[pltpu.VMEM((ext_rows, depth), F32), pltpu.VMEM(raw.shape, F32)],
        compiler_params=pltpu.CompilerParams(vmem_limit_bytes=VMEM_LIMIT),
        cost_estimate=cost(12),
        name="input_pull",
    )(
        d_all, d_outgate, w_query, w_key, w_value, w_outgate, aux, raw, live, rate, w_rates, ext_b,
        x, halo, gain[None, :], d_resid,
    )


def exact_sum(ones, value):
    total = None
    for _ in range(3):
        part = value.astype(BF16)
        value = value - part.astype(F32)
        term = mm(ones, part)
        total = term if total is None else total + term
    return total


def block_sums(rows, reverse):
    shape = (rows, rows)
    one, two = lax.broadcasted_iota(jnp.int32, shape, 0), lax.broadcasted_iota(jnp.int32, shape, 1)
    order = (one <= two) if reverse else (one >= two)
    return ((one // BLOCK == two // BLOCK) & order).astype(BF16)


def softplus(v):
    return jnp.maximum(v, 0.0) + jnp.log1p(jnp.exp(-jnp.abs(v)))


def rates_kernel(
    heads, lengths_ref, x_ref, gain_ref, wbeta_ref, wdecay_ref, bias_in_ref, rate_in_ref,
    ext_ref, raw_ref, live_ref, acol_ref, arow_ref, halo_ref, weight_ref, rate_ref,
    edge_ref, got_ref, sems,
):
    rows = x_ref.shape[0]
    blocks = rows // BLOCK
    wide = heads * REFLECTS
    seq, count = lax.axis_index("seq"), lax.axis_size("seq")
    behind, before = lax.rem(seq + 1, count), lax.rem(seq + count - 1, count)
    barrier = pltpu.get_barrier_semaphore()
    for place in (behind, before):
        pl.semaphore_signal(barrier, inc=1, device_id={"seq": place}, device_id_type=MESH)
    edge_ref[...] = x_ref[rows - HALO :, :]
    copy = pltpu.make_async_remote_copy(
        src_ref=edge_ref,
        dst_ref=got_ref,
        send_sem=sems.at[0],
        recv_sem=sems.at[1],
        device_id={"seq": behind},
        device_id_type=MESH,
    )

    def normed(field):
        field = field.astype(F32)
        return (
            field * lax.rsqrt(jnp.mean(field * field, axis=-1, keepdims=True) + 1e-06) * gain_ref[...]
        ).astype(BF16)

    pl.semaphore_wait(barrier, 2)
    copy.start()
    xn = normed(x_ref[...])
    ext_ref[pl.ds(HALO, rows), :] = xn
    blank = jnp.zeros((128 - wide - heads, wbeta_ref.shape[1]), F32)
    weight = jnp.concatenate([wbeta_ref[...].astype(F32), wdecay_ref[...].astype(F32), blank], axis=0).astype(BF16)
    weight_ref[...] = weight
    empty = jnp.zeros((1, 128 - wide - heads), F32)
    bias = jnp.concatenate([bias_in_ref[...], jnp.zeros((1, heads), F32), empty], axis=1)
    rate = jnp.concatenate([jnp.zeros((1, wide), F32), rate_in_ref[...], empty], axis=1)
    rate_ref[...] = rate
    raw = mm(xn, weight, NT)
    raw_ref[...] = raw
    row = lax.axis_index("seq") * rows + lax.broadcasted_iota(jnp.int32, (rows, 1), 0)
    place, end = row, 0
    for i in range(lengths_ref.shape[1]):
        begin, end = end, end + lengths_ref[0, i] + (SHORTEST - 1)
        place = jnp.where((row >= begin) & (row < end), row - begin, place)
    live_ref[...] = (place >= lax.broadcasted_iota(jnp.int32, (rows, 8), 1)).astype(F32)
    beta = sigmoid(raw + bias)
    log_rate = jnp.where(place == 0, RESET_LOG, -rate * softplus(raw))
    lane = lax.broadcasted_iota(jnp.int32, raw.shape, 1)
    both = jnp.where(lane < wide, beta, exact_sum(block_sums(rows, False), log_rate))
    turned = both.T
    arow_ref[...] = jnp.zeros_like(arow_ref)
    acol_ref[...] = jnp.zeros_like(acol_ref)
    for h in range(heads):
        for b in range(blocks):
            tokens = slice(b * BLOCK, (b + 1) * BLOCK)
            for j in range(REFLECTS):
                steps = slice(j * BLOCK, (j + 1) * BLOCK)
                at = h * REFLECTS + j
                acol_ref[h, b, steps, 0:1] = both[tokens, wide + h : wide + h + 1]
                acol_ref[h, b, steps, 1:2] = both[tokens, at : at + 1]
                arow_ref[h, b, 0:1, steps] = turned[wide + h : wide + h + 1, tokens]
                arow_ref[h, b, 1:2, steps] = turned[at : at + 1, tokens]
    copy.wait()
    halo = jnp.where(seq > 0, got_ref[...].astype(F32), 0.0)
    halo_ref[...] = halo.astype(BF16)
    ext_ref[0:HALO, :] = normed(halo)


def rates_forward(lengths, x, gain, w_beta, w_decay, bias, rate, heads):
    rows, depth = x.shape
    blocks = rows // BLOCK
    out = jax.ShapeDtypeStruct
    vmem = pl.BlockSpec(memory_space=pltpu.VMEM)
    return pl.pallas_call(
        partial(rates_kernel, heads),
        in_specs=[pl.BlockSpec(memory_space=pltpu.SMEM)] + [vmem] * 6,
        out_specs=[vmem] * 8,
        out_shape=[
            out((rows + HALO, depth), BF16),
            out((rows, 128), F32),
            out((rows, 8), F32),
            out((heads, blocks, STEPS, 8), F32),
            out((heads, blocks, 8, STEPS), F32),
            out((HALO, depth), BF16),
            out((128, depth), BF16),
            out((1, 128), F32),
        ],
        scratch_shapes=[
            pltpu.VMEM((HALO, depth), BF16), pltpu.VMEM((HALO, depth), BF16), pltpu.SemaphoreType.DMA((2,)),
        ],
        compiler_params=pltpu.CompilerParams(
            collective_id=4, has_side_effects=True, vmem_limit_bytes=VMEM_LIMIT
        ),
        cost_estimate=cost(6),
        name="rates_forward",
    )(lengths, x, gain[None, :], w_beta.T, w_decay.T, bias[None, :], rate[None, :])


CHUNK = 256
RING = 6


def flip(bit, other):
    return bit + other - 2 * bit * other


def relative_source(depth):
    block = depth // 32
    seq, group = lax.axis_index("seq"), lax.axis_index("dp")
    index = lax.broadcasted_iota(jnp.int32, (depth, 1), 0)
    row, place, side = index % block, (index // block) % 16, index // (16 * block)
    x = flip(seq % 2, place // 8)
    y = flip((seq // 2) % 2, (place // 4) % 2)
    z = flip((seq // 4) % 2, (place // 2) % 2) + 2 * flip(seq // 8, place % 2)
    return ((((group + side) % 2) * 16 + z * 4 + y * 2 + x) * block + row)


def middle_kernel(
    compact, count, oloc_ref, oread_ref, start_ref, gate_ref, ogain_ref, x_ref, ext_ref, mgain_ref, ograd_ref,
    maps_ref, wout_hbm, wgate_hbm, wup_hbm, wdown_hbm,
    block_ref, dout_ref, part_ref, dresid_ref, dmgain_ref, dogain_ref,
    *refs,
):
    if compact:
        products, (own_out, got_out, after_ref) = refs[: 2 * GROUPS], refs[2 * GROUPS : 2 * GROUPS + 3]
        refs = refs[2 * GROUPS + 3 :]
        gated_ref, hidden_ref, dgate_ref, dup_ref, doutgate_ref, mlp_ref, branch_ref = refs[:7]
        gated_got, hidden_got, dgate_got, dup_got, doutgate_got, own_ref, other_ref, got_ref = refs[7:15]
        other_edge, got_edge, core_sem, chunk_sem, inbox, outbox, landed = refs[15:22]
        carry_sems, staged, stage_sem, refs = refs[22:26], refs[26 : 26 + 2 * GROUPS], refs[26 + 2 * GROUPS], refs[27 + 2 * GROUPS :]
    else:
        gated_ref, hidden_ref, dgate_ref, dup_ref, doutgate_ref, mlp_ref, branch_ref = refs[:7]
        refs = refs[7:]
    wout, wgate, wup, wdown, down_ref, dmlp_ref, sem_out, sems = refs
    heads, rows, width = oread_ref.shape
    depth = x_ref.shape[1]
    chunks = hidden_ref.shape[1] // CHUNK
    fetch_out = pltpu.make_async_copy(wout_hbm, wout, sem_out)
    fetch_out.start()

    def lanes_of(c):
        return pl.ds(pl.multiple_of(c * CHUNK, CHUNK), CHUNK)

    def fetches(c):
        slot = c % RING
        return (
            pltpu.make_async_copy(wgate_hbm.at[:, lanes_of(c)], wgate.at[slot], sems.at[slot, 0]),
            pltpu.make_async_copy(wup_hbm.at[:, lanes_of(c)], wup.at[slot], sems.at[slot, 1]),
            pltpu.make_async_copy(wdown_hbm.at[lanes_of(c), :], wdown.at[slot], sems.at[slot, 2]),
        )

    for c in range(RING):
        for copy in fetches(c):
            copy.start()
    core = {"dp": 1 - lax.axis_index("dp")}

    def to_core(source, target, sems, index):
        return pltpu.make_async_remote_copy(
            src_ref=source,
            dst_ref=target,
            send_sem=sems.at[(0,) + index],
            recv_sem=sems.at[(1,) + index],
            device_id=core,
            device_id_type=MESH,
        )

    if compact:
        barrier = greet_group(count)
        pl.semaphore_signal(barrier, inc=1, device_id=core, device_id_type=MESH)
        give, scan, take = carry_steps(
            count, heads, True, part_ref, maps_ref, inbox, outbox, landed, carry_sems
        )
        half = depth // 2
        lane = lax.broadcasted_iota(jnp.int32, (depth, depth), 1)
        chosen = (lane == relative_source(depth)).astype(BF16)
        swaps = []

        def turn(at, value, index):
            turned = mm(chosen, value, NT).astype(BF16)
            cut = slice(at, at + value.shape[0])
            own_ref[:, cut] = turned[:half]
            other_ref[:, cut] = turned[half:]
            swap(other_ref.at[:, cut], got_ref.at[:, cut], index)

        def turn_tokens():
            value = jnp.concatenate([ext_ref[pl.ds(HALO, rows), :], ext_ref[0:HALO, :]], axis=0)
            turned = mm(chosen, value, NT).astype(BF16)
            own_out[...] = turned[:half]
            other_edge[...] = turned[half:]
            swap(other_edge, got_edge, 3)

        def swap(source, target, index):
            swaps.append(to_core(source, target, core_sem, (index,)))
            swaps[-1].start()

    ogain = ogain_ref[...]
    for h in range(heads):
        lanes = slice(h * width, (h + 1) * width)
        out = oloc_ref[:, lanes] + mm(oread_ref[h], start_ref[h])
        dout_ref[:, lanes] = out
        gate = gate_ref[:, lanes]
        r = lax.rsqrt(jnp.mean(out * out, axis=-1, keepdims=True) + 1e-05)
        gated_ref[:, lanes] = (out * r * ogain * (gate * sigmoid(gate))).astype(BF16)
    fetch_out.wait()
    resid = x_ref[...].astype(F32) + mm(gated_ref[...], wout[...])
    dresid_ref[...] = resid
    r = lax.rsqrt(jnp.mean(resid * resid, axis=-1, keepdims=True) + 1e-06)
    mlp_ref[...] = (resid * r * mgain_ref[...]).astype(BF16)
    if compact:
        pl.semaphore_wait(barrier, count)
        swap(gated_ref, gated_got, 4)
    down_ref[...] = jnp.zeros_like(down_ref)
    dmlp_ref[...] = jnp.zeros_like(dmlp_ref)

    def chunk_swaps(c):
        pairs = ((hidden_ref, hidden_got), (dgate_ref, dgate_got), (dup_ref, dup_got))
        return [
            to_core(own.at[:, lanes_of(c)], got.at[:, lanes_of(c)], chunk_sem, (c, i))
            for i, (own, got) in enumerate(pairs)
        ]

    def one(c, carry):
        slot = c % RING
        for copy in fetches(c):
            copy.wait()
        mlp, ograd = mlp_ref[...], ograd_ref[...]
        lanes = lanes_of(c)
        gate, up = mm(mlp, wgate[slot]), mm(mlp, wup[slot])
        d_hidden = mm(ograd, wdown[slot], NT)
        s = sigmoid(gate)
        act = gate * s
        hidden = (act * up).astype(BF16)
        d_gate = (d_hidden * up * (s + act * (1.0 - s))).astype(BF16)
        d_up = (d_hidden * act).astype(BF16)
        hidden_ref[:, lanes] = hidden
        dgate_ref[:, lanes] = d_gate
        dup_ref[:, lanes] = d_up
        if compact:
            for copy in chunk_swaps(c):
                copy.start()
        down_ref[...] += mm(hidden, wdown[slot])
        dmlp_ref[...] += mm(d_gate, wgate[slot], NT) + mm(d_up, wup[slot], NT)

        @pl.when(c + RING < chunks)
        def _():
            for copy in fetches(c + RING):
                copy.start()

        return carry

    lax.fori_loop(0, chunks, one, 0)
    resid = dresid_ref[...]
    block_ref[...] = (resid + down_ref[...]).astype(BF16)
    grad = dmlp_ref[...]
    unit, pulled = norm_pull(resid, mgain_ref[...], grad)
    dmgain_ref[...] = jnp.sum(grad * unit, axis=0, keepdims=True)
    d_resid = ograd_ref[...].astype(F32) + pulled
    dresid_ref[...] = d_resid
    branch_ref[...] = d_resid.astype(BF16)
    dogain = jnp.zeros((1, width), F32)
    for h in range(heads):
        lanes = slice(h * width, (h + 1) * width)
        grad = mm(branch_ref[...], wout[lanes, :], NT)
        out = dout_ref[:, lanes]
        gate = gate_ref[:, lanes]
        r = lax.rsqrt(jnp.mean(out * out, axis=-1, keepdims=True) + 1e-05)
        s = sigmoid(gate)
        unit = out * r
        doutgate_ref[:, lanes] = (grad * unit * ogain * (s + gate * s * (1.0 - s))).astype(BF16)
        through = grad * (gate * s)
        dogain += jnp.sum(through * unit, axis=0, keepdims=True)
        through = through * ogain
        dout = r * (through - unit * jnp.mean(unit * through, axis=-1, keepdims=True))
        dout_ref[:, lanes] = dout
        part_ref[h] = mm(oread_ref[h], dout, TN).astype(BF16)
        if compact:
            give(h)
    dogain_ref[...] = dogain
    if compact:
        turn(0, mlp_ref[...], 0)
        turn(rows, ograd_ref[...], 1)
        swap(doutgate_ref, doutgate_got, 5)
        turn(2 * rows, branch_ref[...], 2)
        turn_tokens()

        def arrived(c, carry):
            for copy in chunk_swaps(c):
                copy.wait()
            return carry

        lax.fori_loop(0, chunks, arrived, 0)
        rhs_own = (dgate_ref, dup_ref, hidden_ref, gated_ref, doutgate_ref)
        rhs_got = (dgate_got, dup_got, hidden_got, gated_got, doutgate_got)
        for copy in swaps[:3]:
            copy.wait()
        lhs_own, lhs_got = (own_ref, own_out), (got_ref, got_edge)
        targets = [staged[2 * group : 2 * group + 2] for group in range(GROUPS)]
        early_products(lhs_own, lhs_got, rhs_own, rhs_got, targets, (0, 1, 2))
        outgoing = [
            pltpu.make_async_copy(source, target, stage_sem.at[i])
            for i, (source, target) in enumerate(zip(staged, products))
        ]
        for copy in outgoing[: 2 * GROUPS - 2]:
            copy.start()
        scan()
        for copy in swaps[3:]:
            copy.wait()
        early_products(lhs_own, lhs_got, rhs_own, rhs_got, targets, (3, 4))
        for copy in outgoing[2 * GROUPS - 2 :]:
            copy.start()
        got_out[...] = got_edge[...]
        for copy in outgoing:
            copy.wait()
        take()
        after_ref[...] = landed[...]


def early_products(lhs_own, lhs_got, rhs_own, rhs_got, targets, which):
    tokens = rhs_own[0].shape[0]
    sizes = [rhs.shape[1] for rhs in rhs_own]
    sides = (0, 0, 1, 2, 3)
    for group in range(GROUPS):
        for sending in (True, False):
            turned = {}
            for job in range(JOBS):
                begin = (group * JOBS + job) * JOB
                for index, column, offset, width in column_pieces(sizes, begin, begin + JOB):
                    if index not in which:
                        continue
                    side = sides[index]
                    if side not in turned:
                        cut = slice(side % 3 * tokens, (side % 3 + 1) * tokens)
                        turned[side] = [
                            half_rows(lhs[side // 3], EARLY_LINKS[group], sending, cut) for lhs in (lhs_own, lhs_got)
                        ]
                    lanes = slice(column, column + width)
                    total = mm(turned[side][0], rhs_own[index][:, lanes]) + mm(
                        turned[side][1], rhs_got[index][:, lanes]
                    )
                    targets[group][0 if sending else 1][job, :, offset : offset + width] = total.astype(BF16)


def middle(
    compact, count, oloc, oread, start, gate_pre, out_gain, x, ext_b, mlp_gain, out_grad, maps,
    w_out, w_gate, w_up, w_down,
):
    heads, rows, width = oread.shape
    depth = x.shape[1]
    ff = w_gate.shape[1]
    out = jax.ShapeDtypeStruct
    vmem, hbm = pl.BlockSpec(memory_space=pltpu.VMEM), pl.BlockSpec(memory_space=pl.ANY)
    columns = heads * width
    chunks = ff // CHUNK
    half = depth // 2
    outs = [
        ((rows, depth), BF16), ((rows, columns), F32), ((heads, width, width), BF16), ((rows, depth), F32),
        ((1, depth), F32), ((1, width), F32),
    ]
    rhs = [((rows, columns), BF16)] + [((rows, ff), BF16)] * 3 + [((rows, columns), BF16)]
    kept = rhs + [((rows, depth), BF16)] * 2
    scratch = []
    dma = pltpu.SemaphoreType.DMA
    if compact:
        product = ((JOBS, half // 2, JOB), BF16)
        outs += [product] * (2 * GROUPS) + [((half, rows + HALO), BF16)] * 2
        outs += [((heads, width, width), BF16), ((rows, columns), BF16)]
        buffers = kept[:4] + kept[5:] + rhs + [((half, 3 * rows), BF16)] * 3 + [((half, rows + HALO), BF16)] * 2
        scratch += [pltpu.VMEM(*buffer) for buffer in buffers] + [dma((2, 6)), dma((2, chunks, 3))]
        scratch += carry_scratch(count, heads, width, width)
        scratch += [pltpu.VMEM(*product)] * (2 * GROUPS) + [dma((2 * GROUPS,))]
    else:
        outs += kept
    scratch += [
        pltpu.VMEM(w_out.shape, BF16),
        pltpu.VMEM((RING, depth, CHUNK), BF16),
        pltpu.VMEM((RING, depth, CHUNK), BF16),
        pltpu.VMEM((RING, CHUNK, depth), BF16),
        pltpu.VMEM((rows, depth), F32),
        pltpu.VMEM((rows, depth), F32),
        dma,
        dma((RING, 3)),
    ]

    def kernel(*refs):
        if not compact:
            middle_kernel(compact, count, *refs)
            return
        late = 20 + 2 * GROUPS + 3
        rest = refs[late + 1 :]
        middle_kernel(compact, count, *refs[:late], *rest[:4], refs[late], *rest[4:])

    params = {"collective_id": 3, "has_side_effects": True} if compact else {}
    return pl.pallas_call(
        kernel,
        in_specs=[vmem] * 10 + [hbm] * 4,
        out_specs=[hbm if compact and shape == product else vmem for shape in outs],
        out_shape=[out(*shape) for shape in outs],
        scratch_shapes=scratch,
        compiler_params=pltpu.CompilerParams(vmem_limit_bytes=VMEM_LIMIT, **params),
        cost_estimate=cost(30),
        name="middle",
    )(
        oloc, oread, start, gate_pre, out_gain[None, :], x, ext_b, mlp_gain[None, :], out_grad, maps,
        w_out, w_gate, w_up, w_down,
    )


def reduce_kernel(
    heads, arr_a, arr_b, arr_c, keep_a, keep_b, keep_c, own_ref, got_ref, rhs_ref, tq_ref, tk_ref, tv_ref, attn_ref, mlp_ref, ogain_ref,
    misc_ref, rates_ref, edge_ref, rim_ref, again_ref,
    gate_out, up_out, down_out, out_out, outgate_out, q_out, k_out, v_out, tq_out, tk_out, tv_out, rest_out,
    edge_out,
    fetched, e_keep, e_send, e_got2, e_got3, e_got4,
    rhs_got, lhs_ref, l_first, l_send, l_keep, l_got1, l_got2, l_got3, l_got4, small_sum, small_got, rim_got,
    dp_sem, e_sem, l_sem, s_sem, f_sem,
):
    seq = lax.axis_index("seq")
    group = lax.axis_index("dp")
    count = lax.axis_size("seq")
    x, y, z = seq % 2, (seq // 2) % 2, seq // 4
    near = (seq + 1 - 2 * x, seq + 2 - 4 * y)
    low_z = seq + 4 - 8 * (z % 2)
    high_z = seq + 8 - 16 * (z // 2)

    def at(place):
        return {"dp": group, "seq": place}

    core = {"dp": 1 - group, "seq": seq}
    before, behind = lax.rem(seq + count - 1, count), lax.rem(seq + 1, count)

    def send(source, target, sems, index, device):
        return pltpu.make_async_remote_copy(
            src_ref=source,
            dst_ref=target,
            send_sem=sems.at[(0,) + index],
            recv_sem=sems.at[(1,) + index],
            device_id=device,
            device_id_type=MESH,
        )

    def fetches(i):
        return [
            pltpu.make_async_copy(source.at[i], fetched.at[j, i], f_sem.at[j, i])
            for j, source in enumerate((arr_a, arr_b, arr_c, keep_a, keep_b, keep_c))
        ]

    def fetch(i, carry):
        for copy in fetches(i):
            copy.start()
        return carry

    lax.fori_loop(0, JOBS, fetch, 0)
    barrier = pltpu.get_barrier_semaphore()
    everyone = [core] + [at(place) for place in (near[0], near[1], low_z, high_z, before, behind)]
    for device in everyone:
        pl.semaphore_signal(barrier, inc=1, device_id=device, device_id_type=MESH)
    rim = send(rim_ref, rim_got, dp_sem, (1,), at(before))
    hops = [core, at(high_z), at(low_z), at(near[0]), at(near[1])]

    def hop(step):
        return send(small_sum.at[step], small_got.at[step], s_sem, (step,), hops[step])

    def next_hop(step):
        hop(step - 1).wait_recv()
        small_sum[step] = small_sum[step - 1] + small_got[step - 1]
        if step < len(hops):
            hop(step).start()

    depth = tq_ref.shape[1]
    small_sum[0, 0:KW] = tq_ref[...]
    for half in range(2):
        lanes = pl.ds(half * depth, depth)
        small_sum[0, KW * (1 + half) : KW * (2 + half)] = tk_ref[:, lanes]
        small_sum[0, KW * (3 + half) : KW * (4 + half)] = tv_ref[:, lanes]
    small_sum[0, 5 * KW : 6 * KW] = jnp.zeros((KW, depth), F32)
    small_sum[0, 5 * KW : 5 * KW + 1] = attn_ref[...]
    small_sum[0, 5 * KW + 1 : 5 * KW + 2] = mlp_ref[...]
    gains = ogain_ref.shape[1]
    small_sum[0, 5 * KW + 2 : 5 * KW + 3, 0:gains] = ogain_ref[...]
    small_sum[0, 5 * KW + 2 : 5 * KW + 3, gains : gains + misc_ref.shape[1]] = misc_ref[...]
    small_sum[0, 6 * KW :] = rates_ref[...]
    for p in range(2):
        for side, lhs in enumerate((own_ref, got_ref)):
            for sending in range(2):
                lhs_ref[p, side, sending] = half_rows(lhs[...], LATE_LINKS[p], sending)
    swap = send(rhs_ref, rhs_got, dp_sem, (0,), core)
    pl.semaphore_wait(barrier, len(everyone))
    hop(0).start()
    swap.start()
    rim.start()

    places = (near[0], near[1], low_z, high_z)
    quarter = e_got2.shape[2]
    eighth, share = quarter // 2, quarter // 4

    def exchange(p, i, stage, sent, got, sems, links):
        begin = (0, 0, quarter, quarter + eighth)[stage]
        target = places[links[p][stage]]
        return send(sent.at[p, i, pl.ds(begin, got.shape[2])], got.at[p, i], sems, (p, i, stage), at(target))

    def early(p, i, stage):
        return exchange(p, i, stage, e_send, (None, e_got2, e_got3, e_got4)[stage], e_sem, EARLY_LINKS)

    def late(p, i, stage):
        sent = l_first if stage == 0 else l_send
        return exchange(p, i, stage, sent, (l_got1, l_got2, l_got3, l_got4)[stage], l_sem, LATE_LINKS)

    def early2(i, carry):
        for copy in fetches(i):
            copy.wait()
        for p in range(GROUPS):
            total = fetched[p, i].astype(F32) + fetched[GROUPS + p, i].astype(F32)
            e_keep[p, i] = total[:quarter].astype(BF16)
            e_send[p, i, 0:quarter] = total[quarter:].astype(BF16)
            early(p, i, 1).start()
        return carry

    def onward(p, i, copy_of, keep, sent, got, stage, begin):
        copy_of(p, i, stage).wait_recv()
        rows = got.shape[2]
        half = rows // 2
        total = keep[p, i, 0:rows].astype(F32) + got[p, i].astype(F32)
        keep[p, i, 0:half] = total[:half].astype(BF16)
        sent[p, i, begin : begin + half] = total[half:].astype(BF16)
        copy_of(p, i, stage + 1).start()

    def later(i, carry, copy_of, keep, sent, got, stage, begin):
        for p in range(keep.shape[0]):
            onward(p, i, copy_of, keep, sent, got, stage, begin)
        return carry

    lax.fori_loop(0, JOBS, early2, 0)
    next_hop(1)
    swap.wait_recv()
    job = l_got1.shape[-1]
    late_jobs = LATE_JOBS // 2
    tokens = rhs_ref.shape[0]

    def product(m, p, sending):
        lanes = pl.ds(pl.multiple_of(m * job, job), job)
        total = mm(lhs_ref[p, 0, int(sending)], rhs_ref[:, lanes]) + mm(
            lhs_ref[p, 1, int(sending)], rhs_got[:, lanes]
        )
        return total[:quarter], total[quarter:]

    def late1(i, carry):
        for p in range(2):
            low, high = product(2 * i + p, p, True)
            l_first[p, i, 0:quarter] = low.astype(BF16)
            l_first[p, i, quarter : 2 * quarter] = high.astype(BF16)
            late(p, i, 0).start()
        return carry

    def late2(i, carry):
        for p in range(2):
            low, high = product(2 * i + p, p, False)
            late(p, i, 0).wait_recv()
            l_keep[p, i] = (low + l_got1[p, i, 0:quarter].astype(F32)).astype(BF16)
            l_send[p, i, 0:quarter] = (high + l_got1[p, i, quarter : 2 * quarter].astype(F32)).astype(BF16)
            late(p, i, 1).start()
        return carry

    lag = JOBS - late_jobs

    def low_turn(i, carry):
        later(i, carry, early, e_keep, e_send, e_got2, 1, quarter)

        @pl.when(i == lag)
        def _():
            next_hop(2)

        @pl.when(i >= lag)
        def _():
            late1(i - lag, carry)

        return carry

    def high_turn(i, carry):
        later(i, carry, early, e_keep, e_send, e_got3, 2, quarter + eighth)

        @pl.when(i >= lag)
        def _():
            late2(i - lag, carry)

        return carry

    lax.fori_loop(0, JOBS, low_turn, 0)
    next_hop(3)
    lax.fori_loop(0, JOBS, high_turn, 0)
    next_hop(4)
    rim.wait_recv()
    inside = (seq < count - 1).astype(F32)
    _, pulled = norm_pull(edge_ref[1], again_ref[...], edge_ref[0] + inside * rim_got[...])
    edge_out[...] = (edge_ref[2] + pulled).astype(BF16)
    late_low = partial(later, copy_of=late, keep=l_keep, sent=l_send, got=l_got2, stage=1, begin=quarter)
    lax.fori_loop(0, late_jobs, late_low, 0)
    next_hop(5)
    late_high = partial(later, copy_of=late, keep=l_keep, sent=l_send, got=l_got3, stage=2, begin=quarter + eighth)
    lax.fori_loop(0, late_jobs, late_high, 0)
    early_outs = (gate_out, up_out, down_out, out_out, outgate_out)
    for i in range(JOBS):
        for p in range(GROUPS):
            early(p, i, 3).wait_recv()
            total = e_keep[p, i, 0:share].astype(F32) + e_got4[p, i].astype(F32)
            first = (p * JOBS + i) * JOB
            for output, to, begin, width in column_pieces([o.shape[1] for o in early_outs], first, first + JOB):
                early_outs[output][:, to : to + width] = total[:, begin : begin + width]
    tq_out[...] = small_sum[5, 0:KW]
    for half in range(2):
        lanes = pl.ds(half * depth, depth)
        tk_out[:, lanes] = small_sum[5, KW * (1 + half) : KW * (2 + half)]
        tv_out[:, lanes] = small_sum[5, KW * (3 + half) : KW * (4 + half)]
    rest_out[...] = small_sum[5, 5 * KW :]
    width = q_out.shape[1] // heads
    for i in range(late_jobs):
        for p in range(2):
            late(p, i, 3).wait_recv()
            total = l_keep[p, i, 0:share].astype(F32) + l_got4[p, i].astype(F32)
            for begin in range(0, job, width):
                head, part = divmod(((2 * i + p) * job + begin) // width, 5)
                if part == 0:
                    target, to = q_out, head * width
                else:
                    target, to = (k_out, v_out)[(part - 1) // 2], (2 * head + (part - 1) % 2) * width
                target[:, to : to + width] = total[:, begin : begin + width]

    def early_sent(i, carry):
        for p in range(GROUPS):
            for stage in (1, 2, 3):
                early(p, i, stage).wait_send()
        return carry

    def late_sent(i, carry):
        for p in range(2):
            for stage in (0, 1, 2, 3):
                late(p, i, stage).wait_send()
        return carry

    lax.fori_loop(0, JOBS, early_sent, 0)
    lax.fori_loop(0, late_jobs, late_sent, 0)
    swap.wait_send()
    rim.wait_send()
    for step in range(len(hops)):
        hop(step).wait_send()


def reduce_all(arrived, kept, own, got, rhs, taps, gains, rates, edge, rim, gain, ff, heads):
    half = own.shape[0] // 2
    quarter, eighth, share = half // 2, half // 4, half // 8
    count = LATE_JOBS // 2
    columns = rhs.shape[1] // 5
    job = rhs.shape[1] // LATE_JOBS
    depth = rates.shape[1]
    small_rows = 6 * KW + rates.shape[0]
    out = jax.ShapeDtypeStruct
    vmem = pl.BlockSpec(memory_space=pltpu.VMEM)

    def stages(groups, jobs, width):
        return [((groups, jobs, rows, width), BF16) for rows in (quarter, eighth, share)]

    buffers = [((2 * GROUPS, JOBS, half, JOB), BF16)]
    buffers += [((GROUPS, JOBS, quarter, JOB), BF16), ((GROUPS, JOBS, half, JOB), BF16)]
    buffers += stages(GROUPS, JOBS, JOB)
    buffers += [(rhs.shape, BF16), ((2, 2, 2, half, own.shape[1]), BF16)] + [((2, count, half, job), BF16)] * 2 + [((2, count, quarter, job), BF16)]
    buffers += [((2, count, half, job), BF16)] + stages(2, count, job)
    buffers += [((6, small_rows, depth), F32), ((5, small_rows, depth), F32), (rim.shape, F32)]
    dma = pltpu.SemaphoreType.DMA
    shapes = [(share, ff)] * 3 + [(share, columns)] * 3 + [(share, 2 * columns)] * 2
    shapes += [tap.shape for tap in taps] + [(small_rows - 5 * KW, depth)]
    return pl.pallas_call(
        partial(reduce_kernel, heads),
        in_specs=[pl.BlockSpec(memory_space=pl.ANY)] * (2 * GROUPS) + [vmem] * 14,
        out_specs=[vmem] * 13,
        out_shape=[out(shape, F32) for shape in shapes] + [out(rim.shape, BF16)],
        scratch_shapes=[pltpu.VMEM(shape, kind) for shape, kind in buffers]
        + [dma((2, 2)), dma((2, GROUPS, JOBS, 4)), dma((2, 2, count, 4)), dma((2, 5)), dma((2 * GROUPS, JOBS))],
        compiler_params=pltpu.CompilerParams(
            collective_id=2, has_side_effects=True, vmem_limit_bytes=VMEM_LIMIT
        ),
        cost_estimate=cost(90),
        name="reduce_all",
    )(*arrived, *kept, own, got, rhs, *taps, *gains, rates, edge, rim, gain)


def finish_kernel(marks, grad_ref, edge_ref, rest_ref, *refs):
    count = (len(refs) - 8) // 2
    sources, (grad_out, *outs) = refs[:count], refs[count:]
    rows = grad_ref.shape[0]
    grad_out[0 : rows - HALO, :] = grad_ref[0 : rows - HALO, :]
    grad_out[rows - HALO :, :] = edge_ref[...]
    for source, target in zip(sources, outs):
        target[...] = source[...]
    again, mlp, beta, rate, gain, bias, decay = outs[count:]
    rest = rest_ref[...]
    share, depth = again.shape[1], rest.shape[1]
    place = lax.axis_index("dp") * lax.axis_size("seq") + lax.axis_index("seq")
    own = pltpu.roll(rest, lax.rem(depth - place * share, depth), 1)[:, :share]
    again[...] = own[0:1]
    mlp[...] = own[1:2]
    beta[...] = own[4 : 4 + beta.shape[0]]
    rate[...] = own[4 + beta.shape[0] :]
    for target, begin in zip((gain, bias, decay), marks):
        target[...] = rest_ref[2:3, begin : begin + target.shape[1]]


def finish(input_grad, edge_grad, rest, values, share, width, heads):
    wide, narrow = heads * REFLECTS, heads
    shapes = [value.shape for value in values]
    shapes += [(1, share)] * 2 + [(wide, share), (narrow, share), (1, width), (1, wide), (1, narrow)]
    out = jax.ShapeDtypeStruct
    vmem = pl.BlockSpec(memory_space=pltpu.VMEM)
    return pl.pallas_call(
        partial(finish_kernel, (0, width, width + wide)),
        in_specs=[vmem] * (3 + len(values)),
        out_specs=[vmem] * (1 + len(shapes)),
        out_shape=[out(input_grad.shape, BF16)] + [out(shape, F32) for shape in shapes],
        compiler_params=pltpu.CompilerParams(vmem_limit_bytes=VMEM_LIMIT),
        cost_estimate=cost(3),
        name="finish",
    )(input_grad, edge_grad, rest, *values)


def dot32(a, b, dims=NN):
    return lax.dot_general(a, b, dims, preferred_element_type=F32)


def swap_core(value):
    count = lax.axis_size("dp")
    return lax.ppermute(value, "dp", [(i, (i + 1) % count) for i in range(count)])


def neighbour_route(bit):
    return [(i, i ^ bit) for i in range(16)]


def by_head(field, heads, begin, size):
    rows = field.shape[0]
    return field.reshape(rows, heads, -1)[:, :, begin : begin + size].reshape(rows, heads * size)


def per_device(
    block_input, lengths, attn_gain, w_query, w_key, w_value, w_outgate, w_beta, w_decay, beta_bias,
    decay_rate, conv_query, conv_key, conv_value, out_gain, w_out, mlp_gain, w_gate, w_up, w_down,
    out_grad,
):
    rows, depth = block_input.shape
    heads = decay_rate.shape[0]
    width = out_gain.shape[0]
    count = lax.axis_size("seq")
    seq = lax.axis_index("seq")
    group = lax.axis_index("dp")
    compact = count == 16
    wide = heads * REFLECTS
    ext_b, raw, live, acol, arow, halo, w_rates, rate = rates_forward(
        lengths, block_input, attn_gain, w_beta, w_decay, beta_bias, decay_rate, heads
    )
    taps = (conv_query, conv_key, conv_value)
    pre, gate_pre, oloc, oread, *saved, start, all_maps = mixer_forward(
        ext_b, w_query, w_key, w_value, w_outgate, taps, live, acol, arow, heads, width, count
    )
    block_output, d_out, part, d_resid, grad_mlp_gain, grad_out_gain, *rest = middle(
        compact, count, oloc, oread, start, gate_pre, out_gain, block_input, ext_b, mlp_gain, out_grad,
        all_maps, w_out, w_gate, w_up, w_down,
    )
    if compact:
        products, (own_l, got_l, after, d_outgate_b) = rest[: 2 * GROUPS], rest[2 * GROUPS :]
        arrived = [
            lax.ppermute(sent, "seq", neighbour_route(1 << links[0])) for sent, links in zip(products[::2], EARLY_LINKS)
        ]
    else:
        gated_b, hidden_b, d_gate_b, d_up_b, d_outgate_b, mlp_b, d_branch_b = rest
        after = carry_back(part, all_maps, count)
    d_all, d_tap_q, d_tap_k, d_tap_v, aux = mixer_backward(
        pre, taps, live, acol, arow, saved, start, after, d_out
    )
    input_grad, edge, rim, grad_attn_gain, grad_rates, misc = input_pull(
        d_all, d_outgate_b, (w_query, w_key, w_value, w_outgate), aux, raw, live, rate, w_rates, ext_b,
        block_input, halo, attn_gain, d_resid, heads,
    )
    last = width + wide + heads
    gains = (grad_attn_gain, grad_mlp_gain, grad_out_gain, misc)
    d_taps = (d_tap_q, d_tap_k, d_tap_v)
    devices = count * lax.axis_size("dp")
    share = depth // devices
    if compact:
        sums = reduce_all(
            arrived, products[1::2], own_l, got_l, d_all, d_taps, gains, grad_rates,
            edge, rim, attn_gain[None, :], w_gate.shape[1], heads,
        )
        trunk, taps_out, rest, edge_grad = sums[5:8], sums[8:11], sums[11], sums[12]
    else:
        normed_e = jnp.concatenate([ext_b[HALO:], ext_b[:HALO]], axis=0)
        normed_b = ext_b[HALO:]
        xf = block_input.astype(F32)
        tail = edge[0] + lax.ppermute(rim, "seq", [(i, i - 1) for i in range(1, count)])
        _, pulled = norm_pull(edge[1], attn_gain[None, :], tail)
        edge_grad = (edge[2] + pulled).astype(BF16)
        line = jnp.pad(jnp.concatenate(gains[2:], axis=1), ((0, 0), (0, depth - width - 128)))
        line = jnp.concatenate([*gains[:2], line, jnp.zeros((1, depth), F32)], axis=0)
        small = lax.psum(d_taps + (line, grad_rates), ("dp", "seq"))
        taps_out, rest = small[:3], jnp.concatenate(small[3:], axis=0)
        trunk = [by_head(d_all, heads, begin * width, size * width) for begin, size in ((0, 1), (1, 2), (3, 2))]
        pairs = zip(
            (mlp_b, mlp_b, out_grad, d_branch_b, normed_b) + (normed_e,) * 3, (d_gate_b, d_up_b, hidden_b, gated_b, d_outgate_b) + tuple(trunk)
        )
        sums = [
            lax.psum_scatter(dot32(lhs, rhs, TN), ("dp", "seq"), scatter_dimension=0, tiled=True)
            for lhs, rhs in pairs
        ]
        trunk = sums[5:]
    values = (*trunk, sums[4], *taps_out, sums[0], sums[1], sums[3], sums[2])
    done = finish(input_grad, edge_grad, rest, values, share, width, heads)
    (
        input_grad, g_query, g_key, g_value, g_outgate, g_conv_q, g_conv_k, g_conv_v, g_gate, g_up, g_out, g_down,
        g_attn, g_mlp, g_beta, g_decay, g_gain, g_bias, g_rate,
    ) = done
    return (
        block_output,
        input_grad,
        g_attn[0],
        g_query,
        g_key,
        g_value,
        g_outgate,
        g_beta.T,
        g_decay.T,
        g_bias[0],
        g_rate[0],
        g_conv_q,
        g_conv_k,
        g_conv_v,
        g_gain[0],
        g_out.T,
        g_mlp[0],
        g_gate,
        g_up,
        g_down.T,
    )


def solution(mesh):
    tokens = P(("dp", "seq"), None)
    column = P(None, ("dp", "seq"))
    vector = P(("dp", "seq"))
    in_specs = (tokens, P("dp", None)) + (P(),) * 18 + (tokens,)
    out_specs = (
        (tokens, tokens, vector)
        + (tokens,) * 6
        + (P(),) * 6
        + (column, vector, tokens, tokens, column)
    )
    return jax.shard_map(
        per_device, mesh=mesh, in_specs=in_specs, out_specs=out_specs, check_vma=False
    )
```

```python
from functools import partial

import jax
import jax.numpy as jnp
from jax import lax
from jax.experimental import pallas as pl
from jax.experimental.pallas import tpu as pltpu
from jax.sharding import PartitionSpec as P

REFLECTS = 2
KW = 4
BLOCK = 64
SHORTEST = 1024
STEPS = BLOCK * REFLECTS
HALO = 8
RESET_LOG = -80.0
MESH = pl.DeviceIdType.MESH
F32 = jnp.float32
BF16 = jnp.bfloat16
NN = (((1,), (0,)), ((), ()))
NT = (((1,), (1,)), ((), ()))
TN = (((0,), (0,)), ((), ()))
VMEM_LIMIT = 56 * 1024 * 1024
FORWARD_HEADS = 2
BACKWARD_HEADS = 1


def cost(microseconds):
    return pl.CostEstimate(
        flops=int(microseconds * 1e9), bytes_accessed=int(microseconds * 1e6), transcendentals=0
    )


def mm(a, b, dims=NN):
    return lax.dot_general(a.astype(BF16), b.astype(BF16), dims, preferred_element_type=F32)


def halves(a):
    high = a.astype(BF16)
    return high, (a - high.astype(F32)).astype(BF16)


def mm3(a, b):
    ah, al = halves(a)
    bh, bl = halves(b)
    return mm(jnp.concatenate([ah, al], axis=1), jnp.concatenate([bh, bh], axis=0)) + mm(ah, bl)


def mm2(a, b, dims=NN):
    ah, al = halves(a)
    return mm(ah, b, dims) + mm(al, b, dims)


def mm2t(a, b, dims=NN):
    bh, bl = halves(b)
    return mm(a, bh, dims) + mm(a, bl, dims)


def sigmoid(v):
    return 1.0 / (1.0 + jnp.exp(-v))


def step_ids(shape, axis):
    index = lax.broadcasted_iota(jnp.int32, shape, axis)
    return index % BLOCK, index // BLOCK


def step_masks():
    shape = (STEPS, STEPS)
    tm, jm = step_ids(shape, 0)
    tn, jn = step_ids(shape, 1)
    strict = (tm > tn) | ((tm == tn) & (jm > jn))
    size = 4
    first = tm // size == tn // size
    merges = []
    while size < BLOCK:
        merges.append((tm // (2 * size) == tn // (2 * size)) & (tm // size != tn // size))
        size = 2 * size
    eye = ((tm == tn) & (jm == jn)).astype(F32)
    return tm >= tn, strict, first, merges, eye


def unit_lower_inverse(systems, first, merges, eye):
    neg = [jnp.where(first, -a, 0.0) for a in systems]
    inv = [eye + n for n in neg]
    for _ in range(2):
        neg = [mm3(n, n) for n in neg]
        inv = [t + mm3(t, n) for t, n in zip(inv, neg)]
    for merge in merges:
        off = [mm3(jnp.where(merge, a, 0.0), t) for a, t in zip(systems, inv)]
        inv = [t - mm3(t, o) for t, o in zip(inv, off)]
    return inv


def conv_parts(ext_ref, taps, live, columns, rows):
    total = None
    for back in range(KW):
        part = ext_ref[pl.ds(HALO - back, rows), columns] * taps[KW - 1 - back : KW - back, :]
        if back > 0:
            part = part * live[:, back : back + 1]
        total = part if total is None else total + part
    return total


def head_features(ext_ref, tq, tk, tv, live, rows, width):
    conv = [
        conv_parts(ext_ref, tq, live, pl.ds(0, width), rows),
        conv_parts(ext_ref, tk[:, :width], live, pl.ds(width, width), rows),
        conv_parts(ext_ref, tk[:, width:], live, pl.ds(2 * width, width), rows),
        conv_parts(ext_ref, tv[:, :width], live, pl.ds(3 * width, width), rows),
        conv_parts(ext_ref, tv[:, width:], live, pl.ds(4 * width, width), rows),
    ]
    return conv


def unit_rows(act):
    return lax.rsqrt(jnp.sum(act * act, axis=-1, keepdims=True) + 1e-06)


def greet_group(count):
    place, group = lax.axis_index("seq"), lax.axis_index("dp")
    barrier = pltpu.get_barrier_semaphore()

    def greet(step, carry):
        peer = lax.rem(place + step, count)
        pl.semaphore_signal(barrier, inc=1, device_id=(group, peer), device_id_type=MESH)
        return carry

    lax.fori_loop(1, count, greet, 0)
    return barrier


def carry_steps(count, heads, backward, part_ref, maps_ref, inbox, outbox, landed, sems):
    send_sem, recv_sem, back_sem, land_sem = sems
    place, group = lax.axis_index("seq"), lax.axis_index("dp")
    width = landed.shape[-1]
    stride = count // 16

    def keeper(h):
        return (2 * h + group) * stride

    def outgoing(h):
        return pltpu.make_async_remote_copy(
            src_ref=part_ref.at[h],
            dst_ref=inbox.at[place],
            send_sem=send_sem.at[h],
            recv_sem=recv_sem.at[place],
            device_id=(group, keeper(h)),
            device_id_type=MESH,
        )

    def send(h):
        @pl.when(place != keeper(h))
        def _():
            outgoing(h).start()

        @pl.when(place == keeper(h))
        def _():
            inbox[pl.ds(place, 1)] = part_ref[pl.ds(h, 1)]

    def scan_head(h):
        def returning(where):
            return pltpu.make_async_remote_copy(
                src_ref=outbox.at[where],
                dst_ref=landed.at[h],
                send_sem=back_sem.at[where],
                recv_sem=land_sem.at[h],
                device_id=(group, where),
                device_id_type=MESH,
            )

        def lap(step, state):
            where = count - 1 - step if backward else step
            outbox[pl.ds(where, 1)] = state[None].astype(BF16)

            @pl.when(where != place)
            def _():
                returning(where).start()
                pltpu.make_async_remote_copy(
                    src_ref=part_ref.at[h],
                    dst_ref=inbox.at[where],
                    send_sem=send_sem.at[h],
                    recv_sem=recv_sem.at[where],
                    device_id=(group, where),
                    device_id_type=MESH,
                ).wait_recv()

            @pl.when(where == place)
            def _():
                landed[h : h + 1] = outbox[pl.ds(where, 1)]

            got = inbox[pl.ds(where, 1)][0]
            high, low = halves(state)
            both = jnp.concatenate([high, low], axis=1)
            if backward:
                moved = mm(maps_ref[pl.ds(where, 1)][0][:, width:], both, TN)
            else:
                moved = mm(got[:, width:], both)
            return moved[:, :width] + moved[:, width:] + got[:, :width].astype(F32)

        lax.fori_loop(0, count, lap, jnp.zeros((width, width), F32))

        def finish(where, carry):
            @pl.when(where != place)
            def _():
                returning(where).wait_send()

            return carry

        return lambda: lax.fori_loop(0, count, finish, 0)

    def scan():
        for h in range(heads):

            @pl.when(place == keeper(h))
            def _(h=h):
                scan_head(h)()

    def take():
        for h in range(heads):

            @pl.when(place != keeper(h))
            def _(h=h):
                outgoing(h).wait_send()
                pltpu.make_async_remote_copy(
                    src_ref=outbox.at[0],
                    dst_ref=landed.at[h],
                    send_sem=back_sem.at[0],
                    recv_sem=land_sem.at[h],
                    device_id=(group, keeper(h)),
                    device_id_type=MESH,
                ).wait_recv()

    return send, scan, take


def carry_scratch(count, heads, width, columns):
    dma = pltpu.SemaphoreType.DMA
    return [
        pltpu.VMEM((count, width, columns), BF16),
        pltpu.VMEM((count, width, width), BF16),
        pltpu.VMEM((heads, width, width), BF16),
        dma((heads,)),
        dma((count,)),
        dma((count,)),
        dma((heads,)),
    ]


def mixer_forward_kernel(
    count, every_head, xn_ref, wq_ref, wk_ref, wv_ref, wg_ref, tq_ref, tk_ref, tv_ref, live_ref, acol_ref, arow_ref,
    pre_ref, gate_ref, oloc_ref, oread_ref, inv_ref, delta_ref, state_ref, turn_ref, carry_ref, start_ref, maps_ref,
    ext_ref, part_ref, inbox, outbox, landed, *sems,
):
    heads, rows, width = oread_ref.shape
    turn_at = pl.program_id(0)
    barrier = pltpu.get_barrier_semaphore()

    @pl.when(turn_at == 0)
    def _():
        greet_group(count)

    give, scan, take = carry_steps(count, every_head, False, part_ref, None, inbox, outbox, landed, sems)
    blocks = rows // BLOCK
    xn = xn_ref[...]
    live = live_ref[...]
    gate_ref[...] = mm(xn[HALO:], wg_ref[...])
    query, key, value = mm(xn, wq_ref[...]), mm(xn, wk_ref[...]), mm(xn, wv_ref[...])
    reach, strict, first, merges, eye = step_masks()
    cut = [slice(b * BLOCK, (b + 1) * BLOCK) for b in range(blocks)]
    every = [(n, b) for n in range(heads) for b in range(blocks)]
    qb, kb, vb = {}, {}, {}
    for n in range(heads):
        one, two = slice(n * width, (n + 1) * width), slice(2 * n * width, 2 * (n + 1) * width)
        pre = jnp.concatenate([query[:, one], key[:, two], value[:, two]], axis=1).astype(BF16)
        pre_ref[n] = pre
        ext_ref[n] = pre.astype(F32)
        conv = head_features(ext_ref.at[n], tq_ref[:, one], tk_ref[:, two], tv_ref[:, two], live, rows, width)
        act = [c * sigmoid(c) for c in conv]
        q = (act[0] * unit_rows(act[0]) * width ** (-0.5)).astype(BF16)
        k = [(a * unit_rows(a)).astype(BF16) for a in act[1:3]]
        v = [a.astype(BF16) for a in act[3:5]]
        for b in range(blocks):
            qb[n, b] = q[cut[b]]
            kb[n, b] = jnp.concatenate([k[0][cut[b]], k[1][cut[b]]], axis=0)
            vb[n, b] = jnp.concatenate([v[0][cut[b]], v[1][cut[b]]], axis=0)
    ccol = {at: acol_ref[at[0], at[1], :, 0:1] for at in every}
    bcol = {at: acol_ref[at[0], at[1], :, 1:2] for at in every}
    crow = {at: arow_ref[at[0], at[1], 0:1, :] for at in every}
    brow = {at: arow_ref[at[0], at[1], 1:2, :] for at in every}
    fade = {at: jnp.exp(jnp.where(reach, ccol[at] - crow[at], -1e30)) for at in every}
    system = [jnp.where(strict, fade[at] * mm(kb[at], kb[at], NT), 0.0) * bcol[at] for at in every]
    inv = dict(zip(every, unit_lower_inverse(system, first, merges, eye)))
    for at in every:
        inv_ref[at[0], at[1]] = inv[at].astype(BF16)
    local = {at: mm2(inv[at] * brow[at], vb[at]) for at in every}
    reads = {at: mm2(inv[at] * (brow[at] * jnp.exp(crow[at])), kb[at]) for at in every}
    score = {at: fade[at][:BLOCK] * mm(qb[at], kb[at], NT) for at in every}
    grow = {at: jnp.exp(ccol[at]) for at in every}
    last = {at: ccol[at][BLOCK - 1 : BLOCK] for at in every}
    tail = {at: kb[at].astype(F32) * jnp.exp(last[at] - ccol[at]) for at in every}
    both = {at: jnp.concatenate([local[at], -reads[at]], axis=1).astype(BF16) for at in every}
    turn = {at: mm(tail[at], both[at], TN) for at in every}
    query_out = {at: mm(score[at], both[at]) for at in every}
    state = {}
    for n in range(heads):
        now = jnp.concatenate([jnp.zeros((width, width), F32), eye], axis=1)
        for b in range(blocks):
            at = (n, b)
            state[at] = now
            step = turn[at][:, width:].astype(BF16)
            turn_ref[n, b] = step
            fixed = jnp.concatenate([turn[at][:, :width], jnp.zeros((width, width), F32)], axis=1)
            now = jnp.exp(last[at]) * now + fixed + mm(step, now)
        part_ref[pl.ds(turn_at * heads + n, 1)] = now.astype(BF16)[None]

    @pl.when(turn_at == 0)
    def _():
        pl.semaphore_wait(barrier, count - 1)

    for n in range(heads):
        give(turn_at * heads + n)
    for at in every:
        n, b = at
        carried = query_out[at][:, width:] + grow[at][:BLOCK] * qb[at].astype(F32)
        low = state[at].astype(BF16)
        carry_ref[n, b] = carried.astype(BF16)
        state_ref[n, b] = low
        fixed = jnp.concatenate([local[at], jnp.zeros((STEPS, width), F32)], axis=1)
        delta_ref[n, b] = (fixed - mm(reads[at], low)).astype(BF16)
        out = mm(carried, low)
        oloc_ref[cut[b], n * width : (n + 1) * width] = out[:, :width] + query_out[at][:, :width]
        oread_ref[n, cut[b], :] = out[:, width:].astype(BF16)

    @pl.when(turn_at == pl.num_programs(0) - 1)
    def _():
        scan()
        take()
        start_ref[...] = landed[...]
        maps_ref[...] = inbox[...]


def head_columns(rows, width):
    return pl.BlockSpec((rows, width), lambda h: (0, h))


def whole(shape):
    return pl.BlockSpec(shape, lambda h: (0,) * len(shape))


def per_head(shape, group=1):
    return pl.BlockSpec((group,) + shape, lambda h: (h,) + (0,) * len(shape))


def mixer_forward(xn, w_query, w_key, w_value, w_outgate, taps, live, acol, arow, heads, width, count):
    ext_rows, depth = xn.shape
    rows = ext_rows - HALO
    blocks = rows // BLOCK
    conv_query, conv_key, conv_value = taps
    out = jax.ShapeDtypeStruct
    return pl.pallas_call(
        partial(mixer_forward_kernel, count, heads),
        grid=(heads // FORWARD_HEADS,),
        in_specs=[
            whole((ext_rows, depth)),
            head_columns(depth, FORWARD_HEADS * width),
            head_columns(depth, 2 * FORWARD_HEADS * width),
            head_columns(depth, 2 * FORWARD_HEADS * width),
            head_columns(depth, FORWARD_HEADS * width),
            head_columns(KW, FORWARD_HEADS * width),
            head_columns(KW, 2 * FORWARD_HEADS * width),
            head_columns(KW, 2 * FORWARD_HEADS * width),
            whole(live.shape),
            per_head(acol.shape[1:], FORWARD_HEADS),
            per_head(arow.shape[1:], FORWARD_HEADS),
        ],
        out_specs=[
            per_head((ext_rows, 5 * width), FORWARD_HEADS),
            head_columns(rows, FORWARD_HEADS * width),
            head_columns(rows, FORWARD_HEADS * width),
            per_head((rows, width), FORWARD_HEADS),
            per_head((blocks, STEPS, STEPS), FORWARD_HEADS),
            per_head((blocks, STEPS, 2 * width), FORWARD_HEADS),
            per_head((blocks, width, 2 * width), FORWARD_HEADS),
            per_head((blocks, width, width), FORWARD_HEADS),
            per_head((blocks, BLOCK, width), FORWARD_HEADS),
            whole((heads, width, width)),
            whole((count, width, 2 * width)),
        ],
        out_shape=[
            out((heads, ext_rows, 5 * width), BF16),
            out((rows, heads * width), F32),
            out((rows, heads * width), F32),
            out((heads, rows, width), BF16),
            out((heads, blocks, STEPS, STEPS), BF16),
            out((heads, blocks, STEPS, 2 * width), BF16),
            out((heads, blocks, width, 2 * width), BF16),
            out((heads, blocks, width, width), BF16),
            out((heads, blocks, BLOCK, width), BF16),
            out((heads, width, width), BF16),
            out((count, width, 2 * width), BF16),
        ],
        scratch_shapes=[
            pltpu.VMEM((FORWARD_HEADS, ext_rows, 5 * width), F32),
            pltpu.VMEM((heads, width, 2 * width), BF16),
        ]
        + carry_scratch(count, heads, width, 2 * width),
        compiler_params=pltpu.CompilerParams(
            collective_id=0, has_side_effects=True, vmem_limit_bytes=VMEM_LIMIT
        ),
        cost_estimate=cost(40),
        name="mixer_forward",
    )(xn, w_query, w_key, w_value, w_outgate, conv_query, conv_key, conv_value, live, acol, arow)


def conv_pull(ext_ref, pad_ref, d_conv, taps, live, columns, rows, dtap_ref):
    total = None
    for back in range(KW):
        part = d_conv if back == 0 else d_conv * live[:, back : back + 1]
        source = ext_ref[pl.ds(HALO - back, rows), columns]
        dtap_ref[KW - 1 - back : KW - back, :] = jnp.sum(part * source, axis=0, keepdims=True)
        pad_ref[pl.ds(HALO, rows), :] = part
        moved = pad_ref[pl.ds(back, rows + HALO), :] * taps[KW - 1 - back : KW - back, :]
        total = moved if total is None else total + moved
    return total


def silu_pull(c, grad):
    s = sigmoid(c)
    return grad * (s + c * s * (1.0 - s))


def unit_pull(act, grad, scale):
    r = unit_rows(act)
    return scale * r * (grad - act * (r * r * jnp.sum(act * grad, axis=-1, keepdims=True)))


def mixer_backward_kernel(
    pre_ref, tq_ref, tk_ref, tv_ref, live_ref, acol_ref, arow_ref,
    inv_ref, delta_ref, state_ref, turn_ref, carry_ref, start_ref, after_ref, dout_ref,
    d_ref, dtq_ref, dtk_ref, dtv_ref, aux_ref,
    ext_ref, pad_ref,
):
    heads = pre_ref.shape[0]
    rows = dout_ref.shape[0]
    width = start_ref.shape[-1]
    blocks = rows // BLOCK
    live = live_ref[...]
    every = [(n, b) for n in range(heads) for b in range(blocks)]
    cut = [slice(b * BLOCK, (b + 1) * BLOCK) for b in range(blocks)]
    conv, act, qb, kb, dout = {}, {}, {}, {}, {}
    for n in range(heads):
        one, two = slice(n * width, (n + 1) * width), slice(2 * n * width, 2 * (n + 1) * width)
        ext_ref[n] = pre_ref[n].astype(F32)
        conv[n] = head_features(ext_ref.at[n], tq_ref[:, one], tk_ref[:, two], tv_ref[:, two], live, rows, width)
        act[n] = [c * sigmoid(c) for c in conv[n][:3]]
        q = (act[n][0] * unit_rows(act[n][0]) * width ** (-0.5)).astype(BF16)
        k = [(a * unit_rows(a)).astype(BF16) for a in act[n][1:]]
        for b in range(blocks):
            qb[n, b] = q[cut[b]]
            kb[n, b] = jnp.concatenate([k[0][cut[b]], k[1][cut[b]]], axis=0)
            dout[n, b] = dout_ref[cut[b], one]
    reach, strict, _, _, _ = step_masks()
    ccol = {at: acol_ref[at[0], at[1], :, 0:1] for at in every}
    bcol = {at: acol_ref[at[0], at[1], :, 1:2] for at in every}
    crow = {at: arow_ref[at[0], at[1], 0:1, :] for at in every}
    last = {at: ccol[at][BLOCK - 1 : BLOCK] for at in every}
    grow = {at: jnp.exp(ccol[at]) for at in every}
    weight = {at: jnp.exp(last[at] - ccol[at]) for at in every}
    ahead = {at: mm(carry_ref[at[0], at[1]], dout[at], TN) for at in every}
    after = {}
    for n in range(heads):
        now = after_ref[n].astype(F32)
        for b in range(blocks - 1, -1, -1):
            after[n, b] = now
            now = jnp.exp(last[n, b]) * now + ahead[n, b] + mm(turn_ref[n, b], now, TN)
    fade = {at: jnp.exp(jnp.where(reach, ccol[at] - crow[at], -1e30)) for at in every}
    delta = {
        at: delta_ref[at[0], at[1], :, :width].astype(F32) + mm(delta_ref[at[0], at[1], :, width:], start_ref[at[0]])
        for at in every
    }
    state = {
        at: state_ref[at[0], at[1], :, :width].astype(F32) + mm(state_ref[at[0], at[1], :, width:], start_ref[at[0]])
        for at in every
    }
    score = {at: fade[at][:BLOCK] * mm(qb[at], kb[at], NT) for at in every}
    d_delta = {at: mm(score[at], dout[at], TN) + weight[at] * mm2t(kb[at], after[at]) for at in every}
    d_rhs = {at: mm2t(inv_ref[at[0], at[1]], d_delta[at], TN) for at in every}
    d_score = {at: (fade[at][:BLOCK] * mm(dout[at], delta[at], NT)).astype(BF16) for at in every}
    d_tail = {at: weight[at] * mm(delta[at], after[at], NT) for at in every}
    d_gram = {
        at: jnp.where(strict, -bcol[at] * fade[at] * mm(d_rhs[at], delta[at], NT), 0.0).astype(BF16) for at in every
    }
    dq = {at: mm(grow[at][:BLOCK] * dout[at], state[at], NT) + mm(d_score[at], kb[at]) for at in every}
    dk_row = {
        at: mm(-(bcol[at] * grow[at]) * d_rhs[at], state[at], NT) + mm(d_gram[at], kb[at]) for at in every
    }
    dk_col = {at: mm(d_gram[at], kb[at], TN) + mm(d_score[at], qb[at], TN) + d_tail[at] for at in every}
    tok = lax.broadcasted_iota(jnp.int32, (BLOCK, 1), 0)
    for at in every:
        kf = kb[at].astype(F32)
        d_beta = (1.0 - bcol[at]) * jnp.sum(d_rhs[at] * delta[at], axis=-1, keepdims=True)
        d_log = jnp.sum(kf * (dk_row[at] - dk_col[at]), axis=-1, keepdims=True)
        d_logq = jnp.sum(qb[at].astype(F32) * dq[at], axis=-1, keepdims=True)
        d_last = jnp.sum(kf * d_tail[at]) + jnp.sum(jnp.exp(last[at]) * after[at] * state[at])
        d_token = d_log[:BLOCK] + d_log[BLOCK:] + d_logq + jnp.where(tok == BLOCK - 1, d_last, 0.0)
        aux_ref[at[0], at[1], :, 0:1] = d_beta
        aux_ref[at[0], at[1], 0:BLOCK, 1:2] = d_token
    pad_ref[0:HALO, :] = jnp.zeros((HALO, width), F32)
    pad_ref[pl.ds(HALO + rows, HALO), :] = jnp.zeros((HALO, width), F32)
    for n in range(heads):
        keys = {b: dk_row[n, b] + dk_col[n, b] for b in range(blocks)}
        values = {b: bcol[n, b] * d_rhs[n, b] for b in range(blocks)}
        d_act = [
            jnp.concatenate([dq[n, b] for b in range(blocks)], axis=0),
            jnp.concatenate([keys[b][:BLOCK] for b in range(blocks)], axis=0),
            jnp.concatenate([keys[b][BLOCK:] for b in range(blocks)], axis=0),
            jnp.concatenate([values[b][:BLOCK] for b in range(blocks)], axis=0),
            jnp.concatenate([values[b][BLOCK:] for b in range(blocks)], axis=0),
        ]
        for i, scale in enumerate((width ** (-0.5), 1.0, 1.0)):
            d_act[i] = unit_pull(act[n][i], d_act[i], scale)
        sides = (
            (tq_ref, dtq_ref, n),
            (tk_ref, dtk_ref, 2 * n),
            (tk_ref, dtk_ref, 2 * n + 1),
            (tv_ref, dtv_ref, 2 * n),
            (tv_ref, dtv_ref, 2 * n + 1),
        )
        for i, (tap_ref, dtap_ref, at) in enumerate(sides):
            lanes = pl.ds(at * width, width)
            grad = conv_pull(
                ext_ref.at[n], pad_ref, silu_pull(conv[n][i], d_act[i]), tap_ref[:, lanes], live,
                pl.ds(i * width, width), rows, dtap_ref.at[:, lanes],
            )
            target = pl.ds((5 * n + i) * width, width)
            d_ref[0:rows, target] = grad[HALO:].astype(BF16)
            d_ref[rows : rows + HALO, target] = grad[:HALO].astype(BF16)


def mixer_backward(pre, taps, live, acol, arow, saved, start, after, dout):
    heads, ext_rows, _ = pre.shape
    rows = ext_rows - HALO
    width = start.shape[-1]
    conv_query, conv_key, conv_value = taps
    out = jax.ShapeDtypeStruct
    columns = heads * width
    group = BACKWARD_HEADS
    tap_specs = [head_columns(KW, times * group * width) for times in (1, 2, 2)]
    return pl.pallas_call(
        mixer_backward_kernel,
        grid=(heads // group,),
        in_specs=[per_head(pre.shape[1:], group)]
        + tap_specs
        + [whole(live.shape)]
        + [per_head(value.shape[1:], group) for value in (acol, arow, *saved, start, after)]
        + [head_columns(rows, group * width)],
        out_specs=[head_columns(ext_rows, 5 * group * width)] + tap_specs + [per_head(acol.shape[1:], group)],
        out_shape=[
            out((ext_rows, 5 * columns), BF16),
            out((KW, columns), F32),
            out((KW, 2 * columns), F32),
            out((KW, 2 * columns), F32),
            out(acol.shape, F32),
        ],
        scratch_shapes=[
            pltpu.VMEM((group, ext_rows, 5 * width), F32),
            pltpu.VMEM((rows + 2 * HALO, width), F32),
        ],
        compiler_params=pltpu.CompilerParams(vmem_limit_bytes=VMEM_LIMIT),
        cost_estimate=cost(35),
        name="mixer_backward",
    )(pre, conv_query, conv_key, conv_value, live, acol, arow, *saved, start, after, dout)


def carry_kernel(count, heads, part_ref, maps_ref, result_ref, inbox, outbox, landed, *sems):
    barrier = greet_group(count)
    pl.semaphore_wait(barrier, count - 1)
    send, scan, take = carry_steps(count, heads, True, part_ref, maps_ref, inbox, outbox, landed, sems)
    for h in range(heads):
        send(h)
    scan()
    take()
    result_ref[...] = landed[...]


def carry_back(part, maps, count):
    heads, width, _ = part.shape
    vmem = pl.BlockSpec(memory_space=pltpu.VMEM)
    return pl.pallas_call(
        partial(carry_kernel, count, heads),
        in_specs=[vmem] * 2,
        out_specs=vmem,
        out_shape=jax.ShapeDtypeStruct((heads, width, width), BF16),
        scratch_shapes=carry_scratch(count, heads, width, width),
        compiler_params=pltpu.CompilerParams(
            collective_id=1, has_side_effects=True, vmem_limit_bytes=VMEM_LIMIT
        ),
        cost_estimate=cost(24),
        name="carry_back",
    )(part, maps)


JOBS = 7
JOB = 512
GROUPS = 3
LATE_JOBS = 10
EARLY_LINKS = ((0, 1, 2, 3), (1, 2, 0, 3), (2, 0, 1, 3))
LATE_LINKS = ((0, 1, 2, 3), (1, 0, 2, 3))


def half_rows(lhs, links, sending, lanes=slice(None)):
    edge = lhs.shape[0] // 8
    parts = []
    for second in range(2):
        for third in range(2):
            move = {links[0]: int(sending), links[1]: second, links[2]: third}
            block = 4 * move[0] + 2 * move[1] + move[2]
            parts.append(lhs[block * edge : (block + 1) * edge, lanes])
    return jnp.concatenate(parts, axis=0)


def column_pieces(sizes, begin, end):
    at, pieces = 0, []
    for index, size in enumerate(sizes):
        low, high = max(at, begin), min(at + size, end)
        if low < high:
            pieces.append((index, low - at, low - begin, high - low))
        at += size
    return pieces


def input_pull_kernel(
    d_ref, dg_ref, wq_ref, wk_ref, wv_ref, wg_ref, aux_ref, raw_ref, live_ref, rate_ref, wr_ref, ext_ref,
    x_ref, halo_ref, gain_ref, resid_ref,
    grad_ref, edge_ref, rim_ref, dgain_ref, drates_ref, misc_ref, total_ref, rates_ref,
):
    head = pl.program_id(0)
    rows = dg_ref.shape[0]
    width = dg_ref.shape[1] // PULL_HEADS
    group = PULL_HEADS
    part = None
    for n in range(group):
        d = d_ref[:, n * 5 * width : (n + 1) * 5 * width]
        two = slice(2 * n * width, 2 * (n + 1) * width)
        term = (
            mm(d[:, :width], wq_ref[:, n * width : (n + 1) * width], NT)
            + mm(d[:, width : 3 * width], wk_ref[:, two], NT)
            + mm(d[:, 3 * width :], wv_ref[:, two], NT)
        )
        part = term if part is None else part + term
    more = mm(dg_ref[...], wg_ref[...], NT)

    @pl.when(head == 0)
    def _():
        heads, blocks = aux_ref.shape[:2]
        wide = heads * REFLECTS
        rates_ref[...] = jnp.zeros_like(rates_ref)
        for h in range(heads):
            for b in range(blocks):
                tokens = slice(b * BLOCK, (b + 1) * BLOCK)
                for j in range(REFLECTS):
                    at = h * REFLECTS + j
                    rates_ref[tokens, at : at + 1] = aux_ref[h, b, j * BLOCK : (j + 1) * BLOCK, 0:1]
                rates_ref[tokens, wide + h : wide + h + 1] = aux_ref[h, b, 0:BLOCK, 1:2]
        value, raw = rates_ref[...], raw_ref[...]
        d_log = exact_sum(block_sums(rows, True), value) * live_ref[:, 1:2]
        lane = lax.broadcasted_iota(jnp.int32, raw.shape, 1)
        d_raw = jnp.where(lane < wide, value, -rate_ref[...] * sigmoid(raw) * d_log)
        summed = jnp.where(lane < wide, value, -softplus(raw) * d_log)
        misc_ref[...] = jnp.sum(summed, axis=0, keepdims=True)
        d_raw = d_raw.astype(BF16)
        drates_ref[...] = mm(d_raw, ext_ref[pl.ds(HALO, rows), :], TN)[: drates_ref.shape[0]]
        total_ref[...] = part
        total_ref[0:rows, :] += more + mm(d_raw, wr_ref[...])

    @pl.when(head > 0)
    def _():
        total_ref[...] += part
        total_ref[0:rows, :] += more

    @pl.when(head == pl.num_programs(0) - 1)
    def _():
        grad = total_ref[...]
        unit, pulled = norm_pull(x_ref[...].astype(F32), gain_ref[...], grad[:rows])
        grad_ref[...] = (resid_ref[...] + pulled).astype(BF16)
        halo_unit, _ = norm_pull(halo_ref[...].astype(F32), gain_ref[...], grad[rows:])
        dgain_ref[...] = jnp.sum(grad[:rows] * unit, axis=0, keepdims=True) + jnp.sum(
            grad[rows:] * halo_unit, axis=0, keepdims=True
        )
        edge_ref[0] = grad[rows - HALO : rows]
        edge_ref[1] = x_ref[rows - HALO :, :].astype(F32)
        edge_ref[2] = resid_ref[rows - HALO :, :]
        rim_ref[...] = grad[rows:]


def norm_pull(x, gain, grad):
    r = lax.rsqrt(jnp.mean(x * x, axis=-1, keepdims=True) + 1e-06)
    unit = x * r
    through = grad * gain
    return unit, r * (through - unit * jnp.mean(unit * through, axis=-1, keepdims=True))


PULL_HEADS = 2


def input_pull(d_all, d_outgate, weights, aux, raw, live, rate, w_rates, ext_b, x, halo, gain, d_resid, heads):
    rows, depth = x.shape
    ext_rows = rows + HALO
    width = d_outgate.shape[1] // heads * PULL_HEADS
    out = jax.ShapeDtypeStruct
    w_query, w_key, w_value, w_outgate = weights
    rates = heads * (REFLECTS + 1)
    return pl.pallas_call(
        input_pull_kernel,
        grid=(heads // PULL_HEADS,),
        in_specs=[
            head_columns(ext_rows, 5 * width),
            head_columns(rows, width),
            head_columns(depth, width),
            head_columns(depth, 2 * width),
            head_columns(depth, 2 * width),
            head_columns(depth, width),
            whole(aux.shape),
            whole(raw.shape),
            whole(live.shape),
            whole(rate.shape),
            whole(w_rates.shape),
            whole(ext_b.shape),
            whole(x.shape),
            whole(halo.shape),
            whole((1, depth)),
            whole(d_resid.shape),
        ],
        out_specs=[
            whole((rows, depth)), whole((3, HALO, depth)), whole((HALO, depth)), whole((1, depth)),
            whole((rates, depth)), whole((1, raw.shape[1])),
        ],
        out_shape=[
            out((rows, depth), BF16),
            out((3, HALO, depth), F32),
            out((HALO, depth), F32),
            out((1, depth), F32),
            out((rates, depth), F32),
            out((1, raw.shape[1]), F32),
        ],
        scratch_shapes=[pltpu.VMEM((ext_rows, depth), F32), pltpu.VMEM(raw.shape, F32)],
        compiler_params=pltpu.CompilerParams(vmem_limit_bytes=VMEM_LIMIT),
        cost_estimate=cost(12),
        name="input_pull",
    )(
        d_all, d_outgate, w_query, w_key, w_value, w_outgate, aux, raw, live, rate, w_rates, ext_b,
        x, halo, gain[None, :], d_resid,
    )


def exact_sum(ones, value):
    total = None
    for _ in range(3):
        part = value.astype(BF16)
        value = value - part.astype(F32)
        term = mm(ones, part)
        total = term if total is None else total + term
    return total


def block_sums(rows, reverse):
    shape = (rows, rows)
    one, two = lax.broadcasted_iota(jnp.int32, shape, 0), lax.broadcasted_iota(jnp.int32, shape, 1)
    order = (one <= two) if reverse else (one >= two)
    return ((one // BLOCK == two // BLOCK) & order).astype(BF16)


def softplus(v):
    return jnp.maximum(v, 0.0) + jnp.log1p(jnp.exp(-jnp.abs(v)))


def rates_kernel(
    heads, lengths_ref, x_ref, gain_ref, wbeta_ref, wdecay_ref, bias_in_ref, rate_in_ref,
    ext_ref, raw_ref, live_ref, acol_ref, arow_ref, halo_ref, weight_ref, rate_ref,
    edge_ref, got_ref, sems,
):
    rows = x_ref.shape[0]
    blocks = rows // BLOCK
    wide = heads * REFLECTS
    seq, count = lax.axis_index("seq"), lax.axis_size("seq")
    behind, before = lax.rem(seq + 1, count), lax.rem(seq + count - 1, count)
    barrier = pltpu.get_barrier_semaphore()
    for place in (behind, before):
        pl.semaphore_signal(barrier, inc=1, device_id={"seq": place}, device_id_type=MESH)
    edge_ref[...] = x_ref[rows - HALO :, :]
    copy = pltpu.make_async_remote_copy(
        src_ref=edge_ref,
        dst_ref=got_ref,
        send_sem=sems.at[0],
        recv_sem=sems.at[1],
        device_id={"seq": behind},
        device_id_type=MESH,
    )

    def normed(field):
        field = field.astype(F32)
        return (
            field * lax.rsqrt(jnp.mean(field * field, axis=-1, keepdims=True) + 1e-06) * gain_ref[...]
        ).astype(BF16)

    pl.semaphore_wait(barrier, 2)
    copy.start()
    xn = normed(x_ref[...])
    ext_ref[pl.ds(HALO, rows), :] = xn
    blank = jnp.zeros((128 - wide - heads, wbeta_ref.shape[1]), F32)
    weight = jnp.concatenate([wbeta_ref[...].astype(F32), wdecay_ref[...].astype(F32), blank], axis=0).astype(BF16)
    weight_ref[...] = weight
    empty = jnp.zeros((1, 128 - wide - heads), F32)
    bias = jnp.concatenate([bias_in_ref[...], jnp.zeros((1, heads), F32), empty], axis=1)
    rate = jnp.concatenate([jnp.zeros((1, wide), F32), rate_in_ref[...], empty], axis=1)
    rate_ref[...] = rate
    raw = mm(xn, weight, NT)
    raw_ref[...] = raw
    row = lax.axis_index("seq") * rows + lax.broadcasted_iota(jnp.int32, (rows, 1), 0)
    place, end = row, 0
    for i in range(lengths_ref.shape[1]):
        begin, end = end, end + lengths_ref[0, i] + (SHORTEST - 1)
        place = jnp.where((row >= begin) & (row < end), row - begin, place)
    live_ref[...] = (place >= lax.broadcasted_iota(jnp.int32, (rows, 8), 1)).astype(F32)
    beta = sigmoid(raw + bias)
    log_rate = jnp.where(place == 0, RESET_LOG, -rate * softplus(raw))
    lane = lax.broadcasted_iota(jnp.int32, raw.shape, 1)
    both = jnp.where(lane < wide, beta, exact_sum(block_sums(rows, False), log_rate))
    turned = both.T
    arow_ref[...] = jnp.zeros_like(arow_ref)
    acol_ref[...] = jnp.zeros_like(acol_ref)
    for h in range(heads):
        for b in range(blocks):
            tokens = slice(b * BLOCK, (b + 1) * BLOCK)
            for j in range(REFLECTS):
                steps = slice(j * BLOCK, (j + 1) * BLOCK)
                at = h * REFLECTS + j
                acol_ref[h, b, steps, 0:1] = both[tokens, wide + h : wide + h + 1]
                acol_ref[h, b, steps, 1:2] = both[tokens, at : at + 1]
                arow_ref[h, b, 0:1, steps] = turned[wide + h : wide + h + 1, tokens]
                arow_ref[h, b, 1:2, steps] = turned[at : at + 1, tokens]
    copy.wait()
    halo = jnp.where(seq > 0, got_ref[...].astype(F32), 0.0)
    halo_ref[...] = halo.astype(BF16)
    ext_ref[0:HALO, :] = normed(halo)


def rates_forward(lengths, x, gain, w_beta, w_decay, bias, rate, heads):
    rows, depth = x.shape
    blocks = rows // BLOCK
    out = jax.ShapeDtypeStruct
    vmem = pl.BlockSpec(memory_space=pltpu.VMEM)
    return pl.pallas_call(
        partial(rates_kernel, heads),
        in_specs=[pl.BlockSpec(memory_space=pltpu.SMEM)] + [vmem] * 6,
        out_specs=[vmem] * 8,
        out_shape=[
            out((rows + HALO, depth), BF16),
            out((rows, 128), F32),
            out((rows, 8), F32),
            out((heads, blocks, STEPS, 8), F32),
            out((heads, blocks, 8, STEPS), F32),
            out((HALO, depth), BF16),
            out((128, depth), BF16),
            out((1, 128), F32),
        ],
        scratch_shapes=[
            pltpu.VMEM((HALO, depth), BF16), pltpu.VMEM((HALO, depth), BF16), pltpu.SemaphoreType.DMA((2,)),
        ],
        compiler_params=pltpu.CompilerParams(
            collective_id=4, has_side_effects=True, vmem_limit_bytes=VMEM_LIMIT
        ),
        cost_estimate=cost(6),
        name="rates_forward",
    )(lengths, x, gain[None, :], w_beta.T, w_decay.T, bias[None, :], rate[None, :])


CHUNK = 256
RING = 6


def flip(bit, other):
    return bit + other - 2 * bit * other


def relative_source(depth):
    block = depth // 32
    seq, group = lax.axis_index("seq"), lax.axis_index("dp")
    index = lax.broadcasted_iota(jnp.int32, (depth, 1), 0)
    row, place, side = index % block, (index // block) % 16, index // (16 * block)
    x = flip(seq % 2, place // 8)
    y = flip((seq // 2) % 2, (place // 4) % 2)
    z = flip((seq // 4) % 2, (place // 2) % 2) + 2 * flip(seq // 8, place % 2)
    return ((((group + side) % 2) * 16 + z * 4 + y * 2 + x) * block + row)


def middle_kernel(
    compact, count, oloc_ref, oread_ref, start_ref, gate_ref, ogain_ref, x_ref, ext_ref, mgain_ref, ograd_ref,
    maps_ref, wout_hbm, wgate_hbm, wup_hbm, wdown_hbm,
    block_ref, dout_ref, part_ref, dresid_ref, dmgain_ref, dogain_ref,
    *refs,
):
    if compact:
        products, (own_out, got_out, after_ref) = refs[: 2 * GROUPS], refs[2 * GROUPS : 2 * GROUPS + 3]
        refs = refs[2 * GROUPS + 3 :]
        gated_ref, hidden_ref, dgate_ref, dup_ref, doutgate_ref, mlp_ref, branch_ref = refs[:7]
        gated_got, hidden_got, dgate_got, dup_got, doutgate_got, own_ref, other_ref, got_ref = refs[7:15]
        other_edge, got_edge, core_sem, chunk_sem, inbox, outbox, landed = refs[15:22]
        carry_sems, staged, stage_sem, refs = refs[22:26], refs[26 : 26 + 2 * GROUPS], refs[26 + 2 * GROUPS], refs[27 + 2 * GROUPS :]
    else:
        gated_ref, hidden_ref, dgate_ref, dup_ref, doutgate_ref, mlp_ref, branch_ref = refs[:7]
        refs = refs[7:]
    wout, wgate, wup, wdown, down_ref, dmlp_ref, sem_out, sems = refs
    heads, rows, width = oread_ref.shape
    depth = x_ref.shape[1]
    chunks = hidden_ref.shape[1] // CHUNK
    fetch_out = pltpu.make_async_copy(wout_hbm, wout, sem_out)
    fetch_out.start()

    def lanes_of(c):
        return pl.ds(pl.multiple_of(c * CHUNK, CHUNK), CHUNK)

    def fetches(c):
        slot = c % RING
        return (
            pltpu.make_async_copy(wgate_hbm.at[:, lanes_of(c)], wgate.at[slot], sems.at[slot, 0]),
            pltpu.make_async_copy(wup_hbm.at[:, lanes_of(c)], wup.at[slot], sems.at[slot, 1]),
            pltpu.make_async_copy(wdown_hbm.at[lanes_of(c), :], wdown.at[slot], sems.at[slot, 2]),
        )

    for c in range(RING):
        for copy in fetches(c):
            copy.start()
    core = {"dp": 1 - lax.axis_index("dp")}

    def to_core(source, target, sems, index):
        return pltpu.make_async_remote_copy(
            src_ref=source,
            dst_ref=target,
            send_sem=sems.at[(0,) + index],
            recv_sem=sems.at[(1,) + index],
            device_id=core,
            device_id_type=MESH,
        )

    if compact:
        barrier = greet_group(count)
        pl.semaphore_signal(barrier, inc=1, device_id=core, device_id_type=MESH)
        give, scan, take = carry_steps(
            count, heads, True, part_ref, maps_ref, inbox, outbox, landed, carry_sems
        )
        half = depth // 2
        lane = lax.broadcasted_iota(jnp.int32, (depth, depth), 1)
        chosen = (lane == relative_source(depth)).astype(BF16)
        swaps = []

        def turn(at, value, index):
            turned = mm(chosen, value, NT).astype(BF16)
            cut = slice(at, at + value.shape[0])
            own_ref[:, cut] = turned[:half]
            other_ref[:, cut] = turned[half:]
            swap(other_ref.at[:, cut], got_ref.at[:, cut], index)

        def turn_tokens():
            value = jnp.concatenate([ext_ref[pl.ds(HALO, rows), :], ext_ref[0:HALO, :]], axis=0)
            turned = mm(chosen, value, NT).astype(BF16)
            own_out[...] = turned[:half]
            other_edge[...] = turned[half:]
            swap(other_edge, got_edge, 3)

        def swap(source, target, index):
            swaps.append(to_core(source, target, core_sem, (index,)))
            swaps[-1].start()

    ogain = ogain_ref[...]
    for h in range(heads):
        lanes = slice(h * width, (h + 1) * width)
        out = oloc_ref[:, lanes] + mm(oread_ref[h], start_ref[h])
        dout_ref[:, lanes] = out
        gate = gate_ref[:, lanes]
        r = lax.rsqrt(jnp.mean(out * out, axis=-1, keepdims=True) + 1e-05)
        gated_ref[:, lanes] = (out * r * ogain * (gate * sigmoid(gate))).astype(BF16)
    fetch_out.wait()
    resid = x_ref[...].astype(F32) + mm(gated_ref[...], wout[...])
    dresid_ref[...] = resid
    r = lax.rsqrt(jnp.mean(resid * resid, axis=-1, keepdims=True) + 1e-06)
    mlp_ref[...] = (resid * r * mgain_ref[...]).astype(BF16)
    if compact:
        pl.semaphore_wait(barrier, count)
        swap(gated_ref, gated_got, 4)
    down_ref[...] = jnp.zeros_like(down_ref)
    dmlp_ref[...] = jnp.zeros_like(dmlp_ref)

    def chunk_swaps(c):
        pairs = ((hidden_ref, hidden_got), (dgate_ref, dgate_got), (dup_ref, dup_got))
        return [
            to_core(own.at[:, lanes_of(c)], got.at[:, lanes_of(c)], chunk_sem, (c, i))
            for i, (own, got) in enumerate(pairs)
        ]

    def one(c, carry):
        slot = c % RING
        for copy in fetches(c):
            copy.wait()
        mlp, ograd = mlp_ref[...], ograd_ref[...]
        lanes = lanes_of(c)
        gate, up = mm(mlp, wgate[slot]), mm(mlp, wup[slot])
        d_hidden = mm(ograd, wdown[slot], NT)
        s = sigmoid(gate)
        act = gate * s
        hidden = (act * up).astype(BF16)
        d_gate = (d_hidden * up * (s + act * (1.0 - s))).astype(BF16)
        d_up = (d_hidden * act).astype(BF16)
        hidden_ref[:, lanes] = hidden
        dgate_ref[:, lanes] = d_gate
        dup_ref[:, lanes] = d_up
        if compact:
            for copy in chunk_swaps(c):
                copy.start()
        down_ref[...] += mm(hidden, wdown[slot])
        dmlp_ref[...] += mm(d_gate, wgate[slot], NT) + mm(d_up, wup[slot], NT)

        @pl.when(c + RING < chunks)
        def _():
            for copy in fetches(c + RING):
                copy.start()

        return carry

    lax.fori_loop(0, chunks, one, 0)
    resid = dresid_ref[...]
    block_ref[...] = (resid + down_ref[...]).astype(BF16)
    grad = dmlp_ref[...]
    unit, pulled = norm_pull(resid, mgain_ref[...], grad)
    dmgain_ref[...] = jnp.sum(grad * unit, axis=0, keepdims=True)
    d_resid = ograd_ref[...].astype(F32) + pulled
    dresid_ref[...] = d_resid
    branch_ref[...] = d_resid.astype(BF16)
    dogain = jnp.zeros((1, width), F32)
    for h in range(heads):
        lanes = slice(h * width, (h + 1) * width)
        grad = mm(branch_ref[...], wout[lanes, :], NT)
        out = dout_ref[:, lanes]
        gate = gate_ref[:, lanes]
        r = lax.rsqrt(jnp.mean(out * out, axis=-1, keepdims=True) + 1e-05)
        s = sigmoid(gate)
        unit = out * r
        doutgate_ref[:, lanes] = (grad * unit * ogain * (s + gate * s * (1.0 - s))).astype(BF16)
        through = grad * (gate * s)
        dogain += jnp.sum(through * unit, axis=0, keepdims=True)
        through = through * ogain
        dout = r * (through - unit * jnp.mean(unit * through, axis=-1, keepdims=True))
        dout_ref[:, lanes] = dout
        part_ref[h] = mm(oread_ref[h], dout, TN).astype(BF16)
        if compact:
            give(h)
    dogain_ref[...] = dogain
    if compact:
        turn(0, mlp_ref[...], 0)
        turn(rows, ograd_ref[...], 1)
        swap(doutgate_ref, doutgate_got, 5)
        turn(2 * rows, branch_ref[...], 2)
        turn_tokens()

        def arrived(c, carry):
            for copy in chunk_swaps(c):
                copy.wait()
            return carry

        lax.fori_loop(0, chunks, arrived, 0)
        rhs_own = (dgate_ref, dup_ref, hidden_ref, gated_ref, doutgate_ref)
        rhs_got = (dgate_got, dup_got, hidden_got, gated_got, doutgate_got)
        for copy in swaps[:3]:
            copy.wait()
        lhs_own, lhs_got = (own_ref, own_out), (got_ref, got_edge)
        targets = [staged[2 * group : 2 * group + 2] for group in range(GROUPS)]
        early_products(lhs_own, lhs_got, rhs_own, rhs_got, targets, (0, 1, 2))
        outgoing = [
            pltpu.make_async_copy(source, target, stage_sem.at[i])
            for i, (source, target) in enumerate(zip(staged, products))
        ]
        for copy in outgoing[: 2 * GROUPS - 2]:
            copy.start()
        scan()
        for copy in swaps[3:]:
            copy.wait()
        early_products(lhs_own, lhs_got, rhs_own, rhs_got, targets, (3, 4))
        for copy in outgoing[2 * GROUPS - 2 :]:
            copy.start()
        got_out[...] = got_edge[...]
        for copy in outgoing:
            copy.wait()
        take()
        after_ref[...] = landed[...]


def early_products(lhs_own, lhs_got, rhs_own, rhs_got, targets, which):
    tokens = rhs_own[0].shape[0]
    sizes = [rhs.shape[1] for rhs in rhs_own]
    sides = (0, 0, 1, 2, 3)
    for group in range(GROUPS):
        for sending in (True, False):
            turned = {}
            for job in range(JOBS):
                begin = (group * JOBS + job) * JOB
                for index, column, offset, width in column_pieces(sizes, begin, begin + JOB):
                    if index not in which:
                        continue
                    side = sides[index]
                    if side not in turned:
                        cut = slice(side % 3 * tokens, (side % 3 + 1) * tokens)
                        turned[side] = [
                            half_rows(lhs[side // 3], EARLY_LINKS[group], sending, cut) for lhs in (lhs_own, lhs_got)
                        ]
                    lanes = slice(column, column + width)
                    total = mm(turned[side][0], rhs_own[index][:, lanes]) + mm(
                        turned[side][1], rhs_got[index][:, lanes]
                    )
                    targets[group][0 if sending else 1][job, :, offset : offset + width] = total.astype(BF16)


def middle(
    compact, count, oloc, oread, start, gate_pre, out_gain, x, ext_b, mlp_gain, out_grad, maps,
    w_out, w_gate, w_up, w_down,
):
    heads, rows, width = oread.shape
    depth = x.shape[1]
    ff = w_gate.shape[1]
    out = jax.ShapeDtypeStruct
    vmem, hbm = pl.BlockSpec(memory_space=pltpu.VMEM), pl.BlockSpec(memory_space=pl.ANY)
    columns = heads * width
    chunks = ff // CHUNK
    half = depth // 2
    outs = [
        ((rows, depth), BF16), ((rows, columns), F32), ((heads, width, width), BF16), ((rows, depth), F32),
        ((1, depth), F32), ((1, width), F32),
    ]
    rhs = [((rows, columns), BF16)] + [((rows, ff), BF16)] * 3 + [((rows, columns), BF16)]
    kept = rhs + [((rows, depth), BF16)] * 2
    scratch = []
    dma = pltpu.SemaphoreType.DMA
    if compact:
        product = ((JOBS, half // 2, JOB), BF16)
        outs += [product] * (2 * GROUPS) + [((half, rows + HALO), BF16)] * 2
        outs += [((heads, width, width), BF16), ((rows, columns), BF16)]
        buffers = kept[:4] + kept[5:] + rhs + [((half, 3 * rows), BF16)] * 3 + [((half, rows + HALO), BF16)] * 2
        scratch += [pltpu.VMEM(*buffer) for buffer in buffers] + [dma((2, 6)), dma((2, chunks, 3))]
        scratch += carry_scratch(count, heads, width, width)
        scratch += [pltpu.VMEM(*product)] * (2 * GROUPS) + [dma((2 * GROUPS,))]
    else:
        outs += kept
    scratch += [
        pltpu.VMEM(w_out.shape, BF16),
        pltpu.VMEM((RING, depth, CHUNK), BF16),
        pltpu.VMEM((RING, depth, CHUNK), BF16),
        pltpu.VMEM((RING, CHUNK, depth), BF16),
        pltpu.VMEM((rows, depth), F32),
        pltpu.VMEM((rows, depth), F32),
        dma,
        dma((RING, 3)),
    ]

    def kernel(*refs):
        if not compact:
            middle_kernel(compact, count, *refs)
            return
        late = 20 + 2 * GROUPS + 3
        rest = refs[late + 1 :]
        middle_kernel(compact, count, *refs[:late], *rest[:4], refs[late], *rest[4:])

    params = {"collective_id": 3, "has_side_effects": True} if compact else {}
    return pl.pallas_call(
        kernel,
        in_specs=[vmem] * 10 + [hbm] * 4,
        out_specs=[hbm if compact and shape == product else vmem for shape in outs],
        out_shape=[out(*shape) for shape in outs],
        scratch_shapes=scratch,
        compiler_params=pltpu.CompilerParams(vmem_limit_bytes=VMEM_LIMIT, **params),
        cost_estimate=cost(30),
        name="middle",
    )(
        oloc, oread, start, gate_pre, out_gain[None, :], x, ext_b, mlp_gain[None, :], out_grad, maps,
        w_out, w_gate, w_up, w_down,
    )


def reduce_kernel(
    heads, arr_a, arr_b, arr_c, keep_a, keep_b, keep_c, own_ref, got_ref, rhs_ref, tq_ref, tk_ref, tv_ref, attn_ref, mlp_ref, ogain_ref,
    misc_ref, rates_ref, edge_ref, rim_ref, again_ref,
    gate_out, up_out, down_out, out_out, outgate_out, q_out, k_out, v_out, tq_out, tk_out, tv_out, rest_out,
    edge_out,
    fetched, e_keep, e_send, e_got2, e_got3, e_got4,
    rhs_got, lhs_ref, l_first, l_send, l_keep, l_got1, l_got2, l_got3, l_got4, small_sum, small_send, small_got, rim_got,
    dp_sem, e_sem, l_sem, s_sem, f_sem,
):
    seq = lax.axis_index("seq")
    group = lax.axis_index("dp")
    count = lax.axis_size("seq")
    x, y, z = seq % 2, (seq // 2) % 2, seq // 4
    near = (seq + 1 - 2 * x, seq + 2 - 4 * y)
    low_z = seq + 4 - 8 * (z % 2)
    high_z = seq + 8 - 16 * (z // 2)

    def at(place):
        return {"dp": group, "seq": place}

    core = {"dp": 1 - group, "seq": seq}
    before, behind = lax.rem(seq + count - 1, count), lax.rem(seq + 1, count)

    def send(source, target, sems, index, device):
        return pltpu.make_async_remote_copy(
            src_ref=source,
            dst_ref=target,
            send_sem=sems.at[(0,) + index],
            recv_sem=sems.at[(1,) + index],
            device_id=device,
            device_id_type=MESH,
        )

    def fetches(i):
        return [
            pltpu.make_async_copy(source.at[i], fetched.at[j, i], f_sem.at[j, i])
            for j, source in enumerate((arr_a, arr_b, arr_c, keep_a, keep_b, keep_c))
        ]

    def fetch(i, carry):
        for copy in fetches(i):
            copy.start()
        return carry

    lax.fori_loop(0, JOBS, fetch, 0)
    barrier = pltpu.get_barrier_semaphore()
    everyone = [core] + [at(place) for place in (near[0], near[1], low_z, high_z, before, behind)]
    for device in everyone:
        pl.semaphore_signal(barrier, inc=1, device_id=device, device_id_type=MESH)
    rim = send(rim_ref, rim_got, dp_sem, (1,), at(before))
    hops = [core, at(high_z), at(low_z), at(near[0]), at(near[1])]

    def hop(step):
        return send(small_send.at[step], small_got.at[step], s_sem, (step,), hops[step])

    def next_hop(step):
        hop(step - 1).wait_recv()
        total = small_send[step - 1].astype(F32) + small_got[step - 1].astype(F32)
        if step < len(hops):
            small_send[step] = total.astype(BF16)
            hop(step).start()
        else:
            small_sum[1] = total

    depth = tq_ref.shape[1]
    small_sum[0, 0:KW] = tq_ref[...]
    for half in range(2):
        lanes = pl.ds(half * depth, depth)
        small_sum[0, KW * (1 + half) : KW * (2 + half)] = tk_ref[:, lanes]
        small_sum[0, KW * (3 + half) : KW * (4 + half)] = tv_ref[:, lanes]
    small_sum[0, 5 * KW : 6 * KW] = jnp.zeros((KW, depth), F32)
    small_sum[0, 5 * KW : 5 * KW + 1] = attn_ref[...]
    small_sum[0, 5 * KW + 1 : 5 * KW + 2] = mlp_ref[...]
    gains = ogain_ref.shape[1]
    small_sum[0, 5 * KW + 2 : 5 * KW + 3, 0:gains] = ogain_ref[...]
    small_sum[0, 5 * KW + 2 : 5 * KW + 3, gains : gains + misc_ref.shape[1]] = misc_ref[...]
    small_sum[0, 6 * KW :] = rates_ref[...]
    for p in range(2):
        for side, lhs in enumerate((own_ref, got_ref)):
            for sending in range(2):
                lhs_ref[p, side, sending] = half_rows(lhs[...], LATE_LINKS[p], sending)
    small_send[0] = small_sum[0].astype(BF16)
    swap = send(rhs_ref, rhs_got, dp_sem, (0,), core)
    pl.semaphore_wait(barrier, len(everyone))
    hop(0).start()
    swap.start()
    rim.start()

    places = (near[0], near[1], low_z, high_z)
    quarter = e_got2.shape[2]
    eighth, share = quarter // 2, quarter // 4

    def exchange(p, i, stage, sent, got, sems, links):
        begin = (0, 0, quarter, quarter + eighth)[stage]
        target = places[links[p][stage]]
        return send(sent.at[p, i, pl.ds(begin, got.shape[2])], got.at[p, i], sems, (p, i, stage), at(target))

    def early(p, i, stage):
        return exchange(p, i, stage, e_send, (None, e_got2, e_got3, e_got4)[stage], e_sem, EARLY_LINKS)

    def late(p, i, stage):
        sent = l_first if stage == 0 else l_send
        return exchange(p, i, stage, sent, (l_got1, l_got2, l_got3, l_got4)[stage], l_sem, LATE_LINKS)

    def early2(i, carry):
        for copy in fetches(i):
            copy.wait()
        for p in range(GROUPS):
            total = fetched[p, i].astype(F32) + fetched[GROUPS + p, i].astype(F32)
            e_keep[p, i] = total[:quarter].astype(BF16)
            e_send[p, i, 0:quarter] = total[quarter:].astype(BF16)
            early(p, i, 1).start()
        return carry

    def onward(p, i, copy_of, keep, sent, got, stage, begin):
        copy_of(p, i, stage).wait_recv()
        rows = got.shape[2]
        half = rows // 2
        total = keep[p, i, 0:rows].astype(F32) + got[p, i].astype(F32)
        keep[p, i, 0:half] = total[:half].astype(BF16)
        sent[p, i, begin : begin + half] = total[half:].astype(BF16)
        copy_of(p, i, stage + 1).start()

    def later(i, carry, copy_of, keep, sent, got, stage, begin):
        for p in range(keep.shape[0]):
            onward(p, i, copy_of, keep, sent, got, stage, begin)
        return carry

    lax.fori_loop(0, JOBS, early2, 0)
    next_hop(1)
    swap.wait_recv()
    job = l_got1.shape[-1]
    late_jobs = LATE_JOBS // 2
    tokens = rhs_ref.shape[0]

    def product(m, p, sending):
        lanes = pl.ds(pl.multiple_of(m * job, job), job)
        total = mm(lhs_ref[p, 0, int(sending)], rhs_ref[:, lanes]) + mm(
            lhs_ref[p, 1, int(sending)], rhs_got[:, lanes]
        )
        return total[:quarter], total[quarter:]

    def late1(i, carry):
        for p in range(2):
            low, high = product(2 * i + p, p, True)
            l_first[p, i, 0:quarter] = low.astype(BF16)
            l_first[p, i, quarter : 2 * quarter] = high.astype(BF16)
            late(p, i, 0).start()
        return carry

    def late2(i, carry):
        for p in range(2):
            low, high = product(2 * i + p, p, False)
            late(p, i, 0).wait_recv()
            l_keep[p, i] = (low + l_got1[p, i, 0:quarter].astype(F32)).astype(BF16)
            l_send[p, i, 0:quarter] = (high + l_got1[p, i, quarter : 2 * quarter].astype(F32)).astype(BF16)
            late(p, i, 1).start()
        return carry

    lag = JOBS - late_jobs

    def low_turn(i, carry):
        later(i, carry, early, e_keep, e_send, e_got2, 1, quarter)

        @pl.when(i == lag)
        def _():
            next_hop(2)

        @pl.when(i >= lag)
        def _():
            late1(i - lag, carry)

        return carry

    def high_turn(i, carry):
        later(i, carry, early, e_keep, e_send, e_got3, 2, quarter + eighth)

        @pl.when(i >= lag)
        def _():
            late2(i - lag, carry)

        return carry

    lax.fori_loop(0, JOBS, low_turn, 0)
    next_hop(3)
    lax.fori_loop(0, JOBS, high_turn, 0)
    next_hop(4)
    rim.wait_recv()
    inside = (seq < count - 1).astype(F32)
    _, pulled = norm_pull(edge_ref[1], again_ref[...], edge_ref[0] + inside * rim_got[...])
    edge_out[...] = (edge_ref[2] + pulled).astype(BF16)
    late_low = partial(later, copy_of=late, keep=l_keep, sent=l_send, got=l_got2, stage=1, begin=quarter)
    lax.fori_loop(0, late_jobs, late_low, 0)
    next_hop(5)
    late_high = partial(later, copy_of=late, keep=l_keep, sent=l_send, got=l_got3, stage=2, begin=quarter + eighth)
    lax.fori_loop(0, late_jobs, late_high, 0)
    early_outs = (gate_out, up_out, down_out, out_out, outgate_out)
    for i in range(JOBS):
        for p in range(GROUPS):
            early(p, i, 3).wait_recv()
            total = e_keep[p, i, 0:share].astype(F32) + e_got4[p, i].astype(F32)
            first = (p * JOBS + i) * JOB
            for output, to, begin, width in column_pieces([o.shape[1] for o in early_outs], first, first + JOB):
                early_outs[output][:, to : to + width] = total[:, begin : begin + width]
    tq_out[...] = small_sum[1, 0:KW]
    for half in range(2):
        lanes = pl.ds(half * depth, depth)
        tk_out[:, lanes] = small_sum[1, KW * (1 + half) : KW * (2 + half)]
        tv_out[:, lanes] = small_sum[1, KW * (3 + half) : KW * (4 + half)]
    rest_out[...] = small_sum[1, 5 * KW :]
    width = q_out.shape[1] // heads
    for i in range(late_jobs):
        for p in range(2):
            late(p, i, 3).wait_recv()
            total = l_keep[p, i, 0:share].astype(F32) + l_got4[p, i].astype(F32)
            for begin in range(0, job, width):
                head, part = divmod(((2 * i + p) * job + begin) // width, 5)
                if part == 0:
                    target, to = q_out, head * width
                else:
                    target, to = (k_out, v_out)[(part - 1) // 2], (2 * head + (part - 1) % 2) * width
                target[:, to : to + width] = total[:, begin : begin + width]

    def early_sent(i, carry):
        for p in range(GROUPS):
            for stage in (1, 2, 3):
                early(p, i, stage).wait_send()
        return carry

    def late_sent(i, carry):
        for p in range(2):
            for stage in (0, 1, 2, 3):
                late(p, i, stage).wait_send()
        return carry

    lax.fori_loop(0, JOBS, early_sent, 0)
    lax.fori_loop(0, late_jobs, late_sent, 0)
    swap.wait_send()
    rim.wait_send()
    for step in range(len(hops)):
        hop(step).wait_send()


def reduce_all(arrived, kept, own, got, rhs, taps, gains, rates, edge, rim, gain, ff, heads):
    half = own.shape[0] // 2
    quarter, eighth, share = half // 2, half // 4, half // 8
    count = LATE_JOBS // 2
    columns = rhs.shape[1] // 5
    job = rhs.shape[1] // LATE_JOBS
    depth = rates.shape[1]
    small_rows = 6 * KW + rates.shape[0]
    out = jax.ShapeDtypeStruct
    vmem = pl.BlockSpec(memory_space=pltpu.VMEM)

    def stages(groups, jobs, width):
        return [((groups, jobs, rows, width), BF16) for rows in (quarter, eighth, share)]

    buffers = [((2 * GROUPS, JOBS, half, JOB), BF16)]
    buffers += [((GROUPS, JOBS, quarter, JOB), BF16), ((GROUPS, JOBS, half, JOB), BF16)]
    buffers += stages(GROUPS, JOBS, JOB)
    buffers += [(rhs.shape, BF16), ((2, 2, 2, half, own.shape[1]), BF16)] + [((2, count, half, job), BF16)] * 2 + [((2, count, quarter, job), BF16)]
    buffers += [((2, count, half, job), BF16)] + stages(2, count, job)
    buffers += [((2, small_rows, depth), F32)] + [((5, small_rows, depth), BF16)] * 2 + [(rim.shape, F32)]
    dma = pltpu.SemaphoreType.DMA
    shapes = [(share, ff)] * 3 + [(share, columns)] * 3 + [(share, 2 * columns)] * 2
    shapes += [tap.shape for tap in taps] + [(small_rows - 5 * KW, depth)]
    return pl.pallas_call(
        partial(reduce_kernel, heads),
        in_specs=[pl.BlockSpec(memory_space=pl.ANY)] * (2 * GROUPS) + [vmem] * 14,
        out_specs=[vmem] * 13,
        out_shape=[out(shape, F32) for shape in shapes] + [out(rim.shape, BF16)],
        scratch_shapes=[pltpu.VMEM(shape, kind) for shape, kind in buffers]
        + [dma((2, 2)), dma((2, GROUPS, JOBS, 4)), dma((2, 2, count, 4)), dma((2, 5)), dma((2 * GROUPS, JOBS))],
        compiler_params=pltpu.CompilerParams(
            collective_id=2, has_side_effects=True, vmem_limit_bytes=VMEM_LIMIT
        ),
        cost_estimate=cost(90),
        name="reduce_all",
    )(*arrived, *kept, own, got, rhs, *taps, *gains, rates, edge, rim, gain)


def finish_kernel(marks, grad_ref, edge_ref, rest_ref, *refs):
    count = (len(refs) - 8) // 2
    sources, (grad_out, *outs) = refs[:count], refs[count:]
    rows = grad_ref.shape[0]
    grad_out[0 : rows - HALO, :] = grad_ref[0 : rows - HALO, :]
    grad_out[rows - HALO :, :] = edge_ref[...]
    for source, target in zip(sources, outs):
        target[...] = source[...]
    again, mlp, beta, rate, gain, bias, decay = outs[count:]
    rest = rest_ref[...]
    share, depth = again.shape[1], rest.shape[1]
    place = lax.axis_index("dp") * lax.axis_size("seq") + lax.axis_index("seq")
    own = pltpu.roll(rest, lax.rem(depth - place * share, depth), 1)[:, :share]
    again[...] = own[0:1]
    mlp[...] = own[1:2]
    beta[...] = own[4 : 4 + beta.shape[0]]
    rate[...] = own[4 + beta.shape[0] :]
    for target, begin in zip((gain, bias, decay), marks):
        target[...] = rest_ref[2:3, begin : begin + target.shape[1]]


def finish(input_grad, edge_grad, rest, values, share, width, heads):
    wide, narrow = heads * REFLECTS, heads
    shapes = [(value.shape, value.dtype) for value in values]
    shapes += [(shape, F32) for shape in [(1, share)] * 2 + [(wide, share), (narrow, share), (1, width), (1, wide), (1, narrow)]]
    out = jax.ShapeDtypeStruct
    vmem = pl.BlockSpec(memory_space=pltpu.VMEM)
    return pl.pallas_call(
        partial(finish_kernel, (0, width, width + wide)),
        in_specs=[vmem] * (3 + len(values)),
        out_specs=[vmem] * (1 + len(shapes)),
        out_shape=[out(input_grad.shape, BF16)] + [out(*shape) for shape in shapes],
        compiler_params=pltpu.CompilerParams(vmem_limit_bytes=VMEM_LIMIT),
        cost_estimate=cost(3),
        name="finish",
    )(input_grad, edge_grad, rest, *values)


def dot32(a, b, dims=NN):
    return lax.dot_general(a, b, dims, preferred_element_type=F32)


def swap_core(value):
    count = lax.axis_size("dp")
    return lax.ppermute(value, "dp", [(i, (i + 1) % count) for i in range(count)])


def neighbour_route(bit):
    return [(i, i ^ bit) for i in range(16)]


def by_head(field, heads, begin, size):
    rows = field.shape[0]
    return field.reshape(rows, heads, -1)[:, :, begin : begin + size].reshape(rows, heads * size)


def per_device(
    block_input, lengths, attn_gain, w_query, w_key, w_value, w_outgate, w_beta, w_decay, beta_bias,
    decay_rate, conv_query, conv_key, conv_value, out_gain, w_out, mlp_gain, w_gate, w_up, w_down,
    out_grad,
):
    rows, depth = block_input.shape
    heads = decay_rate.shape[0]
    width = out_gain.shape[0]
    count = lax.axis_size("seq")
    seq = lax.axis_index("seq")
    group = lax.axis_index("dp")
    compact = count == 16
    wide = heads * REFLECTS
    ext_b, raw, live, acol, arow, halo, w_rates, rate = rates_forward(
        lengths, block_input, attn_gain, w_beta, w_decay, beta_bias, decay_rate, heads
    )
    taps = (conv_query, conv_key, conv_value)
    pre, gate_pre, oloc, oread, *saved, start, all_maps = mixer_forward(
        ext_b, w_query, w_key, w_value, w_outgate, taps, live, acol, arow, heads, width, count
    )
    block_output, d_out, part, d_resid, grad_mlp_gain, grad_out_gain, *rest = middle(
        compact, count, oloc, oread, start, gate_pre, out_gain, block_input, ext_b, mlp_gain, out_grad,
        all_maps, w_out, w_gate, w_up, w_down,
    )
    if compact:
        products, (own_l, got_l, after, d_outgate_b) = rest[: 2 * GROUPS], rest[2 * GROUPS :]
        arrived = [
            lax.ppermute(sent, "seq", neighbour_route(1 << links[0])) for sent, links in zip(products[::2], EARLY_LINKS)
        ]
    else:
        gated_b, hidden_b, d_gate_b, d_up_b, d_outgate_b, mlp_b, d_branch_b = rest
        after = carry_back(part, all_maps, count)
    d_all, d_tap_q, d_tap_k, d_tap_v, aux = mixer_backward(
        pre, taps, live, acol, arow, saved, start, after, d_out
    )
    input_grad, edge, rim, grad_attn_gain, grad_rates, misc = input_pull(
        d_all, d_outgate_b, (w_query, w_key, w_value, w_outgate), aux, raw, live, rate, w_rates, ext_b,
        block_input, halo, attn_gain, d_resid, heads,
    )
    last = width + wide + heads
    gains = (grad_attn_gain, grad_mlp_gain, grad_out_gain, misc)
    d_taps = (d_tap_q, d_tap_k, d_tap_v)
    devices = count * lax.axis_size("dp")
    share = depth // devices
    if compact:
        sums = reduce_all(
            arrived, products[1::2], own_l, got_l, d_all, d_taps, gains, grad_rates,
            edge, rim, attn_gain[None, :], w_gate.shape[1], heads,
        )
        trunk, taps_out, rest, edge_grad = sums[5:8], sums[8:11], sums[11], sums[12]
    else:
        normed_e = jnp.concatenate([ext_b[HALO:], ext_b[:HALO]], axis=0)
        normed_b = ext_b[HALO:]
        xf = block_input.astype(F32)
        tail = edge[0] + lax.ppermute(rim, "seq", [(i, i - 1) for i in range(1, count)])
        _, pulled = norm_pull(edge[1], attn_gain[None, :], tail)
        edge_grad = (edge[2] + pulled).astype(BF16)
        line = jnp.pad(jnp.concatenate(gains[2:], axis=1), ((0, 0), (0, depth - width - 128)))
        line = jnp.concatenate([*gains[:2], line, jnp.zeros((1, depth), F32)], axis=0)
        small = lax.psum(d_taps + (line, grad_rates), ("dp", "seq"))
        taps_out, rest = small[:3], jnp.concatenate(small[3:], axis=0)
        trunk = [by_head(d_all, heads, begin * width, size * width) for begin, size in ((0, 1), (1, 2), (3, 2))]
        pairs = zip(
            (mlp_b, mlp_b, out_grad, d_branch_b, normed_b) + (normed_e,) * 3, (d_gate_b, d_up_b, hidden_b, gated_b, d_outgate_b) + tuple(trunk)
        )
        sums = [
            lax.psum_scatter(dot32(lhs, rhs, TN), ("dp", "seq"), scatter_dimension=0, tiled=True)
            for lhs, rhs in pairs
        ]
        trunk = sums[5:]
    values = (block_output, *trunk, sums[4], *taps_out, sums[0], sums[1], sums[3], sums[2])
    done = finish(input_grad, edge_grad, rest, values, share, width, heads)
    (
        input_grad, block_output, g_query, g_key, g_value, g_outgate, g_conv_q, g_conv_k, g_conv_v, g_gate, g_up, g_out, g_down,
        g_attn, g_mlp, g_beta, g_decay, g_gain, g_bias, g_rate,
    ) = done
    return (
        block_output,
        input_grad,
        g_attn[0],
        g_query,
        g_key,
        g_value,
        g_outgate,
        g_beta.T,
        g_decay.T,
        g_bias[0],
        g_rate[0],
        g_conv_q,
        g_conv_k,
        g_conv_v,
        g_gain[0],
        g_out.T,
        g_mlp[0],
        g_gate,
        g_up,
        g_down.T,
    )


def solution(mesh):
    tokens = P(("dp", "seq"), None)
    column = P(None, ("dp", "seq"))
    vector = P(("dp", "seq"))
    in_specs = (tokens, P("dp", None)) + (P(),) * 18 + (tokens,)
    out_specs = (
        (tokens, tokens, vector)
        + (tokens,) * 6
        + (P(),) * 6
        + (column, vector, tokens, tokens, column)
    )
    return jax.shard_map(
        per_device, mesh=mesh, in_specs=in_specs, out_specs=out_specs, check_vma=False
    )
```

```python
from functools import partial

import jax
import jax.numpy as jnp
from jax import lax
from jax.experimental import pallas as pl
from jax.experimental.pallas import tpu as pltpu
from jax.sharding import PartitionSpec as P

REFLECTS = 2
KW = 4
BLOCK = 64
SHORTEST = 1024
STEPS = BLOCK * REFLECTS
HALO = 8
RESET_LOG = -80.0
MESH = pl.DeviceIdType.MESH
F32 = jnp.float32
BF16 = jnp.bfloat16
NN = (((1,), (0,)), ((), ()))
NT = (((1,), (1,)), ((), ()))
TN = (((0,), (0,)), ((), ()))
VMEM_LIMIT = 56 * 1024 * 1024
FORWARD_HEADS = 2
BACKWARD_HEADS = 1


def cost(microseconds):
    return pl.CostEstimate(
        flops=int(microseconds * 1e9), bytes_accessed=int(microseconds * 1e6), transcendentals=0
    )


def mm(a, b, dims=NN):
    return lax.dot_general(a.astype(BF16), b.astype(BF16), dims, preferred_element_type=F32)


def halves(a):
    high = a.astype(BF16)
    return high, (a - high.astype(F32)).astype(BF16)


def mm3(a, b):
    ah, al = halves(a)
    bh, bl = halves(b)
    return mm(jnp.concatenate([ah, al], axis=1), jnp.concatenate([bh, bh], axis=0)) + mm(ah, bl)


def mm2(a, b, dims=NN):
    ah, al = halves(a)
    return mm(ah, b, dims) + mm(al, b, dims)


def mm2t(a, b, dims=NN):
    bh, bl = halves(b)
    return mm(a, bh, dims) + mm(a, bl, dims)


def sigmoid(v):
    return 1.0 / (1.0 + jnp.exp(-v))


def step_ids(shape, axis):
    index = lax.broadcasted_iota(jnp.int32, shape, axis)
    return index % BLOCK, index // BLOCK


def step_masks():
    shape = (STEPS, STEPS)
    tm, jm = step_ids(shape, 0)
    tn, jn = step_ids(shape, 1)
    strict = (tm > tn) | ((tm == tn) & (jm > jn))
    size = 4
    first = tm // size == tn // size
    merges = []
    while size < BLOCK:
        merges.append((tm // (2 * size) == tn // (2 * size)) & (tm // size != tn // size))
        size = 2 * size
    eye = ((tm == tn) & (jm == jn)).astype(F32)
    return tm >= tn, strict, first, merges, eye


def unit_lower_inverse(systems, first, merges, eye):
    neg = [jnp.where(first, -a, 0.0) for a in systems]
    inv = [eye + n for n in neg]
    for _ in range(2):
        neg = [mm3(n, n) for n in neg]
        inv = [t + mm3(t, n) for t, n in zip(inv, neg)]
    for merge in merges:
        off = [mm3(jnp.where(merge, a, 0.0), t) for a, t in zip(systems, inv)]
        inv = [t - mm3(t, o) for t, o in zip(inv, off)]
    return inv


def conv_parts(ext_ref, taps, live, columns, rows):
    total = None
    for back in range(KW):
        part = ext_ref[pl.ds(HALO - back, rows), columns] * taps[KW - 1 - back : KW - back, :]
        if back > 0:
            part = part * live[:, back : back + 1]
        total = part if total is None else total + part
    return total


def head_features(ext_ref, tq, tk, tv, live, rows, width):
    conv = [
        conv_parts(ext_ref, tq, live, pl.ds(0, width), rows),
        conv_parts(ext_ref, tk[:, :width], live, pl.ds(width, width), rows),
        conv_parts(ext_ref, tk[:, width:], live, pl.ds(2 * width, width), rows),
        conv_parts(ext_ref, tv[:, :width], live, pl.ds(3 * width, width), rows),
        conv_parts(ext_ref, tv[:, width:], live, pl.ds(4 * width, width), rows),
    ]
    return conv


def unit_rows(act):
    return lax.rsqrt(jnp.sum(act * act, axis=-1, keepdims=True) + 1e-06)


def greet_group(count):
    place, group = lax.axis_index("seq"), lax.axis_index("dp")
    barrier = pltpu.get_barrier_semaphore()

    def greet(step, carry):
        peer = lax.rem(place + step, count)
        pl.semaphore_signal(barrier, inc=1, device_id=(group, peer), device_id_type=MESH)
        return carry

    lax.fori_loop(1, count, greet, 0)
    return barrier


def carry_steps(count, heads, backward, part_ref, maps_ref, inbox, outbox, landed, sems):
    send_sem, recv_sem, back_sem, land_sem = sems
    place, group = lax.axis_index("seq"), lax.axis_index("dp")
    width = landed.shape[-1]
    stride = count // 16

    def keeper(h):
        return (2 * h + group) * stride

    def outgoing(h):
        return pltpu.make_async_remote_copy(
            src_ref=part_ref.at[h],
            dst_ref=inbox.at[place],
            send_sem=send_sem.at[h],
            recv_sem=recv_sem.at[place],
            device_id=(group, keeper(h)),
            device_id_type=MESH,
        )

    def send(h):
        @pl.when(place != keeper(h))
        def _():
            outgoing(h).start()

        @pl.when(place == keeper(h))
        def _():
            inbox[pl.ds(place, 1)] = part_ref[pl.ds(h, 1)]

    def scan_head(h):
        def returning(where):
            return pltpu.make_async_remote_copy(
                src_ref=outbox.at[where],
                dst_ref=landed.at[h],
                send_sem=back_sem.at[where],
                recv_sem=land_sem.at[h],
                device_id=(group, where),
                device_id_type=MESH,
            )

        def lap(step, state):
            where = count - 1 - step if backward else step
            outbox[pl.ds(where, 1)] = state[None].astype(BF16)

            @pl.when(where != place)
            def _():
                returning(where).start()
                pltpu.make_async_remote_copy(
                    src_ref=part_ref.at[h],
                    dst_ref=inbox.at[where],
                    send_sem=send_sem.at[h],
                    recv_sem=recv_sem.at[where],
                    device_id=(group, where),
                    device_id_type=MESH,
                ).wait_recv()

            @pl.when(where == place)
            def _():
                landed[h : h + 1] = outbox[pl.ds(where, 1)]

            got = inbox[pl.ds(where, 1)][0]
            high, low = halves(state)
            both = jnp.concatenate([high, low], axis=1)
            if backward:
                moved = mm(maps_ref[pl.ds(where, 1)][0][:, width:], both, TN)
            else:
                moved = mm(got[:, width:], both)
            return moved[:, :width] + moved[:, width:] + got[:, :width].astype(F32)

        lax.fori_loop(0, count, lap, jnp.zeros((width, width), F32))

        def finish(where, carry):
            @pl.when(where != place)
            def _():
                returning(where).wait_send()

            return carry

        return lambda: lax.fori_loop(0, count, finish, 0)

    def scan():
        for h in range(heads):

            @pl.when(place == keeper(h))
            def _(h=h):
                scan_head(h)()

    def take():
        for h in range(heads):

            @pl.when(place != keeper(h))
            def _(h=h):
                outgoing(h).wait_send()
                pltpu.make_async_remote_copy(
                    src_ref=outbox.at[0],
                    dst_ref=landed.at[h],
                    send_sem=back_sem.at[0],
                    recv_sem=land_sem.at[h],
                    device_id=(group, keeper(h)),
                    device_id_type=MESH,
                ).wait_recv()

    return send, scan, take


def carry_scratch(count, heads, width, columns):
    dma = pltpu.SemaphoreType.DMA
    return [
        pltpu.VMEM((count, width, columns), BF16),
        pltpu.VMEM((count, width, width), BF16),
        pltpu.VMEM((heads, width, width), BF16),
        dma((heads,)),
        dma((count,)),
        dma((count,)),
        dma((heads,)),
    ]


def mixer_forward_kernel(
    count, every_head, xn_ref, wq_ref, wk_ref, wv_ref, wg_ref, tq_ref, tk_ref, tv_ref, live_ref, acol_ref, arow_ref,
    pre_ref, gate_ref, oloc_ref, oread_ref, inv_ref, delta_ref, state_ref, turn_ref, carry_ref, start_ref, maps_ref,
    ext_ref, part_ref, inbox, outbox, landed, *sems,
):
    heads, rows, width = oread_ref.shape
    turn_at = pl.program_id(0)
    barrier = pltpu.get_barrier_semaphore()

    @pl.when(turn_at == 0)
    def _():
        greet_group(count)

    give, scan, take = carry_steps(count, every_head, False, part_ref, None, inbox, outbox, landed, sems)
    blocks = rows // BLOCK
    xn = xn_ref[...]
    live = live_ref[...]
    gate_ref[...] = mm(xn[HALO:], wg_ref[...])
    query, key, value = mm(xn, wq_ref[...]), mm(xn, wk_ref[...]), mm(xn, wv_ref[...])
    reach, strict, first, merges, eye = step_masks()
    cut = [slice(b * BLOCK, (b + 1) * BLOCK) for b in range(blocks)]
    every = [(n, b) for n in range(heads) for b in range(blocks)]
    qb, kb, vb = {}, {}, {}
    for n in range(heads):
        one, two = slice(n * width, (n + 1) * width), slice(2 * n * width, 2 * (n + 1) * width)
        pre = jnp.concatenate([query[:, one], key[:, two], value[:, two]], axis=1).astype(BF16)
        pre_ref[n] = pre
        ext_ref[n] = pre.astype(F32)
        conv = head_features(ext_ref.at[n], tq_ref[:, one], tk_ref[:, two], tv_ref[:, two], live, rows, width)
        act = [c * sigmoid(c) for c in conv]
        q = (act[0] * unit_rows(act[0]) * width ** (-0.5)).astype(BF16)
        k = [(a * unit_rows(a)).astype(BF16) for a in act[1:3]]
        v = [a.astype(BF16) for a in act[3:5]]
        for b in range(blocks):
            qb[n, b] = q[cut[b]]
            kb[n, b] = jnp.concatenate([k[0][cut[b]], k[1][cut[b]]], axis=0)
            vb[n, b] = jnp.concatenate([v[0][cut[b]], v[1][cut[b]]], axis=0)
    ccol = {at: acol_ref[at[0], at[1], :, 0:1] for at in every}
    bcol = {at: acol_ref[at[0], at[1], :, 1:2] for at in every}
    crow = {at: arow_ref[at[0], at[1], 0:1, :] for at in every}
    brow = {at: arow_ref[at[0], at[1], 1:2, :] for at in every}
    fade = {at: jnp.exp(jnp.where(reach, ccol[at] - crow[at], -1e30)) for at in every}
    system = [jnp.where(strict, fade[at] * mm(kb[at], kb[at], NT), 0.0) * bcol[at] for at in every]
    inv = dict(zip(every, unit_lower_inverse(system, first, merges, eye)))
    for at in every:
        inv_ref[at[0], at[1]] = inv[at].astype(BF16)
    local = {at: mm2(inv[at] * brow[at], vb[at]) for at in every}
    reads = {at: mm2(inv[at] * (brow[at] * jnp.exp(crow[at])), kb[at]) for at in every}
    score = {at: fade[at][:BLOCK] * mm(qb[at], kb[at], NT) for at in every}
    grow = {at: jnp.exp(ccol[at]) for at in every}
    last = {at: ccol[at][BLOCK - 1 : BLOCK] for at in every}
    tail = {at: kb[at].astype(F32) * jnp.exp(last[at] - ccol[at]) for at in every}
    both = {at: jnp.concatenate([local[at], -reads[at]], axis=1).astype(BF16) for at in every}
    turn = {at: mm(tail[at], both[at], TN) for at in every}
    query_out = {at: mm(score[at], both[at]) for at in every}
    state = {}
    for n in range(heads):
        now = jnp.concatenate([jnp.zeros((width, width), F32), eye], axis=1)
        for b in range(blocks):
            at = (n, b)
            state[at] = now
            step = turn[at][:, width:].astype(BF16)
            turn_ref[n, b] = step
            fixed = jnp.concatenate([turn[at][:, :width], jnp.zeros((width, width), F32)], axis=1)
            now = jnp.exp(last[at]) * now + fixed + mm(step, now)
        part_ref[pl.ds(turn_at * heads + n, 1)] = now.astype(BF16)[None]

    @pl.when(turn_at == 0)
    def _():
        pl.semaphore_wait(barrier, count - 1)

    for n in range(heads):
        give(turn_at * heads + n)
    for at in every:
        n, b = at
        carried = query_out[at][:, width:] + grow[at][:BLOCK] * qb[at].astype(F32)
        low = state[at].astype(BF16)
        carry_ref[n, b] = carried.astype(BF16)
        state_ref[n, b] = low
        fixed = jnp.concatenate([local[at], jnp.zeros((STEPS, width), F32)], axis=1)
        delta_ref[n, b] = (fixed - mm(reads[at], low)).astype(BF16)
        out = mm(carried, low)
        oloc_ref[cut[b], n * width : (n + 1) * width] = out[:, :width] + query_out[at][:, :width]
        oread_ref[n, cut[b], :] = out[:, width:].astype(BF16)

    @pl.when(turn_at == pl.num_programs(0) - 1)
    def _():
        scan()
        take()
        start_ref[...] = landed[...]
        maps_ref[...] = inbox[...]


def head_columns(rows, width):
    return pl.BlockSpec((rows, width), lambda h: (0, h))


def whole(shape):
    return pl.BlockSpec(shape, lambda h: (0,) * len(shape))


def per_head(shape, group=1):
    return pl.BlockSpec((group,) + shape, lambda h: (h,) + (0,) * len(shape))


def mixer_forward(xn, w_query, w_key, w_value, w_outgate, taps, live, acol, arow, heads, width, count):
    ext_rows, depth = xn.shape
    rows = ext_rows - HALO
    blocks = rows // BLOCK
    conv_query, conv_key, conv_value = taps
    out = jax.ShapeDtypeStruct
    return pl.pallas_call(
        partial(mixer_forward_kernel, count, heads),
        grid=(heads // FORWARD_HEADS,),
        in_specs=[
            whole((ext_rows, depth)),
            head_columns(depth, FORWARD_HEADS * width),
            head_columns(depth, 2 * FORWARD_HEADS * width),
            head_columns(depth, 2 * FORWARD_HEADS * width),
            head_columns(depth, FORWARD_HEADS * width),
            head_columns(KW, FORWARD_HEADS * width),
            head_columns(KW, 2 * FORWARD_HEADS * width),
            head_columns(KW, 2 * FORWARD_HEADS * width),
            whole(live.shape),
            per_head(acol.shape[1:], FORWARD_HEADS),
            per_head(arow.shape[1:], FORWARD_HEADS),
        ],
        out_specs=[
            per_head((ext_rows, 5 * width), FORWARD_HEADS),
            head_columns(rows, FORWARD_HEADS * width),
            head_columns(rows, FORWARD_HEADS * width),
            per_head((rows, width), FORWARD_HEADS),
            per_head((blocks, STEPS, STEPS), FORWARD_HEADS),
            per_head((blocks, STEPS, 2 * width), FORWARD_HEADS),
            per_head((blocks, width, 2 * width), FORWARD_HEADS),
            per_head((blocks, width, width), FORWARD_HEADS),
            per_head((blocks, BLOCK, width), FORWARD_HEADS),
            whole((heads, width, width)),
            whole((count, width, 2 * width)),
        ],
        out_shape=[
            out((heads, ext_rows, 5 * width), BF16),
            out((rows, heads * width), F32),
            out((rows, heads * width), F32),
            out((heads, rows, width), BF16),
            out((heads, blocks, STEPS, STEPS), BF16),
            out((heads, blocks, STEPS, 2 * width), BF16),
            out((heads, blocks, width, 2 * width), BF16),
            out((heads, blocks, width, width), BF16),
            out((heads, blocks, BLOCK, width), BF16),
            out((heads, width, width), BF16),
            out((count, width, 2 * width), BF16),
        ],
        scratch_shapes=[
            pltpu.VMEM((FORWARD_HEADS, ext_rows, 5 * width), F32),
            pltpu.VMEM((heads, width, 2 * width), BF16),
        ]
        + carry_scratch(count, heads, width, 2 * width),
        compiler_params=pltpu.CompilerParams(
            collective_id=0, has_side_effects=True, vmem_limit_bytes=VMEM_LIMIT
        ),
        cost_estimate=cost(40),
        name="mixer_forward",
    )(xn, w_query, w_key, w_value, w_outgate, conv_query, conv_key, conv_value, live, acol, arow)


def conv_pull(ext_ref, pad_ref, d_conv, taps, live, columns, rows, dtap_ref):
    total = None
    for back in range(KW):
        part = d_conv if back == 0 else d_conv * live[:, back : back + 1]
        source = ext_ref[pl.ds(HALO - back, rows), columns]
        dtap_ref[KW - 1 - back : KW - back, :] = jnp.sum(part * source, axis=0, keepdims=True)
        pad_ref[pl.ds(HALO, rows), :] = part
        moved = pad_ref[pl.ds(back, rows + HALO), :] * taps[KW - 1 - back : KW - back, :]
        total = moved if total is None else total + moved
    return total


def silu_pull(c, grad):
    s = sigmoid(c)
    return grad * (s + c * s * (1.0 - s))


def unit_pull(act, grad, scale):
    r = unit_rows(act)
    return scale * r * (grad - act * (r * r * jnp.sum(act * grad, axis=-1, keepdims=True)))


def mixer_backward_kernel(
    pre_ref, tq_ref, tk_ref, tv_ref, live_ref, acol_ref, arow_ref,
    inv_ref, delta_ref, state_ref, turn_ref, carry_ref, start_ref, after_ref, dout_ref,
    d_ref, dtq_ref, dtk_ref, dtv_ref, aux_ref,
    ext_ref, pad_ref,
):
    heads = pre_ref.shape[0]
    rows = dout_ref.shape[0]
    width = start_ref.shape[-1]
    blocks = rows // BLOCK
    live = live_ref[...]
    every = [(n, b) for n in range(heads) for b in range(blocks)]
    cut = [slice(b * BLOCK, (b + 1) * BLOCK) for b in range(blocks)]
    conv, act, qb, kb, dout = {}, {}, {}, {}, {}
    for n in range(heads):
        one, two = slice(n * width, (n + 1) * width), slice(2 * n * width, 2 * (n + 1) * width)
        ext_ref[n] = pre_ref[n].astype(F32)
        conv[n] = head_features(ext_ref.at[n], tq_ref[:, one], tk_ref[:, two], tv_ref[:, two], live, rows, width)
        act[n] = [c * sigmoid(c) for c in conv[n][:3]]
        q = (act[n][0] * unit_rows(act[n][0]) * width ** (-0.5)).astype(BF16)
        k = [(a * unit_rows(a)).astype(BF16) for a in act[n][1:]]
        for b in range(blocks):
            qb[n, b] = q[cut[b]]
            kb[n, b] = jnp.concatenate([k[0][cut[b]], k[1][cut[b]]], axis=0)
            dout[n, b] = dout_ref[cut[b], one]
    reach, strict, _, _, _ = step_masks()
    ccol = {at: acol_ref[at[0], at[1], :, 0:1] for at in every}
    bcol = {at: acol_ref[at[0], at[1], :, 1:2] for at in every}
    crow = {at: arow_ref[at[0], at[1], 0:1, :] for at in every}
    last = {at: ccol[at][BLOCK - 1 : BLOCK] for at in every}
    grow = {at: jnp.exp(ccol[at]) for at in every}
    weight = {at: jnp.exp(last[at] - ccol[at]) for at in every}
    ahead = {at: mm(carry_ref[at[0], at[1]], dout[at], TN) for at in every}
    after = {}
    for n in range(heads):
        now = after_ref[n].astype(F32)
        for b in range(blocks - 1, -1, -1):
            after[n, b] = now
            now = jnp.exp(last[n, b]) * now + ahead[n, b] + mm(turn_ref[n, b], now, TN)
    fade = {at: jnp.exp(jnp.where(reach, ccol[at] - crow[at], -1e30)) for at in every}
    delta = {
        at: delta_ref[at[0], at[1], :, :width].astype(F32) + mm(delta_ref[at[0], at[1], :, width:], start_ref[at[0]])
        for at in every
    }
    state = {
        at: state_ref[at[0], at[1], :, :width].astype(F32) + mm(state_ref[at[0], at[1], :, width:], start_ref[at[0]])
        for at in every
    }
    score = {at: fade[at][:BLOCK] * mm(qb[at], kb[at], NT) for at in every}
    d_delta = {at: mm(score[at], dout[at], TN) + weight[at] * mm2t(kb[at], after[at]) for at in every}
    d_rhs = {at: mm2t(inv_ref[at[0], at[1]], d_delta[at], TN) for at in every}
    d_score = {at: (fade[at][:BLOCK] * mm(dout[at], delta[at], NT)).astype(BF16) for at in every}
    d_tail = {at: weight[at] * mm(delta[at], after[at], NT) for at in every}
    d_gram = {
        at: jnp.where(strict, -bcol[at] * fade[at] * mm(d_rhs[at], delta[at], NT), 0.0).astype(BF16) for at in every
    }
    dq = {at: mm(grow[at][:BLOCK] * dout[at], state[at], NT) + mm(d_score[at], kb[at]) for at in every}
    dk_row = {
        at: mm(-(bcol[at] * grow[at]) * d_rhs[at], state[at], NT) + mm(d_gram[at], kb[at]) for at in every
    }
    dk_col = {at: mm(d_gram[at], kb[at], TN) + mm(d_score[at], qb[at], TN) + d_tail[at] for at in every}
    tok = lax.broadcasted_iota(jnp.int32, (BLOCK, 1), 0)
    for at in every:
        kf = kb[at].astype(F32)
        d_beta = (1.0 - bcol[at]) * jnp.sum(d_rhs[at] * delta[at], axis=-1, keepdims=True)
        d_log = jnp.sum(kf * (dk_row[at] - dk_col[at]), axis=-1, keepdims=True)
        d_logq = jnp.sum(qb[at].astype(F32) * dq[at], axis=-1, keepdims=True)
        d_last = jnp.sum(kf * d_tail[at]) + jnp.sum(jnp.exp(last[at]) * after[at] * state[at])
        d_token = d_log[:BLOCK] + d_log[BLOCK:] + d_logq + jnp.where(tok == BLOCK - 1, d_last, 0.0)
        aux_ref[at[0], at[1], :, 0:1] = d_beta
        aux_ref[at[0], at[1], 0:BLOCK, 1:2] = d_token
    pad_ref[0:HALO, :] = jnp.zeros((HALO, width), F32)
    pad_ref[pl.ds(HALO + rows, HALO), :] = jnp.zeros((HALO, width), F32)
    for n in range(heads):
        keys = {b: dk_row[n, b] + dk_col[n, b] for b in range(blocks)}
        values = {b: bcol[n, b] * d_rhs[n, b] for b in range(blocks)}
        d_act = [
            jnp.concatenate([dq[n, b] for b in range(blocks)], axis=0),
            jnp.concatenate([keys[b][:BLOCK] for b in range(blocks)], axis=0),
            jnp.concatenate([keys[b][BLOCK:] for b in range(blocks)], axis=0),
            jnp.concatenate([values[b][:BLOCK] for b in range(blocks)], axis=0),
            jnp.concatenate([values[b][BLOCK:] for b in range(blocks)], axis=0),
        ]
        for i, scale in enumerate((width ** (-0.5), 1.0, 1.0)):
            d_act[i] = unit_pull(act[n][i], d_act[i], scale)
        sides = (
            (tq_ref, dtq_ref, n),
            (tk_ref, dtk_ref, 2 * n),
            (tk_ref, dtk_ref, 2 * n + 1),
            (tv_ref, dtv_ref, 2 * n),
            (tv_ref, dtv_ref, 2 * n + 1),
        )
        for i, (tap_ref, dtap_ref, at) in enumerate(sides):
            lanes = pl.ds(at * width, width)
            grad = conv_pull(
                ext_ref.at[n], pad_ref, silu_pull(conv[n][i], d_act[i]), tap_ref[:, lanes], live,
                pl.ds(i * width, width), rows, dtap_ref.at[:, lanes],
            )
            target = pl.ds((5 * n + i) * width, width)
            d_ref[0:rows, target] = grad[HALO:].astype(BF16)
            d_ref[rows : rows + HALO, target] = grad[:HALO].astype(BF16)


def mixer_backward(pre, taps, live, acol, arow, saved, start, after, dout):
    heads, ext_rows, _ = pre.shape
    rows = ext_rows - HALO
    width = start.shape[-1]
    conv_query, conv_key, conv_value = taps
    out = jax.ShapeDtypeStruct
    columns = heads * width
    group = BACKWARD_HEADS
    tap_specs = [head_columns(KW, times * group * width) for times in (1, 2, 2)]
    return pl.pallas_call(
        mixer_backward_kernel,
        grid=(heads // group,),
        in_specs=[per_head(pre.shape[1:], group)]
        + tap_specs
        + [whole(live.shape)]
        + [per_head(value.shape[1:], group) for value in (acol, arow, *saved, start, after)]
        + [head_columns(rows, group * width)],
        out_specs=[head_columns(ext_rows, 5 * group * width)] + tap_specs + [per_head(acol.shape[1:], group)],
        out_shape=[
            out((ext_rows, 5 * columns), BF16),
            out((KW, columns), F32),
            out((KW, 2 * columns), F32),
            out((KW, 2 * columns), F32),
            out(acol.shape, F32),
        ],
        scratch_shapes=[
            pltpu.VMEM((group, ext_rows, 5 * width), F32),
            pltpu.VMEM((rows + 2 * HALO, width), F32),
        ],
        compiler_params=pltpu.CompilerParams(vmem_limit_bytes=VMEM_LIMIT),
        cost_estimate=cost(35),
        name="mixer_backward",
    )(pre, conv_query, conv_key, conv_value, live, acol, arow, *saved, start, after, dout)


def carry_kernel(count, heads, part_ref, maps_ref, result_ref, inbox, outbox, landed, *sems):
    barrier = greet_group(count)
    pl.semaphore_wait(barrier, count - 1)
    send, scan, take = carry_steps(count, heads, True, part_ref, maps_ref, inbox, outbox, landed, sems)
    for h in range(heads):
        send(h)
    scan()
    take()
    result_ref[...] = landed[...]


def carry_back(part, maps, count):
    heads, width, _ = part.shape
    vmem = pl.BlockSpec(memory_space=pltpu.VMEM)
    return pl.pallas_call(
        partial(carry_kernel, count, heads),
        in_specs=[vmem] * 2,
        out_specs=vmem,
        out_shape=jax.ShapeDtypeStruct((heads, width, width), BF16),
        scratch_shapes=carry_scratch(count, heads, width, width),
        compiler_params=pltpu.CompilerParams(
            collective_id=1, has_side_effects=True, vmem_limit_bytes=VMEM_LIMIT
        ),
        cost_estimate=cost(24),
        name="carry_back",
    )(part, maps)


JOBS = 7
JOB = 512
GROUPS = 3
LATE_JOBS = 10
EARLY_LINKS = ((0, 1, 2, 3), (1, 2, 0, 3), (2, 0, 1, 3))
LATE_LINKS = ((0, 1, 2, 3), (1, 0, 2, 3))


def half_rows(lhs, links, sending, lanes=slice(None)):
    edge = lhs.shape[0] // 8
    parts = []
    for second in range(2):
        for third in range(2):
            move = {links[0]: int(sending), links[1]: second, links[2]: third}
            block = 4 * move[0] + 2 * move[1] + move[2]
            parts.append(lhs[block * edge : (block + 1) * edge, lanes])
    return jnp.concatenate(parts, axis=0)


def column_pieces(sizes, begin, end):
    at, pieces = 0, []
    for index, size in enumerate(sizes):
        low, high = max(at, begin), min(at + size, end)
        if low < high:
            pieces.append((index, low - at, low - begin, high - low))
        at += size
    return pieces


def input_pull_kernel(
    d_ref, dg_ref, wq_ref, wk_ref, wv_ref, wg_ref, aux_ref, raw_ref, live_ref, rate_ref, wr_ref, ext_ref,
    x_ref, halo_ref, gain_ref, resid_ref,
    grad_ref, edge_ref, rim_ref, dgain_ref, drates_ref, misc_ref, total_ref, rates_ref,
):
    head = pl.program_id(0)
    rows = dg_ref.shape[0]
    width = dg_ref.shape[1] // PULL_HEADS
    group = PULL_HEADS
    part = None
    for n in range(group):
        d = d_ref[:, n * 5 * width : (n + 1) * 5 * width]
        two = slice(2 * n * width, 2 * (n + 1) * width)
        term = (
            mm(d[:, :width], wq_ref[:, n * width : (n + 1) * width], NT)
            + mm(d[:, width : 3 * width], wk_ref[:, two], NT)
            + mm(d[:, 3 * width :], wv_ref[:, two], NT)
        )
        part = term if part is None else part + term
    more = mm(dg_ref[...], wg_ref[...], NT)

    @pl.when(head == 0)
    def _():
        heads, blocks = aux_ref.shape[:2]
        wide = heads * REFLECTS
        rates_ref[...] = jnp.zeros_like(rates_ref)
        for h in range(heads):
            for b in range(blocks):
                tokens = slice(b * BLOCK, (b + 1) * BLOCK)
                for j in range(REFLECTS):
                    at = h * REFLECTS + j
                    rates_ref[tokens, at : at + 1] = aux_ref[h, b, j * BLOCK : (j + 1) * BLOCK, 0:1]
                rates_ref[tokens, wide + h : wide + h + 1] = aux_ref[h, b, 0:BLOCK, 1:2]
        value, raw = rates_ref[...], raw_ref[...]
        d_log = exact_sum(block_sums(rows, True), value) * live_ref[:, 1:2]
        lane = lax.broadcasted_iota(jnp.int32, raw.shape, 1)
        d_raw = jnp.where(lane < wide, value, -rate_ref[...] * sigmoid(raw) * d_log)
        summed = jnp.where(lane < wide, value, -softplus(raw) * d_log)
        misc_ref[...] = jnp.sum(summed, axis=0, keepdims=True)
        d_raw = d_raw.astype(BF16)
        drates_ref[...] = mm(d_raw, ext_ref[pl.ds(HALO, rows), :], TN)[: drates_ref.shape[0]]
        total_ref[...] = part
        total_ref[0:rows, :] += more + mm(d_raw, wr_ref[...])

    @pl.when(head > 0)
    def _():
        total_ref[...] += part
        total_ref[0:rows, :] += more

    @pl.when(head == pl.num_programs(0) - 1)
    def _():
        grad = total_ref[...]
        unit, pulled = norm_pull(x_ref[...].astype(F32), gain_ref[...], grad[:rows])
        grad_ref[...] = (resid_ref[...] + pulled).astype(BF16)
        halo_unit, _ = norm_pull(halo_ref[...].astype(F32), gain_ref[...], grad[rows:])
        dgain_ref[...] = jnp.sum(grad[:rows] * unit, axis=0, keepdims=True) + jnp.sum(
            grad[rows:] * halo_unit, axis=0, keepdims=True
        )
        edge_ref[0] = grad[rows - HALO : rows]
        edge_ref[1] = x_ref[rows - HALO :, :].astype(F32)
        edge_ref[2] = resid_ref[rows - HALO :, :]
        rim_ref[...] = grad[rows:]


def norm_pull(x, gain, grad):
    r = lax.rsqrt(jnp.mean(x * x, axis=-1, keepdims=True) + 1e-06)
    unit = x * r
    through = grad * gain
    return unit, r * (through - unit * jnp.mean(unit * through, axis=-1, keepdims=True))


PULL_HEADS = 2


def input_pull(d_all, d_outgate, weights, aux, raw, live, rate, w_rates, ext_b, x, halo, gain, d_resid, heads):
    rows, depth = x.shape
    ext_rows = rows + HALO
    width = d_outgate.shape[1] // heads * PULL_HEADS
    out = jax.ShapeDtypeStruct
    w_query, w_key, w_value, w_outgate = weights
    rates = heads * (REFLECTS + 1)
    return pl.pallas_call(
        input_pull_kernel,
        grid=(heads // PULL_HEADS,),
        in_specs=[
            head_columns(ext_rows, 5 * width),
            head_columns(rows, width),
            head_columns(depth, width),
            head_columns(depth, 2 * width),
            head_columns(depth, 2 * width),
            head_columns(depth, width),
            whole(aux.shape),
            whole(raw.shape),
            whole(live.shape),
            whole(rate.shape),
            whole(w_rates.shape),
            whole(ext_b.shape),
            whole(x.shape),
            whole(halo.shape),
            whole((1, depth)),
            whole(d_resid.shape),
        ],
        out_specs=[
            whole((rows, depth)), whole((3, HALO, depth)), whole((HALO, depth)), whole((1, depth)),
            whole((rates, depth)), whole((1, raw.shape[1])),
        ],
        out_shape=[
            out((rows, depth), BF16),
            out((3, HALO, depth), F32),
            out((HALO, depth), F32),
            out((1, depth), F32),
            out((rates, depth), F32),
            out((1, raw.shape[1]), F32),
        ],
        scratch_shapes=[pltpu.VMEM((ext_rows, depth), F32), pltpu.VMEM(raw.shape, F32)],
        compiler_params=pltpu.CompilerParams(vmem_limit_bytes=VMEM_LIMIT),
        cost_estimate=cost(12),
        name="input_pull",
    )(
        d_all, d_outgate, w_query, w_key, w_value, w_outgate, aux, raw, live, rate, w_rates, ext_b,
        x, halo, gain[None, :], d_resid,
    )


def exact_sum(ones, value):
    total = None
    for _ in range(3):
        part = value.astype(BF16)
        value = value - part.astype(F32)
        term = mm(ones, part)
        total = term if total is None else total + term
    return total


def block_sums(rows, reverse):
    shape = (rows, rows)
    one, two = lax.broadcasted_iota(jnp.int32, shape, 0), lax.broadcasted_iota(jnp.int32, shape, 1)
    order = (one <= two) if reverse else (one >= two)
    return ((one // BLOCK == two // BLOCK) & order).astype(BF16)


def softplus(v):
    return jnp.maximum(v, 0.0) + jnp.log1p(jnp.exp(-jnp.abs(v)))


def rates_kernel(
    heads, lengths_ref, x_ref, gain_ref, wbeta_ref, wdecay_ref, bias_in_ref, rate_in_ref,
    ext_ref, raw_ref, live_ref, acol_ref, arow_ref, halo_ref, weight_ref, rate_ref,
    edge_ref, got_ref, sems,
):
    rows = x_ref.shape[0]
    blocks = rows // BLOCK
    wide = heads * REFLECTS
    seq, count = lax.axis_index("seq"), lax.axis_size("seq")
    behind, before = lax.rem(seq + 1, count), lax.rem(seq + count - 1, count)
    barrier = pltpu.get_barrier_semaphore()
    for place in (behind, before):
        pl.semaphore_signal(barrier, inc=1, device_id={"seq": place}, device_id_type=MESH)
    edge_ref[...] = x_ref[rows - HALO :, :]
    copy = pltpu.make_async_remote_copy(
        src_ref=edge_ref,
        dst_ref=got_ref,
        send_sem=sems.at[0],
        recv_sem=sems.at[1],
        device_id={"seq": behind},
        device_id_type=MESH,
    )

    def normed(field):
        field = field.astype(F32)
        return (
            field * lax.rsqrt(jnp.mean(field * field, axis=-1, keepdims=True) + 1e-06) * gain_ref[...]
        ).astype(BF16)

    pl.semaphore_wait(barrier, 2)
    copy.start()
    xn = normed(x_ref[...])
    ext_ref[pl.ds(HALO, rows), :] = xn
    blank = jnp.zeros((128 - wide - heads, wbeta_ref.shape[1]), F32)
    weight = jnp.concatenate([wbeta_ref[...].astype(F32), wdecay_ref[...].astype(F32), blank], axis=0).astype(BF16)
    weight_ref[...] = weight
    empty = jnp.zeros((1, 128 - wide - heads), F32)
    bias = jnp.concatenate([bias_in_ref[...], jnp.zeros((1, heads), F32), empty], axis=1)
    rate = jnp.concatenate([jnp.zeros((1, wide), F32), rate_in_ref[...], empty], axis=1)
    rate_ref[...] = rate
    raw = mm(xn, weight, NT)
    raw_ref[...] = raw
    row = lax.axis_index("seq") * rows + lax.broadcasted_iota(jnp.int32, (rows, 1), 0)
    place, end = row, 0
    for i in range(lengths_ref.shape[1]):
        begin, end = end, end + lengths_ref[0, i] + (SHORTEST - 1)
        place = jnp.where((row >= begin) & (row < end), row - begin, place)
    live_ref[...] = (place >= lax.broadcasted_iota(jnp.int32, (rows, 8), 1)).astype(F32)
    beta = sigmoid(raw + bias)
    log_rate = jnp.where(place == 0, RESET_LOG, -rate * softplus(raw))
    lane = lax.broadcasted_iota(jnp.int32, raw.shape, 1)
    both = jnp.where(lane < wide, beta, exact_sum(block_sums(rows, False), log_rate))
    turned = both.T
    arow_ref[...] = jnp.zeros_like(arow_ref)
    acol_ref[...] = jnp.zeros_like(acol_ref)
    for h in range(heads):
        for b in range(blocks):
            tokens = slice(b * BLOCK, (b + 1) * BLOCK)
            for j in range(REFLECTS):
                steps = slice(j * BLOCK, (j + 1) * BLOCK)
                at = h * REFLECTS + j
                acol_ref[h, b, steps, 0:1] = both[tokens, wide + h : wide + h + 1]
                acol_ref[h, b, steps, 1:2] = both[tokens, at : at + 1]
                arow_ref[h, b, 0:1, steps] = turned[wide + h : wide + h + 1, tokens]
                arow_ref[h, b, 1:2, steps] = turned[at : at + 1, tokens]
    copy.wait()
    halo = jnp.where(seq > 0, got_ref[...].astype(F32), 0.0)
    halo_ref[...] = halo.astype(BF16)
    ext_ref[0:HALO, :] = normed(halo)


def rates_forward(lengths, x, gain, w_beta, w_decay, bias, rate, heads):
    rows, depth = x.shape
    blocks = rows // BLOCK
    out = jax.ShapeDtypeStruct
    vmem = pl.BlockSpec(memory_space=pltpu.VMEM)
    return pl.pallas_call(
        partial(rates_kernel, heads),
        in_specs=[pl.BlockSpec(memory_space=pltpu.SMEM)] + [vmem] * 6,
        out_specs=[vmem] * 8,
        out_shape=[
            out((rows + HALO, depth), BF16),
            out((rows, 128), F32),
            out((rows, 8), F32),
            out((heads, blocks, STEPS, 8), F32),
            out((heads, blocks, 8, STEPS), F32),
            out((HALO, depth), BF16),
            out((128, depth), BF16),
            out((1, 128), F32),
        ],
        scratch_shapes=[
            pltpu.VMEM((HALO, depth), BF16), pltpu.VMEM((HALO, depth), BF16), pltpu.SemaphoreType.DMA((2,)),
        ],
        compiler_params=pltpu.CompilerParams(
            collective_id=4, has_side_effects=True, vmem_limit_bytes=VMEM_LIMIT
        ),
        cost_estimate=cost(6),
        name="rates_forward",
    )(lengths, x, gain[None, :], w_beta.T, w_decay.T, bias[None, :], rate[None, :])


CHUNK = 256
RING = 6


def flip(bit, other):
    return bit + other - 2 * bit * other


def relative_source(depth):
    block = depth // 32
    seq, group = lax.axis_index("seq"), lax.axis_index("dp")
    index = lax.broadcasted_iota(jnp.int32, (depth, 1), 0)
    row, place, side = index % block, (index // block) % 16, index // (16 * block)
    x = flip(seq % 2, place // 8)
    y = flip((seq // 2) % 2, (place // 4) % 2)
    z = flip((seq // 4) % 2, (place // 2) % 2) + 2 * flip(seq // 8, place % 2)
    return ((((group + side) % 2) * 16 + z * 4 + y * 2 + x) * block + row)


def middle_kernel(
    compact, count, oloc_ref, oread_ref, start_ref, gate_ref, ogain_ref, x_ref, ext_ref, mgain_ref, ograd_ref,
    maps_ref, wout_hbm, wgate_hbm, wup_hbm, wdown_hbm,
    block_ref, dout_ref, part_ref, dresid_ref, dmgain_ref, dogain_ref,
    *refs,
):
    if compact:
        products, (own_out, got_out, after_ref) = refs[: 2 * GROUPS], refs[2 * GROUPS : 2 * GROUPS + 3]
        refs = refs[2 * GROUPS + 3 :]
        gated_ref, hidden_ref, dgate_ref, dup_ref, doutgate_ref, mlp_ref, branch_ref = refs[:7]
        gated_got, hidden_got, dgate_got, dup_got, doutgate_got, own_ref, other_ref, got_ref = refs[7:15]
        other_edge, got_edge, core_sem, chunk_sem, inbox, outbox, landed = refs[15:22]
        carry_sems, staged, stage_sem, refs = refs[22:26], refs[26 : 26 + 2 * GROUPS], refs[26 + 2 * GROUPS], refs[27 + 2 * GROUPS :]
    else:
        gated_ref, hidden_ref, dgate_ref, dup_ref, doutgate_ref, mlp_ref, branch_ref = refs[:7]
        refs = refs[7:]
    wout, wgate, wup, wdown, down_ref, dmlp_ref, sem_out, sems = refs
    heads, rows, width = oread_ref.shape
    depth = x_ref.shape[1]
    chunks = hidden_ref.shape[1] // CHUNK
    fetch_out = pltpu.make_async_copy(wout_hbm, wout, sem_out)
    fetch_out.start()

    def lanes_of(c):
        return pl.ds(pl.multiple_of(c * CHUNK, CHUNK), CHUNK)

    def fetches(c):
        slot = c % RING
        return (
            pltpu.make_async_copy(wgate_hbm.at[:, lanes_of(c)], wgate.at[slot], sems.at[slot, 0]),
            pltpu.make_async_copy(wup_hbm.at[:, lanes_of(c)], wup.at[slot], sems.at[slot, 1]),
            pltpu.make_async_copy(wdown_hbm.at[lanes_of(c), :], wdown.at[slot], sems.at[slot, 2]),
        )

    for c in range(RING):
        for copy in fetches(c):
            copy.start()
    core = {"dp": 1 - lax.axis_index("dp")}

    def to_core(source, target, sems, index):
        return pltpu.make_async_remote_copy(
            src_ref=source,
            dst_ref=target,
            send_sem=sems.at[(0,) + index],
            recv_sem=sems.at[(1,) + index],
            device_id=core,
            device_id_type=MESH,
        )

    if compact:
        barrier = greet_group(count)
        pl.semaphore_signal(barrier, inc=1, device_id=core, device_id_type=MESH)
        give, scan, take = carry_steps(
            count, heads, True, part_ref, maps_ref, inbox, outbox, landed, carry_sems
        )
        half = depth // 2
        lane = lax.broadcasted_iota(jnp.int32, (depth, depth), 1)
        chosen = (lane == relative_source(depth)).astype(BF16)
        swaps = []

        def turn(at, value, index):
            turned = mm(chosen, value, NT).astype(BF16)
            cut = slice(at, at + value.shape[0])
            own_ref[:, cut] = turned[:half]
            other_ref[:, cut] = turned[half:]
            swap(other_ref.at[:, cut], got_ref.at[:, cut], index)

        def turn_tokens():
            value = jnp.concatenate([ext_ref[pl.ds(HALO, rows), :], ext_ref[0:HALO, :]], axis=0)
            turned = mm(chosen, value, NT).astype(BF16)
            own_out[...] = turned[:half]
            other_edge[...] = turned[half:]
            swap(other_edge, got_edge, 3)

        def swap(source, target, index):
            swaps.append(to_core(source, target, core_sem, (index,)))
            swaps[-1].start()

    ogain = ogain_ref[...]
    for h in range(heads):
        lanes = slice(h * width, (h + 1) * width)
        out = oloc_ref[:, lanes] + mm(oread_ref[h], start_ref[h])
        dout_ref[:, lanes] = out
        gate = gate_ref[:, lanes]
        r = lax.rsqrt(jnp.mean(out * out, axis=-1, keepdims=True) + 1e-05)
        gated_ref[:, lanes] = (out * r * ogain * (gate * sigmoid(gate))).astype(BF16)
    fetch_out.wait()
    resid = x_ref[...].astype(F32) + mm(gated_ref[...], wout[...])
    dresid_ref[...] = resid
    r = lax.rsqrt(jnp.mean(resid * resid, axis=-1, keepdims=True) + 1e-06)
    mlp_ref[...] = (resid * r * mgain_ref[...]).astype(BF16)
    if compact:
        pl.semaphore_wait(barrier, count)
        swap(gated_ref, gated_got, 4)
    down_ref[...] = jnp.zeros_like(down_ref)
    dmlp_ref[...] = jnp.zeros_like(dmlp_ref)

    def chunk_swaps(c):
        pairs = ((hidden_ref, hidden_got), (dgate_ref, dgate_got), (dup_ref, dup_got))
        return [
            to_core(own.at[:, lanes_of(c)], got.at[:, lanes_of(c)], chunk_sem, (c, i))
            for i, (own, got) in enumerate(pairs)
        ]

    def one(c, carry):
        slot = c % RING
        for copy in fetches(c):
            copy.wait()
        mlp, ograd = mlp_ref[...], ograd_ref[...]
        lanes = lanes_of(c)
        gate, up = mm(mlp, wgate[slot]), mm(mlp, wup[slot])
        d_hidden = mm(ograd, wdown[slot], NT)
        s = sigmoid(gate)
        act = gate * s
        hidden = (act * up).astype(BF16)
        d_gate = (d_hidden * up * (s + act * (1.0 - s))).astype(BF16)
        d_up = (d_hidden * act).astype(BF16)
        hidden_ref[:, lanes] = hidden
        dgate_ref[:, lanes] = d_gate
        dup_ref[:, lanes] = d_up
        if compact:
            for copy in chunk_swaps(c):
                copy.start()
        down_ref[...] += mm(hidden, wdown[slot])
        dmlp_ref[...] += mm(d_gate, wgate[slot], NT) + mm(d_up, wup[slot], NT)

        @pl.when(c + RING < chunks)
        def _():
            for copy in fetches(c + RING):
                copy.start()

        return carry

    lax.fori_loop(0, chunks, one, 0)
    resid = dresid_ref[...]
    block_ref[...] = (resid + down_ref[...]).astype(BF16)
    grad = dmlp_ref[...]
    unit, pulled = norm_pull(resid, mgain_ref[...], grad)
    dmgain_ref[...] = jnp.sum(grad * unit, axis=0, keepdims=True)
    d_resid = ograd_ref[...].astype(F32) + pulled
    dresid_ref[...] = d_resid
    branch_ref[...] = d_resid.astype(BF16)
    dogain = jnp.zeros((1, width), F32)
    for h in range(heads):
        lanes = slice(h * width, (h + 1) * width)
        grad = mm(branch_ref[...], wout[lanes, :], NT)
        out = dout_ref[:, lanes]
        gate = gate_ref[:, lanes]
        r = lax.rsqrt(jnp.mean(out * out, axis=-1, keepdims=True) + 1e-05)
        s = sigmoid(gate)
        unit = out * r
        doutgate_ref[:, lanes] = (grad * unit * ogain * (s + gate * s * (1.0 - s))).astype(BF16)
        through = grad * (gate * s)
        dogain += jnp.sum(through * unit, axis=0, keepdims=True)
        through = through * ogain
        dout = r * (through - unit * jnp.mean(unit * through, axis=-1, keepdims=True))
        dout_ref[:, lanes] = dout
        part_ref[h] = mm(oread_ref[h], dout, TN).astype(BF16)
        if compact:
            give(h)
    dogain_ref[...] = dogain
    if compact:
        turn(0, mlp_ref[...], 0)
        turn(rows, ograd_ref[...], 1)
        swap(doutgate_ref, doutgate_got, 5)
        turn(2 * rows, branch_ref[...], 2)
        turn_tokens()

        def arrived(c, carry):
            for copy in chunk_swaps(c):
                copy.wait()
            return carry

        lax.fori_loop(0, chunks, arrived, 0)
        rhs_own = (dgate_ref, dup_ref, hidden_ref, gated_ref, doutgate_ref)
        rhs_got = (dgate_got, dup_got, hidden_got, gated_got, doutgate_got)
        for copy in swaps[:3]:
            copy.wait()
        lhs_own, lhs_got = (own_ref, own_out), (got_ref, got_edge)
        targets = [staged[2 * group : 2 * group + 2] for group in range(GROUPS)]
        early_products(lhs_own, lhs_got, rhs_own, rhs_got, targets, (0, 1, 2))
        outgoing = [
            pltpu.make_async_copy(source, target, stage_sem.at[i])
            for i, (source, target) in enumerate(zip(staged, products))
        ]
        for copy in outgoing[: 2 * GROUPS - 2]:
            copy.start()
        scan()
        for copy in swaps[3:]:
            copy.wait()
        early_products(lhs_own, lhs_got, rhs_own, rhs_got, targets, (3, 4))
        for copy in outgoing[2 * GROUPS - 2 :]:
            copy.start()
        got_out[...] = got_edge[...]
        for copy in outgoing:
            copy.wait()
        take()
        after_ref[...] = landed[...]


def early_products(lhs_own, lhs_got, rhs_own, rhs_got, targets, which):
    tokens = rhs_own[0].shape[0]
    sizes = [rhs.shape[1] for rhs in rhs_own]
    sides = (0, 0, 1, 2, 3)
    for group in range(GROUPS):
        for sending in (True, False):
            turned = {}
            for job in range(JOBS):
                begin = (group * JOBS + job) * JOB
                for index, column, offset, width in column_pieces(sizes, begin, begin + JOB):
                    if index not in which:
                        continue
                    side = sides[index]
                    if side not in turned:
                        cut = slice(side % 3 * tokens, (side % 3 + 1) * tokens)
                        turned[side] = [
                            half_rows(lhs[side // 3], EARLY_LINKS[group], sending, cut) for lhs in (lhs_own, lhs_got)
                        ]
                    lanes = slice(column, column + width)
                    total = mm(turned[side][0], rhs_own[index][:, lanes]) + mm(
                        turned[side][1], rhs_got[index][:, lanes]
                    )
                    targets[group][0 if sending else 1][job, :, offset : offset + width] = total.astype(BF16)


def middle(
    compact, count, oloc, oread, start, gate_pre, out_gain, x, ext_b, mlp_gain, out_grad, maps,
    w_out, w_gate, w_up, w_down,
):
    heads, rows, width = oread.shape
    depth = x.shape[1]
    ff = w_gate.shape[1]
    out = jax.ShapeDtypeStruct
    vmem, hbm = pl.BlockSpec(memory_space=pltpu.VMEM), pl.BlockSpec(memory_space=pl.ANY)
    columns = heads * width
    chunks = ff // CHUNK
    half = depth // 2
    outs = [
        ((rows, depth), BF16), ((rows, columns), F32), ((heads, width, width), BF16), ((rows, depth), F32),
        ((1, depth), F32), ((1, width), F32),
    ]
    rhs = [((rows, columns), BF16)] + [((rows, ff), BF16)] * 3 + [((rows, columns), BF16)]
    kept = rhs + [((rows, depth), BF16)] * 2
    scratch = []
    dma = pltpu.SemaphoreType.DMA
    if compact:
        product = ((JOBS, half // 2, JOB), BF16)
        outs += [product] * (2 * GROUPS) + [((half, rows + HALO), BF16)] * 2
        outs += [((heads, width, width), BF16), ((rows, columns), BF16)]
        buffers = kept[:4] + kept[5:] + rhs + [((half, 3 * rows), BF16)] * 3 + [((half, rows + HALO), BF16)] * 2
        scratch += [pltpu.VMEM(*buffer) for buffer in buffers] + [dma((2, 6)), dma((2, chunks, 3))]
        scratch += carry_scratch(count, heads, width, width)
        scratch += [pltpu.VMEM(*product)] * (2 * GROUPS) + [dma((2 * GROUPS,))]
    else:
        outs += kept
    scratch += [
        pltpu.VMEM(w_out.shape, BF16),
        pltpu.VMEM((RING, depth, CHUNK), BF16),
        pltpu.VMEM((RING, depth, CHUNK), BF16),
        pltpu.VMEM((RING, CHUNK, depth), BF16),
        pltpu.VMEM((rows, depth), F32),
        pltpu.VMEM((rows, depth), F32),
        dma,
        dma((RING, 3)),
    ]

    def kernel(*refs):
        if not compact:
            middle_kernel(compact, count, *refs)
            return
        late = 20 + 2 * GROUPS + 3
        rest = refs[late + 1 :]
        middle_kernel(compact, count, *refs[:late], *rest[:4], refs[late], *rest[4:])

    params = {"collective_id": 3, "has_side_effects": True} if compact else {}
    return pl.pallas_call(
        kernel,
        in_specs=[vmem] * 10 + [hbm] * 4,
        out_specs=[hbm if compact and shape == product else vmem for shape in outs],
        out_shape=[out(*shape) for shape in outs],
        scratch_shapes=scratch,
        compiler_params=pltpu.CompilerParams(vmem_limit_bytes=VMEM_LIMIT, **params),
        cost_estimate=cost(30),
        name="middle",
    )(
        oloc, oread, start, gate_pre, out_gain[None, :], x, ext_b, mlp_gain[None, :], out_grad, maps,
        w_out, w_gate, w_up, w_down,
    )


def reduce_kernel(
    heads, arr_a, arr_b, arr_c, keep_a, keep_b, keep_c, own_ref, got_ref, rhs_ref, tq_ref, tk_ref, tv_ref, attn_ref, mlp_ref, ogain_ref,
    misc_ref, rates_ref, edge_ref, rim_ref, again_ref,
    gate_out, up_out, down_out, out_out, outgate_out, q_out, k_out, v_out, tq_out, tk_out, tv_out, rest_out,
    edge_out,
    fetched, e_keep, e_send, e_got2, e_got3, e_got4,
    rhs_got, lhs_ref, l_first, l_send, l_keep, l_got1, l_got2, l_got3, l_got4, small_sum, small_send, small_got, rim_got,
    dp_sem, e_sem, l_sem, s_sem, f_sem,
):
    seq = lax.axis_index("seq")
    group = lax.axis_index("dp")
    count = lax.axis_size("seq")
    x, y, z = seq % 2, (seq // 2) % 2, seq // 4
    near = (seq + 1 - 2 * x, seq + 2 - 4 * y)
    low_z = seq + 4 - 8 * (z % 2)
    high_z = seq + 8 - 16 * (z // 2)

    def at(place):
        return {"dp": group, "seq": place}

    core = {"dp": 1 - group, "seq": seq}
    before, behind = lax.rem(seq + count - 1, count), lax.rem(seq + 1, count)

    def send(source, target, sems, index, device):
        return pltpu.make_async_remote_copy(
            src_ref=source,
            dst_ref=target,
            send_sem=sems.at[(0,) + index],
            recv_sem=sems.at[(1,) + index],
            device_id=device,
            device_id_type=MESH,
        )

    def fetches(i):
        return [
            pltpu.make_async_copy(source.at[i], fetched.at[j, i], f_sem.at[j, i])
            for j, source in enumerate((arr_a, arr_b, arr_c, keep_a, keep_b, keep_c))
        ]

    def fetch(i, carry):
        for copy in fetches(i):
            copy.start()
        return carry

    lax.fori_loop(0, JOBS, fetch, 0)
    barrier = pltpu.get_barrier_semaphore()
    everyone = [core] + [at(place) for place in (near[0], near[1], low_z, high_z, before, behind)]
    for device in everyone:
        pl.semaphore_signal(barrier, inc=1, device_id=device, device_id_type=MESH)
    rim = send(rim_ref, rim_got, dp_sem, (1,), at(before))
    hops = [core, at(high_z), at(low_z), at(near[0]), at(near[1])]

    def hop(step):
        return send(small_send.at[step], small_got.at[step], s_sem, (step,), hops[step])

    def next_hop(step):
        hop(step - 1).wait_recv()
        total = small_send[step - 1].astype(F32) + small_got[step - 1].astype(F32)
        if step < len(hops):
            small_send[step] = total.astype(BF16)
            hop(step).start()
        else:
            small_sum[1] = total

    depth = tq_ref.shape[1]
    small_sum[0, 0:KW] = tq_ref[...]
    for half in range(2):
        lanes = pl.ds(half * depth, depth)
        small_sum[0, KW * (1 + half) : KW * (2 + half)] = tk_ref[:, lanes]
        small_sum[0, KW * (3 + half) : KW * (4 + half)] = tv_ref[:, lanes]
    small_sum[0, 5 * KW : 6 * KW] = jnp.zeros((KW, depth), F32)
    small_sum[0, 5 * KW : 5 * KW + 1] = attn_ref[...]
    small_sum[0, 5 * KW + 1 : 5 * KW + 2] = mlp_ref[...]
    gains = ogain_ref.shape[1]
    small_sum[0, 5 * KW + 2 : 5 * KW + 3, 0:gains] = ogain_ref[...]
    small_sum[0, 5 * KW + 2 : 5 * KW + 3, gains : gains + misc_ref.shape[1]] = misc_ref[...]
    small_sum[0, 6 * KW :] = rates_ref[...]
    for p in range(2):
        for side, lhs in enumerate((own_ref, got_ref)):
            for sending in range(2):
                lhs_ref[p, side, sending] = half_rows(lhs[...], LATE_LINKS[p], sending)
    small_send[0] = small_sum[0].astype(BF16)
    swap = send(rhs_ref, rhs_got, dp_sem, (0,), core)
    pl.semaphore_wait(barrier, len(everyone))
    hop(0).start()
    swap.start()
    rim.start()

    places = (near[0], near[1], low_z, high_z)
    quarter = e_got2.shape[2]
    eighth, share = quarter // 2, quarter // 4

    def exchange(p, i, stage, sent, got, sems, links):
        begin = (0, 0, quarter, quarter + eighth)[stage]
        target = places[links[p][stage]]
        return send(sent.at[p, i, pl.ds(begin, got.shape[2])], got.at[p, i], sems, (p, i, stage), at(target))

    def early(p, i, stage):
        return exchange(p, i, stage, e_send, (None, e_got2, e_got3, e_got4)[stage], e_sem, EARLY_LINKS)

    def late(p, i, stage):
        sent = l_first if stage == 0 else l_send
        return exchange(p, i, stage, sent, (l_got1, l_got2, l_got3, l_got4)[stage], l_sem, LATE_LINKS)

    def early2(i, carry):
        for copy in fetches(i):
            copy.wait()
        for p in range(GROUPS):
            total = fetched[p, i].astype(F32) + fetched[GROUPS + p, i].astype(F32)
            e_keep[p, i] = total[:quarter].astype(BF16)
            e_send[p, i, 0:quarter] = total[quarter:].astype(BF16)
            early(p, i, 1).start()
        return carry

    def onward(p, i, copy_of, keep, sent, got, stage, begin):
        copy_of(p, i, stage).wait_recv()
        rows = got.shape[2]
        half = rows // 2
        total = keep[p, i, 0:rows].astype(F32) + got[p, i].astype(F32)
        keep[p, i, 0:half] = total[:half].astype(BF16)
        sent[p, i, begin : begin + half] = total[half:].astype(BF16)
        copy_of(p, i, stage + 1).start()

    def later(i, carry, copy_of, keep, sent, got, stage, begin):
        for p in range(keep.shape[0]):
            onward(p, i, copy_of, keep, sent, got, stage, begin)
        return carry

    lax.fori_loop(0, JOBS, early2, 0)
    next_hop(1)
    swap.wait_recv()
    job = l_got1.shape[-1]
    late_jobs = LATE_JOBS // 2
    tokens = rhs_ref.shape[0]

    def product(m, p, sending):
        lanes = pl.ds(pl.multiple_of(m * job, job), job)
        total = mm(lhs_ref[p, 0, int(sending)], rhs_ref[:, lanes]) + mm(
            lhs_ref[p, 1, int(sending)], rhs_got[:, lanes]
        )
        return total[:quarter], total[quarter:]

    def late1(i, carry):
        for p in range(2):
            low, high = product(2 * i + p, p, True)
            l_first[p, i, 0:quarter] = low.astype(BF16)
            l_first[p, i, quarter : 2 * quarter] = high.astype(BF16)
            late(p, i, 0).start()
        return carry

    def late2(i, carry):
        for p in range(2):
            low, high = product(2 * i + p, p, False)
            late(p, i, 0).wait_recv()
            l_keep[p, i] = (low + l_got1[p, i, 0:quarter].astype(F32)).astype(BF16)
            l_send[p, i, 0:quarter] = (high + l_got1[p, i, quarter : 2 * quarter].astype(F32)).astype(BF16)
            late(p, i, 1).start()
        return carry

    lag = JOBS - late_jobs

    def low_turn(i, carry):
        later(i, carry, early, e_keep, e_send, e_got2, 1, quarter)

        @pl.when(i == lag)
        def _():
            next_hop(2)

        @pl.when(i < late_jobs)
        def _():
            late1(i, carry)

        return carry

    def high_turn(i, carry):
        later(i, carry, early, e_keep, e_send, e_got3, 2, quarter + eighth)

        @pl.when(i >= lag)
        def _():
            late2(i - lag, carry)

        return carry

    lax.fori_loop(0, JOBS, low_turn, 0)
    next_hop(3)
    lax.fori_loop(0, JOBS, high_turn, 0)
    next_hop(4)
    rim.wait_recv()
    inside = (seq < count - 1).astype(F32)
    _, pulled = norm_pull(edge_ref[1], again_ref[...], edge_ref[0] + inside * rim_got[...])
    edge_out[...] = (edge_ref[2] + pulled).astype(BF16)
    late_low = partial(later, copy_of=late, keep=l_keep, sent=l_send, got=l_got2, stage=1, begin=quarter)
    lax.fori_loop(0, late_jobs, late_low, 0)
    next_hop(5)
    late_high = partial(later, copy_of=late, keep=l_keep, sent=l_send, got=l_got3, stage=2, begin=quarter + eighth)
    lax.fori_loop(0, late_jobs, late_high, 0)
    early_outs = (gate_out, up_out, down_out, out_out, outgate_out)
    for i in range(JOBS):
        for p in range(GROUPS):
            early(p, i, 3).wait_recv()
            total = e_keep[p, i, 0:share].astype(F32) + e_got4[p, i].astype(F32)
            first = (p * JOBS + i) * JOB
            for output, to, begin, width in column_pieces([o.shape[1] for o in early_outs], first, first + JOB):
                early_outs[output][:, to : to + width] = total[:, begin : begin + width]
    tq_out[...] = small_sum[1, 0:KW]
    for half in range(2):
        lanes = pl.ds(half * depth, depth)
        tk_out[:, lanes] = small_sum[1, KW * (1 + half) : KW * (2 + half)]
        tv_out[:, lanes] = small_sum[1, KW * (3 + half) : KW * (4 + half)]
    rest_out[...] = small_sum[1, 5 * KW :]
    width = q_out.shape[1] // heads
    for i in range(late_jobs):
        for p in range(2):
            late(p, i, 3).wait_recv()
            total = l_keep[p, i, 0:share].astype(F32) + l_got4[p, i].astype(F32)
            for begin in range(0, job, width):
                head, part = divmod(((2 * i + p) * job + begin) // width, 5)
                if part == 0:
                    target, to = q_out, head * width
                else:
                    target, to = (k_out, v_out)[(part - 1) // 2], (2 * head + (part - 1) % 2) * width
                target[:, to : to + width] = total[:, begin : begin + width]

    def early_sent(i, carry):
        for p in range(GROUPS):
            for stage in (1, 2, 3):
                early(p, i, stage).wait_send()
        return carry

    def late_sent(i, carry):
        for p in range(2):
            for stage in (0, 1, 2, 3):
                late(p, i, stage).wait_send()
        return carry

    lax.fori_loop(0, JOBS, early_sent, 0)
    lax.fori_loop(0, late_jobs, late_sent, 0)
    swap.wait_send()
    rim.wait_send()
    for step in range(len(hops)):
        hop(step).wait_send()


def reduce_all(arrived, kept, own, got, rhs, taps, gains, rates, edge, rim, gain, ff, heads):
    half = own.shape[0] // 2
    quarter, eighth, share = half // 2, half // 4, half // 8
    count = LATE_JOBS // 2
    columns = rhs.shape[1] // 5
    job = rhs.shape[1] // LATE_JOBS
    depth = rates.shape[1]
    small_rows = 6 * KW + rates.shape[0]
    out = jax.ShapeDtypeStruct
    vmem = pl.BlockSpec(memory_space=pltpu.VMEM)

    def stages(groups, jobs, width):
        return [((groups, jobs, rows, width), BF16) for rows in (quarter, eighth, share)]

    buffers = [((2 * GROUPS, JOBS, half, JOB), BF16)]
    buffers += [((GROUPS, JOBS, quarter, JOB), BF16), ((GROUPS, JOBS, half, JOB), BF16)]
    buffers += stages(GROUPS, JOBS, JOB)
    buffers += [(rhs.shape, BF16), ((2, 2, 2, half, own.shape[1]), BF16)] + [((2, count, half, job), BF16)] * 2 + [((2, count, quarter, job), BF16)]
    buffers += [((2, count, half, job), BF16)] + stages(2, count, job)
    buffers += [((2, small_rows, depth), F32)] + [((5, small_rows, depth), BF16)] * 2 + [(rim.shape, F32)]
    dma = pltpu.SemaphoreType.DMA
    shapes = [(share, ff)] * 3 + [(share, columns)] * 3 + [(share, 2 * columns)] * 2
    shapes += [tap.shape for tap in taps] + [(small_rows - 5 * KW, depth)]
    return pl.pallas_call(
        partial(reduce_kernel, heads),
        in_specs=[pl.BlockSpec(memory_space=pl.ANY)] * (2 * GROUPS) + [vmem] * 14,
        out_specs=[vmem] * 13,
        out_shape=[out(shape, F32) for shape in shapes] + [out(rim.shape, BF16)],
        scratch_shapes=[pltpu.VMEM(shape, kind) for shape, kind in buffers]
        + [dma((2, 2)), dma((2, GROUPS, JOBS, 4)), dma((2, 2, count, 4)), dma((2, 5)), dma((2 * GROUPS, JOBS))],
        compiler_params=pltpu.CompilerParams(
            collective_id=2, has_side_effects=True, vmem_limit_bytes=VMEM_LIMIT
        ),
        cost_estimate=cost(90),
        name="reduce_all",
    )(*arrived, *kept, own, got, rhs, *taps, *gains, rates, edge, rim, gain)


def finish_kernel(marks, grad_ref, edge_ref, rest_ref, *refs):
    count = (len(refs) - 8) // 2
    sources, (grad_out, *outs) = refs[:count], refs[count:]
    rows = grad_ref.shape[0]
    grad_out[0 : rows - HALO, :] = grad_ref[0 : rows - HALO, :]
    grad_out[rows - HALO :, :] = edge_ref[...]
    for source, target in zip(sources, outs):
        target[...] = source[...]
    again, mlp, beta, rate, gain, bias, decay = outs[count:]
    rest = rest_ref[...]
    share, depth = again.shape[1], rest.shape[1]
    place = lax.axis_index("dp") * lax.axis_size("seq") + lax.axis_index("seq")
    own = pltpu.roll(rest, lax.rem(depth - place * share, depth), 1)[:, :share]
    again[...] = own[0:1]
    mlp[...] = own[1:2]
    beta[...] = own[4 : 4 + beta.shape[0]]
    rate[...] = own[4 + beta.shape[0] :]
    for target, begin in zip((gain, bias, decay), marks):
        target[...] = rest_ref[2:3, begin : begin + target.shape[1]]


def finish(input_grad, edge_grad, rest, values, share, width, heads):
    wide, narrow = heads * REFLECTS, heads
    shapes = [(value.shape, value.dtype) for value in values]
    shapes += [(shape, F32) for shape in [(1, share)] * 2 + [(wide, share), (narrow, share), (1, width), (1, wide), (1, narrow)]]
    out = jax.ShapeDtypeStruct
    vmem = pl.BlockSpec(memory_space=pltpu.VMEM)
    return pl.pallas_call(
        partial(finish_kernel, (0, width, width + wide)),
        in_specs=[vmem] * (3 + len(values)),
        out_specs=[vmem] * (1 + len(shapes)),
        out_shape=[out(input_grad.shape, BF16)] + [out(*shape) for shape in shapes],
        compiler_params=pltpu.CompilerParams(vmem_limit_bytes=VMEM_LIMIT),
        cost_estimate=cost(3),
        name="finish",
    )(input_grad, edge_grad, rest, *values)


def dot32(a, b, dims=NN):
    return lax.dot_general(a, b, dims, preferred_element_type=F32)


def swap_core(value):
    count = lax.axis_size("dp")
    return lax.ppermute(value, "dp", [(i, (i + 1) % count) for i in range(count)])


def neighbour_route(bit):
    return [(i, i ^ bit) for i in range(16)]


def by_head(field, heads, begin, size):
    rows = field.shape[0]
    return field.reshape(rows, heads, -1)[:, :, begin : begin + size].reshape(rows, heads * size)


def per_device(
    block_input, lengths, attn_gain, w_query, w_key, w_value, w_outgate, w_beta, w_decay, beta_bias,
    decay_rate, conv_query, conv_key, conv_value, out_gain, w_out, mlp_gain, w_gate, w_up, w_down,
    out_grad,
):
    rows, depth = block_input.shape
    heads = decay_rate.shape[0]
    width = out_gain.shape[0]
    count = lax.axis_size("seq")
    seq = lax.axis_index("seq")
    group = lax.axis_index("dp")
    compact = count == 16
    wide = heads * REFLECTS
    ext_b, raw, live, acol, arow, halo, w_rates, rate = rates_forward(
        lengths, block_input, attn_gain, w_beta, w_decay, beta_bias, decay_rate, heads
    )
    taps = (conv_query, conv_key, conv_value)
    pre, gate_pre, oloc, oread, *saved, start, all_maps = mixer_forward(
        ext_b, w_query, w_key, w_value, w_outgate, taps, live, acol, arow, heads, width, count
    )
    block_output, d_out, part, d_resid, grad_mlp_gain, grad_out_gain, *rest = middle(
        compact, count, oloc, oread, start, gate_pre, out_gain, block_input, ext_b, mlp_gain, out_grad,
        all_maps, w_out, w_gate, w_up, w_down,
    )
    if compact:
        products, (own_l, got_l, after, d_outgate_b) = rest[: 2 * GROUPS], rest[2 * GROUPS :]
        arrived = [
            lax.ppermute(sent, "seq", neighbour_route(1 << links[0])) for sent, links in zip(products[::2], EARLY_LINKS)
        ]
    else:
        gated_b, hidden_b, d_gate_b, d_up_b, d_outgate_b, mlp_b, d_branch_b = rest
        after = carry_back(part, all_maps, count)
    d_all, d_tap_q, d_tap_k, d_tap_v, aux = mixer_backward(
        pre, taps, live, acol, arow, saved, start, after, d_out
    )
    input_grad, edge, rim, grad_attn_gain, grad_rates, misc = input_pull(
        d_all, d_outgate_b, (w_query, w_key, w_value, w_outgate), aux, raw, live, rate, w_rates, ext_b,
        block_input, halo, attn_gain, d_resid, heads,
    )
    last = width + wide + heads
    gains = (grad_attn_gain, grad_mlp_gain, grad_out_gain, misc)
    d_taps = (d_tap_q, d_tap_k, d_tap_v)
    devices = count * lax.axis_size("dp")
    share = depth // devices
    if compact:
        sums = reduce_all(
            arrived, products[1::2], own_l, got_l, d_all, d_taps, gains, grad_rates,
            edge, rim, attn_gain[None, :], w_gate.shape[1], heads,
        )
        trunk, taps_out, rest, edge_grad = sums[5:8], sums[8:11], sums[11], sums[12]
    else:
        normed_e = jnp.concatenate([ext_b[HALO:], ext_b[:HALO]], axis=0)
        normed_b = ext_b[HALO:]
        xf = block_input.astype(F32)
        tail = edge[0] + lax.ppermute(rim, "seq", [(i, i - 1) for i in range(1, count)])
        _, pulled = norm_pull(edge[1], attn_gain[None, :], tail)
        edge_grad = (edge[2] + pulled).astype(BF16)
        line = jnp.pad(jnp.concatenate(gains[2:], axis=1), ((0, 0), (0, depth - width - 128)))
        line = jnp.concatenate([*gains[:2], line, jnp.zeros((1, depth), F32)], axis=0)
        small = lax.psum(d_taps + (line, grad_rates), ("dp", "seq"))
        taps_out, rest = small[:3], jnp.concatenate(small[3:], axis=0)
        trunk = [by_head(d_all, heads, begin * width, size * width) for begin, size in ((0, 1), (1, 2), (3, 2))]
        pairs = zip(
            (mlp_b, mlp_b, out_grad, d_branch_b, normed_b) + (normed_e,) * 3, (d_gate_b, d_up_b, hidden_b, gated_b, d_outgate_b) + tuple(trunk)
        )
        sums = [
            lax.psum_scatter(dot32(lhs, rhs, TN), ("dp", "seq"), scatter_dimension=0, tiled=True)
            for lhs, rhs in pairs
        ]
        trunk = sums[5:]
    values = (block_output, *trunk, sums[4], *taps_out, sums[0], sums[1], sums[3], sums[2])
    done = finish(input_grad, edge_grad, rest, values, share, width, heads)
    (
        input_grad, block_output, g_query, g_key, g_value, g_outgate, g_conv_q, g_conv_k, g_conv_v, g_gate, g_up, g_out, g_down,
        g_attn, g_mlp, g_beta, g_decay, g_gain, g_bias, g_rate,
    ) = done
    return (
        block_output,
        input_grad,
        g_attn[0],
        g_query,
        g_key,
        g_value,
        g_outgate,
        g_beta.T,
        g_decay.T,
        g_bias[0],
        g_rate[0],
        g_conv_q,
        g_conv_k,
        g_conv_v,
        g_gain[0],
        g_out.T,
        g_mlp[0],
        g_gate,
        g_up,
        g_down.T,
    )


def solution(mesh):
    tokens = P(("dp", "seq"), None)
    column = P(None, ("dp", "seq"))
    vector = P(("dp", "seq"))
    in_specs = (tokens, P("dp", None)) + (P(),) * 18 + (tokens,)
    out_specs = (
        (tokens, tokens, vector)
        + (tokens,) * 6
        + (P(),) * 6
        + (column, vector, tokens, tokens, column)
    )
    return jax.shard_map(
        per_device, mesh=mesh, in_specs=in_specs, out_specs=out_specs, check_vma=False
    )
```
